32 devices in a mesh: dp: 16 (over z, y, x), mp: 2 (over core).
Axes of the slice: x: 2, y: 2, z: 4, core: 2. Of those that a mesh axis runs over, the one named last changes fastest.
Arguments:
- decoder_in: bfloat16 [16, 512, 768], P('dp'), may hold values from -6 to 6
- encoder_out: bfloat16 [16, 1024, 768], P(None, 'dp'), may hold values from -6 to 6
- lengths: int32 [16], replicated, may hold values from 256 to 1024, as said below
- key_mask: int32 [16, 1024], replicated, may hold values 0 or 1
- assign: int32 [16], replicated, may hold values from 0 to 15, each once
- buckets: int32 [512, 512], replicated, may hold values from 0 to 31, as said below
- norm_one: float32 [768], replicated, may hold values from 0.5 to 1.5
- norm_two: float32 [768], replicated, may hold values from 0.5 to 1.5
- norm_three: float32 [768], replicated, may hold values from 0.5 to 1.5
- self_query: float32 [768, 768], P('dp', 'mp'), may hold values from -0.109375 to 0.109375
- self_key: float32 [768, 768], P('dp', 'mp'), may hold values from -0.109375 to 0.109375
- self_value: float32 [768, 768], P('dp', 'mp'), may hold values from -0.21875 to 0.21875
- self_output: float32 [768, 768], P('mp', 'dp'), may hold values from -0.875 to 0.875
- cross_query: float32 [768, 768], P('dp', 'mp'), may hold values from -0.109375 to 0.109375
- cross_key: float32 [768, 768], P('dp', 'mp'), may hold values from -0.109375 to 0.109375
- cross_value: float32 [768, 768], P('dp', 'mp'), may hold values from -0.21875 to 0.21875
- cross_output: float32 [768, 768], P('mp', 'dp'), may hold values from -1.75 to 1.75
- ffn_gate: float32 [768, 2048], P('dp', 'mp'), may hold values from -0.21875 to 0.21875
- ffn_up: float32 [768, 2048], P('dp', 'mp'), may hold values from -0.21875 to 0.21875
- ffn_down: float32 [2048, 768], P('mp', 'dp'), may hold values from -0.125 to 0.125
- bias_table: float32 [32, 12], P(None, 'mp'), may hold values from -4 to 4
- cotangent: bfloat16 [16, 512, 768], P('dp'), may hold values from -6 to 6
Outputs:
- layer_out: bfloat16 [16, 512, 768], P('dp')
- decoder_grad: float32 [16, 512, 768], P('dp')
- encoder_grad: bfloat16 [16, 1024, 768], P(None, 'dp', 'mp')
- grad_norm_one: float32 [768], replicated
- grad_norm_two: float32 [768], replicated
- grad_norm_three: float32 [768], replicated
- grad_self_query: float32 [768, 768], P('dp', 'mp')
- grad_self_key: float32 [768, 768], P('dp', 'mp')
- grad_self_value: float32 [768, 768], P('dp', 'mp')
- grad_self_output: float32 [768, 768], P('mp', 'dp')
- grad_cross_query: float32 [768, 768], P('dp', 'mp')
- grad_cross_key: float32 [768, 768], P('dp', 'mp')
- grad_cross_value: float32 [768, 768], P('dp', 'mp')
- grad_cross_output: float32 [768, 768], P('mp', 'dp')
- grad_ffn_gate: float32 [768, 2048], P('dp', 'mp')
- grad_ffn_up: float32 [768, 2048], P('dp', 'mp')
- grad_ffn_down: float32 [2048, 768], P('mp', 'dp')
- grad_bias_table: float32 [32, 12], P(None, 'mp')
The draws below stay inside these ranges and needn't reach their ends.
Inputs may be any that keep to these rules, and one draw needn't show every extreme that they name: `lengths`: every example's encoder length; the longest is exactly 1024. `assign`: each example is held by exactly one slot. `buckets`: entry (i, j) depends only on max(i - j, 0).
All inputs are finite; a program needn't handle non-finite values.
Results may differ from the reference program's by a relative error of at most 0.024.
The reference program's roundings to bfloat16 on the way count: a program that leaves them out, or rounds other values in their place, can miss the bound.
Values may be sent and summed in bfloat16 or wider, within the bound.
No kernel may reach another device: no remote copies, remote signals or barrier semaphores. Data moves between devices by JAX's collectives and lax.ppermute only.
A program may use at most 256 MiB of HBM per device.

```python
import math
import jax
import jax.numpy as jnp
from jax import lax

D = 768
HEADS = 12
HEAD_DIM = 64
FF = 2048
BUCKETS = 32
TGT = 512
EXAMPLES = 16
ENC_CAP = 1024


def draw_lengths(key, part):
    base = jax.random.randint(key, (EXAMPLES,), ENC_CAP // 4, ENC_CAP + 1)
    longest = jax.random.randint(jax.random.fold_in(key, 11), (), 0, EXAMPLES)
    return jnp.where(jnp.arange(EXAMPLES) == longest, ENC_CAP, base).astype(jnp.int32)


def draw_buckets(key, part):
    exact = BUCKETS // 2
    limits = [int(math.ceil(exact * (128.0 / exact) ** (step / (BUCKETS - exact)))) for step in range(1, BUCKETS - exact)]
    rows_index = jnp.arange(TGT, dtype=jnp.int32)
    distance = jnp.maximum(rows_index[:, None] - rows_index[None, :], 0)
    larger = jnp.zeros((TGT, TGT), jnp.int32)
    for bound in limits:
        larger = larger + (distance >= bound).astype(jnp.int32)
    drawn = jnp.where(distance < exact, distance, exact + larger)
    labels = jax.random.permutation(key, BUCKETS).astype(jnp.int32)
    return labels[drawn].astype(jnp.int32)


def with_ends(array, own_key, low, largest):
    longest = array.shape.index(max(array.shape))
    spots = []
    for shift in (0, 1):
        where = [jax.random.randint(jax.random.fold_in(own_key, axis), (), 0, length) for axis, length in enumerate(array.shape)]
        where[longest] = (where[longest] + shift) % array.shape[longest]
        spots.append(tuple(where))
    return array.at[spots[0]].set(low).at[spots[1]].set(largest)


def block_levels(own_key, shape, cuts, smallest, top_value):
    level, own = 1.0, jax.random.fold_in(own_key, 6)
    for position, blocks in cuts:
        draws = jnp.exp(jax.random.uniform(jax.random.fold_in(own, position), (blocks,), jnp.float32, smallest / len(cuts), top_value / len(cuts)))
        level = level * jnp.repeat(draws, shape[position] // blocks).reshape([-1 if axis == position else 1 for axis in range(len(shape))])
    return level


def noise(rng, dims, width, most, shards=(), held_as=jnp.bfloat16):
    factor_of = block_levels(rng, dims, shards, -0.22, 0.18) if shards else 1.0
    entries = jax.random.normal(rng, dims, jnp.float32) * width * factor_of
    return jnp.minimum(jnp.maximum(entries, -most), most).astype(held_as)


def setup_inputs(seed: int = 0) -> dict:
    seeds = jax.random.split(jax.random.key(seed), 23)
    return {
        "decoder_in": noise(seeds[0], (EXAMPLES, TGT, D), 1.0, 6.0, ((0, 16),)),
        "encoder_out": noise(seeds[1], (EXAMPLES, ENC_CAP, D), 1.0, 6.0, ((1, 16),)),
        "lengths": draw_lengths(jax.random.fold_in(seeds[22], 71), 0),
        "key_mask": with_ends((jax.random.randint(seeds[3], (EXAMPLES, ENC_CAP), 0, 8) < 7).astype(jnp.int32), jax.random.fold_in(seeds[3], 1), 0, 1),
        "assign": jax.random.permutation(seeds[4], EXAMPLES).astype(jnp.int32),
        "buckets": draw_buckets(jax.random.fold_in(seeds[22], 71), 0),
        "norm_one": jnp.clip(1.0 + 0.1 * jax.random.normal(seeds[6], (D,), jnp.float32), 0.5, 1.5),
        "norm_two": jnp.clip(1.0 + 0.1 * jax.random.normal(seeds[7], (D,), jnp.float32), 0.5, 1.5),
        "norm_three": jnp.clip(1.0 + 0.1 * jax.random.normal(seeds[8], (D,), jnp.float32), 0.5, 1.5),
        "self_query": noise(seeds[9], (D, HEADS * HEAD_DIM), (4 * D) ** -0.5, 0.109375, ((0, 16), (1, 2)), jnp.float32),
        "self_key": noise(seeds[10], (D, HEADS * HEAD_DIM), (4 * D) ** -0.5, 0.109375, ((0, 16), (1, 2)), jnp.float32),
        "self_value": noise(seeds[11], (D, HEADS * HEAD_DIM), D ** -0.5, 0.21875, ((0, 16), (1, 2)), jnp.float32),
        "self_output": noise(seeds[12], (HEADS * HEAD_DIM, D), (D // 16) ** -0.5, 0.875, ((0, 2), (1, 16)), jnp.float32),
        "cross_query": noise(seeds[13], (D, HEADS * HEAD_DIM), (4 * D) ** -0.5, 0.109375, ((0, 16), (1, 2)), jnp.float32),
        "cross_key": noise(seeds[14], (D, HEADS * HEAD_DIM), (4 * D) ** -0.5, 0.109375, ((0, 16), (1, 2)), jnp.float32),
        "cross_value": noise(seeds[15], (D, HEADS * HEAD_DIM), D ** -0.5, 0.21875, ((0, 16), (1, 2)), jnp.float32),
        "cross_output": noise(seeds[16], (HEADS * HEAD_DIM, D), (D // 64) ** -0.5, 1.75, ((0, 2), (1, 16)), jnp.float32),
        "ffn_gate": noise(seeds[17], (D, FF), D ** -0.5, 0.21875, ((0, 16), (1, 2)), jnp.float32),
        "ffn_up": noise(seeds[18], (D, FF), D ** -0.5, 0.21875, ((0, 16), (1, 2)), jnp.float32),
        "ffn_down": noise(seeds[19], (FF, D), FF ** -0.5, 0.125, ((0, 2), (1, 16)), jnp.float32),
        "bias_table": noise(seeds[20], (BUCKETS, HEADS), 0.7, 4.0, ((1, 2),), jnp.float32),
        "cotangent": noise(seeds[21], (EXAMPLES, TGT, D), 1.0, 6.0, ((0, 16),)),
    }


@jax.custom_vjp
def low(v):
    return lax.optimization_barrier(v.astype(jnp.bfloat16)).astype(jnp.float32)

@jax.custom_vjp
def low_back(v):
    return v

def low_keep(v):
    return (low(v), None)

def low_pass(kept, grad):
    return (grad,)

def back_keep(v):
    return (v, None)

def back_low(kept, grad):
    return (low(grad),)
low.defvjp(low_keep, low_pass)
low_back.defvjp(back_keep, back_low)
HIGH = lax.Precision.HIGHEST
EPS = 1e-06
NEGATIVE = -1000000000.0

def rms_norm(value, gain):
    return value * lax.rsqrt(lax.optimization_barrier(jnp.mean(value * value, axis=-1, keepdims=True)) + EPS) * gain

def project(value, weight):
    return jnp.dot(value, weight, precision=HIGH)

def attend(query, keys, values, extra, valid):
    tokens = query.shape[0]
    length = keys.shape[0]
    query_heads = query.reshape(tokens, HEADS, HEAD_DIM)
    key_heads = keys.reshape(length, HEADS, HEAD_DIM)
    value_heads = values.reshape(length, HEADS, HEAD_DIM)
    scores = low_back(jnp.einsum('thd,shd->hts', query_heads, key_heads, precision=HIGH)) + extra
    scores = jnp.where(valid, scores, NEGATIVE)
    probs = low(jax.nn.softmax(scores, axis=-1))
    mixed = jnp.einsum('hts,shd->thd', probs, value_heads, precision=HIGH).reshape(tokens, HEADS * HEAD_DIM)
    return low(low_back(mixed))

def reference(decoder_in, encoder_out, lengths, key_mask, assign, buckets, norm_one, norm_two, norm_three, self_query, self_key, self_value, self_output, cross_query, cross_key, cross_value, cross_output, ffn_gate, ffn_up, ffn_down, bias_table, cotangent):
    positions = jnp.arange(ENC_CAP)
    live = (positions[None, :] < lengths[assign][:, None]) & ((key_mask[assign] == 1) | (positions[None, :] == 0))
    causal = (jnp.arange(TGT)[:, None] >= jnp.arange(TGT)[None, :])[None]

    def forward(decoder, encoder, gain_one, gain_two, gain_three, w_query, w_key, w_value, w_output, c_query, c_key, c_value, c_output, w_gate, w_up, w_down, table):
        w_query, w_key, w_value, w_output = (low(w_query), low(w_key), low(w_value), low(w_output))
        c_query, c_key, c_value, c_output = (low(c_query), low(c_key), low(c_value), low(c_output))
        w_gate, w_up, w_down = (low(w_gate), low(w_up), low(w_down))
        extra = jnp.transpose(table[buckets], (2, 0, 1))
        rows_all = encoder[assign]

        def layer(inputs):
            tokens, rows, valid = inputs
            normed = low(rms_norm(tokens, gain_one))
            query = low(low_back(project(normed, w_query)))
            keys = low(low_back(project(normed, w_key)))
            values = low(low_back(project(normed, w_value)))
            attended = attend(query, keys, values, extra, causal)
            h_one = tokens + low_back(project(attended, w_output))
            normed = low(rms_norm(h_one, gain_two))
            cross_q = low(low_back(project(normed, c_query)))
            cross_k = low(low_back(project(rows, c_key)))
            cross_v = low(low_back(project(rows, c_value)))
            cross_att = attend(cross_q, cross_k, cross_v, 0.0, valid[None, None, :])
            h_two = h_one + low_back(project(cross_att, c_output))
            normed = low(rms_norm(h_two, gain_three))
            gate = low_back(project(normed, w_gate))
            up = low_back(project(normed, w_up))
            act = low(low_back(jax.nn.gelu(gate, approximate=True) * up))
            return h_two + low_back(project(act, w_down))
        return lax.map(jax.checkpoint(layer), (decoder, rows_all, live))
    primal, pull = jax.vjp(forward, decoder_in.astype(jnp.float32), encoder_out.astype(jnp.float32), norm_one, norm_two, norm_three, self_query, self_key, self_value, self_output, cross_query, cross_key, cross_value, cross_output, ffn_gate, ffn_up, ffn_down, bias_table)
    grads = pull(cotangent.astype(jnp.float32))
    return (primal.astype(jnp.bfloat16), grads[0], grads[1].astype(jnp.bfloat16), grads[2], grads[3], grads[4], grads[5], grads[6], grads[7], grads[8], grads[9], grads[10], grads[11], grads[12], grads[13], grads[14], grads[15], grads[16])
```

```python
import functools

import jax
import jax.numpy as jnp
from jax import lax
from jax.experimental import pallas as pl
from jax.experimental.pallas import tpu as pltpu
from jax.sharding import PartitionSpec as P

HEAD_DIM = 64
PAIR = 2 * HEAD_DIM
QUERIES = 256
KEYS = 1024
TILE = 128

EPS = 1e-06
NEGATIVE = -1000000000.0
BF16 = jnp.bfloat16
F32 = jnp.float32


def norm_apply(value, gain):
    return value * lax.rsqrt(jnp.mean(value * value, axis=-1, keepdims=True) + EPS) * gain


def mixer(gate, up):
    return jax.nn.gelu(gate, approximate=True) * up


def dot(left, right, dims):
    return lax.dot_general(left, right, (dims, ((), ())), preferred_element_type=F32)


def nn(left, right):
    return dot(left, right, ((1,), (0,)))


def nt(left, right):
    return dot(left, right, ((1,), (1,)))


def tn(left, right):
    return dot(left, right, ((0,), (0,)))


def swap(value, mask, size):
    return lax.ppermute(value, "dp", [(i, i ^ mask) for i in range(size)])


def swap_cores(value):
    return lax.ppermute(value, "mp", [(0, 1), (1, 0)])


def cut_of(columns):
    return (columns // TILE + 1) // 2 * TILE


def gather_rows(shard, size):
    outer = size // 4
    cut = cut_of(shard.shape[1])
    if outer <= 4:
        rows = jnp.concatenate([shard] + [swap(shard, 4 * k, size) for k in range(1, outer)])
    else:
        rows, mask = shard, 4
        while mask < size:
            rows = jnp.concatenate([rows, swap(rows, mask, size)])
            mask *= 2
    quarter = rows.shape[0]
    left, right = rows[:, :cut], rows[:, cut:]
    left = jnp.concatenate([left, swap(left, 2, size)])
    right = jnp.concatenate([right, swap(right, 1, size)])
    left_more, right_more = swap(left, 1, size), swap(right, 2, size)
    left = jnp.concatenate([left, left_more])
    right = jnp.concatenate(
        [right[:quarter], right_more[:quarter], right[quarter:], right_more[quarter:]]
    )
    return jnp.concatenate([left, right], axis=1)


def scatter_rows(grad, size):
    outer = size // 4
    quarter = grad.shape[0] // 4
    half = 2 * quarter
    cut = cut_of(grad.shape[1])
    low = grad.astype(BF16)
    left, right = low[:, :cut], low[:, cut:]
    left_in = swap(left[half:], 1, size)
    right_out = jnp.concatenate([right[quarter:half], right[half + quarter :]])
    right_in = swap(right_out, 2, size)
    left = left[:half].astype(F32) + left_in.astype(F32)
    right = jnp.concatenate([right[:quarter], right[half : half + quarter]]).astype(
        F32
    ) + right_in.astype(F32)
    left_in = swap(left[quarter:].astype(BF16), 2, size)
    right_in = swap(right[quarter:].astype(BF16), 1, size)
    left = left[:quarter] + left_in.astype(F32)
    right = right[:quarter] + right_in.astype(F32)
    rows = jnp.concatenate([left, right], axis=1)
    if outer <= 4:
        count = quarter // outer
        total = rows[:count]
        for k in range(1, outer):
            total = total + swap(
                rows[k * count : (k + 1) * count].astype(BF16), 4 * k, size
            ).astype(F32)
        return total
    mask = size // 2
    while mask >= 4:
        count = rows.shape[0] // 2
        rows = rows[:count] + swap(rows[count:].astype(BF16), mask, size).astype(F32)
        mask //= 2
    return rows


def sum_devices(value, size):
    value = value + swap_cores(value)
    value = value + swap(value, 1, size)
    value = value + swap(value, 2, size)
    if size <= 16:
        total = value
        for k in range(1, size // 4):
            total = total + swap(value, 4 * k, size)
        return total
    mask = 4
    while mask < size:
        value = value + swap(value, mask, size)
        mask *= 2
    return value


def each_chunk(count, size, body):
    if count == 1:
        body(0)
    else:
        pl.loop(0, count)(lambda step: body(pl.multiple_of(step * size, size)))


def of_head(value, head):
    lane = lax.broadcasted_iota(jnp.int32, value.shape, 1)
    return jnp.where(lane // HEAD_DIM == head, value, jnp.zeros_like(value))


def cross_forward_kernel(q_ref, k_ref, v_ref, dead_ref, out_ref, lse_ref, s_ref, acc_ref):
    targets, capacity = q_ref.shape[0], k_ref.shape[0]
    size = min(capacity, KEYS)
    count = capacity // size
    for head in range(2):
        rows = slice(head * HEAD_DIM, (head + 1) * HEAD_DIM)
        for start in range(0, targets, QUERIES):
            cols = slice(start, start + QUERIES)
            query = of_head(q_ref[cols, :], head)
            top = jnp.full((1, QUERIES), NEGATIVE * 2, F32)
            lse_ref[0, head : head + 1, cols] = top

            def scores(base):
                keys = pl.ds(base, size)
                score = nt(k_ref[keys, :], query) + dead_ref[keys, 0:1]
                s_ref[keys, :] = score
                lse_ref[0, head : head + 1, cols] = jnp.maximum(
                    lse_ref[0, head : head + 1, cols], jnp.max(score, axis=0, keepdims=True)
                )

            each_chunk(count, size, scores)
            top = lse_ref[0, head : head + 1, cols]
            lse_ref[0, head : head + 1, cols] = jnp.zeros((1, QUERIES), F32)

            def weights(base):
                keys = pl.ds(base, size)
                weight = jnp.exp(s_ref[keys, :] - top)
                s_ref[keys, :] = weight
                lse_ref[0, head : head + 1, cols] += jnp.sum(weight, axis=0, keepdims=True)

            each_chunk(count, size, weights)
            total = lse_ref[0, head : head + 1, cols]
            lse_ref[0, head : head + 1, cols] = top + jnp.log(total)
            scale = 1.0 / total
            acc_ref[rows, cols] = jnp.zeros((HEAD_DIM, QUERIES), F32)

            def mix(base):
                keys = pl.ds(base, size)
                probs = (s_ref[keys, :] * scale).astype(BF16)
                acc_ref[rows, cols] += tn(v_ref[keys, :], probs)[rows]

            each_chunk(count, size, mix)
    out_ref[...] = acc_ref[...].T.astype(BF16)


def cross_backward_kernel(
    q_ref, k_ref, v_ref, dead_ref, lse_ref, go_ref, dq_ref, dk_ref, dv_ref,
    p_ref, dp_ref, dqt_ref, dk_acc, dv_acc, delta_ref,
):
    targets, capacity = q_ref.shape[0], k_ref.shape[0]
    size = min(capacity, KEYS)
    count = capacity // size
    dk_acc[...] = jnp.zeros_like(dk_acc)
    dv_acc[...] = jnp.zeros_like(dv_acc)
    for head in range(2):
        rows = slice(head * HEAD_DIM, (head + 1) * HEAD_DIM)
        for start in range(0, targets, QUERIES):
            cols = slice(start, start + QUERIES)
            query = of_head(q_ref[cols, :], head)
            grad = of_head(go_ref[cols, :], head)
            lse = lse_ref[0, head : head + 1, cols]
            delta_ref[...] = jnp.zeros_like(delta_ref)

            def first(base):
                keys = pl.ds(base, size)
                probs = jnp.exp(nt(k_ref[keys, :], query) + dead_ref[keys, 0:1] - lse)
                grad_probs = nt(v_ref[keys, :], grad)
                p_ref[keys, :] = probs
                dp_ref[keys, :] = grad_probs
                delta_ref[...] += jnp.sum(probs * grad_probs, axis=0, keepdims=True)

            each_chunk(count, size, first)
            delta = delta_ref[...]
            dqt_ref[rows, cols] = jnp.zeros((HEAD_DIM, QUERIES), F32)

            def second(base):
                keys = pl.ds(base, size)
                probs = p_ref[keys, :]
                dv_acc[keys, :] += nn(probs.astype(BF16), grad)
                low = (probs * (dp_ref[keys, :] - delta)).astype(BF16)
                dk_acc[keys, :] += nn(low, query)
                dqt_ref[rows, cols] += tn(k_ref[keys, :], low)[rows]

            each_chunk(count, size, second)
    dq_ref[...] = dqt_ref[...].T.astype(BF16)
    dk_ref[...] = dk_acc[...].astype(BF16)
    dv_ref[...] = dv_acc[...].astype(BF16)


def skewed(row, block):
    low = row[:, (block - 1) * TILE : block * TILE] if block else jnp.zeros((1, TILE), F32)
    both = jnp.concatenate([low, row[:, block * TILE : (block + 1) * TILE]], axis=1)
    both = jnp.broadcast_to(both, (TILE, 2 * TILE))
    return pltpu.roll(both, 0, 1, stride=1, stride_axis=0)[:, TILE:]


def unskewed(tile):
    both = jnp.concatenate([jnp.zeros_like(tile), tile], axis=1)
    total = both[:8]
    for base in range(8, TILE, 8):
        total = total + pltpu.roll(both[base : base + 8], 2 * TILE - base, 1)
    row = lax.broadcasted_iota(jnp.int32, total.shape, 0)
    for bit in (1, 2, 4):
        total = jnp.where(row & bit != 0, pltpu.roll(total, 2 * TILE - bit, 1), total)
    return jnp.sum(total, axis=0, keepdims=True)


def self_scores(k_ref, query, tiles, start):
    keys = start + QUERIES
    columns = []
    for i in range(start // TILE, keys // TILE):
        columns.append(
            jnp.concatenate([tiles[max(i - j, 0)] for j in range(keys // TILE)], axis=0)
        )
    score = nt(k_ref[:keys, :], query) + jnp.concatenate(columns, axis=1)
    key = lax.broadcasted_iota(jnp.int32, score.shape, 0)
    spot = lax.broadcasted_iota(jnp.int32, score.shape, 1) + start
    return jnp.where(key <= spot, score, NEGATIVE)


def self_forward_kernel(q_ref, k_ref, v_ref, bias_ref, out_ref, lse_ref, acc_ref):
    targets = q_ref.shape[0]
    for head in range(2):
        rows = slice(head * HEAD_DIM, (head + 1) * HEAD_DIM)
        row = bias_ref[0, head : head + 1, :]
        tiles = [skewed(row, block) for block in range(targets // TILE)]
        for start in range(0, targets, QUERIES):
            cols = slice(start, start + QUERIES)
            query = of_head(q_ref[cols, :], head)
            score = self_scores(k_ref, query, tiles, start)
            top = jnp.max(score, axis=0, keepdims=True)
            weight = jnp.exp(score - top)
            total = jnp.sum(weight, axis=0, keepdims=True)
            lse_ref[0, head : head + 1, cols] = top + jnp.log(total)
            probs = (weight * (1.0 / total)).astype(BF16)
            acc_ref[rows, cols] = tn(v_ref[: start + QUERIES, :], probs)[rows]
    out_ref[...] = acc_ref[...].T.astype(BF16)


def self_backward_kernel(
    q_ref, k_ref, v_ref, bias_ref, lse_ref, go_ref, dq_ref, dk_ref, dv_ref, dbias_ref,
    dqt_ref, dk_acc, dv_acc,
):
    targets = q_ref.shape[0]
    dk_acc[...] = jnp.zeros_like(dk_acc)
    dv_acc[...] = jnp.zeros_like(dv_acc)
    blocks = targets // TILE
    for head in range(2):
        rows = slice(head * HEAD_DIM, (head + 1) * HEAD_DIM)
        row = bias_ref[0, head : head + 1, :]
        tiles = [skewed(row, block) for block in range(blocks)]
        sums = [jnp.zeros((TILE, TILE), F32) for block in range(blocks)]
        for start in range(0, targets, QUERIES):
            cols = slice(start, start + QUERIES)
            keys = start + QUERIES
            query = of_head(q_ref[cols, :], head)
            grad = of_head(go_ref[cols, :], head)
            score = self_scores(k_ref, query, tiles, start)
            probs = jnp.exp(score - lse_ref[0, head : head + 1, cols])
            grad_probs = nt(v_ref[:keys, :], grad)
            delta = jnp.sum(probs * grad_probs, axis=0, keepdims=True)
            dv_acc[:keys, :] += nn(probs.astype(BF16), grad)
            grad_scores = probs * (grad_probs - delta)
            for i in range(start // TILE, keys // TILE):
                for j in range(i + 1):
                    sums[i - j] = sums[i - j] + grad_scores[
                        j * TILE : (j + 1) * TILE, i * TILE - start : (i + 1) * TILE - start
                    ]
            low = grad_scores.astype(BF16)
            dk_acc[:keys, :] += nn(low, query)
            dqt_ref[rows, cols] = tn(k_ref[:keys, :], low)[rows]
        lines = [unskewed(tile) for tile in sums]
        parts = []
        for block in range(blocks):
            part = lines[block][:, TILE:]
            if block + 1 < blocks:
                part = part + lines[block + 1][:, :TILE]
            parts.append(part)
        dbias_ref[0, head : head + 1, :] = jnp.concatenate(parts, axis=1)
    dq_ref[...] = dqt_ref[...].T.astype(BF16)
    dk_ref[...] = dk_acc[...].astype(BF16)
    dv_ref[...] = dv_acc[...].astype(BF16)


def pair_call(kernel, ins, outs, scratch, flops):
    def spec(shape, whole=False):
        if whole:
            return pl.BlockSpec(shape, lambda pair: (0, 0))
        if len(shape) == 3:
            return pl.BlockSpec((1,) + shape[1:], lambda pair: (pair, 0, 0))
        return pl.BlockSpec((shape[0], PAIR), lambda pair: (0, pair))

    pairs = ins[0].shape[1] // PAIR
    size = sum(value.size * value.dtype.itemsize for value in ins)
    return pl.pallas_call(
        kernel,
        grid=(pairs,),
        in_specs=[spec(value.shape, value.dtype == F32 and value.ndim == 2) for value in ins],
        out_specs=[spec(value.shape) for value in outs],
        out_shape=outs,
        scratch_shapes=scratch,
        compiler_params=pltpu.CompilerParams(vmem_limit_bytes=60 * 1024 * 1024),
        cost_estimate=pl.CostEstimate(flops=flops, bytes_accessed=size, transcendentals=flops // 256),
    )(*ins)


def struct(shape, dtype):
    return jax.ShapeDtypeStruct(shape, dtype)


def cross_forward(query, keys, values, dead):
    targets, width = query.shape
    capacity = keys.shape[0]
    return pair_call(
        cross_forward_kernel,
        [query, keys, values, dead],
        [struct(query.shape, BF16), struct((width // PAIR, 8, targets), F32)],
        [pltpu.VMEM((capacity, QUERIES), F32), pltpu.VMEM((PAIR, targets), F32)],
        4 * targets * capacity * width,
    )


def cross_backward(query, keys, values, dead, lse, grad):
    targets, width = query.shape
    capacity = keys.shape[0]
    return pair_call(
        cross_backward_kernel,
        [query, keys, values, dead, lse, grad],
        [struct(query.shape, BF16), struct(keys.shape, BF16), struct(keys.shape, BF16)],
        [
            pltpu.VMEM((capacity, QUERIES), F32),
            pltpu.VMEM((capacity, QUERIES), F32),
            pltpu.VMEM((PAIR, targets), F32),
            pltpu.VMEM((capacity, PAIR), F32),
            pltpu.VMEM((capacity, PAIR), F32),
            pltpu.VMEM((1, QUERIES), F32),
        ],
        10 * targets * capacity * width,
    )


def self_forward(query, keys, values, bias):
    targets, width = query.shape
    return pair_call(
        self_forward_kernel,
        [query, keys, values, bias],
        [struct(query.shape, BF16), struct((width // PAIR, 8, targets), F32)],
        [pltpu.VMEM((PAIR, targets), F32)],
        3 * targets * targets * width,
    )


def self_backward(query, keys, values, bias, lse, grad):
    targets, width = query.shape
    return pair_call(
        self_backward_kernel,
        [query, keys, values, bias, lse, grad],
        [
            struct(query.shape, BF16),
            struct(query.shape, BF16),
            struct(query.shape, BF16),
            struct((width // PAIR, 8, targets), F32),
        ],
        [
            pltpu.VMEM((PAIR, targets), F32),
            pltpu.VMEM((targets, PAIR), F32),
            pltpu.VMEM((targets, PAIR), F32),
        ],
        8 * targets * targets * width,
    )


def norm_back(value, gain, grad):
    root = lax.rsqrt(jnp.mean(value * value, axis=-1, keepdims=True) + EPS)
    scaled = grad * gain
    inner = jnp.mean(value * scaled, axis=-1, keepdims=True)
    return root * scaled - value * (root * root * root * inner)


def gain_grad(value, grad):
    root = lax.rsqrt(jnp.mean(value * value, axis=-1, keepdims=True) + EPS)
    return jnp.sum(grad * value * root, axis=0)


def shards(
    decoder_in,
    encoder_out,
    lengths,
    key_mask,
    assign,
    buckets,
    norm_one,
    norm_two,
    norm_three,
    self_query,
    self_key,
    self_value,
    self_output,
    cross_query,
    cross_key,
    cross_value,
    cross_output,
    ffn_gate,
    ffn_up,
    ffn_down,
    bias_table,
    cotangent,
    *,
    size,
):
    rank = lax.axis_index("dp")
    core = lax.axis_index("mp")
    targets, width = decoder_in.shape[1:]
    capacity = key_mask.shape[1]
    block = width // size
    outer = size // 4
    half = width // 2
    heads = bias_table.shape[1]

    spots = jnp.arange(size, dtype=jnp.int32)
    masks = spots // (2 * outer) + 2 * (spots // outer % 2) + 4 * (spots % outer)
    owner = rank ^ masks
    other = rank ^ spots
    place = (other % 2) * (2 * outer) + (other // 2 % 2) * outer + other // 4
    source = (owner[:, None] * block + jnp.arange(block, dtype=jnp.int32)[None, :]).reshape(-1)
    order = (jnp.arange(width, dtype=jnp.int32)[:, None] == source[None, :]).astype(BF16)

    def true_rows(value):
        return value.reshape(size, block, -1)[place].reshape(width, -1)

    def own_rows(value):
        return value.reshape(size, block, -1)[owner].reshape(width, -1)

    def low(*shards):
        return jnp.concatenate([value.astype(BF16) for value in shards], axis=1)

    qkv = gather_rows(low(self_query, self_key, self_value), size)
    part = self_query.shape[1]
    attend = gather_rows(
        low(self_output.T, cross_query, cross_output.T, cross_key, cross_value), size
    )
    ffn = gather_rows(low(ffn_gate, ffn_up), size)
    down = gather_rows(ffn_down.T.astype(BF16), size)
    output_one, query_two, output_two = (
        attend[:, i * part : (i + 1) * part] for i in range(3)
    )
    key_value = true_rows(attend[:, 3 * part :])
    hidden = ffn_gate.shape[1]

    mine = assign[rank]
    sent = lax.dynamic_slice_in_dim(encoder_out, core * half, half, 2)[assign]
    own = lax.all_to_all(sent, "dp", split_axis=0, concat_axis=0, tiled=True)
    own = own.reshape(capacity, half)
    peer = swap_cores(own)
    encoded = jnp.where(
        core == 0, jnp.concatenate([own, peer], axis=1), jnp.concatenate([peer, own], axis=1)
    )
    cross_kv = nn(encoded, key_value).astype(BF16)
    cross_k, cross_v = cross_kv[:, :part], cross_kv[:, part:]

    positions = jnp.arange(capacity, dtype=jnp.int32)
    live = (positions < lengths[mine]) & ((key_mask[mine] == 1) | (positions == 0))
    dead = jnp.broadcast_to(jnp.where(live, 0.0, NEGATIVE)[:, None], (capacity, TILE))
    labels = buckets[:, 0]
    which = labels[None, :] == jnp.arange(bias_table.shape[0], dtype=jnp.int32)[:, None]
    bias = jnp.sum(jnp.where(which[None], bias_table.T[:, :, None], 0.0), axis=1)
    bias = jnp.pad(bias.reshape(heads // 2, 2, targets), ((0, 0), (0, 6), (0, 0)))

    gains = jnp.stack([norm_one, norm_two, norm_three]).reshape(3, size, block)
    gain_one, gain_two, gain_three = gains[:, owner].reshape(3, width)
    tokens = nn(decoder_in[0], order)
    cot = nn(cotangent[0], order).astype(BF16)

    normed_one = norm_apply(tokens, gain_one).astype(BF16)
    mixed = nn(normed_one, qkv).astype(BF16)
    query, keys, values = (mixed[:, i * part : (i + 1) * part] for i in range(3))
    attended, lse_self = self_forward(query, keys, values, bias)
    partial = nt(attended, output_one)
    h_one = tokens + (partial + swap_cores(partial))
    normed_two = norm_apply(h_one, gain_two).astype(BF16)
    cross_q = nn(normed_two, query_two).astype(BF16)
    cross_att, lse_cross = cross_forward(cross_q, cross_k, cross_v, dead)
    partial = nt(cross_att, output_two)
    h_two = h_one + (partial + swap_cores(partial))
    normed_three = norm_apply(h_two, gain_three).astype(BF16)
    gate_up = nn(normed_three, ffn)
    gate, up = gate_up[:, :hidden], gate_up[:, hidden:]
    act, pull_mixer = jax.vjp(mixer, gate, up)
    act = act.astype(BF16)
    partial = nt(act, down)
    layer_out = (h_two + (partial + swap_cores(partial))).astype(BF16)
    layer_out = nt(layer_out, order).astype(BF16)

    grad_act = nn(cot, down).astype(BF16)
    grad_gate, grad_up = pull_mixer(grad_act.astype(F32))
    grad_gate_up = jnp.concatenate([grad_gate.astype(BF16), grad_up.astype(BF16)], axis=1)
    grad_down = tn(cot, act)
    grad_ffn = tn(normed_three, grad_gate_up)
    sum_down = scatter_rows(grad_down, size)
    sum_ffn = scatter_rows(grad_ffn, size)
    partial = nt(grad_gate_up, ffn)
    grad_normed = partial + swap_cores(partial)
    g_two = cot.astype(F32) + norm_back(h_two, gain_three, grad_normed)
    gain_grad_three = gain_grad(h_two, partial)

    low_two = g_two.astype(BF16)
    grad_cross_att = nn(low_two, output_two).astype(BF16)
    grad_cross_q, grad_cross_k, grad_cross_v = cross_backward(
        cross_q, cross_k, cross_v, dead, lse_cross, grad_cross_att
    )
    grad_cross_kv = jnp.concatenate([grad_cross_k, grad_cross_v], axis=1)
    partial = nt(grad_cross_q, query_two)
    grad_normed = partial + swap_cores(partial)
    g_one = g_two + norm_back(h_one, gain_two, grad_normed)
    gain_grad_two = gain_grad(h_one, partial)
    low_one = g_one.astype(BF16)
    grad_kv = own_rows(tn(encoded, grad_cross_kv).astype(BF16))
    grad_attend = jnp.concatenate(
        [
            tn(low_one, attended).astype(BF16),
            tn(normed_two, grad_cross_q).astype(BF16),
            tn(low_two, cross_att).astype(BF16),
            grad_kv,
        ],
        axis=1,
    )
    sum_attend = scatter_rows(grad_attend, size)

    terms = nt(grad_cross_kv, key_value)
    kept = lax.dynamic_slice_in_dim(terms, core * half, half, 1)
    given = lax.dynamic_slice_in_dim(terms, half - core * half, half, 1).astype(BF16)
    terms = (kept + swap_cores(given).astype(F32)).astype(BF16)
    back = lax.all_to_all(
        terms.reshape(size, capacity // size, half), "dp", split_axis=0, concat_axis=0, tiled=True
    )
    inverse = jnp.zeros_like(assign).at[assign].set(jnp.arange(size, dtype=jnp.int32))
    encoder_grad = back[inverse]

    grad_attended = nn(low_one, output_one).astype(BF16)
    grad_query, grad_keys, grad_values, diagonals = self_backward(
        query, keys, values, bias, lse_self, grad_attended
    )
    grad_mixed = jnp.concatenate([grad_query, grad_keys, grad_values], axis=1)
    sum_mixed = scatter_rows(tn(normed_one, grad_mixed), size)
    partial = nt(grad_mixed, qkv)
    grad_normed = partial + swap_cores(partial)
    decoder_grad = g_one + norm_back(tokens, gain_one, grad_normed)
    decoder_grad = lax.dot_general(
        decoder_grad,
        order.astype(F32),
        (((1,), (1,)), ((), ())),
        precision=lax.Precision.HIGHEST,
        preferred_element_type=F32,
    )
    gain_grad_one = gain_grad(tokens, partial)

    diagonals = diagonals[:, :2].reshape(heads, targets)
    grad_table = jnp.sum(jnp.where(which[:, None], diagonals[None], 0.0), axis=2)
    grad_gains = jnp.stack([gain_grad_one, gain_grad_two, gain_grad_three])
    grad_gains = grad_gains.reshape(3, size, block)[:, place].reshape(-1)
    table = jnp.where(
        jnp.arange(2)[:, None] == core, grad_table.reshape(1, -1), 0.0
    ).reshape(-1)
    small = jnp.concatenate([grad_gains, table])
    small = jnp.pad(small, (0, -small.size % (8 * TILE))).reshape(-1, TILE)
    small = sum_devices(small, size).reshape(-1)
    grad_gains = small[: 3 * width].reshape(3, width)
    grad_table = lax.dynamic_slice_in_dim(
        small, 3 * width + core * grad_table.size, grad_table.size
    ).reshape(grad_table.shape)

    def parts(value, count):
        step = value.shape[1] // count
        return [value[:, i * step : (i + 1) * step] for i in range(count)]

    grad_self_query, grad_self_key, grad_self_value = parts(sum_mixed, 3)
    grad_output_one, grad_cross_query, grad_output_two, grad_cross_key, grad_cross_value = parts(
        sum_attend, 5
    )
    grad_ffn_gate, grad_ffn_up = parts(sum_ffn, 2)
    return (
        layer_out[None],
        decoder_grad[None],
        encoder_grad,
        grad_gains[0],
        grad_gains[1],
        grad_gains[2],
        grad_self_query,
        grad_self_key,
        grad_self_value,
        grad_output_one.T,
        grad_cross_query,
        grad_cross_key,
        grad_cross_value,
        grad_output_two.T,
        grad_ffn_gate,
        grad_ffn_up,
        sum_down.T,
        grad_table,
    )


def solution(mesh):
    in_specs = (
        P("dp", None, None),
        P(None, "dp", None),
        P(),
        P(),
        P(),
        P(),
        P(),
        P(),
        P(),
        P("dp", "mp"),
        P("dp", "mp"),
        P("dp", "mp"),
        P("mp", "dp"),
        P("dp", "mp"),
        P("dp", "mp"),
        P("dp", "mp"),
        P("mp", "dp"),
        P("dp", "mp"),
        P("dp", "mp"),
        P("mp", "dp"),
        P(None, "mp"),
        P("dp", None, None),
    )
    out_specs = (
        P("dp", None, None),
        P("dp", None, None),
        P(None, "dp", "mp"),
        P(),
        P(),
        P(),
        P("dp", "mp"),
        P("dp", "mp"),
        P("dp", "mp"),
        P("mp", "dp"),
        P("dp", "mp"),
        P("dp", "mp"),
        P("dp", "mp"),
        P("mp", "dp"),
        P("dp", "mp"),
        P("dp", "mp"),
        P("mp", "dp"),
        P(None, "mp"),
    )
    body = functools.partial(shards, size=mesh.shape["dp"])
    return jax.shard_map(body, mesh=mesh, in_specs=in_specs, out_specs=out_specs, check_vma=False)
```

```python
import functools

import jax
import jax.numpy as jnp
from jax import lax
from jax.experimental import pallas as pl
from jax.experimental.pallas import tpu as pltpu
from jax.sharding import PartitionSpec as P

HEAD_DIM = 64
PAIR = 2 * HEAD_DIM
QUERIES = 256
KEYS = 1024
TILE = 128
WIDE = 256
ROWS = 64

EPS = 1e-06
NEGATIVE = -1000000000.0
GELU_ROOT = 0.7978845608028654
GELU_CUBE = 0.044715
BF16 = jnp.bfloat16
F32 = jnp.float32


def dot(left, right, dims):
    return lax.dot_general(left, right, (dims, ((), ())), preferred_element_type=F32)


def nn(left, right):
    return dot(left, right, ((1,), (0,)))


def nt(left, right):
    return dot(left, right, ((1,), (1,)))


def tn(left, right):
    return dot(left, right, ((0,), (0,)))


def struct(shape, dtype):
    return jax.ShapeDtypeStruct(shape, dtype)


def thirds(value):
    high = lax.reduce_precision(value, 8, 7)
    middle = lax.reduce_precision(value - high, 8, 7)
    return [part.astype(BF16) for part in (high, middle, value - high - middle)]


def swap(value, mask, size):
    return lax.ppermute(value, "dp", [(i, i ^ mask) for i in range(size)])


def swap_cores(value):
    return lax.ppermute(value, "mp", [(0, 1), (1, 0)])


def after(values, *others):
    return lax.optimization_barrier((values, others))[0]


def gather_outer(shard, size):
    if size <= 16:
        return [shard] + [swap(shard, mask, size) for mask in range(4, size, 4)]
    mask = 4
    while mask < size:
        shard = jnp.concatenate([shard, swap(shard, mask, size)])
        mask *= 2
    return [shard]


def gather_first(pieces, size):
    rows, columns = sum(piece.shape[0] for piece in pieces), pieces[0].shape[1]
    left, right = kernel_call(
        stack_kernel, pieces, [struct((rows, columns // 2), BF16)] * 2, []
    )
    return left, right


def gather_second(state, size):
    left = state[0]
    return kernel_call(
        join_kernel, list(state), [struct((2 * left.shape[0], left.shape[1]), BF16)] * 2, []
    )


def send_first(halves, size):
    left, right = halves
    return left, swap(left, 2, size), right, swap(right, 1, size)


def send_second(halves, size):
    left, right = halves
    return [left, swap(left, 1, size)], [right, swap(right, 2, size)]


def scatter_first(grads, size):
    left, left_out, right, right_out = grads
    return left, right, swap(left_out, 1, size), swap(right_out, 2, size)


def scatter_second_parts(state):
    return add_call(scatter_second_kernel, state, 0.5)


def scatter_second_send(parts, size):
    keep, left_out, right_out = parts
    return keep, swap(left_out, 2, size), swap(right_out, 1, size)


def scatter_outer_parts(state):
    return add_call(scatter_outer_kernel, state, 0.25)


def scatter_outer_send(parts, size):
    keep, *outs = parts
    if size == 16:
        return [keep] + [swap(out, 4 * (k + 1), size) for k, out in enumerate(outs)]
    rows = jnp.concatenate([keep] + [out.astype(F32) for out in outs])
    mask = size // 2
    while mask >= 4:
        count = rows.shape[0] // 2
        rows = rows[:count] + swap(rows[count:].astype(BF16), mask, size).astype(F32)
        mask //= 2
    return [rows]


def scatter_last(state):
    total = state[0]
    for value in state[1:]:
        total = total + value.astype(F32)
    return total


def sum_devices(value, size):
    value = value + swap(value, 1, size)
    value = value + swap(value, 2, size)
    if size <= 16:
        return functools.reduce(
            lambda total, mask: total + swap(value, mask, size), range(4, size, 4), value
        )
    mask = 4
    while mask < size:
        value = value + swap(value, mask, size)
        mask *= 2
    return value


def kernel_call(kernel, ins, outs, scratch, time=2, grid=None, in_specs=None, out_specs=None):
    everywhere = pl.BlockSpec(memory_space=pltpu.VMEM)
    return pl.pallas_call(
        kernel,
        out_shape=outs,
        in_specs=in_specs or [everywhere] * len(ins),
        out_specs=out_specs or [everywhere] * len(outs),
        scratch_shapes=scratch,
        compiler_params=pltpu.CompilerParams(vmem_limit_bytes=58 * 1024 * 1024),
        cost_estimate=pl.CostEstimate(
            flops=time * 1000000000, bytes_accessed=1, transcendentals=0
        ),
        **({"grid": grid} if grid else {}),
    )(*ins)


IN_VMEM = pl.BlockSpec(memory_space=pltpu.VMEM)
IN_PLACE = pl.BlockSpec(memory_space=pl.ANY)
IN_SMEM = pl.BlockSpec(memory_space=pltpu.SMEM)


def stack_kernel(*refs):
    *in_refs, left_ref, right_ref = refs
    half = left_ref.shape[1]
    start = 0
    for ref in in_refs:
        rows = slice(start, start + ref.shape[0])
        left_ref[rows, :] = ref[:, :half]
        right_ref[rows, :] = ref[:, half:]
        start += ref.shape[0]


def join_kernel(left_ref, left_in_ref, right_ref, right_in_ref, left_out, right_out):
    count = left_ref.shape[0]
    left_out[:count, :] = left_ref[...]
    left_out[count:, :] = left_in_ref[...]
    right_out[:count, :] = right_ref[...]
    right_out[count:, :] = right_in_ref[...]


def scatter_second_kernel(left_ref, right_ref, left_in_ref, right_in_ref, keep_ref, *out_refs):
    count, half = keep_ref.shape[0], left_ref.shape[1]
    halves = ((left_ref, left_in_ref, out_refs[0]), (right_ref, right_in_ref, out_refs[1]))
    for i, (own_ref, in_ref, out_ref) in enumerate(halves):
        keep_ref[:, i * half : (i + 1) * half] = own_ref[:count, :].astype(F32) + in_ref[
            :count, :
        ].astype(F32)
        out_ref[...] = (
            own_ref[count:, :].astype(F32) + in_ref[count:, :].astype(F32)
        ).astype(BF16)


def scatter_outer_kernel(keep_ref, left_in_ref, right_in_ref, *out_refs):
    count, half = out_refs[0].shape[0], left_in_ref.shape[1]
    for k, out_ref in enumerate(out_refs):
        rows = slice(k * count, (k + 1) * count)
        for i, in_ref in enumerate((left_in_ref, right_in_ref)):
            cols = slice(i * half, (i + 1) * half)
            out_ref[:, cols] = (keep_ref[rows, cols] + in_ref[rows, :].astype(F32)).astype(
                out_ref.dtype
            )


def add_call(kernel, ins, share):
    rows, half = ins[-1].shape
    if share == 0.5:
        outs = [struct((rows // 2, 2 * half), F32)] + [struct((rows // 2, half), BF16)] * 2
    else:
        outs = [struct((rows // 4, 2 * half), dtype) for dtype in (F32, BF16, BF16, BF16)]
    return kernel_call(kernel, list(ins), outs, [])


def cast_kernel(*refs):
    *in_refs, out_ref = refs
    start = 0
    for ref in in_refs:
        out_ref[:, start : start + ref.shape[1]] = ref[...].astype(BF16)
        start += ref.shape[1]


def low(*values):
    width = sum(value.shape[1] for value in values)
    return kernel_call(
        cast_kernel, list(values), [struct((values[0].shape[0], width), BF16)], []
    )[0]


def each_rows(count, body):
    @pl.loop(0, count // ROWS)
    def step(i):
        body(pl.ds(pl.multiple_of(i * ROWS, ROWS), ROWS))


def each_tile(start, width, body):
    @pl.loop(0, width // WIDE)
    def step(i):
        body(pl.ds(pl.multiple_of(start + i * WIDE, WIDE), WIDE))


def fetch(left, right, weights_ref, sems, first=0):
    moves = []
    start = left[0].shape[1] if left else 0
    for i, ref in enumerate(left):
        count = ref.shape[0]
        moves.append((ref, weights_ref.at[i * count : (i + 1) * count, :start]))
    columns = weights_ref.shape[1] - start
    for i, ref in enumerate(right):
        count = ref.shape[0] // 2
        for x in range(2):
            place = (2 * x + i) * count
            moves.append(
                (
                    ref.at[x * count : (x + 1) * count, first : first + columns],
                    weights_ref.at[place : place + count, start:],
                )
            )
    copies = [pltpu.make_async_copy(*move, sems.at[i]) for i, move in enumerate(moves)]
    for copy in copies:
        copy.start()
    return copies


def deliver(grads_ref, out_refs, sems):
    left, left_out, right, right_out = out_refs
    rows, cols = left.shape[0] // 2, left.shape[1]
    moves = [
        (left.at[:, :], 0, 2, 0),
        (left_out.at[:, :], 2, 2, 0),
        (right.at[:rows, :], 0, 1, 1),
        (right.at[rows:, :], 2, 1, 1),
        (right_out.at[:rows, :], 1, 1, 1),
        (right_out.at[rows:, :], 3, 1, 1),
    ]
    copies = []
    for i, (target, place, count, side) in enumerate(moves):
        spot = grads_ref.at[
            place * rows : (place + count) * rows, side * cols : (side + 1) * cols
        ]
        copies.append(pltpu.make_async_copy(spot, target, sems.at[i]))
    for copy in copies:
        copy.start()
    for copy in copies:
        copy.wait()


def grad_structs(width, columns):
    return [struct((width // 2, columns // 2), BF16)] * 4


def root_of(value):
    return lax.rsqrt(jnp.mean(value * value, axis=-1, keepdims=True) + EPS)


def norm_back(value, gain, grad):
    root = root_of(value)
    scaled = grad * gain
    inner = jnp.mean(value * scaled, axis=-1, keepdims=True)
    back = root * scaled - value * (root * root * root * inner)
    return back, jnp.sum(grad * value * root, axis=0, keepdims=True)


def rows_kernel(
    tokens_ref, cot_ref, gains_ref, source_ref, tokens_out, cot_out, gains_out, order_ref, normed_ref
):
    width = tokens_ref.shape[1]
    spot = lax.broadcasted_iota(jnp.int32, (width, width), 0)
    order_ref[...] = jnp.where(spot == source_ref[0:1, :], 1.0, 0.0).astype(BF16)
    order = order_ref[...]
    high, middle, rest = (nn(value, order) for value in thirds(gains_ref[...]))
    gains_out[...] = high + (middle + rest)
    tokens_out[...] = nn(tokens_ref[...], order)
    cot_out[...] = nn(cot_ref[...], order).astype(BF16)
    gain = gains_out[0:1, :]

    def norm(rows):
        value = tokens_out[rows, :]
        normed_ref[rows, :] = (value * root_of(value) * gain).astype(BF16)

    each_rows(tokens_ref.shape[0], norm)


def queries_of(capacity):
    return QUERIES if capacity <= 2 * KEYS else TILE


def each_chunk(count, size, body):
    if count == 1:
        body(0)
    else:
        pl.loop(0, count)(lambda step: body(pl.multiple_of(step * size, size)))


def each_pair(pairs, body):
    @pl.loop(0, pairs)
    def step(pair):
        body(pair, lambda which: pl.ds(pl.multiple_of((which * pairs + pair) * PAIR, PAIR), PAIR))


def of_head(value, head):
    lane = lax.broadcasted_iota(jnp.int32, value.shape, 1)
    return jnp.where(lane // HEAD_DIM == head, value, jnp.zeros_like(value))


def cross_forward_pair(q_ref, k_ref, v_ref, dead_ref, out_ref, lse_ref, s_ref, acc_ref):
    targets, capacity = q_ref.shape[0], k_ref.shape[0]
    size = min(capacity, KEYS)
    count = capacity // size
    queries = s_ref.shape[1]
    for head in range(2):
        rows = slice(head * HEAD_DIM, (head + 1) * HEAD_DIM)
        line = slice(head, head + 1)
        for start in range(0, targets, queries):
            cols = slice(start, start + queries)
            query = of_head(q_ref[cols, :], head)
            lse_ref[line, cols] = jnp.full((1, queries), NEGATIVE * 2, F32)

            def scores(base):
                keys = pl.ds(base, size)
                score = nt(k_ref[keys, :], query) + dead_ref[keys, 0:1]
                s_ref[keys, :] = score
                lse_ref[line, cols] = jnp.maximum(
                    lse_ref[line, cols], jnp.max(score, axis=0, keepdims=True)
                )

            each_chunk(count, size, scores)
            top = lse_ref[line, cols]
            lse_ref[line, cols] = jnp.zeros((1, queries), F32)

            def weights(base):
                keys = pl.ds(base, size)
                weight = jnp.exp(s_ref[keys, :] - top)
                s_ref[keys, :] = weight
                lse_ref[line, cols] += jnp.sum(weight, axis=0, keepdims=True)

            each_chunk(count, size, weights)
            total = lse_ref[line, cols]
            lse_ref[line, cols] = top + jnp.log(total)
            scale = 1.0 / total
            acc_ref[rows, cols] = jnp.zeros((HEAD_DIM, queries), F32)

            def mix(base):
                keys = pl.ds(base, size)
                probs = (s_ref[keys, :] * scale).astype(BF16)
                acc_ref[rows, cols] += tn(v_ref[keys, :], probs)[rows]

            each_chunk(count, size, mix)
    out_ref[...] = acc_ref[...].T.astype(BF16)


def cross_backward_pair(
    q_ref, k_ref, v_ref, dead_ref, lse_ref, go_ref, dq_ref, dk_ref, dv_ref,
    p_ref, dp_ref, dqt_ref, dk_acc, dv_acc, delta_ref,
):
    targets, capacity = q_ref.shape[0], k_ref.shape[0]
    size = min(capacity, KEYS)
    count = capacity // size
    queries = p_ref.shape[1]
    dk_acc[...] = jnp.zeros_like(dk_acc)
    dv_acc[...] = jnp.zeros_like(dv_acc)
    for head in range(2):
        rows = slice(head * HEAD_DIM, (head + 1) * HEAD_DIM)
        for start in range(0, targets, queries):
            cols = slice(start, start + queries)
            query = of_head(q_ref[cols, :], head)
            grad = of_head(go_ref[cols, :], head)
            lse = lse_ref[head : head + 1, cols]
            delta_ref[...] = jnp.zeros_like(delta_ref)

            def first(base):
                keys = pl.ds(base, size)
                probs = jnp.exp(nt(k_ref[keys, :], query) + dead_ref[keys, 0:1] - lse)
                grad_probs = nt(v_ref[keys, :], grad)
                p_ref[keys, :] = probs
                dp_ref[keys, :] = grad_probs
                delta_ref[...] += jnp.sum(probs * grad_probs, axis=0, keepdims=True)

            each_chunk(count, size, first)
            delta = delta_ref[...]
            dqt_ref[rows, cols] = jnp.zeros((HEAD_DIM, queries), F32)

            def second(base):
                keys = pl.ds(base, size)
                probs = p_ref[keys, :]
                dv_acc[keys, :] += nn(probs.astype(BF16), grad)
                low = (probs * (dp_ref[keys, :] - delta)).astype(BF16)
                dk_acc[keys, :] += nn(low, query)
                dqt_ref[rows, cols] += tn(k_ref[keys, :], low)[rows]

            each_chunk(count, size, second)
    dq_ref[...] = dqt_ref[...].T.astype(BF16)
    dk_ref[...] = dk_acc[...].astype(BF16)
    dv_ref[...] = dv_acc[...].astype(BF16)


def skewed(row, block):
    before = row[:, (block - 1) * TILE : block * TILE] if block else jnp.zeros((1, TILE), F32)
    both = jnp.concatenate([before, row[:, block * TILE : (block + 1) * TILE]], axis=1)
    both = jnp.broadcast_to(both, (TILE, 2 * TILE))
    return pltpu.roll(both, 0, 1, stride=1, stride_axis=0)[:, TILE:]


def unskewed(tile):
    both = jnp.concatenate([jnp.zeros_like(tile), tile], axis=1)
    total = both[:8]
    for base in range(8, TILE, 8):
        total = total + pltpu.roll(both[base : base + 8], 2 * TILE - base, 1)
    row = lax.broadcasted_iota(jnp.int32, total.shape, 0)
    for bit in (1, 2, 4):
        total = jnp.where(row & bit != 0, pltpu.roll(total, 2 * TILE - bit, 1), total)
    return jnp.sum(total, axis=0, keepdims=True)


def self_scores(k_ref, query, tiles, start):
    keys = start + QUERIES
    columns = []
    for i in range(start // TILE, keys // TILE):
        columns.append(
            jnp.concatenate([tiles[max(i - j, 0)] for j in range(keys // TILE)], axis=0)
        )
    score = nt(k_ref[:keys, :], query) + jnp.concatenate(columns, axis=1)
    key = lax.broadcasted_iota(jnp.int32, score.shape, 0)
    spot = lax.broadcasted_iota(jnp.int32, score.shape, 1) + start
    return jnp.where(key <= spot, score, NEGATIVE)


def self_forward_pair(q_ref, k_ref, v_ref, bias_ref, out_ref, lse_ref, acc_ref):
    targets = q_ref.shape[0]
    for head in range(2):
        rows = slice(head * HEAD_DIM, (head + 1) * HEAD_DIM)
        row = bias_ref[head : head + 1, :]
        tiles = [skewed(row, block) for block in range(targets // TILE)]
        for start in range(0, targets, QUERIES):
            cols = slice(start, start + QUERIES)
            query = of_head(q_ref[cols, :], head)
            score = self_scores(k_ref, query, tiles, start)
            top = jnp.max(score, axis=0, keepdims=True)
            weight = jnp.exp(score - top)
            total = jnp.sum(weight, axis=0, keepdims=True)
            lse_ref[head : head + 1, cols] = top + jnp.log(total)
            probs = (weight * (1.0 / total)).astype(BF16)
            acc_ref[rows, cols] = tn(v_ref[: start + QUERIES, :], probs)[rows]
    out_ref[...] = acc_ref[...].T.astype(BF16)


def self_backward_pair(
    q_ref, k_ref, v_ref, bias_ref, lse_ref, go_ref, dq_ref, dk_ref, dv_ref, dbias_ref,
    dqt_ref, dk_acc, dv_acc,
):
    targets = q_ref.shape[0]
    dk_acc[...] = jnp.zeros_like(dk_acc)
    dv_acc[...] = jnp.zeros_like(dv_acc)
    blocks = targets // TILE
    for head in range(2):
        rows = slice(head * HEAD_DIM, (head + 1) * HEAD_DIM)
        row = bias_ref[head : head + 1, :]
        tiles = [skewed(row, block) for block in range(blocks)]
        sums = [jnp.zeros((TILE, TILE), F32) for block in range(blocks)]
        for start in range(0, targets, QUERIES):
            cols = slice(start, start + QUERIES)
            keys = start + QUERIES
            query = of_head(q_ref[cols, :], head)
            grad = of_head(go_ref[cols, :], head)
            score = self_scores(k_ref, query, tiles, start)
            probs = jnp.exp(score - lse_ref[head : head + 1, cols])
            grad_probs = nt(v_ref[:keys, :], grad)
            delta = jnp.sum(probs * grad_probs, axis=0, keepdims=True)
            dv_acc[:keys, :] += nn(probs.astype(BF16), grad)
            grad_scores = probs * (grad_probs - delta)
            for i in range(start // TILE, keys // TILE):
                for j in range(i + 1):
                    sums[i - j] = sums[i - j] + grad_scores[
                        j * TILE : (j + 1) * TILE, i * TILE - start : (i + 1) * TILE - start
                    ]
            low_scores = grad_scores.astype(BF16)
            dk_acc[:keys, :] += nn(low_scores, query)
            dqt_ref[rows, cols] = tn(k_ref[:keys, :], low_scores)[rows]
        lines = [unskewed(tile) for tile in sums]
        parts = []
        for block in range(blocks):
            part = lines[block][:, TILE:]
            if block + 1 < blocks:
                part = part + lines[block + 1][:, :TILE]
            parts.append(part)
        dbias_ref[head : head + 1, :] = jnp.concatenate(parts, axis=1)
    dq_ref[...] = dqt_ref[...].T.astype(BF16)
    dk_ref[...] = dk_acc[...].astype(BF16)
    dv_ref[...] = dv_acc[...].astype(BF16)


def self_forward_kernel(
    normed_ref, bias_ref, *refs
):
    mixed_ref, attended_ref, lse_ref, partial_ref, weights_ref, acc_ref, sems = refs[2:]
    copies = fetch(refs[:2], [], weights_ref, sems)
    for copy in copies:
        copy.wait()
    part = attended_ref.shape[1]
    pairs = part // PAIR
    normed = normed_ref[...]

    @pl.loop(0, 3 * part // TILE)
    def project(i):
        cols = pl.ds(pl.multiple_of(i * TILE, TILE), TILE)
        mixed_ref[:, cols] = nn(normed, weights_ref[:, cols]).astype(BF16)

    def attend(pair, cols):
        self_forward_pair(
            *(mixed_ref.at[:, cols(i)] for i in range(3)),
            bias_ref.at[pair], attended_ref.at[:, cols(0)], lse_ref.at[pair], acc_ref,
        )

    each_pair(pairs, attend)
    partial_ref[...] = nt(attended_ref[...], weights_ref[:, 3 * part :])


def self_forward(normed, bias, quarters):
    targets, width = normed.shape
    columns = quarters[0].shape[1]
    part = columns // 4
    pairs = part // PAIR
    return kernel_call(
        self_forward_kernel,
        [normed, bias, *quarters],
        [
            struct((targets, 3 * part), BF16),
            struct((targets, part), BF16),
            struct((pairs, 8, targets), F32),
            struct((targets, width), F32),
        ],
        [
            pltpu.VMEM((width, columns), BF16),
            pltpu.VMEM((PAIR, targets), F32),
            pltpu.SemaphoreType.DMA((6,)),
        ],
        in_specs=[IN_VMEM] * 2 + [IN_PLACE] * 2,
        time=12,
    )


def encoder_kernel(core_ref, own_ref, peer_ref, order_ref, *refs):
    encoded_ref, out_ref, weights_ref, sems = refs[2:]

    @pl.when(pl.program_id(0) == 0)
    def load():
        for copy in fetch([], refs[:2], weights_ref, sems, weights_ref.shape[1]):
            copy.wait()

    core, half = core_ref[0], own_ref.shape[1]
    own_rows = pl.ds(pl.multiple_of(core * half, half), half)
    peer_rows = pl.ds(pl.multiple_of(half - core * half, half), half)
    encoded = nn(own_ref[...], order_ref[own_rows, :]) + nn(peer_ref[...], order_ref[peer_rows, :])
    encoded_ref[...] = encoded.astype(BF16)
    encoded = encoded_ref[...]

    def project(cols):
        out_ref[:, cols] = nn(encoded, weights_ref[:, cols]).astype(BF16)

    each_tile(0, out_ref.shape[1], project)


def encoder_call(core, own, peer, order, quarters):
    capacity, half = own.shape
    width = 2 * half
    columns = quarters[0].shape[1] // 2
    size = min(capacity, KEYS)
    block = lambda cols: pl.BlockSpec((size, cols), lambda i: (i, 0))
    return kernel_call(
        encoder_kernel,
        [core, own, peer, order, *quarters],
        [struct((capacity, width), BF16), struct((capacity, columns), BF16)],
        [pltpu.VMEM((width, columns), BF16), pltpu.SemaphoreType.DMA((4,))],
        grid=(capacity // size,),
        in_specs=[IN_SMEM, block(half), block(half), IN_VMEM] + [IN_PLACE] * 2,
        out_specs=[block(width), block(columns)],
        time=8,
    )


def cross_forward_kernel(tokens_ref, partial_ref, peer_ref, gains_ref, kv_ref, dead_ref, *refs):
    (
        h_ref, normed_ref, query_ref, att_ref, lse_ref, out_ref, more_ref,
        weights_ref, s_ref, acc_ref, sems,
    ) = refs[2:]
    copies = fetch([], refs[:2], weights_ref, sems)
    gain = gains_ref[1:2, :]

    def norm(rows):
        value = tokens_ref[rows, :] + (partial_ref[rows, :] + peer_ref[rows, :])
        h_ref[rows, :] = value
        normed_ref[rows, :] = (value * root_of(value) * gain).astype(BF16)

    each_rows(h_ref.shape[0], norm)
    for copy in copies:
        copy.wait()
    part = query_ref.shape[1]
    pairs = part // PAIR
    query_ref[...] = nn(normed_ref[...], weights_ref[:, :part]).astype(BF16)

    def attend(pair, cols):
        cross_forward_pair(
            query_ref.at[:, cols(0)], kv_ref.at[:, cols(0)], kv_ref.at[:, cols(1)], dead_ref,
            att_ref.at[:, cols(0)], lse_ref.at[pair], s_ref, acc_ref,
        )

    each_pair(pairs, attend)
    count = out_ref.shape[0]
    out_ref[...] = nt(att_ref[:count, :], weights_ref[:, part:])
    more_ref[...] = nt(att_ref[count:, :], weights_ref[:, part:])


def cross_forward(tokens, partial, peer, gains, key_value, dead, quarters):
    targets, width = tokens.shape
    capacity, columns = key_value.shape
    part = columns // 2
    pairs = part // PAIR
    return kernel_call(
        cross_forward_kernel,
        [tokens, partial, peer, gains, key_value, dead, *quarters],
        [
            struct((targets, width), F32),
            struct((targets, width), BF16),
            struct((targets, part), BF16),
            struct((targets, part), BF16),
            struct((pairs, 8, targets), F32),
            struct((targets // 2, width), F32),
            struct((targets // 2, width), F32),
        ],
        [
            pltpu.VMEM((width, columns), BF16),
            pltpu.VMEM((capacity, queries_of(capacity)), F32),
            pltpu.VMEM((PAIR, targets), F32),
            pltpu.SemaphoreType.DMA((4,)),
        ],
        in_specs=[IN_VMEM] * 6 + [IN_PLACE] * 2,
        time=16,
    )


def ffn_kernel(
    before_ref, first_ref, second_ref, first_in_ref, second_in_ref, gains_ref, cot_ref, *refs
):
    h_ref, down_ref, back_ref, *outs = refs[4:11]
    weights_ref, grads_ref, normed_ref, normed_t, cot_t, in_sems, out_sems = refs[11:]
    copies = fetch(refs[:2], refs[2:4], weights_ref, in_sems)
    gain = gains_ref[2:3, :]
    count = first_ref.shape[0]
    halves = ((first_ref, first_in_ref), (second_ref, second_in_ref))
    for i, (partial_ref, peer_ref) in enumerate(halves):

        def norm(rows):
            own = pl.ds(pl.multiple_of(rows.start + i * count, ROWS), ROWS)
            value = before_ref[own, :] + (partial_ref[rows, :] + peer_ref[rows, :])
            h_ref[own, :] = value
            normed_ref[own, :] = (value * root_of(value) * gain).astype(BF16)

        each_rows(count, norm)
    normed_t[...] = normed_ref[...].T
    cot_t[...] = cot_ref[...].T
    down_ref[...] = jnp.zeros_like(down_ref)
    back_ref[...] = jnp.zeros_like(back_ref)
    for copy in copies:
        copy.wait()
    hidden = weights_ref.shape[1] // 3

    @pl.loop(0, hidden // WIDE)
    def tile(i):
        gates, ups, downs = (
            pl.ds(pl.multiple_of(k * hidden + i * WIDE, WIDE), WIDE) for k in range(3)
        )
        normed = normed_ref[...]
        gate = nn(normed, weights_ref[:, gates])
        up = nn(normed, weights_ref[:, ups])
        grad_act = nn(cot_ref[...], weights_ref[:, downs]).astype(BF16).astype(F32)
        square = gate * gate
        curve = jnp.tanh(GELU_ROOT * (gate + GELU_CUBE * (square * gate)))
        share = 0.5 * (1.0 + curve)
        gelu = gate * share
        slope = share + (0.5 * gate) * (1.0 - curve * curve) * (
            GELU_ROOT * (1.0 + (3.0 * GELU_CUBE) * square)
        )
        act = (gelu * up).astype(BF16)
        grad_gate = (grad_act * up * slope).astype(BF16)
        grad_up = (grad_act * gelu).astype(BF16)
        back_ref[...] += nt(grad_gate, weights_ref[:, gates]) + nt(grad_up, weights_ref[:, ups])
        down_ref[...] += nt(act, weights_ref[:, downs])
        grads_ref[:, gates] = nn(normed_t[...], grad_gate).astype(BF16)
        grads_ref[:, ups] = nn(normed_t[...], grad_up).astype(BF16)
        grads_ref[:, downs] = nn(cot_t[...], act).astype(BF16)

    deliver(grads_ref, outs, out_sems)


def ffn_call(before, partials, peers, gains, cot, quarters):
    targets, width = before.shape
    columns = 2 * quarters[0].shape[1]
    return kernel_call(
        ffn_kernel,
        [before, *partials, *peers, gains, cot, *quarters],
        [struct((targets, width), F32)] * 3 + grad_structs(width, columns),
        [
            pltpu.VMEM((width, columns), BF16),
            pltpu.VMEM((width, columns), BF16),
            pltpu.VMEM((targets, width), BF16),
            pltpu.VMEM((width, targets), BF16),
            pltpu.VMEM((width, targets), BF16),
            pltpu.SemaphoreType.DMA((6,)),
            pltpu.SemaphoreType.DMA((6,)),
        ],
        in_specs=[IN_VMEM] * 7 + [IN_PLACE] * 4,
        out_specs=[IN_VMEM] * 3 + [IN_PLACE] * 4,
        time=20,
    )


def cross_backward_kernel(
    cot_ref, partial_ref, peer_ref, h_ref, gains_ref, query_ref, kv_ref, dead_ref, lse_ref, *refs
):
    (
        g_ref, low_ref, dq_ref, dkv_ref, back_ref, gain_grad_ref,
        weights_ref, go_ref, p_ref, dp_ref, dqt_ref, dk_acc, dv_acc, delta_ref, sems,
    ) = refs[2:]
    copies = fetch([], refs[:2], weights_ref, sems)
    gain = gains_ref[2:3, :]
    gain_grad_ref[...] = jnp.zeros_like(gain_grad_ref)

    def norm(rows):
        back, gain_grad = norm_back(h_ref[rows, :], gain, partial_ref[rows, :] + peer_ref[rows, :])
        gain_grad_ref[0:1, :] += gain_grad
        value = cot_ref[rows, :].astype(F32) + back
        g_ref[rows, :] = value
        low_ref[rows, :] = value.astype(BF16)

    each_rows(h_ref.shape[0], norm)
    for copy in copies:
        copy.wait()
    part = query_ref.shape[1]
    pairs = part // PAIR
    go_ref[...] = nn(low_ref[...], weights_ref[:, part:]).astype(BF16)

    def attend(pair, cols):
        cross_backward_pair(
            query_ref.at[:, cols(0)], kv_ref.at[:, cols(0)], kv_ref.at[:, cols(1)], dead_ref,
            lse_ref.at[pair], go_ref.at[:, cols(0)],
            dq_ref.at[:, cols(0)], dkv_ref.at[:, cols(0)], dkv_ref.at[:, cols(1)],
            p_ref, dp_ref, dqt_ref, dk_acc, dv_acc, delta_ref,
        )

    each_pair(pairs, attend)
    back_ref[...] = nt(dq_ref[...], weights_ref[:, :part])


def cross_backward(cot, partial, peer, before, gains, query, key_value, dead, lse, quarters):
    targets, width = cot.shape
    capacity, columns = key_value.shape
    return kernel_call(
        cross_backward_kernel,
        [cot, partial, peer, before, gains, query, key_value, dead, lse, *quarters],
        [
            struct((targets, width), F32),
            struct((targets, width), BF16),
            struct(query.shape, BF16),
            struct(key_value.shape, BF16),
            struct((targets, width), F32),
            struct((8, width), F32),
        ],
        [
            pltpu.VMEM((width, columns), BF16),
            pltpu.VMEM(query.shape, BF16),
            pltpu.VMEM((capacity, queries_of(capacity)), F32),
            pltpu.VMEM((capacity, queries_of(capacity)), F32),
            pltpu.VMEM((PAIR, targets), F32),
            pltpu.VMEM((capacity, PAIR), F32),
            pltpu.VMEM((capacity, PAIR), F32),
            pltpu.VMEM((1, queries_of(capacity)), F32),
            pltpu.SemaphoreType.DMA((4,)),
        ],
        in_specs=[IN_VMEM] * 9 + [IN_PLACE] * 2,
        time=18,
    )


def cross_grads_kernel(
    core_ref, normed_ref, dq_ref, low_ref, att_ref, order_ref, encoded_ref, dkv_ref, *refs
):
    kept_ref, given_ref, *outs = refs[2:8]
    weights_ref, acc_ref, grads_ref, in_sems, out_sems = refs[8:]
    step = pl.program_id(0)
    part = dq_ref.shape[1]

    @pl.when(step == 0)
    def load():
        copies = fetch([], refs[:2], weights_ref, in_sems, weights_ref.shape[1])
        grads_ref[:, :part] = tn(normed_ref[...], dq_ref[...]).astype(BF16)
        grads_ref[:, part : 2 * part] = tn(low_ref[...], att_ref[...]).astype(BF16)
        acc_ref[...] = jnp.zeros_like(acc_ref)
        for copy in copies:
            copy.wait()

    encoded_t = encoded_ref[...].T

    def project(cols):
        acc_ref[:, cols] += nn(encoded_t, dkv_ref[:, cols])

    each_tile(0, acc_ref.shape[1], project)
    core, half = core_ref[0], kept_ref.shape[1]
    terms = nt(dkv_ref[...], weights_ref[...]).astype(BF16)
    own_rows = pl.ds(pl.multiple_of(core * half, half), half)
    peer_rows = pl.ds(pl.multiple_of(half - core * half, half), half)
    kept_ref[...] = nt(terms, order_ref[own_rows, :]).astype(BF16)
    given_ref[...] = nt(terms, order_ref[peer_rows, :]).astype(BF16)

    @pl.when(step == pl.num_programs(0) - 1)
    def store():
        grads_ref[:, 2 * part :] = acc_ref[...].astype(BF16)
        deliver(grads_ref, outs, out_sems)


def cross_grads(core, normed, dq, low_two, attended, order, encoded, dkv, quarters):
    capacity, width = encoded.shape
    columns = dkv.shape[1]
    size = min(capacity, KEYS)
    block = lambda cols: pl.BlockSpec((size, cols), lambda i: (i, 0))
    return kernel_call(
        cross_grads_kernel,
        [core, normed, dq, low_two, attended, order, encoded, dkv, *quarters],
        [struct((capacity, width // 2), BF16)] * 2 + grad_structs(width, 2 * columns),
        [
            pltpu.VMEM((width, columns), BF16),
            pltpu.VMEM((width, columns), F32),
            pltpu.VMEM((width, 2 * columns), BF16),
            pltpu.SemaphoreType.DMA((4,)),
            pltpu.SemaphoreType.DMA((6,)),
        ],
        grid=(capacity // size,),
        in_specs=[IN_SMEM] + [IN_VMEM] * 5 + [block(width), block(columns)] + [IN_PLACE] * 2,
        out_specs=[block(width // 2)] * 2 + [IN_PLACE] * 4,
        time=12,
    )


def self_backward_kernel(
    core_ref, g_in_ref, partial_ref, peer_ref, h_ref, gains_ref, mixed_ref, bias_ref, lse_ref,
    attended_ref, normed_ref, tokens_ref, gain_three_ref, order_ref, labels_ref, *refs
):
    g_ref, back_ref, small_ref, *outs = refs[2:9]
    (
        weights_ref, grads_ref, low_ref, go_ref, dmixed_ref, dbias_ref,
        dqt_ref, dk_acc, dv_acc, gain_ref, in_sems, out_sems,
    ) = refs[9:]
    copies = fetch(refs[:2], [], weights_ref, in_sems)
    gain = gains_ref[1:2, :]
    gain_ref[...] = jnp.zeros_like(gain_ref)

    def norm(rows):
        back, gain_grad = norm_back(h_ref[rows, :], gain, partial_ref[rows, :] + peer_ref[rows, :])
        gain_ref[1:2, :] += gain_grad
        value = g_in_ref[rows, :] + back
        g_ref[rows, :] = value
        low_ref[rows, :] = value.astype(BF16)

    each_rows(h_ref.shape[0], norm)
    for copy in copies:
        copy.wait()
    part = attended_ref.shape[1]
    pairs = part // PAIR
    go_ref[...] = nn(low_ref[...], weights_ref[:, 3 * part :]).astype(BF16)
    dbias_ref[...] = jnp.zeros_like(dbias_ref)

    def attend(pair, cols):
        self_backward_pair(
            *(mixed_ref.at[:, cols(i)] for i in range(3)),
            bias_ref.at[pair], lse_ref.at[pair], go_ref.at[:, cols(0)],
            *(dmixed_ref.at[:, cols(i)] for i in range(3)),
            dbias_ref.at[pair], dqt_ref, dk_acc, dv_acc,
        )

    each_pair(pairs, attend)
    back_ref[...] = nt(dmixed_ref[...], weights_ref[:, : 3 * part])
    normed_t = normed_ref[...].T

    @pl.loop(0, 3 * part // TILE)
    def project(i):
        cols = pl.ds(pl.multiple_of(i * TILE, TILE), TILE)
        grads_ref[:, cols] = nn(normed_t, dmixed_ref[:, cols]).astype(BF16)

    grads_ref[:, 3 * part :] = tn(low_ref[...], attended_ref[...]).astype(BF16)

    def sums(rows):
        value = tokens_ref[rows, :]
        gain_ref[0:1, :] += jnp.sum(back_ref[rows, :] * value * root_of(value), axis=0, keepdims=True)

    each_rows(h_ref.shape[0], sums)
    core = core_ref[0]
    first = jnp.where(core == 0, 1.0, 0.0)
    line = lax.broadcasted_iota(jnp.int32, gain_ref.shape, 0)
    gains = gain_ref[...] + jnp.where(line == 2, gain_three_ref[0:1, :], 0.0)
    gains = gains * jnp.where(line == 0, 1.0, first)
    high, middle, rest = (nt(value, order_ref[...]) for value in thirds(gains))
    small_ref[...] = jnp.zeros_like(small_ref)
    small_ref[0:8, :] = high + (middle + rest)
    bucket = lax.broadcasted_iota(jnp.int32, (labels_ref.shape[0], TILE), 1)
    which = jnp.where(labels_ref[:, 0:1] == bucket, 1.0, 0.0).astype(BF16)
    for pair in range(pairs):
        high, middle, rest = (nn(value, which) for value in thirds(dbias_ref[pair]))
        table = high + (middle + rest)
        for side in range(2):
            spot = side * pairs + pair
            small_ref[8:, spot * TILE : (spot + 1) * TILE] = table * jnp.where(
                core == side, 1.0, 0.0
            )
    deliver(grads_ref, outs, out_sems)


def self_backward(
    core, g_in, partial, peer, before, gains, mixed, bias, lse, attended, normed, tokens,
    gain_three, order, labels, quarters,
):
    targets, width = g_in.shape
    part = attended.shape[1]
    pairs = part // PAIR
    return kernel_call(
        self_backward_kernel,
        [
            core, g_in, partial, peer, before, gains, mixed, bias, lse, attended, normed, tokens,
            gain_three, order, labels, *quarters,
        ],
        [
            struct((targets, width), F32),
            struct((targets, width), F32),
            struct((16, width), F32),
        ]
        + grad_structs(width, 4 * part),
        [
            pltpu.VMEM((width, 4 * part), BF16),
            pltpu.VMEM((width, 4 * part), BF16),
            pltpu.VMEM((targets, width), BF16),
            pltpu.VMEM((targets, part), BF16),
            pltpu.VMEM((targets, 3 * part), BF16),
            pltpu.VMEM((pairs, 8, targets), F32),
            pltpu.VMEM((PAIR, targets), F32),
            pltpu.VMEM((targets, PAIR), F32),
            pltpu.VMEM((targets, PAIR), F32),
            pltpu.VMEM((8, width), F32),
            pltpu.SemaphoreType.DMA((6,)),
            pltpu.SemaphoreType.DMA((6,)),
        ],
        in_specs=[IN_SMEM] + [IN_VMEM] * 14 + [IN_PLACE] * 2,
        out_specs=[IN_VMEM] * 3 + [IN_PLACE] * 4,
        time=22,
    )


def last_kernel(
    g_ref, partial_ref, peer_ref, tokens_ref, gains_ref, h_ref, down_ref, down_in_ref, order_ref,
    grad_ref, out_ref,
):
    gain = gains_ref[0:1, :]
    order = order_ref[...]

    def finish(rows):
        back, unused = norm_back(
            tokens_ref[rows, :], gain, partial_ref[rows, :] + peer_ref[rows, :]
        )
        high, middle, rest = (nt(value, order) for value in thirds(g_ref[rows, :] + back))
        grad_ref[rows, :] = high + (middle + rest)
        value = h_ref[rows, :] + (down_ref[rows, :] + down_in_ref[rows, :])
        out_ref[rows, :] = nt(value.astype(BF16), order).astype(BF16)

    count = 4 * ROWS

    @pl.loop(0, g_ref.shape[0] // count)
    def step(i):
        finish(pl.ds(pl.multiple_of(i * count, count), count))


def shards(
    decoder_in,
    encoder_out,
    lengths,
    key_mask,
    assign,
    buckets,
    norm_one,
    norm_two,
    norm_three,
    self_query,
    self_key,
    self_value,
    self_output,
    cross_query,
    cross_key,
    cross_value,
    cross_output,
    ffn_gate,
    ffn_up,
    ffn_down,
    bias_table,
    cotangent,
    *,
    size,
):
    rank = lax.axis_index("dp")
    core = lax.axis_index("mp")
    targets, width = decoder_in.shape[1:]
    capacity = key_mask.shape[1]
    block = width // size
    outer = size // 4
    half = width // 2
    heads = bias_table.shape[1]
    which_core = core.reshape(1)

    spots = jnp.arange(width, dtype=jnp.int32)
    spot = spots // block
    masks = spot // (2 * outer) + 2 * (spot // outer % 2) + 4 * (spot % outer)
    source = jnp.broadcast_to(((rank ^ masks) * block + spots % block)[None], (8, width))

    weights = gather_outer(
        low(
            self_query, self_key, self_value, self_output.T,
            cross_query, cross_output.T, cross_key, cross_value,
        ),
        size,
    )
    gains = jnp.concatenate(
        [norm_one[None], norm_two[None], norm_three[None], jnp.zeros((5, width), F32)]
    )
    tokens, cot, gains, order, normed_one = kernel_call(
        rows_kernel,
        [decoder_in[0], cotangent[0], gains, source],
        [
            struct((targets, width), F32),
            struct((targets, width), BF16),
            struct((8, width), F32),
            struct((width, width), BF16),
            struct((targets, width), BF16),
        ],
        [],
    )
    ffn = low(ffn_gate, ffn_up, ffn_down.T)

    sent = lax.dynamic_slice_in_dim(encoder_out, core * half, half, 2)[assign]
    weights, ffn, normed_one, sent = after((weights, ffn, normed_one, sent))
    weights = gather_first(weights, size)
    weights, ffn, sent = after((weights, ffn, sent))
    weights = send_first(weights, size)
    own = lax.all_to_all(sent, "dp", split_axis=0, concat_axis=0, tiled=True)
    own = own.reshape(capacity, half)
    labels, bias_table, lengths = after((buckets[:, :TILE], bias_table, lengths), weights[0])
    mine = assign[rank]
    positions = jnp.arange(capacity, dtype=jnp.int32)
    live = (positions < lengths[mine]) & ((key_mask[mine] == 1) | (positions == 0))
    dead = jnp.broadcast_to(jnp.where(live, 0.0, NEGATIVE)[:, None], (capacity, TILE))
    which = labels[None, :, 0] == jnp.arange(bias_table.shape[0], dtype=jnp.int32)[:, None]
    bias = jnp.sum(jnp.where(which[None], bias_table.T[:, :, None], 0.0), axis=1)
    bias = jnp.pad(bias.reshape(heads // 2, 2, targets), ((0, 0), (0, 6), (0, 0)))

    weights, own, ffn, bias, dead = after((weights, own, ffn, bias, dead))
    weights = gather_second(weights, size)
    weights, ffn = after((weights, ffn))
    weights = send_second(weights, size)
    ffn = gather_outer(ffn, size)

    weights, own, ffn = after((weights, own, ffn))
    ffn = gather_first(ffn, size)
    ffn, weights, own = after((ffn, weights, own))
    ffn = send_first(ffn, size)
    own_peer = swap_cores(own)
    left, right = weights
    mixed, attended, lse_self, partial_one = self_forward(normed_one, bias, left)
    ffn, mixed, attended, lse_self, partial_one, own, own_peer = after(
        (ffn, mixed, attended, lse_self, partial_one, own, own_peer)
    )
    ffn = gather_second(ffn, size)
    ffn, partial_one, own = after((ffn, partial_one, own))
    ffn = send_second(ffn, size)
    peer_one = swap_cores(partial_one)
    encoded, key_value = encoder_call(which_core, own, own_peer, order, right)
    h_one, normed_two, cross_q, cross_att, lse_cross, *partial_two = cross_forward(
        tokens, partial_one, peer_one, gains, key_value, dead, right
    )
    peer_two = [swap_cores(value) for value in partial_two]
    h_two, partial_down, partial_three, *grads = ffn_call(
        h_one, partial_two, peer_two, gains, cot, ffn[0] + ffn[1]
    )

    ffn = scatter_first(grads, size)
    peer_three = swap_cores(partial_three)
    g_two, low_two, dq, dkv, partial_four, gain_three = cross_backward(
        cot, partial_three, peer_three, h_two, gains, cross_q, key_value, dead, lse_cross, right
    )
    ffn, dq, dkv, low_two, partial_four = after((ffn, dq, dkv, low_two, partial_four))
    ffn = scatter_second_parts(ffn)
    ffn, dq, dkv, low_two, partial_four = after((ffn, dq, dkv, low_two, partial_four))
    ffn = scatter_second_send(ffn, size)
    peer_four = swap_cores(partial_four)
    kept, given, *grads = cross_grads(
        which_core, normed_two, dq, low_two, cross_att, order, encoded, dkv, right
    )
    ffn, kept, given, grads, peer_four = after((ffn, kept, given, grads, peer_four))
    ffn = scatter_outer_parts(ffn)
    ffn, kept, given, grads, peer_four = after((ffn, kept, given, grads, peer_four))
    cross = scatter_first(grads, size)
    ffn = scatter_outer_send(ffn, size)
    taken = swap_cores(given)
    g_one, partial_five, small, *grads = self_backward(
        which_core, g_two, partial_four, peer_four, h_one, gains, mixed, bias, lse_self, attended,
        normed_one, tokens, gain_three, order, labels, left,
    )
    ffn, cross, kept, taken, g_one, partial_five, small, grads = after(
        (ffn, cross, kept, taken, g_one, partial_five, small, grads)
    )
    last = scatter_first(grads, size)
    peer_five = swap_cores(partial_five)
    peer_down = swap_cores(partial_down)
    terms = (kept.astype(F32) + taken.astype(F32)).astype(BF16)
    cross = scatter_second_send(scatter_second_parts(cross), size)
    back = lax.all_to_all(
        terms.reshape(size, capacity // size, half), "dp", split_axis=0, concat_axis=0, tiled=True
    )
    sum_ffn = scatter_last(ffn)
    decoder_grad, layer_out = kernel_call(
        last_kernel,
        [g_one, partial_five, peer_five, tokens, gains, h_two, partial_down, peer_down, order],
        [struct((targets, width), F32), struct((targets, width), BF16)],
        [],
        time=10,
    )
    last, cross, layer_out, sum_ffn, small = after((last, cross, layer_out, sum_ffn, small))
    last, cross = scatter_second_parts(last), scatter_outer_parts(cross)
    last, cross, back = after((last, cross, back))
    last = scatter_second_send(last, size)
    cross = scatter_outer_send(cross, size)
    small = small + swap_cores(small)
    last, small = after((last, small))
    last = scatter_outer_parts(last)
    last, small, back = after((last, small, back))
    last = scatter_outer_send(last, size)
    small = sum_devices(small, size)
    inverse = jnp.zeros_like(assign).at[assign].set(jnp.arange(size, dtype=jnp.int32))
    encoder_grad = back[inverse]
    sum_cross, sum_self = scatter_last(cross), scatter_last(last)

    table = small[8:10].reshape(2, 2, heads // 2, TILE)[:, :, :, : bias_table.shape[0]]
    table = lax.dynamic_index_in_dim(table, core, 1, keepdims=False)
    grad_table = table.transpose(1, 0, 2).reshape(heads, -1).T

    def parts(value, count):
        step = value.shape[1] // count
        return [value[:, i * step : (i + 1) * step] for i in range(count)]

    grad_self_query, grad_self_key, grad_self_value, grad_output_one = parts(sum_self, 4)
    grad_cross_query, grad_output_two, grad_cross_key, grad_cross_value = parts(sum_cross, 4)
    grad_ffn_gate, grad_ffn_up, grad_ffn_down = parts(sum_ffn, 3)
    return (
        layer_out[None],
        decoder_grad[None],
        encoder_grad,
        small[0],
        small[1],
        small[2],
        grad_self_query,
        grad_self_key,
        grad_self_value,
        grad_output_one.T,
        grad_cross_query,
        grad_cross_key,
        grad_cross_value,
        grad_output_two.T,
        grad_ffn_gate,
        grad_ffn_up,
        grad_ffn_down.T,
        grad_table,
    )


def solution(mesh):
    in_specs = (
        P("dp", None, None),
        P(None, "dp", None),
        P(),
        P(),
        P(),
        P(),
        P(),
        P(),
        P(),
        P("dp", "mp"),
        P("dp", "mp"),
        P("dp", "mp"),
        P("mp", "dp"),
        P("dp", "mp"),
        P("dp", "mp"),
        P("dp", "mp"),
        P("mp", "dp"),
        P("dp", "mp"),
        P("dp", "mp"),
        P("mp", "dp"),
        P(None, "mp"),
        P("dp", None, None),
    )
    out_specs = (
        P("dp", None, None),
        P("dp", None, None),
        P(None, "dp", "mp"),
        P(),
        P(),
        P(),
        P("dp", "mp"),
        P("dp", "mp"),
        P("dp", "mp"),
        P("mp", "dp"),
        P("dp", "mp"),
        P("dp", "mp"),
        P("dp", "mp"),
        P("mp", "dp"),
        P("dp", "mp"),
        P("dp", "mp"),
        P("mp", "dp"),
        P(None, "mp"),
    )
    body = functools.partial(shards, size=mesh.shape["dp"])
    return jax.shard_map(body, mesh=mesh, in_specs=in_specs, out_specs=out_specs, check_vma=False)
```

```python
import functools

import jax
import jax.numpy as jnp
from jax import lax
from jax.experimental import pallas as pl
from jax.experimental.pallas import tpu as pltpu
from jax.sharding import PartitionSpec as P

HEAD_DIM = 64
PAIR = 2 * HEAD_DIM
QUERIES = 256
KEYS = 1024
TILE = 128
WIDE = 256
HIDDEN = 512
ROWS = 64

EPS = 1e-06
NEGATIVE = -1000000000.0
GELU_ROOT = 0.7978845608028654
GELU_CUBE = 0.044715
BF16 = jnp.bfloat16
F32 = jnp.float32


def dot(left, right, dims):
    return lax.dot_general(left, right, (dims, ((), ())), preferred_element_type=F32)


def nn(left, right):
    return dot(left, right, ((1,), (0,)))


def nt(left, right):
    return dot(left, right, ((1,), (1,)))


def tn(left, right):
    return dot(left, right, ((0,), (0,)))


def struct(shape, dtype):
    return jax.ShapeDtypeStruct(shape, dtype)


def halves(value):
    high = value.astype(BF16)
    return high, (value - high.astype(F32)).astype(BF16)


def swap(value, mask, size):
    return lax.ppermute(value, "dp", [(i, i ^ mask) for i in range(size)])


def swap_cores(value):
    return lax.ppermute(value, "mp", [(0, 1), (1, 0)])


def after(values, *others):
    return lax.optimization_barrier((values, others))[0]


def gather_outer(shard, size, late=()):
    if size <= 16:
        held = after(shard, late)
        ins = [swap(held if mask + 4 == size else shard, mask, size) for mask in range(4, size, 4)]
        return [shard] + ins
    shard = after(shard, late)
    mask = 4
    while mask < size:
        shard = jnp.concatenate([shard, swap(shard, mask, size)])
        mask *= 2
    return [shard]


def gather_first(pieces, size):
    rows, half = sum(piece.shape[0] for piece in pieces), pieces[0].shape[1] // 2
    return kernel_call(stack_kernel, list(pieces), [struct((rows, half), BF16)] * 2, [])


def gather_second(state, size, time=2):
    rows, half = state[0].shape
    outs = [struct((2 * rows, half), BF16)] * 2
    return kernel_call(join_kernel, list(state), outs, [], time=time)


def send_first(halves, size):
    left, right = halves
    return left, swap(left, 2, size), right, swap(right, 1, size)


def send_second(halves, size):
    left, right = halves
    return [left, swap(left, 1, size)], [right, swap(right, 2, size)]


def scatter_first(grads, size):
    left, left_out, right, right_out = grads
    return left, right, swap(left_out, 1, size), swap(right_out, 2, size)


def scatter_second_parts(state, time=2):
    left = state[0]
    rows, half = left.shape[0] // 2, left.shape[1]
    outs = kernel_call(
        scatter_second_kernel,
        list(state),
        [struct((rows, half), BF16)] * 2,
        [],
        time=time,
        grid=(1,),
        in_specs=[pl.BlockSpec((rows, half), lambda i: (1, 0))] * 4,
        out_specs=[pl.BlockSpec((rows, half), lambda i: (0, 0))] * 2,
    )
    return (*state, *outs)


def scatter_second_send(parts, size):
    *state, left_out, right_out = parts
    return (*state, swap(left_out, 2, size), swap(right_out, 1, size))


def scatter_outer_parts(state, *sides):
    rows, half = state[-1].shape
    ins = [value for side in sides for value in state[side::2]]
    width = len(sides) * half
    return kernel_call(
        scatter_outer_kernel,
        ins,
        [struct((rows // 4, width), dtype) for dtype in (F32, BF16, BF16, BF16)],
        [],
        grid=(1,),
        in_specs=[pl.BlockSpec((rows, half), lambda i: (0, 0))] * len(ins),
        out_specs=[pl.BlockSpec((rows // 4, width), lambda i: (0, 0))] * 4,
    )


def scatter_outer_send(parts, size):
    keep, *outs = parts
    if size == 16:
        return [keep] + [swap(out, 4 * (k + 1), size) for k, out in enumerate(outs)]
    rows = jnp.concatenate([keep] + [out.astype(F32) for out in outs])
    mask = size // 2
    while mask >= 4:
        count = rows.shape[0] // 2
        rows = rows[:count] + swap(rows[count:].astype(BF16), mask, size).astype(F32)
        mask //= 2
    return [rows]


def scatter_last(state):
    total = state[0]
    for value in state[1:]:
        total = total + value.astype(F32)
    return total


def kernel_call(kernel, ins, outs, scratch, time=2, grid=None, in_specs=None, out_specs=None):
    everywhere = pl.BlockSpec(memory_space=pltpu.VMEM)
    return pl.pallas_call(
        kernel,
        out_shape=outs,
        in_specs=in_specs or [everywhere] * len(ins),
        out_specs=out_specs or [everywhere] * len(outs),
        scratch_shapes=scratch,
        compiler_params=pltpu.CompilerParams(vmem_limit_bytes=58 * 1024 * 1024),
        cost_estimate=pl.CostEstimate(
            flops=time * 1000000000, bytes_accessed=1, transcendentals=0
        ),
        **({"grid": grid} if grid else {}),
    )(*ins)


IN_VMEM = pl.BlockSpec(memory_space=pltpu.VMEM)
IN_PLACE = pl.BlockSpec(memory_space=pl.ANY)
IN_SMEM = pl.BlockSpec(memory_space=pltpu.SMEM)


def stack_kernel(*refs):
    *in_refs, left_ref, right_ref = refs
    half = left_ref.shape[1]
    start = 0
    for ref in in_refs:
        rows = slice(start, start + ref.shape[0])
        left_ref[rows, :] = ref[:, :half]
        right_ref[rows, :] = ref[:, half:]
        start += ref.shape[0]


def join_kernel(left_ref, left_in_ref, right_ref, right_in_ref, left_out, right_out):
    count = left_ref.shape[0]
    left_out[:count, :] = left_ref[...]
    left_out[count:, :] = left_in_ref[...]
    right_out[:count, :] = right_ref[...]
    right_out[count:, :] = right_in_ref[...]


def scatter_second_kernel(left_ref, right_ref, left_in_ref, right_in_ref, left_out, right_out):
    left_out[...] = (left_ref[...].astype(F32) + left_in_ref[...].astype(F32)).astype(BF16)
    right_out[...] = (right_ref[...].astype(F32) + right_in_ref[...].astype(F32)).astype(BF16)


def scatter_outer_kernel(*refs):
    *in_refs, keep_ref, first_ref, second_ref, third_ref = refs
    count = keep_ref.shape[0]
    for side in range(len(in_refs) // 3):
        own_ref, in_ref, more_ref = in_refs[3 * side : 3 * side + 3]
        half = own_ref.shape[1]
        cols = slice(side * half, (side + 1) * half)
        for k, out_ref in enumerate((keep_ref, first_ref, second_ref, third_ref)):
            rows = slice(k * count, (k + 1) * count)
            total = own_ref[rows, :].astype(F32) + in_ref[rows, :].astype(F32)
            out_ref[:, cols] = (total + more_ref[rows, :].astype(F32)).astype(out_ref.dtype)


def cast_kernel(*refs):
    *in_refs, out_ref = refs
    start = 0
    for ref in in_refs:
        out_ref[:, start : start + ref.shape[1]] = ref[...].astype(BF16)
        start += ref.shape[1]


def low(*values):
    width = sum(value.shape[1] for value in values)
    return kernel_call(
        cast_kernel, list(values), [struct((values[0].shape[0], width), BF16)], []
    )[0]


def each_rows(count, body):
    @pl.loop(0, count // ROWS)
    def step(i):
        body(pl.ds(pl.multiple_of(i * ROWS, ROWS), ROWS))


def each_tile(start, width, body):
    @pl.loop(0, width // WIDE)
    def step(i):
        body(pl.ds(pl.multiple_of(start + i * WIDE, WIDE), WIDE))


def fetch(left, right, weights_ref, sems, first=0):
    moves = []
    start = left[0].shape[1] if left else 0
    for i, ref in enumerate(left):
        count = ref.shape[0]
        moves.append((ref, weights_ref.at[i * count : (i + 1) * count, :start]))
    columns = weights_ref.shape[1] - start
    for i, ref in enumerate(right):
        count = ref.shape[0] // 2
        for x in range(2):
            place = (2 * x + i) * count
            moves.append(
                (
                    ref.at[x * count : (x + 1) * count, first : first + columns],
                    weights_ref.at[place : place + count, start:],
                )
            )
    copies = [pltpu.make_async_copy(*move, sems.at[i]) for i, move in enumerate(moves)]
    for copy in copies:
        copy.start()
    return copies


def deliver(grads_ref, out_refs, sems, columns, first=0):
    left, left_out, right, right_out = out_refs
    rows, half = left.shape[0] // 2, left.shape[1]
    side = columns.start // half
    if side == 0:
        moves = [(left, 0, 0, 2), (left_out, 0, 2, 2)]
    else:
        moves = [(right, 0, 0, 1), (right, 1, 2, 1), (right_out, 0, 1, 1), (right_out, 1, 3, 1)]
    copies = []
    for target, spot, place, count in moves:
        copies.append(
            pltpu.make_async_copy(
                grads_ref.at[place * rows : (place + count) * rows, columns],
                target.at[
                    spot * rows : (spot + count) * rows,
                    columns.start - side * half : columns.stop - side * half,
                ],
                sems.at[first + len(copies)],
            )
        )
    for copy in copies:
        copy.start()
    return copies


def deliver_all(grads_ref, out_refs, sems):
    half = out_refs[0].shape[1]
    copies = deliver(grads_ref, out_refs, sems, slice(0, half))
    copies += deliver(grads_ref, out_refs, sems, slice(half, 2 * half), 2)
    for copy in copies:
        copy.wait()


def grad_structs(width, columns):
    return [struct((width // 2, columns // 2), BF16)] * 4


def root_of(value):
    return lax.rsqrt(jnp.mean(value * value, axis=-1, keepdims=True) + EPS)


def norm_back(value, gain, grad):
    root = root_of(value)
    scaled = grad * gain
    inner = jnp.mean(value * scaled, axis=-1, keepdims=True)
    back = root * scaled - value * (root * root * root * inner)
    return back, jnp.sum(grad * value * root, axis=0, keepdims=True)


def rows_kernel(
    tokens_ref, cot_ref, gains_ref, source_ref,
    tokens_out, cot_out, cot_t_out, gains_out, order_ref, turned_ref, normed_ref,
):
    width = tokens_ref.shape[1]
    spot = lax.broadcasted_iota(jnp.int32, (width, width), 0)
    order_ref[...] = jnp.where(spot == source_ref[0:1, :], 1.0, 0.0).astype(BF16)
    order = order_ref[...]
    turned_ref[...] = order.T
    high = gains_ref[...].astype(BF16)
    middle, rest = halves(gains_ref[...] - high.astype(F32))
    gains_out[...] = nn(high, order) + (nn(middle, order) + nn(rest, order))
    tokens_out[...] = nn(tokens_ref[...], order)
    cot_out[...] = nn(cot_ref[...], order).astype(BF16)
    cot_t_out[...] = cot_out[...].T
    gain = gains_out[0:1, :]

    def norm(rows):
        value = tokens_out[rows, :]
        normed_ref[rows, :] = (value * root_of(value) * gain).astype(BF16)

    each_rows(tokens_ref.shape[0], norm)


def queries_of(capacity):
    return QUERIES if capacity <= 2 * KEYS else TILE


def each_chunk(count, size, body):
    if count == 1:
        body(0)
    else:
        pl.loop(0, count)(lambda step: body(pl.multiple_of(step * size, size)))


def each_pair(pairs, body):
    @pl.loop(0, pairs)
    def step(pair):
        body(pair, lambda which: pl.ds(pl.multiple_of((which * pairs + pair) * PAIR, PAIR), PAIR))


def of_head(value, head):
    lane = lax.broadcasted_iota(jnp.int32, value.shape, 1)
    return jnp.where(lane // HEAD_DIM == head, value, jnp.zeros_like(value))


def cross_forward_pair(q_ref, k_ref, v_ref, dead_ref, out_ref, lse_ref, s_ref, acc_ref):
    targets, capacity = q_ref.shape[0], k_ref.shape[0]
    size = min(capacity, KEYS)
    count = capacity // size
    queries = s_ref.shape[1]
    for head in range(2):
        rows = slice(head * HEAD_DIM, (head + 1) * HEAD_DIM)
        line = slice(head, head + 1)
        for start in range(0, targets, queries):
            cols = slice(start, start + queries)
            query = of_head(q_ref[cols, :], head)
            lse_ref[line, cols] = jnp.full((1, queries), NEGATIVE * 2, F32)

            def scores(base):
                keys = pl.ds(base, size)
                score = nt(k_ref[keys, :], query) + dead_ref[keys, 0:1]
                s_ref[keys, :] = score
                lse_ref[line, cols] = jnp.maximum(
                    lse_ref[line, cols], jnp.max(score, axis=0, keepdims=True)
                )

            each_chunk(count, size, scores)
            top = lse_ref[line, cols]
            lse_ref[line, cols] = jnp.zeros((1, queries), F32)

            def weights(base):
                keys = pl.ds(base, size)
                weight = jnp.exp(s_ref[keys, :] - top)
                s_ref[keys, :] = weight
                lse_ref[line, cols] += jnp.sum(weight, axis=0, keepdims=True)

            each_chunk(count, size, weights)
            total = lse_ref[line, cols]
            lse_ref[line, cols] = top + jnp.log(total)
            scale = 1.0 / total
            acc_ref[rows, cols] = jnp.zeros((HEAD_DIM, queries), F32)

            def mix(base):
                keys = pl.ds(base, size)
                probs = (s_ref[keys, :] * scale).astype(BF16)
                acc_ref[rows, cols] += tn(v_ref[keys, :], probs)[rows]

            each_chunk(count, size, mix)
    out_ref[...] = acc_ref[...].T.astype(BF16)


def cross_backward_pair(
    q_ref, k_ref, v_ref, dead_ref, lse_ref, go_ref, dq_ref, dk_ref, dv_ref,
    p_ref, dp_ref, dqt_ref, dk_acc, dv_acc, delta_ref,
):
    targets, capacity = q_ref.shape[0], k_ref.shape[0]
    size = min(capacity, KEYS)
    count = capacity // size
    queries = p_ref.shape[1]
    dk_acc[...] = jnp.zeros_like(dk_acc)
    dv_acc[...] = jnp.zeros_like(dv_acc)
    for head in range(2):
        rows = slice(head * HEAD_DIM, (head + 1) * HEAD_DIM)
        for start in range(0, targets, queries):
            cols = slice(start, start + queries)
            query = of_head(q_ref[cols, :], head)
            grad = of_head(go_ref[cols, :], head)
            lse = lse_ref[head : head + 1, cols]
            delta_ref[...] = jnp.zeros_like(delta_ref)

            def first(base):
                keys = pl.ds(base, size)
                probs = jnp.exp(nt(k_ref[keys, :], query) + dead_ref[keys, 0:1] - lse)
                grad_probs = nt(v_ref[keys, :], grad)
                p_ref[keys, :] = probs
                dp_ref[keys, :] = grad_probs
                delta_ref[...] += jnp.sum(probs * grad_probs, axis=0, keepdims=True)

            each_chunk(count, size, first)
            delta = delta_ref[...]
            dqt_ref[rows, cols] = jnp.zeros((HEAD_DIM, queries), F32)

            def second(base):
                keys = pl.ds(base, size)
                probs = p_ref[keys, :]
                dv_acc[keys, :] += nn(probs.astype(BF16), grad)
                low = (probs * (dp_ref[keys, :] - delta)).astype(BF16)
                dk_acc[keys, :] += nn(low, query)
                dqt_ref[rows, cols] += tn(k_ref[keys, :], low)[rows]

            each_chunk(count, size, second)
    dq_ref[...] = dqt_ref[...].T.astype(BF16)
    dk_ref[...] = dk_acc[...].astype(BF16)
    dv_ref[...] = dv_acc[...].astype(BF16)


def skewed(row, block):
    before = row[:, (block - 1) * TILE : block * TILE] if block else jnp.zeros((1, TILE), F32)
    both = jnp.concatenate([before, row[:, block * TILE : (block + 1) * TILE]], axis=1)
    both = jnp.broadcast_to(both, (TILE, 2 * TILE))
    return pltpu.roll(both, 0, 1, stride=1, stride_axis=0)[:, TILE:]


def unskewed(tile):
    both = jnp.concatenate([jnp.zeros_like(tile), tile], axis=1)
    total = both[:8]
    for base in range(8, TILE, 8):
        total = total + pltpu.roll(both[base : base + 8], 2 * TILE - base, 1)
    row = lax.broadcasted_iota(jnp.int32, total.shape, 0)
    for bit in (1, 2, 4):
        total = jnp.where(row & bit != 0, pltpu.roll(total, 2 * TILE - bit, 1), total)
    return jnp.sum(total, axis=0, keepdims=True)


def self_scores(k_ref, query, tiles, start):
    keys = start + QUERIES
    columns = []
    for i in range(start // TILE, keys // TILE):
        columns.append(
            jnp.concatenate([tiles[max(i - j, 0)] for j in range(keys // TILE)], axis=0)
        )
    score = nt(k_ref[:keys, :], query) + jnp.concatenate(columns, axis=1)
    key = lax.broadcasted_iota(jnp.int32, score.shape, 0)
    spot = lax.broadcasted_iota(jnp.int32, score.shape, 1) + start
    return jnp.where(key <= spot, score, NEGATIVE)


def self_forward_pair(q_ref, k_ref, v_ref, bias_ref, out_ref, lse_ref, acc_ref):
    targets = q_ref.shape[0]
    for head in range(2):
        rows = slice(head * HEAD_DIM, (head + 1) * HEAD_DIM)
        row = bias_ref[head : head + 1, :]
        tiles = [skewed(row, block) for block in range(targets // TILE)]
        for start in range(0, targets, QUERIES):
            cols = slice(start, start + QUERIES)
            query = of_head(q_ref[cols, :], head)
            score = self_scores(k_ref, query, tiles, start)
            top = jnp.max(score, axis=0, keepdims=True)
            weight = jnp.exp(score - top)
            total = jnp.sum(weight, axis=0, keepdims=True)
            lse_ref[head : head + 1, cols] = top + jnp.log(total)
            probs = (weight * (1.0 / total)).astype(BF16)
            acc_ref[rows, cols] = tn(v_ref[: start + QUERIES, :], probs)[rows]
    out_ref[...] = acc_ref[...].T.astype(BF16)


def self_backward_pair(
    q_ref, k_ref, v_ref, bias_ref, lse_ref, go_ref, dq_ref, dk_ref, dv_ref, dbias_ref,
    dqt_ref, dk_acc, dv_acc,
):
    targets = q_ref.shape[0]
    dk_acc[...] = jnp.zeros_like(dk_acc)
    dv_acc[...] = jnp.zeros_like(dv_acc)
    blocks = targets // TILE
    for head in range(2):
        rows = slice(head * HEAD_DIM, (head + 1) * HEAD_DIM)
        row = bias_ref[head : head + 1, :]
        tiles = [skewed(row, block) for block in range(blocks)]
        sums = [jnp.zeros((TILE, TILE), F32) for block in range(blocks)]
        for start in range(0, targets, QUERIES):
            cols = slice(start, start + QUERIES)
            keys = start + QUERIES
            query = of_head(q_ref[cols, :], head)
            grad = of_head(go_ref[cols, :], head)
            score = self_scores(k_ref, query, tiles, start)
            probs = jnp.exp(score - lse_ref[head : head + 1, cols])
            grad_probs = nt(v_ref[:keys, :], grad)
            delta = jnp.sum(probs * grad_probs, axis=0, keepdims=True)
            dv_acc[:keys, :] += nn(probs.astype(BF16), grad)
            grad_scores = probs * (grad_probs - delta)
            for i in range(start // TILE, keys // TILE):
                for j in range(i + 1):
                    sums[i - j] = sums[i - j] + grad_scores[
                        j * TILE : (j + 1) * TILE, i * TILE - start : (i + 1) * TILE - start
                    ]
            low_scores = grad_scores.astype(BF16)
            dk_acc[:keys, :] += nn(low_scores, query)
            dqt_ref[rows, cols] = tn(k_ref[:keys, :], low_scores)[rows]
        lines = [unskewed(tile) for tile in sums]
        parts = []
        for block in range(blocks):
            part = lines[block][:, TILE:]
            if block + 1 < blocks:
                part = part + lines[block + 1][:, :TILE]
            parts.append(part)
        dbias_ref[head : head + 1, :] = jnp.concatenate(parts, axis=1)
    dq_ref[...] = dqt_ref[...].T.astype(BF16)
    dk_ref[...] = dk_acc[...].astype(BF16)
    dv_ref[...] = dv_acc[...].astype(BF16)


def self_forward_kernel(
    normed_ref, bias_ref, *refs
):
    mixed_ref, attended_ref, lse_ref, partial_ref, weights_ref, acc_ref, sems = refs[2:]
    copies = fetch(refs[:2], [], weights_ref, sems)
    for copy in copies:
        copy.wait()
    part = attended_ref.shape[1]
    pairs = part // PAIR
    normed = normed_ref[...]

    @pl.loop(0, 3 * part // TILE)
    def project(i):
        cols = pl.ds(pl.multiple_of(i * TILE, TILE), TILE)
        mixed_ref[:, cols] = nn(normed, weights_ref[:, cols]).astype(BF16)

    def attend(pair, cols):
        self_forward_pair(
            *(mixed_ref.at[:, cols(i)] for i in range(3)),
            bias_ref.at[pair], attended_ref.at[:, cols(0)], lse_ref.at[pair], acc_ref,
        )

    each_pair(pairs, attend)
    partial_ref[...] = nt(attended_ref[...], weights_ref[:, 3 * part :])


def self_forward(normed, bias, quarters):
    targets, width = normed.shape
    columns = quarters[0].shape[1]
    part = columns // 4
    pairs = part // PAIR
    return kernel_call(
        self_forward_kernel,
        [normed, bias, *quarters],
        [
            struct((targets, 3 * part), BF16),
            struct((targets, part), BF16),
            struct((pairs, 8, targets), F32),
            struct((targets, width), F32),
        ],
        [
            pltpu.VMEM((width, columns), BF16),
            pltpu.VMEM((PAIR, targets), F32),
            pltpu.SemaphoreType.DMA((6,)),
        ],
        in_specs=[IN_VMEM] * 2 + [IN_PLACE] * 2,
        time=12,
    )


def encoder_kernel(core_ref, own_ref, peer_ref, order_ref, *refs):
    encoded_ref, out_ref, weights_ref, sems = refs[2:]

    @pl.when(pl.program_id(0) == 0)
    def load():
        for copy in fetch([], refs[:2], weights_ref, sems, weights_ref.shape[1]):
            copy.wait()

    core, half = core_ref[0], own_ref.shape[1]
    own_rows = pl.ds(pl.multiple_of(core * half, half), half)
    peer_rows = pl.ds(pl.multiple_of(half - core * half, half), half)
    encoded = nn(own_ref[...], order_ref[own_rows, :]) + nn(peer_ref[...], order_ref[peer_rows, :])
    encoded_ref[...] = encoded.astype(BF16)
    encoded = encoded_ref[...]

    def project(cols):
        out_ref[:, cols] = nn(encoded, weights_ref[:, cols]).astype(BF16)

    each_tile(0, out_ref.shape[1], project)


def encoder_call(core, own, peer, order, quarters):
    capacity, half = own.shape
    width = 2 * half
    columns = quarters[0].shape[1] // 2
    size = min(capacity, KEYS)
    block = lambda cols: pl.BlockSpec((size, cols), lambda i: (i, 0))
    return kernel_call(
        encoder_kernel,
        [core, own, peer, order, *quarters],
        [struct((capacity, width), BF16), struct((capacity, columns), BF16)],
        [pltpu.VMEM((width, columns), BF16), pltpu.SemaphoreType.DMA((4,))],
        grid=(capacity // size,),
        in_specs=[IN_SMEM, block(half), block(half), IN_VMEM] + [IN_PLACE] * 2,
        out_specs=[block(width), block(columns)],
        time=8,
    )


def cross_forward_kernel(tokens_ref, partial_ref, peer_ref, gains_ref, kv_ref, dead_ref, *refs):
    (
        h_ref, normed_ref, query_ref, att_ref, lse_ref, out_ref, more_ref,
        weights_ref, s_ref, acc_ref, sems,
    ) = refs[2:]
    copies = fetch([], refs[:2], weights_ref, sems)
    gain = gains_ref[1:2, :]

    def norm(rows):
        value = tokens_ref[rows, :] + (partial_ref[rows, :] + peer_ref[rows, :])
        h_ref[rows, :] = value
        normed_ref[rows, :] = (value * root_of(value) * gain).astype(BF16)

    each_rows(h_ref.shape[0], norm)
    for copy in copies:
        copy.wait()
    part = query_ref.shape[1]
    pairs = part // PAIR
    query_ref[...] = nn(normed_ref[...], weights_ref[:, :part]).astype(BF16)

    def attend(pair, cols):
        cross_forward_pair(
            query_ref.at[:, cols(0)], kv_ref.at[:, cols(0)], kv_ref.at[:, cols(1)], dead_ref,
            att_ref.at[:, cols(0)], lse_ref.at[pair], s_ref, acc_ref,
        )

    each_pair(pairs, attend)
    count = out_ref.shape[0]
    out_ref[...] = nt(att_ref[:count, :], weights_ref[:, part:])
    more_ref[...] = nt(att_ref[count:, :], weights_ref[:, part:])


def cross_forward(tokens, partial, peer, gains, key_value, dead, quarters):
    targets, width = tokens.shape
    capacity, columns = key_value.shape
    part = columns // 2
    pairs = part // PAIR
    return kernel_call(
        cross_forward_kernel,
        [tokens, partial, peer, gains, key_value, dead, *quarters],
        [
            struct((targets, width), F32),
            struct((targets, width), BF16),
            struct((targets, part), BF16),
            struct((targets, part), BF16),
            struct((pairs, 8, targets), F32),
            struct((targets // 2, width), F32),
            struct((targets // 2, width), F32),
        ],
        [
            pltpu.VMEM((width, columns), BF16),
            pltpu.VMEM((capacity, queries_of(capacity)), F32),
            pltpu.VMEM((PAIR, targets), F32),
            pltpu.SemaphoreType.DMA((4,)),
        ],
        in_specs=[IN_VMEM] * 6 + [IN_PLACE] * 2,
        time=16,
    )


def ffn_kernel(
    before_ref, first_ref, second_ref, first_in_ref, second_in_ref, gains_ref, cot_ref, cot_t_ref,
    *refs
):
    h_out, down_ref, back_ref, *outs = refs[4:11]
    weights_ref, grads_ref, h_ref, normed_ref, normed_t, in_sems, out_sems = refs[11:]
    copies = fetch(refs[:2], refs[2:4], weights_ref, in_sems)
    gain = gains_ref[2:3, :]
    count = first_ref.shape[0]
    halves = ((first_ref, first_in_ref), (second_ref, second_in_ref))
    for i, (partial_ref, peer_ref) in enumerate(halves):

        def norm(rows):
            own = pl.ds(pl.multiple_of(rows.start + i * count, ROWS), ROWS)
            value = before_ref[own, :] + (partial_ref[rows, :] + peer_ref[rows, :])
            h_ref[own, :] = value
            normed_ref[own, :] = (value * root_of(value) * gain).astype(BF16)

        each_rows(count, norm)
    h_copy = pltpu.make_async_copy(h_ref, h_out, out_sems.at[18])
    h_copy.start()
    normed_t[...] = normed_ref[...].T
    down_ref[...] = jnp.zeros_like(down_ref)
    back_ref[...] = jnp.zeros_like(back_ref)
    for copy in copies:
        copy.wait()
    hidden = weights_ref.shape[1] // 3
    half = outs[0].shape[1]
    sent = []

    def tile(start):
        gates, ups, downs = (
            slice(k * hidden + start, k * hidden + start + HIDDEN) for k in range(3)
        )
        normed = normed_ref[...]
        gate = nn(normed, weights_ref[:, gates])
        up = nn(normed, weights_ref[:, ups])
        grad_act = nn(cot_ref[...], weights_ref[:, downs]).astype(BF16).astype(F32)
        square = gate * gate
        curve = jnp.tanh(GELU_ROOT * (gate + GELU_CUBE * (square * gate)))
        share = 0.5 * (1.0 + curve)
        gelu = gate * share
        slope = share + (0.5 * gate) * (1.0 - curve * curve) * (
            GELU_ROOT * (1.0 + (3.0 * GELU_CUBE) * square)
        )
        act = (gelu * up).astype(BF16)
        grad_gate = (grad_act * up * slope).astype(BF16)
        grad_up = (grad_act * gelu).astype(BF16)
        grads_ref[:, gates] = nn(normed_t[...], grad_gate).astype(BF16)
        grads_ref[:, ups] = nn(normed_t[...], grad_up).astype(BF16)
        grads_ref[:, downs] = nn(cot_t_ref[...], act).astype(BF16)
        for columns in (gates, ups, downs):
            sent.extend(deliver(grads_ref, outs, out_sems, columns, len(sent)))
        back_ref[...] += nt(grad_gate, weights_ref[:, gates]) + nt(grad_up, weights_ref[:, ups])
        down_ref[...] += nt(act, weights_ref[:, downs])

    for start in range(0, hidden, HIDDEN):
        tile(start)
    for copy in sent:
        copy.wait()
    h_copy.wait()


def ffn_call(before, partials, peers, gains, cot, cot_t, quarters):
    targets, width = before.shape
    columns = 2 * quarters[0].shape[1]
    return kernel_call(
        ffn_kernel,
        [before, *partials, *peers, gains, cot, cot_t, *quarters],
        [struct((targets, width), F32)] * 3 + grad_structs(width, columns),
        [
            pltpu.VMEM((width, columns), BF16),
            pltpu.VMEM((width, columns), BF16),
            pltpu.VMEM((targets, width), F32),
            pltpu.VMEM((targets, width), BF16),
            pltpu.VMEM((width, targets), BF16),
            pltpu.SemaphoreType.DMA((6,)),
            pltpu.SemaphoreType.DMA((19,)),
        ],
        time=20,
        in_specs=[IN_VMEM] * 8 + [IN_PLACE] * 4,
        out_specs=[IN_PLACE] + [IN_VMEM] * 2 + [IN_PLACE] * 4,
    )


def cross_backward_kernel(
    cot_ref, partial_ref, peer_ref, h_ref, gains_ref, query_ref, kv_ref, dead_ref, lse_ref, *refs
):
    (
        g_ref, low_ref, dq_ref, dkv_ref, back_ref, gain_grad_ref,
        weights_ref, go_ref, p_ref, dp_ref, dqt_ref, dk_acc, dv_acc, delta_ref, sems,
    ) = refs[2:]
    copies = fetch([], refs[:2], weights_ref, sems)
    gain = gains_ref[2:3, :]
    gain_grad_ref[...] = jnp.zeros_like(gain_grad_ref)

    def norm(rows):
        back, gain_grad = norm_back(h_ref[rows, :], gain, partial_ref[rows, :] + peer_ref[rows, :])
        gain_grad_ref[0:1, :] += gain_grad
        value = cot_ref[rows, :].astype(F32) + back
        g_ref[rows, :] = value
        low_ref[rows, :] = value.astype(BF16)

    each_rows(h_ref.shape[0], norm)
    for copy in copies:
        copy.wait()
    part = query_ref.shape[1]
    pairs = part // PAIR
    go_ref[...] = nn(low_ref[...], weights_ref[:, part:]).astype(BF16)

    def attend(pair, cols):
        cross_backward_pair(
            query_ref.at[:, cols(0)], kv_ref.at[:, cols(0)], kv_ref.at[:, cols(1)], dead_ref,
            lse_ref.at[pair], go_ref.at[:, cols(0)],
            dq_ref.at[:, cols(0)], dkv_ref.at[:, cols(0)], dkv_ref.at[:, cols(1)],
            p_ref, dp_ref, dqt_ref, dk_acc, dv_acc, delta_ref,
        )

    each_pair(pairs, attend)
    back_ref[...] = nt(dq_ref[...], weights_ref[:, :part])


def cross_backward(cot, partial, peer, before, gains, query, key_value, dead, lse, quarters):
    targets, width = cot.shape
    capacity, columns = key_value.shape
    return kernel_call(
        cross_backward_kernel,
        [cot, partial, peer, before, gains, query, key_value, dead, lse, *quarters],
        [
            struct((targets, width), F32),
            struct((targets, width), BF16),
            struct(query.shape, BF16),
            struct(key_value.shape, BF16),
            struct((targets, width), F32),
            struct((8, width), F32),
        ],
        [
            pltpu.VMEM((width, columns), BF16),
            pltpu.VMEM(query.shape, BF16),
            pltpu.VMEM((capacity, queries_of(capacity)), F32),
            pltpu.VMEM((capacity, queries_of(capacity)), F32),
            pltpu.VMEM((PAIR, targets), F32),
            pltpu.VMEM((capacity, PAIR), F32),
            pltpu.VMEM((capacity, PAIR), F32),
            pltpu.VMEM((1, queries_of(capacity)), F32),
            pltpu.SemaphoreType.DMA((4,)),
        ],
        in_specs=[IN_VMEM] * 9 + [IN_PLACE] * 2,
        time=18,
    )


def cross_grads_kernel(
    core_ref, normed_ref, dq_ref, low_ref, att_ref, order_ref, encoded_ref, dkv_ref, *refs
):
    kept_ref, given_ref, *outs = refs[2:8]
    weights_ref, acc_ref, grads_ref, in_sems, out_sems = refs[8:]
    step = pl.program_id(0)
    part = dq_ref.shape[1]

    @pl.when(step == 0)
    def load():
        copies = fetch([], refs[:2], weights_ref, in_sems, weights_ref.shape[1])
        grads_ref[:, :part] = tn(normed_ref[...], dq_ref[...]).astype(BF16)
        grads_ref[:, part : 2 * part] = tn(low_ref[...], att_ref[...]).astype(BF16)
        acc_ref[...] = jnp.zeros_like(acc_ref)
        for copy in copies:
            copy.wait()

    encoded_t = encoded_ref[...].T

    def project(cols):
        acc_ref[:, cols] += nn(encoded_t, dkv_ref[:, cols])

    each_tile(0, acc_ref.shape[1], project)
    core, half = core_ref[0], kept_ref.shape[1]
    terms = nt(dkv_ref[...], weights_ref[...]).astype(BF16)
    own_cols = pl.ds(pl.multiple_of(core * half, half), half)
    peer_cols = pl.ds(pl.multiple_of(half - core * half, half), half)
    kept_ref[...] = nn(terms, order_ref[:, own_cols]).astype(BF16)
    given_ref[...] = nn(terms, order_ref[:, peer_cols]).astype(BF16)

    @pl.when(step == pl.num_programs(0) - 1)
    def store():
        grads_ref[:, 2 * part :] = acc_ref[...].astype(BF16)
        deliver_all(grads_ref, outs, out_sems)


def cross_grads(core, normed, dq, low_two, attended, order, encoded, dkv, quarters):
    capacity, width = encoded.shape
    columns = dkv.shape[1]
    size = min(capacity, KEYS)
    block = lambda cols: pl.BlockSpec((size, cols), lambda i: (i, 0))
    return kernel_call(
        cross_grads_kernel,
        [core, normed, dq, low_two, attended, order, encoded, dkv, *quarters],
        [struct((capacity, width // 2), BF16)] * 2 + grad_structs(width, 2 * columns),
        [
            pltpu.VMEM((width, columns), BF16),
            pltpu.VMEM((width, columns), F32),
            pltpu.VMEM((width, 2 * columns), BF16),
            pltpu.SemaphoreType.DMA((4,)),
            pltpu.SemaphoreType.DMA((6,)),
        ],
        grid=(capacity // size,),
        in_specs=[IN_SMEM] + [IN_VMEM] * 5 + [block(width), block(columns)] + [IN_PLACE] * 2,
        out_specs=[block(width // 2)] * 2 + [IN_PLACE] * 4,
        time=12,
    )


def self_backward_kernel(
    g_in_ref, partial_ref, peer_ref, h_ref, gains_ref, mixed_ref, bias_ref, lse_ref,
    attended_ref, normed_ref, tokens_ref, gain_three_ref, order_ref, labels_ref, *refs
):
    g_ref, back_ref, small_ref, *outs = refs[2:9]
    (
        weights_ref, grads_ref, low_ref, go_ref, dmixed_ref, dbias_ref,
        dqt_ref, dk_acc, dv_acc, gain_ref, pack_ref, in_sems, out_sems,
    ) = refs[9:]
    copies = fetch(refs[:2], [], weights_ref, in_sems)
    gain = gains_ref[1:2, :]
    gain_ref[...] = jnp.zeros_like(gain_ref)

    def norm(rows):
        back, gain_grad = norm_back(h_ref[rows, :], gain, partial_ref[rows, :] + peer_ref[rows, :])
        gain_ref[1:2, :] += gain_grad
        value = g_in_ref[rows, :] + back
        g_ref[rows, :] = value
        low_ref[rows, :] = value.astype(BF16)

    each_rows(h_ref.shape[0], norm)
    for copy in copies:
        copy.wait()
    part = attended_ref.shape[1]
    pairs = part // PAIR
    go_ref[...] = nn(low_ref[...], weights_ref[:, 3 * part :]).astype(BF16)
    dbias_ref[...] = jnp.zeros_like(dbias_ref)

    def attend(pair, cols):
        self_backward_pair(
            *(mixed_ref.at[:, cols(i)] for i in range(3)),
            bias_ref.at[pair], lse_ref.at[pair], go_ref.at[:, cols(0)],
            *(dmixed_ref.at[:, cols(i)] for i in range(3)),
            dbias_ref.at[pair], dqt_ref, dk_acc, dv_acc,
        )

    each_pair(pairs, attend)
    back_ref[...] = nt(dmixed_ref[...], weights_ref[:, : 3 * part])
    normed_t = normed_ref[...].T

    @pl.loop(0, 3 * part // TILE)
    def project(i):
        cols = pl.ds(pl.multiple_of(i * TILE, TILE), TILE)
        grads_ref[:, cols] = nn(normed_t, dmixed_ref[:, cols]).astype(BF16)

    grads_ref[:, 3 * part :] = tn(low_ref[...], attended_ref[...]).astype(BF16)

    def sums(rows):
        value = tokens_ref[rows, :]
        gain_ref[0:1, :] += jnp.sum(back_ref[rows, :] * value * root_of(value), axis=0, keepdims=True)

    each_rows(h_ref.shape[0], sums)
    gain_ref[2:3, :] = gain_three_ref[0:1, :]
    high, rest = halves(gain_ref[...])
    gain_ref[...] = nn(high, order_ref[...]) + nn(rest, order_ref[...])
    half = pack_ref.shape[1]
    pack_ref[0:3, :] = gain_ref[0:3, :half]
    pack_ref[3:6, :] = gain_ref[0:3, half:]
    bucket = lax.broadcasted_iota(jnp.int32, (labels_ref.shape[0], TILE), 1)
    which = jnp.where(labels_ref[:, 0:1] == bucket, 1.0, 0.0).astype(BF16)
    for pair in range(pairs):
        high, rest = halves(dbias_ref[pair])
        table = nn(high, which) + nn(rest, which)
        pack_ref[6:8, pair * TILE : (pair + 1) * TILE] = table[0:2]
    small_ref[...] = jnp.concatenate(halves(pack_ref[...]), axis=0)
    deliver_all(grads_ref, outs, out_sems)


def self_backward(
    g_in, partial, peer, before, gains, mixed, bias, lse, attended, normed, tokens,
    gain_three, order, labels, quarters,
):
    targets, width = g_in.shape
    part = attended.shape[1]
    pairs = part // PAIR
    return kernel_call(
        self_backward_kernel,
        [
            g_in, partial, peer, before, gains, mixed, bias, lse, attended, normed, tokens,
            gain_three, order, labels, *quarters,
        ],
        [
            struct((targets, width), F32),
            struct((targets, width), F32),
            struct((16, width // 2), BF16),
        ]
        + grad_structs(width, 4 * part),
        [
            pltpu.VMEM((width, 4 * part), BF16),
            pltpu.VMEM((width, 4 * part), BF16),
            pltpu.VMEM((targets, width), BF16),
            pltpu.VMEM((targets, part), BF16),
            pltpu.VMEM((targets, 3 * part), BF16),
            pltpu.VMEM((pairs, 8, targets), F32),
            pltpu.VMEM((PAIR, targets), F32),
            pltpu.VMEM((targets, PAIR), F32),
            pltpu.VMEM((targets, PAIR), F32),
            pltpu.VMEM((8, width), F32),
            pltpu.VMEM((8, width // 2), F32),
            pltpu.SemaphoreType.DMA((6,)),
            pltpu.SemaphoreType.DMA((6,)),
        ],
        in_specs=[IN_VMEM] * 14 + [IN_PLACE] * 2,
        out_specs=[IN_VMEM] * 3 + [IN_PLACE] * 4,
        time=22,
    )


def last_kernel(
    g_ref, partial_ref, peer_ref, tokens_ref, h_ref, down_ref, down_in_ref, gains_ref, order_ref,
    grad_ref, out_ref,
):
    order = order_ref[...]
    value = h_ref[...] + (down_ref[...] + down_in_ref[...])
    out_ref[...] = nn(value.astype(BF16), order).astype(BF16)
    back, unused = norm_back(tokens_ref[...], gains_ref[0:1, :], partial_ref[...] + peer_ref[...])
    high, rest = halves(g_ref[...] + back)
    grad_ref[...] = nn(high, order) + nn(rest, order)


def last_call(*ins):
    targets, width = ins[0].shape
    block = pl.BlockSpec((WIDE, width), lambda i: (i, 0))
    return kernel_call(
        last_kernel,
        list(ins),
        [struct((targets, width), F32), struct((targets, width), BF16)],
        [],
        time=8,
        grid=(targets // WIDE,),
        in_specs=[block] * 7 + [IN_VMEM] * 2,
        out_specs=[block] * 2,
    )


def shards(
    decoder_in,
    encoder_out,
    lengths,
    key_mask,
    assign,
    buckets,
    norm_one,
    norm_two,
    norm_three,
    self_query,
    self_key,
    self_value,
    self_output,
    cross_query,
    cross_key,
    cross_value,
    cross_output,
    ffn_gate,
    ffn_up,
    ffn_down,
    bias_table,
    cotangent,
    *,
    size,
):
    rank = lax.axis_index("dp")
    core = lax.axis_index("mp")
    targets, width = decoder_in.shape[1:]
    capacity = key_mask.shape[1]
    block = width // size
    outer = size // 4
    half = width // 2
    heads = bias_table.shape[1]
    which_core = core.reshape(1)

    spots = jnp.arange(width, dtype=jnp.int32)
    spot = spots // block
    masks = spot // (2 * outer) + 2 * (spot // outer % 2) + 4 * (spot % outer)
    source = jnp.broadcast_to(((rank ^ masks) * block + spots % block)[None], (8, width))

    weights = gather_outer(
        low(
            self_query, self_key, self_value, self_output.T,
            cross_query, cross_output.T, cross_key, cross_value,
        ),
        size,
    )
    gains = jnp.concatenate(
        [norm_one[None], norm_two[None], norm_three[None], jnp.zeros((5, width), F32)]
    )
    tokens, cot, cot_t, gains, order, turned, normed_one = kernel_call(
        rows_kernel,
        [decoder_in[0], cotangent[0], gains, source],
        [
            struct((targets, width), F32),
            struct((targets, width), BF16),
            struct((width, targets), BF16),
            struct((8, width), F32),
            struct((width, width), BF16),
            struct((width, width), BF16),
            struct((targets, width), BF16),
        ],
        [],
    )
    ffn = low(ffn_gate, ffn_up, ffn_down.T)

    sent = lax.dynamic_slice_in_dim(encoder_out, core * half, half, 2)[assign]
    weights, ffn, normed_one, sent = after((weights, ffn, normed_one, sent))
    weights = gather_first(weights, size)
    weights, ffn, sent = after((weights, ffn, sent))
    weights = send_first(weights, size)
    own = lax.all_to_all(sent, "dp", split_axis=0, concat_axis=0, tiled=True)
    own = own.reshape(capacity, half)
    labels, bias_table, lengths = after((buckets[:, :TILE], bias_table, lengths), weights[0])
    mine = assign[rank]
    positions = jnp.arange(capacity, dtype=jnp.int32)
    live = (positions < lengths[mine]) & ((key_mask[mine] == 1) | (positions == 0))
    dead = jnp.broadcast_to(jnp.where(live, 0.0, NEGATIVE)[:, None], (capacity, TILE))
    which = labels[None, :, 0] == jnp.arange(bias_table.shape[0], dtype=jnp.int32)[:, None]
    bias = jnp.sum(jnp.where(which[None], bias_table.T[:, :, None], 0.0), axis=1)
    bias = jnp.pad(bias.reshape(heads // 2, 2, targets), ((0, 0), (0, 6), (0, 0)))

    weights, ffn, bias, dead = after((weights, ffn, bias, dead))
    weights = gather_second(weights, size, time=40)
    weights, ffn = after((weights, ffn))
    weights = send_second(weights, size)
    ffn = gather_outer(ffn, size, own)

    weights, own, ffn = after((weights, own, ffn))
    ffn = gather_first(ffn, size)
    ffn, weights, own = after((ffn, weights, own))
    ffn = send_first(ffn, size)
    own_peer = swap_cores(own)
    left, right = weights
    mixed, attended, lse_self, partial_one = self_forward(normed_one, bias, left)
    ffn, mixed, attended, lse_self, partial_one, own, own_peer = after(
        (ffn, mixed, attended, lse_self, partial_one, own, own_peer)
    )
    ffn = gather_second(ffn, size)
    ffn, partial_one, own = after((ffn, partial_one, own))
    ffn = send_second(ffn, size)
    peer_one = swap_cores(partial_one)
    encoded, key_value = encoder_call(which_core, own, own_peer, order, right)
    h_one, normed_two, cross_q, cross_att, lse_cross, *partial_two = cross_forward(
        tokens, partial_one, peer_one, gains, key_value, dead, right
    )
    peer_two = [swap_cores(value) for value in partial_two]
    h_two, partial_down, partial_three, *grads = ffn_call(
        h_one, partial_two, peer_two, gains, cot, cot_t, ffn[0] + ffn[1]
    )

    ffn = scatter_first(grads, size)
    peer_three = swap_cores(partial_three)
    peer_down = swap_cores(partial_down)
    g_two, low_two, dq, dkv, partial_four, gain_three = cross_backward(
        cot, partial_three, peer_three, h_two, gains, cross_q, key_value, dead, lse_cross, right
    )
    ffn, dq, dkv, low_two, partial_four, peer_down = after(
        (ffn, dq, dkv, low_two, partial_four, peer_down)
    )
    ffn = scatter_second_parts(ffn)
    ffn, dq, dkv, low_two, partial_four = after((ffn, dq, dkv, low_two, partial_four))
    ffn = scatter_second_send(ffn, size)
    peer_four = swap_cores(partial_four)
    kept, given, *grads = cross_grads(
        which_core, normed_two, dq, low_two, cross_att, turned, encoded, dkv, right
    )
    ffn, kept, given, grads, peer_four = after((ffn, kept, given, grads, peer_four))
    ffn = scatter_outer_parts(ffn, 0, 1)
    ffn, kept, given, grads, peer_four = after((ffn, kept, given, grads, peer_four))
    cross = scatter_first(grads, size)
    ffn = scatter_outer_send(ffn, size)
    g_one, partial_five, small, *grads = self_backward(
        g_two, partial_four, peer_four, h_one, gains, mixed, bias, lse_self, attended,
        normed_one, tokens, gain_three, turned, labels, left,
    )
    ffn, cross, given, partial_five, small, grads = after(
        (ffn, cross, given, partial_five, small, grads)
    )
    last = scatter_first(grads, size)
    peer_five = swap_cores(partial_five)
    taken = swap_cores(given)
    cross = scatter_second_send(scatter_second_parts(cross), size)

    terms = (kept.astype(F32) + taken.astype(F32)).astype(BF16).reshape(size, -1, half)
    count = terms.shape[1]
    terms = jnp.concatenate(
        [terms, jnp.broadcast_to(small[None], (size, *small.shape))], axis=1
    )
    back = lax.all_to_all(terms, "dp", split_axis=0, concat_axis=0, tiled=True)
    decoder_grad, layer_out = last_call(
        g_one, partial_five, peer_five, tokens, h_two, partial_down, peer_down, gains, turned
    )
    cross, layer_out = after((cross, layer_out))
    cross = scatter_outer_parts(cross, 0, 1)
    cross, last = after((cross, last))
    cross = scatter_outer_send(cross, size)
    last = scatter_second_parts(last, time=40)
    last = scatter_second_send(last, size)
    last, ffn = after((last, ffn))
    last = scatter_outer_parts(last, 0, 1)
    last, back, ffn = after((last, back, ffn))
    last = scatter_outer_send(last, size)
    inverse = jnp.zeros_like(assign).at[assign].set(jnp.arange(size, dtype=jnp.int32))
    encoder_grad = back[:, :count][inverse]
    small = jnp.sum(back[:, count:].astype(F32), axis=0)
    small = small[:8] + small[8:]
    both = small + swap_cores(small)
    sum_ffn, sum_cross, sum_self = scatter_last(ffn), scatter_last(cross), scatter_last(last)
    table = small[6:8].reshape(2, heads // 2, TILE)[:, :, : bias_table.shape[0]]
    grad_table = table.transpose(1, 0, 2).reshape(heads, -1).T

    def parts(value, count):
        step = value.shape[1] // count
        return [value[:, i * step : (i + 1) * step] for i in range(count)]

    grad_self_query, grad_self_key, grad_self_value, grad_output_one = parts(sum_self, 4)
    grad_cross_query, grad_output_two, grad_cross_key, grad_cross_value = parts(sum_cross, 4)
    grad_ffn_gate, grad_ffn_up, grad_ffn_down = parts(sum_ffn, 3)
    return (
        layer_out[None],
        decoder_grad[None],
        encoder_grad,
        both[0:4:3].reshape(-1),
        small[1:5:3].reshape(-1),
        small[2:6:3].reshape(-1),
        grad_self_query,
        grad_self_key,
        grad_self_value,
        grad_output_one.T,
        grad_cross_query,
        grad_cross_key,
        grad_cross_value,
        grad_output_two.T,
        grad_ffn_gate,
        grad_ffn_up,
        grad_ffn_down.T,
        grad_table,
    )


def solution(mesh):
    in_specs = (
        P("dp", None, None),
        P(None, "dp", None),
        P(),
        P(),
        P(),
        P(),
        P(),
        P(),
        P(),
        P("dp", "mp"),
        P("dp", "mp"),
        P("dp", "mp"),
        P("mp", "dp"),
        P("dp", "mp"),
        P("dp", "mp"),
        P("dp", "mp"),
        P("mp", "dp"),
        P("dp", "mp"),
        P("dp", "mp"),
        P("mp", "dp"),
        P(None, "mp"),
        P("dp", None, None),
    )
    out_specs = (
        P("dp", None, None),
        P("dp", None, None),
        P(None, "dp", "mp"),
        P(),
        P(),
        P(),
        P("dp", "mp"),
        P("dp", "mp"),
        P("dp", "mp"),
        P("mp", "dp"),
        P("dp", "mp"),
        P("dp", "mp"),
        P("dp", "mp"),
        P("mp", "dp"),
        P("dp", "mp"),
        P("dp", "mp"),
        P("mp", "dp"),
        P(None, "mp"),
    )
    body = functools.partial(shards, size=mesh.shape["dp"])
    return jax.shard_map(body, mesh=mesh, in_specs=in_specs, out_specs=out_specs, check_vma=False)
```

```python
import functools

import jax
import jax.numpy as jnp
from jax import lax
from jax.experimental import pallas as pl
from jax.experimental.pallas import tpu as pltpu
from jax.sharding import PartitionSpec as P

HEAD_DIM = 64
PAIR = 2 * HEAD_DIM
QUERIES = 256
KEYS = 1024
TILE = 128
WIDE = 256
HIDDEN = 512
ROWS = 64

EPS = 1e-06
NEGATIVE = -1000000000.0
GELU_ROOT = 0.7978845608028654
GELU_CUBE = 0.044715
BF16 = jnp.bfloat16
F32 = jnp.float32


def dot(left, right, dims):
    return lax.dot_general(left, right, (dims, ((), ())), preferred_element_type=F32)


def nn(left, right):
    return dot(left, right, ((1,), (0,)))


def nt(left, right):
    return dot(left, right, ((1,), (1,)))


def tn(left, right):
    return dot(left, right, ((0,), (0,)))


def struct(shape, dtype):
    return jax.ShapeDtypeStruct(shape, dtype)


def halves(value):
    high = value.astype(BF16)
    return high, (value - high.astype(F32)).astype(BF16)


def swap(value, mask, size):
    return lax.ppermute(value, "dp", [(i, i ^ mask) for i in range(size)])


def swap_cores(value):
    return lax.ppermute(value, "mp", [(0, 1), (1, 0)])


def after(values, *others):
    return lax.optimization_barrier((values, others))[0]


def gather_outer(shard, size, late=()):
    if size == 16:
        far, near = swap(shard, 8, size), swap(shard, 4, size)
        return [shard, near, far, swap(after(far, late), 4, size)]
    shard = after(shard, late)
    mask = 4
    while mask < size:
        shard = jnp.concatenate([shard, swap(shard, mask, size)])
        mask *= 2
    return [shard]


def gather_first(pieces, size):
    rows, half = sum(piece.shape[0] for piece in pieces), pieces[0].shape[1] // 2
    return kernel_call(stack_kernel, list(pieces), [struct((rows, half), BF16)] * 2, [])


def gather_second(state, size, time=2):
    rows, half = state[0].shape
    outs = [struct((2 * rows, half), BF16)] * 2
    return kernel_call(join_kernel, list(state), outs, [], time=time)


def send_first(halves, size):
    left, right = halves
    return left, swap(left, 2, size), right, swap(right, 1, size)


def send_second(halves, size):
    left, right = halves
    return [left, swap(left, 1, size)], [right, swap(right, 2, size)]


def scatter_first(grads, size):
    left, left_out, right, right_out = grads
    return left, right, swap(left_out, 1, size), swap(right_out, 2, size)


def scatter_second_parts(state, time=2):
    left = state[0]
    rows, half = left.shape[0] // 2, left.shape[1]
    outs = kernel_call(
        scatter_second_kernel,
        list(state),
        [struct((rows, half), BF16)] * 2,
        [],
        time=time,
        grid=(1,),
        in_specs=[pl.BlockSpec((rows, half), lambda i: (1, 0))] * 4,
        out_specs=[pl.BlockSpec((rows, half), lambda i: (0, 0))] * 2,
    )
    return (*state, *outs)


def scatter_second_send(parts, size):
    *state, left_out, right_out = parts
    return (*state, swap(left_out, 2, size), swap(right_out, 1, size))


def scatter_outer_parts(state, *sides):
    rows, half = state[-1].shape
    ins = [value for side in sides for value in state[side::2]]
    width = len(sides) * half
    return kernel_call(
        scatter_outer_kernel,
        ins,
        [struct((rows // 4, width), dtype) for dtype in (F32, BF16, BF16, BF16)],
        [],
        grid=(1,),
        in_specs=[pl.BlockSpec((rows, half), lambda i: (0, 0))] * len(ins),
        out_specs=[pl.BlockSpec((rows // 4, width), lambda i: (0, 0))] * 4,
    )


def scatter_pair_parts(state):
    rows, half = state[-1].shape
    outs = [struct((rows // 2, 2 * half), dtype) for dtype in (F32, BF16)]
    return kernel_call(
        scatter_pair_kernel,
        state[0::2] + state[1::2],
        outs,
        [],
        grid=(1,),
        in_specs=[pl.BlockSpec((rows, half), lambda i: (0, 0))] * 6,
        out_specs=[pl.BlockSpec((rows // 2, 2 * half), lambda i: (0, 0))] * 2,
    )


def scatter_pair_send(keep, taken, size):
    count = keep.shape[0] // 2
    rows = keep + taken.astype(F32)
    return [rows[:count], swap(rows[count:].astype(BF16), 8, size)]


def scatter_outer_send(parts, size):
    keep, *outs = parts
    if size == 16:
        return [keep] + [swap(out, 4 * (k + 1), size) for k, out in enumerate(outs)]
    rows = jnp.concatenate([keep] + [out.astype(F32) for out in outs])
    mask = size // 2
    while mask >= 4:
        count = rows.shape[0] // 2
        rows = rows[:count] + swap(rows[count:].astype(BF16), mask, size).astype(F32)
        mask //= 2
    return [rows]


def scatter_last(state):
    total = state[0]
    for value in state[1:]:
        total = total + value.astype(F32)
    return total


def kernel_call(kernel, ins, outs, scratch, time=2, grid=None, in_specs=None, out_specs=None):
    everywhere = pl.BlockSpec(memory_space=pltpu.VMEM)
    return pl.pallas_call(
        kernel,
        out_shape=outs,
        in_specs=in_specs or [everywhere] * len(ins),
        out_specs=out_specs or [everywhere] * len(outs),
        scratch_shapes=scratch,
        compiler_params=pltpu.CompilerParams(vmem_limit_bytes=58 * 1024 * 1024),
        cost_estimate=pl.CostEstimate(
            flops=time * 1000000000, bytes_accessed=1, transcendentals=0
        ),
        **({"grid": grid} if grid else {}),
    )(*ins)


IN_VMEM = pl.BlockSpec(memory_space=pltpu.VMEM)
IN_PLACE = pl.BlockSpec(memory_space=pl.ANY)
IN_SMEM = pl.BlockSpec(memory_space=pltpu.SMEM)


def stack_kernel(*refs):
    *in_refs, left_ref, right_ref = refs
    half = left_ref.shape[1]
    start = 0
    for ref in in_refs:
        rows = slice(start, start + ref.shape[0])
        left_ref[rows, :] = ref[:, :half]
        right_ref[rows, :] = ref[:, half:]
        start += ref.shape[0]


def join_kernel(left_ref, left_in_ref, right_ref, right_in_ref, left_out, right_out):
    count = left_ref.shape[0]
    left_out[:count, :] = left_ref[...]
    left_out[count:, :] = left_in_ref[...]
    right_out[:count, :] = right_ref[...]
    right_out[count:, :] = right_in_ref[...]


def scatter_second_kernel(left_ref, right_ref, left_in_ref, right_in_ref, left_out, right_out):
    left_out[...] = (left_ref[...].astype(F32) + left_in_ref[...].astype(F32)).astype(BF16)
    right_out[...] = (right_ref[...].astype(F32) + right_in_ref[...].astype(F32)).astype(BF16)


def scatter_outer_kernel(*refs):
    *in_refs, keep_ref, first_ref, second_ref, third_ref = refs
    count = keep_ref.shape[0]
    for side in range(len(in_refs) // 3):
        own_ref, in_ref, more_ref = in_refs[3 * side : 3 * side + 3]
        half = own_ref.shape[1]
        cols = slice(side * half, (side + 1) * half)
        for k, out_ref in enumerate((keep_ref, first_ref, second_ref, third_ref)):
            rows = slice(k * count, (k + 1) * count)
            total = own_ref[rows, :].astype(F32) + in_ref[rows, :].astype(F32)
            out_ref[:, cols] = (total + more_ref[rows, :].astype(F32)).astype(out_ref.dtype)


def scatter_pair_kernel(*refs):
    *in_refs, keep_ref, out_ref = refs
    count = keep_ref.shape[0] // 2
    for side in range(2):
        own_ref, in_ref, more_ref = in_refs[3 * side : 3 * side + 3]
        half = own_ref.shape[1]
        cols = slice(side * half, (side + 1) * half)
        for k in range(4):
            rows = slice(k * count, (k + 1) * count)
            total = own_ref[rows, :].astype(F32) + in_ref[rows, :].astype(F32)
            target = out_ref if k % 2 else keep_ref
            spot = slice(k // 2 * count, (k // 2 + 1) * count)
            target[spot, cols] = (total + more_ref[rows, :].astype(F32)).astype(target.dtype)


def cast_kernel(*refs):
    *in_refs, out_ref = refs
    start = 0
    for ref in in_refs:
        out_ref[:, start : start + ref.shape[1]] = ref[...].astype(BF16)
        start += ref.shape[1]


def low(*values):
    width = sum(value.shape[1] for value in values)
    return kernel_call(
        cast_kernel, list(values), [struct((values[0].shape[0], width), BF16)], []
    )[0]


def each_rows(count, body):
    @pl.loop(0, count // ROWS)
    def step(i):
        body(pl.ds(pl.multiple_of(i * ROWS, ROWS), ROWS))


def each_tile(start, width, body):
    @pl.loop(0, width // WIDE)
    def step(i):
        body(pl.ds(pl.multiple_of(start + i * WIDE, WIDE), WIDE))


def fetch(left, right, weights_ref, sems, first=0):
    moves = []
    start = left[0].shape[1] if left else 0
    for i, ref in enumerate(left):
        count = ref.shape[0]
        moves.append((ref, weights_ref.at[i * count : (i + 1) * count, :start]))
    columns = weights_ref.shape[1] - start
    for i, ref in enumerate(right):
        count = ref.shape[0] // 2
        for x in range(2):
            place = (2 * x + i) * count
            moves.append(
                (
                    ref.at[x * count : (x + 1) * count, first : first + columns],
                    weights_ref.at[place : place + count, start:],
                )
            )
    copies = [pltpu.make_async_copy(*move, sems.at[i]) for i, move in enumerate(moves)]
    for copy in copies:
        copy.start()
    return copies


def deliver(grads_ref, out_refs, sems, columns, first=0):
    left, left_out, right, right_out = out_refs
    rows, half = left.shape[0] // 2, left.shape[1]
    side = columns.start // half
    if side == 0:
        moves = [(left, 0, 0, 2), (left_out, 0, 2, 2)]
    else:
        moves = [(right, 0, 0, 1), (right, 1, 2, 1), (right_out, 0, 1, 1), (right_out, 1, 3, 1)]
    copies = []
    for target, spot, place, count in moves:
        copies.append(
            pltpu.make_async_copy(
                grads_ref.at[place * rows : (place + count) * rows, columns],
                target.at[
                    spot * rows : (spot + count) * rows,
                    columns.start - side * half : columns.stop - side * half,
                ],
                sems.at[first + len(copies)],
            )
        )
    return copies


def deliver_all(grads_ref, out_refs, sems):
    half = out_refs[0].shape[1]
    copies = deliver(grads_ref, out_refs, sems, slice(0, half))
    copies += deliver(grads_ref, out_refs, sems, slice(half, 2 * half), 2)
    for copy in copies:
        copy.start()
    for copy in copies:
        copy.wait()


def grad_structs(width, columns):
    return [struct((width // 2, columns // 2), BF16)] * 4


def root_of(value):
    return lax.rsqrt(jnp.mean(value * value, axis=-1, keepdims=True) + EPS)


def norm_back(value, gain, grad):
    root = root_of(value)
    scaled = grad * gain
    inner = jnp.mean(value * scaled, axis=-1, keepdims=True)
    back = root * scaled - value * (root * root * root * inner)
    return back, jnp.sum(grad * value * root, axis=0, keepdims=True)


def rows_kernel(
    tokens_ref, cot_ref, gains_ref, source_ref,
    tokens_out, cot_out, cot_t_out, gains_out, order_ref, turned_ref, normed_ref,
):
    width = tokens_ref.shape[1]
    spot = lax.broadcasted_iota(jnp.int32, (width, width), 0)
    order_ref[...] = jnp.where(spot == source_ref[0:1, :], 1.0, 0.0).astype(BF16)
    order = order_ref[...]
    turned_ref[...] = order.T
    high = gains_ref[...].astype(BF16)
    middle, rest = halves(gains_ref[...] - high.astype(F32))
    gains_out[...] = nn(high, order) + (nn(middle, order) + nn(rest, order))
    tokens_out[...] = nn(tokens_ref[...], order)
    cot_out[...] = nn(cot_ref[...], order).astype(BF16)
    cot_t_out[...] = cot_out[...].T
    gain = gains_out[0:1, :]

    def norm(rows):
        value = tokens_out[rows, :]
        normed_ref[rows, :] = (value * root_of(value) * gain).astype(BF16)

    each_rows(tokens_ref.shape[0], norm)


def queries_of(capacity):
    return QUERIES if capacity <= 2 * KEYS else TILE


def each_chunk(count, size, body):
    if count == 1:
        body(0)
    else:
        pl.loop(0, count)(lambda step: body(pl.multiple_of(step * size, size)))


def each_pair(pairs, body):
    @pl.loop(0, pairs)
    def step(pair):
        body(pair, lambda which: pl.ds(pl.multiple_of((which * pairs + pair) * PAIR, PAIR), PAIR))


def row_of(value, head):
    line = lax.broadcasted_iota(jnp.int32, value.shape, 0)
    return jnp.sum(jnp.where(line == head, value, 0.0), axis=0, keepdims=True)


def of_head(value, head):
    lane = lax.broadcasted_iota(jnp.int32, value.shape, 1)
    return jnp.where(lane // HEAD_DIM == head, value, jnp.zeros_like(value))


def cross_forward_pair(q_ref, k_ref, v_ref, dead_ref, out_ref, lse_ref, s_ref, acc_ref):
    targets, capacity = q_ref.shape[0], k_ref.shape[0]
    size = min(capacity, KEYS)
    count = capacity // size
    queries = s_ref.shape[1]
    for head in range(2):
        rows = slice(head * HEAD_DIM, (head + 1) * HEAD_DIM)
        line = slice(head, head + 1)
        for start in range(0, targets, queries):
            cols = slice(start, start + queries)
            query = of_head(q_ref[cols, :], head)
            lse_ref[line, cols] = jnp.full((1, queries), NEGATIVE * 2, F32)

            def scores(base):
                keys = pl.ds(base, size)
                score = nt(k_ref[keys, :], query) + dead_ref[keys, 0:1]
                s_ref[keys, :] = score
                lse_ref[line, cols] = jnp.maximum(
                    lse_ref[line, cols], jnp.max(score, axis=0, keepdims=True)
                )

            each_chunk(count, size, scores)
            top = lse_ref[line, cols]
            lse_ref[line, cols] = jnp.zeros((1, queries), F32)

            def weights(base):
                keys = pl.ds(base, size)
                weight = jnp.exp(s_ref[keys, :] - top)
                s_ref[keys, :] = weight
                lse_ref[line, cols] += jnp.sum(weight, axis=0, keepdims=True)

            each_chunk(count, size, weights)
            total = lse_ref[line, cols]
            lse_ref[line, cols] = top + jnp.log(total)
            scale = 1.0 / total
            acc_ref[rows, cols] = jnp.zeros((HEAD_DIM, queries), F32)

            def mix(base):
                keys = pl.ds(base, size)
                probs = (s_ref[keys, :] * scale).astype(BF16)
                acc_ref[rows, cols] += tn(v_ref[keys, :], probs)[rows]

            each_chunk(count, size, mix)
    out_ref[...] = acc_ref[...].T.astype(BF16)


def cross_backward_pair(
    q_ref, k_ref, v_ref, dead_ref, lse_ref, go_ref, dq_ref, dk_ref, dv_ref,
    p_ref, dp_ref, dqt_ref, dk_acc, dv_acc, delta_ref,
):
    targets, capacity = q_ref.shape[0], k_ref.shape[0]
    size = min(capacity, KEYS)
    count = capacity // size
    queries = p_ref.shape[1]
    dk_acc[...] = jnp.zeros_like(dk_acc)
    dv_acc[...] = jnp.zeros_like(dv_acc)
    dqt_ref[...] = jnp.zeros_like(dqt_ref)

    @pl.loop(0, 2)
    def each_head(head):
        for start in range(0, targets, queries):
            cols = slice(start, start + queries)
            query = of_head(q_ref[cols, :], head)
            grad = of_head(go_ref[cols, :], head)
            lse = row_of(lse_ref[:, cols], head)
            delta_ref[...] = jnp.zeros_like(delta_ref)

            def first(base):
                keys = pl.ds(base, size)
                probs = jnp.exp(nt(k_ref[keys, :], query) + dead_ref[keys, 0:1] - lse)
                grad_probs = nt(v_ref[keys, :], grad)
                p_ref[keys, :] = probs
                dp_ref[keys, :] = grad_probs
                delta_ref[...] += jnp.sum(probs * grad_probs, axis=0, keepdims=True)

            each_chunk(count, size, first)
            delta = delta_ref[...]

            def second(base):
                keys = pl.ds(base, size)
                probs = p_ref[keys, :]
                dv_acc[keys, :] += nn(probs.astype(BF16), grad)
                low = (probs * (dp_ref[keys, :] - delta)).astype(BF16)
                dk_acc[keys, :] += nn(low, query)
                dqt_ref[:, cols] += tn(of_head(k_ref[keys, :], head), low)

            each_chunk(count, size, second)
    dq_ref[...] = dqt_ref[...].T.astype(BF16)
    dk_ref[...] = dk_acc[...].astype(BF16)
    dv_ref[...] = dv_acc[...].astype(BF16)


def skewed(row, block):
    before = row[:, (block - 1) * TILE : block * TILE] if block else jnp.zeros((1, TILE), F32)
    both = jnp.concatenate([before, row[:, block * TILE : (block + 1) * TILE]], axis=1)
    both = jnp.broadcast_to(both, (TILE, 2 * TILE))
    return pltpu.roll(both, 0, 1, stride=1, stride_axis=0)[:, TILE:]


def unskewed(tile):
    both = jnp.concatenate([jnp.zeros_like(tile), tile], axis=1)
    total = both[:8]
    for base in range(8, TILE, 8):
        total = total + pltpu.roll(both[base : base + 8], 2 * TILE - base, 1)
    row = lax.broadcasted_iota(jnp.int32, total.shape, 0)
    for bit in (1, 2, 4):
        total = jnp.where(row & bit != 0, pltpu.roll(total, 2 * TILE - bit, 1), total)
    return jnp.sum(total, axis=0, keepdims=True)


def self_scores(k_ref, query, tiles, start):
    keys = start + QUERIES
    columns = []
    for i in range(start // TILE, keys // TILE):
        columns.append(
            jnp.concatenate([tiles[max(i - j, 0)] for j in range(keys // TILE)], axis=0)
        )
    score = nt(k_ref[:keys, :], query) + jnp.concatenate(columns, axis=1)
    key = lax.broadcasted_iota(jnp.int32, score.shape, 0)
    spot = lax.broadcasted_iota(jnp.int32, score.shape, 1) + start
    return jnp.where(key <= spot, score, NEGATIVE)


def self_forward_pair(q_ref, k_ref, v_ref, bias_ref, out_ref, lse_ref, acc_ref):
    targets = q_ref.shape[0]
    for head in range(2):
        rows = slice(head * HEAD_DIM, (head + 1) * HEAD_DIM)
        row = bias_ref[head : head + 1, :]
        tiles = [skewed(row, block) for block in range(targets // TILE)]
        for start in range(0, targets, QUERIES):
            cols = slice(start, start + QUERIES)
            query = of_head(q_ref[cols, :], head)
            score = self_scores(k_ref, query, tiles, start)
            top = jnp.max(score, axis=0, keepdims=True)
            weight = jnp.exp(score - top)
            total = jnp.sum(weight, axis=0, keepdims=True)
            lse_ref[head : head + 1, cols] = top + jnp.log(total)
            probs = (weight * (1.0 / total)).astype(BF16)
            acc_ref[rows, cols] = tn(v_ref[: start + QUERIES, :], probs)[rows]
    out_ref[...] = acc_ref[...].T.astype(BF16)


def self_backward_pair(
    q_ref, k_ref, v_ref, bias_ref, lse_ref, go_ref, dq_ref, dk_ref, dv_ref, dbias_ref,
    dqt_ref, dk_acc, dv_acc,
):
    targets = q_ref.shape[0]
    dk_acc[...] = jnp.zeros_like(dk_acc)
    dv_acc[...] = jnp.zeros_like(dv_acc)
    blocks = targets // TILE
    dqt_ref[...] = jnp.zeros_like(dqt_ref)

    @pl.loop(0, 2)
    def each_head(head):
        row = row_of(bias_ref[...], head)
        tiles = [skewed(row, block) for block in range(blocks)]
        sums = [jnp.zeros((TILE, TILE), F32) for block in range(blocks)]
        for start in range(0, targets, QUERIES):
            cols = slice(start, start + QUERIES)
            keys = start + QUERIES
            query = of_head(q_ref[cols, :], head)
            grad = of_head(go_ref[cols, :], head)
            score = self_scores(k_ref, query, tiles, start)
            probs = jnp.exp(score - row_of(lse_ref[:, cols], head))
            grad_probs = nt(v_ref[:keys, :], grad)
            delta = jnp.sum(probs * grad_probs, axis=0, keepdims=True)
            dv_acc[:keys, :] += nn(probs.astype(BF16), grad)
            grad_scores = probs * (grad_probs - delta)
            for i in range(start // TILE, keys // TILE):
                for j in range(i + 1):
                    sums[i - j] = sums[i - j] + grad_scores[
                        j * TILE : (j + 1) * TILE, i * TILE - start : (i + 1) * TILE - start
                    ]
            low_scores = grad_scores.astype(BF16)
            dk_acc[:keys, :] += nn(low_scores, query)
            dqt_ref[:, cols] += tn(of_head(k_ref[:keys, :], head), low_scores)
        lines = [unskewed(tile) for tile in sums]
        parts = []
        for block in range(blocks):
            part = lines[block][:, TILE:]
            if block + 1 < blocks:
                part = part + lines[block + 1][:, :TILE]
            parts.append(part)
        row = jnp.concatenate(parts, axis=1)
        line = lax.broadcasted_iota(jnp.int32, dbias_ref.shape, 0)
        dbias_ref[...] = jnp.where(line == head, row, dbias_ref[...])
    dq_ref[...] = dqt_ref[...].T.astype(BF16)
    dk_ref[...] = dk_acc[...].astype(BF16)
    dv_ref[...] = dv_acc[...].astype(BF16)


def self_forward_kernel(
    normed_ref, bias_ref, *refs
):
    mixed_ref, attended_ref, lse_ref, partial_ref, weights_ref, acc_ref, sems = refs[2:]
    copies = fetch(refs[:2], [], weights_ref, sems)
    for copy in copies:
        copy.wait()
    part = attended_ref.shape[1]
    pairs = part // PAIR
    normed = normed_ref[...]

    @pl.loop(0, 3 * part // TILE)
    def project(i):
        cols = pl.ds(pl.multiple_of(i * TILE, TILE), TILE)
        mixed_ref[:, cols] = nn(normed, weights_ref[:, cols]).astype(BF16)

    def attend(pair, cols):
        self_forward_pair(
            *(mixed_ref.at[:, cols(i)] for i in range(3)),
            bias_ref.at[pair], attended_ref.at[:, cols(0)], lse_ref.at[pair], acc_ref,
        )

    each_pair(pairs, attend)
    partial_ref[...] = nt(attended_ref[...], weights_ref[:, 3 * part :])


def self_forward(normed, bias, quarters):
    targets, width = normed.shape
    columns = quarters[0].shape[1]
    part = columns // 4
    pairs = part // PAIR
    return kernel_call(
        self_forward_kernel,
        [normed, bias, *quarters],
        [
            struct((targets, 3 * part), BF16),
            struct((targets, part), BF16),
            struct((pairs, 8, targets), F32),
            struct((targets, width), F32),
        ],
        [
            pltpu.VMEM((width, columns), BF16),
            pltpu.VMEM((PAIR, targets), F32),
            pltpu.SemaphoreType.DMA((6,)),
        ],
        in_specs=[IN_VMEM] * 2 + [IN_PLACE] * 2,
        time=12,
    )


def encoder_kernel(core_ref, own_ref, peer_ref, order_ref, *refs):
    encoded_ref, out_ref, weights_ref, sems = refs[2:]

    @pl.when(pl.program_id(0) == 0)
    def load():
        for copy in fetch([], refs[:2], weights_ref, sems, weights_ref.shape[1]):
            copy.wait()

    core, half = core_ref[0], own_ref.shape[1]
    own_rows = pl.ds(pl.multiple_of(core * half, half), half)
    peer_rows = pl.ds(pl.multiple_of(half - core * half, half), half)
    encoded = nn(own_ref[...], order_ref[own_rows, :]) + nn(peer_ref[...], order_ref[peer_rows, :])
    encoded_ref[...] = encoded.astype(BF16)
    encoded = encoded_ref[...]

    def project(cols):
        out_ref[:, cols] = nn(encoded, weights_ref[:, cols]).astype(BF16)

    each_tile(0, out_ref.shape[1], project)


def encoder_call(core, own, peer, order, quarters):
    capacity, half = own.shape
    width = 2 * half
    columns = quarters[0].shape[1] // 2
    size = min(capacity, KEYS)
    block = lambda cols: pl.BlockSpec((size, cols), lambda i: (i, 0))
    return kernel_call(
        encoder_kernel,
        [core, own, peer, order, *quarters],
        [struct((capacity, width), BF16), struct((capacity, columns), BF16)],
        [pltpu.VMEM((width, columns), BF16), pltpu.SemaphoreType.DMA((4,))],
        grid=(capacity // size,),
        in_specs=[IN_SMEM, block(half), block(half), IN_VMEM] + [IN_PLACE] * 2,
        out_specs=[block(width), block(columns)],
        time=8,
    )


def cross_forward_kernel(tokens_ref, partial_ref, peer_ref, gains_ref, kv_ref, dead_ref, *refs):
    (
        h_ref, normed_ref, query_ref, att_ref, lse_ref, out_ref, more_ref,
        weights_ref, s_ref, acc_ref, sems,
    ) = refs[2:]
    copies = fetch([], refs[:2], weights_ref, sems)
    gain = gains_ref[1:2, :]

    def norm(rows):
        value = tokens_ref[rows, :] + (partial_ref[rows, :] + peer_ref[rows, :])
        h_ref[rows, :] = value
        normed_ref[rows, :] = (value * root_of(value) * gain).astype(BF16)

    each_rows(h_ref.shape[0], norm)
    for copy in copies:
        copy.wait()
    part = query_ref.shape[1]
    pairs = part // PAIR
    query_ref[...] = nn(normed_ref[...], weights_ref[:, :part]).astype(BF16)

    def attend(pair, cols):
        cross_forward_pair(
            query_ref.at[:, cols(0)], kv_ref.at[:, cols(0)], kv_ref.at[:, cols(1)], dead_ref,
            att_ref.at[:, cols(0)], lse_ref.at[pair], s_ref, acc_ref,
        )

    each_pair(pairs, attend)
    count = out_ref.shape[0]
    out_ref[...] = nt(att_ref[:count, :], weights_ref[:, part:])
    more_ref[...] = nt(att_ref[count:, :], weights_ref[:, part:])


def cross_forward(tokens, partial, peer, gains, key_value, dead, quarters):
    targets, width = tokens.shape
    capacity, columns = key_value.shape
    part = columns // 2
    pairs = part // PAIR
    return kernel_call(
        cross_forward_kernel,
        [tokens, partial, peer, gains, key_value, dead, *quarters],
        [
            struct((targets, width), F32),
            struct((targets, width), BF16),
            struct((targets, part), BF16),
            struct((targets, part), BF16),
            struct((pairs, 8, targets), F32),
            struct((targets // 2, width), F32),
            struct((targets // 2, width), F32),
        ],
        [
            pltpu.VMEM((width, columns), BF16),
            pltpu.VMEM((capacity, queries_of(capacity)), F32),
            pltpu.VMEM((PAIR, targets), F32),
            pltpu.SemaphoreType.DMA((4,)),
        ],
        in_specs=[IN_VMEM] * 6 + [IN_PLACE] * 2,
        time=16,
    )


def ffn_kernel(
    before_ref, first_ref, second_ref, first_in_ref, second_in_ref, gains_ref, cot_ref, cot_t_ref,
    *refs
):
    h_out, down_ref, back_ref, *outs = refs[4:11]
    weights_ref, grads_ref, h_ref, normed_ref, normed_t, in_sems, out_sems = refs[11:]
    copies = fetch(refs[:2], refs[2:4], weights_ref, in_sems)
    gain = gains_ref[2:3, :]
    count = first_ref.shape[0]
    halves = ((first_ref, first_in_ref), (second_ref, second_in_ref))
    for i, (partial_ref, peer_ref) in enumerate(halves):

        def norm(rows):
            own = pl.ds(pl.multiple_of(rows.start + i * count, ROWS), ROWS)
            value = before_ref[own, :] + (partial_ref[rows, :] + peer_ref[rows, :])
            h_ref[own, :] = value
            normed_ref[own, :] = (value * root_of(value) * gain).astype(BF16)

        each_rows(count, norm)
    h_copy = pltpu.make_async_copy(h_ref, h_out, out_sems.at[36])
    h_copy.start()
    normed_t[...] = normed_ref[...].T
    down_ref[...] = jnp.zeros_like(down_ref)
    back_ref[...] = jnp.zeros_like(back_ref)
    for copy in copies:
        copy.wait()
    hidden = weights_ref.shape[1] // 3
    tiles = hidden // HIDDEN

    def sends(i):
        copies = []
        for k in range(3):
            columns = slice(k * hidden + i * HIDDEN, k * hidden + (i + 1) * HIDDEN)
            first = 6 * (i * 3 + k)
            copies += deliver(grads_ref, outs, out_sems, columns, first)
        return copies

    @pl.loop(0, tiles)
    def tile(i):
        gates, ups, downs = (
            pl.ds(pl.multiple_of(k * hidden + i * HIDDEN, HIDDEN), HIDDEN) for k in range(3)
        )
        normed = normed_ref[...]
        gate = nn(normed, weights_ref[:, gates])
        up = nn(normed, weights_ref[:, ups])
        grad_act = nn(cot_ref[...], weights_ref[:, downs]).astype(BF16).astype(F32)
        square = gate * gate
        curve = jnp.tanh(GELU_ROOT * (gate + GELU_CUBE * (square * gate)))
        share = 0.5 * (1.0 + curve)
        gelu = gate * share
        slope = share + (0.5 * gate) * (1.0 - curve * curve) * (
            GELU_ROOT * (1.0 + (3.0 * GELU_CUBE) * square)
        )
        act = (gelu * up).astype(BF16)
        grad_gate = (grad_act * up * slope).astype(BF16)
        grad_up = (grad_act * gelu).astype(BF16)
        grads_ref[:, gates] = nn(normed_t[...], grad_gate).astype(BF16)
        grads_ref[:, ups] = nn(normed_t[...], grad_up).astype(BF16)
        grads_ref[:, downs] = nn(cot_t_ref[...], act).astype(BF16)
        for each in range(tiles):

            @pl.when(i == each)
            def send():
                for copy in sends(each):
                    copy.start()

        back_ref[...] += nt(grad_gate, weights_ref[:, gates]) + nt(grad_up, weights_ref[:, ups])
        down_ref[...] += nt(act, weights_ref[:, downs])

    for i in range(tiles):
        for copy in sends(i):
            copy.wait()
    h_copy.wait()


def ffn_call(before, partials, peers, gains, cot, cot_t, quarters):
    targets, width = before.shape
    columns = 2 * quarters[0].shape[1]
    return kernel_call(
        ffn_kernel,
        [before, *partials, *peers, gains, cot, cot_t, *quarters],
        [struct((targets, width), F32)] * 3 + grad_structs(width, columns),
        [
            pltpu.VMEM((width, columns), BF16),
            pltpu.VMEM((width, columns), BF16),
            pltpu.VMEM((targets, width), F32),
            pltpu.VMEM((targets, width), BF16),
            pltpu.VMEM((width, targets), BF16),
            pltpu.SemaphoreType.DMA((6,)),
            pltpu.SemaphoreType.DMA((37,)),
        ],
        time=20,
        in_specs=[IN_VMEM] * 8 + [IN_PLACE] * 4,
        out_specs=[IN_PLACE] + [IN_VMEM] * 2 + [IN_PLACE] * 4,
    )


def cross_backward_kernel(
    cot_ref, partial_ref, peer_ref, h_ref, gains_ref, query_ref, kv_ref, dead_ref, lse_ref, *refs
):
    (
        g_ref, low_ref, dq_ref, dkv_ref, back_ref, gain_grad_ref,
        weights_ref, go_ref, p_ref, dp_ref, dqt_ref, dk_acc, dv_acc, delta_ref, sems,
    ) = refs[2:]
    copies = fetch([], refs[:2], weights_ref, sems)
    gain = gains_ref[2:3, :]
    gain_grad_ref[...] = jnp.zeros_like(gain_grad_ref)

    def norm(rows):
        back, gain_grad = norm_back(h_ref[rows, :], gain, partial_ref[rows, :] + peer_ref[rows, :])
        gain_grad_ref[0:1, :] += gain_grad
        value = cot_ref[rows, :].astype(F32) + back
        g_ref[rows, :] = value
        low_ref[rows, :] = value.astype(BF16)

    each_rows(h_ref.shape[0], norm)
    for copy in copies:
        copy.wait()
    part = query_ref.shape[1]
    pairs = part // PAIR
    go_ref[...] = nn(low_ref[...], weights_ref[:, part:]).astype(BF16)

    def attend(pair, cols):
        cross_backward_pair(
            query_ref.at[:, cols(0)], kv_ref.at[:, cols(0)], kv_ref.at[:, cols(1)], dead_ref,
            lse_ref.at[pair], go_ref.at[:, cols(0)],
            dq_ref.at[:, cols(0)], dkv_ref.at[:, cols(0)], dkv_ref.at[:, cols(1)],
            p_ref, dp_ref, dqt_ref, dk_acc, dv_acc, delta_ref,
        )

    each_pair(pairs, attend)
    back_ref[...] = nt(dq_ref[...], weights_ref[:, :part])


def cross_backward(cot, partial, peer, before, gains, query, key_value, dead, lse, quarters):
    targets, width = cot.shape
    capacity, columns = key_value.shape
    return kernel_call(
        cross_backward_kernel,
        [cot, partial, peer, before, gains, query, key_value, dead, lse, *quarters],
        [
            struct((targets, width), F32),
            struct((targets, width), BF16),
            struct(query.shape, BF16),
            struct(key_value.shape, BF16),
            struct((targets, width), F32),
            struct((8, width), F32),
        ],
        [
            pltpu.VMEM((width, columns), BF16),
            pltpu.VMEM(query.shape, BF16),
            pltpu.VMEM((capacity, queries_of(capacity)), F32),
            pltpu.VMEM((capacity, queries_of(capacity)), F32),
            pltpu.VMEM((PAIR, targets), F32),
            pltpu.VMEM((capacity, PAIR), F32),
            pltpu.VMEM((capacity, PAIR), F32),
            pltpu.VMEM((1, queries_of(capacity)), F32),
            pltpu.SemaphoreType.DMA((4,)),
        ],
        in_specs=[IN_VMEM] * 9 + [IN_PLACE] * 2,
        time=18,
    )


def cross_grads_kernel(
    core_ref, normed_ref, dq_ref, low_ref, att_ref, order_ref, encoded_ref, dkv_ref, *refs
):
    kept_ref, given_ref, *outs = refs[2:8]
    weights_ref, acc_ref, grads_ref, in_sems, out_sems = refs[8:]
    step = pl.program_id(0)
    part = dq_ref.shape[1]

    @pl.when(step == 0)
    def load():
        copies = fetch([], refs[:2], weights_ref, in_sems, weights_ref.shape[1])
        grads_ref[:, :part] = tn(normed_ref[...], dq_ref[...]).astype(BF16)
        grads_ref[:, part : 2 * part] = tn(low_ref[...], att_ref[...]).astype(BF16)
        acc_ref[...] = jnp.zeros_like(acc_ref)
        for copy in copies:
            copy.wait()

    encoded_t = encoded_ref[...].T

    def project(cols):
        acc_ref[:, cols] += nn(encoded_t, dkv_ref[:, cols])

    each_tile(0, acc_ref.shape[1], project)
    core, half = core_ref[0], kept_ref.shape[1]
    terms = nt(dkv_ref[...], weights_ref[...]).astype(BF16)
    own_cols = pl.ds(pl.multiple_of(core * half, half), half)
    peer_cols = pl.ds(pl.multiple_of(half - core * half, half), half)
    kept_ref[...] = nn(terms, order_ref[:, own_cols]).astype(BF16)
    given_ref[...] = nn(terms, order_ref[:, peer_cols]).astype(BF16)

    @pl.when(step == pl.num_programs(0) - 1)
    def store():
        grads_ref[:, 2 * part :] = acc_ref[...].astype(BF16)
        deliver_all(grads_ref, outs, out_sems)


def cross_grads(core, normed, dq, low_two, attended, order, encoded, dkv, quarters):
    capacity, width = encoded.shape
    columns = dkv.shape[1]
    size = min(capacity, KEYS)
    block = lambda cols: pl.BlockSpec((size, cols), lambda i: (i, 0))
    return kernel_call(
        cross_grads_kernel,
        [core, normed, dq, low_two, attended, order, encoded, dkv, *quarters],
        [struct((capacity, width // 2), BF16)] * 2 + grad_structs(width, 2 * columns),
        [
            pltpu.VMEM((width, columns), BF16),
            pltpu.VMEM((width, columns), F32),
            pltpu.VMEM((width, 2 * columns), BF16),
            pltpu.SemaphoreType.DMA((4,)),
            pltpu.SemaphoreType.DMA((6,)),
        ],
        grid=(capacity // size,),
        in_specs=[IN_SMEM] + [IN_VMEM] * 5 + [block(width), block(columns)] + [IN_PLACE] * 2,
        out_specs=[block(width // 2)] * 2 + [IN_PLACE] * 4,
        time=12,
    )


def self_backward_kernel(
    g_in_ref, partial_ref, peer_ref, h_ref, gains_ref, mixed_ref, bias_ref, lse_ref,
    attended_ref, normed_ref, tokens_ref, gain_three_ref, order_ref, labels_ref, *refs
):
    g_ref, back_ref, small_ref, *outs = refs[2:9]
    (
        weights_ref, grads_ref, low_ref, go_ref, dmixed_ref, dbias_ref,
        dqt_ref, dk_acc, dv_acc, gain_ref, pack_ref, in_sems, out_sems,
    ) = refs[9:]
    copies = fetch(refs[:2], [], weights_ref, in_sems)
    gain = gains_ref[1:2, :]
    gain_ref[...] = jnp.zeros_like(gain_ref)

    def norm(rows):
        back, gain_grad = norm_back(h_ref[rows, :], gain, partial_ref[rows, :] + peer_ref[rows, :])
        gain_ref[1:2, :] += gain_grad
        value = g_in_ref[rows, :] + back
        g_ref[rows, :] = value
        low_ref[rows, :] = value.astype(BF16)

    each_rows(h_ref.shape[0], norm)
    for copy in copies:
        copy.wait()
    part = attended_ref.shape[1]
    pairs = part // PAIR
    go_ref[...] = nn(low_ref[...], weights_ref[:, 3 * part :]).astype(BF16)
    dbias_ref[...] = jnp.zeros_like(dbias_ref)

    def attend(pair, cols):
        self_backward_pair(
            *(mixed_ref.at[:, cols(i)] for i in range(3)),
            bias_ref.at[pair], lse_ref.at[pair], go_ref.at[:, cols(0)],
            *(dmixed_ref.at[:, cols(i)] for i in range(3)),
            dbias_ref.at[pair], dqt_ref, dk_acc, dv_acc,
        )

    each_pair(pairs, attend)
    back_ref[...] = nt(dmixed_ref[...], weights_ref[:, : 3 * part])
    normed_t = normed_ref[...].T

    @pl.loop(0, 3 * part // TILE)
    def project(i):
        cols = pl.ds(pl.multiple_of(i * TILE, TILE), TILE)
        grads_ref[:, cols] = nn(normed_t, dmixed_ref[:, cols]).astype(BF16)

    grads_ref[:, 3 * part :] = tn(low_ref[...], attended_ref[...]).astype(BF16)

    def sums(rows):
        value = tokens_ref[rows, :]
        gain_ref[0:1, :] += jnp.sum(back_ref[rows, :] * value * root_of(value), axis=0, keepdims=True)

    each_rows(h_ref.shape[0], sums)
    gain_ref[2:3, :] = gain_three_ref[0:1, :]
    high, rest = halves(gain_ref[...])
    gain_ref[...] = nn(high, order_ref[...]) + nn(rest, order_ref[...])
    half = pack_ref.shape[1]
    pack_ref[0:3, :] = gain_ref[0:3, :half]
    pack_ref[3:6, :] = gain_ref[0:3, half:]
    bucket = lax.broadcasted_iota(jnp.int32, (labels_ref.shape[0], TILE), 1)
    which = jnp.where(labels_ref[:, 0:1] == bucket, 1.0, 0.0).astype(BF16)
    for pair in range(pairs):
        high, rest = halves(dbias_ref[pair])
        table = nn(high, which) + nn(rest, which)
        pack_ref[6:8, pair * TILE : (pair + 1) * TILE] = table[0:2]
    small_ref[...] = jnp.concatenate(halves(pack_ref[...]), axis=0)
    deliver_all(grads_ref, outs, out_sems)


def self_backward(
    g_in, partial, peer, before, gains, mixed, bias, lse, attended, normed, tokens,
    gain_three, order, labels, quarters,
):
    targets, width = g_in.shape
    part = attended.shape[1]
    pairs = part // PAIR
    return kernel_call(
        self_backward_kernel,
        [
            g_in, partial, peer, before, gains, mixed, bias, lse, attended, normed, tokens,
            gain_three, order, labels, *quarters,
        ],
        [
            struct((targets, width), F32),
            struct((targets, width), F32),
            struct((16, width // 2), BF16),
        ]
        + grad_structs(width, 4 * part),
        [
            pltpu.VMEM((width, 4 * part), BF16),
            pltpu.VMEM((width, 4 * part), BF16),
            pltpu.VMEM((targets, width), BF16),
            pltpu.VMEM((targets, part), BF16),
            pltpu.VMEM((targets, 3 * part), BF16),
            pltpu.VMEM((pairs, 8, targets), F32),
            pltpu.VMEM((PAIR, targets), F32),
            pltpu.VMEM((targets, PAIR), F32),
            pltpu.VMEM((targets, PAIR), F32),
            pltpu.VMEM((8, width), F32),
            pltpu.VMEM((8, width // 2), F32),
            pltpu.SemaphoreType.DMA((6,)),
            pltpu.SemaphoreType.DMA((6,)),
        ],
        in_specs=[IN_VMEM] * 14 + [IN_PLACE] * 2,
        out_specs=[IN_VMEM] * 3 + [IN_PLACE] * 4,
        time=22,
    )


def last_kernel(
    g_ref, partial_ref, peer_ref, tokens_ref, h_ref, down_ref, down_in_ref, gains_ref, order_ref,
    grad_ref, out_ref,
):
    order = order_ref[...]
    value = h_ref[...] + (down_ref[...] + down_in_ref[...])
    out_ref[...] = nn(value.astype(BF16), order).astype(BF16)
    back, unused = norm_back(tokens_ref[...], gains_ref[0:1, :], partial_ref[...] + peer_ref[...])
    high, rest = halves(g_ref[...] + back)
    grad_ref[...] = nn(high, order) + nn(rest, order)


def last_call(*ins):
    targets, width = ins[0].shape
    block = pl.BlockSpec((WIDE, width), lambda i: (i, 0))
    return kernel_call(
        last_kernel,
        list(ins),
        [struct((targets, width), F32), struct((targets, width), BF16)],
        [],
        time=8,
        grid=(targets // WIDE,),
        in_specs=[block] * 7 + [IN_VMEM] * 2,
        out_specs=[block] * 2,
    )


def shards(
    decoder_in,
    encoder_out,
    lengths,
    key_mask,
    assign,
    buckets,
    norm_one,
    norm_two,
    norm_three,
    self_query,
    self_key,
    self_value,
    self_output,
    cross_query,
    cross_key,
    cross_value,
    cross_output,
    ffn_gate,
    ffn_up,
    ffn_down,
    bias_table,
    cotangent,
    *,
    size,
):
    rank = lax.axis_index("dp")
    core = lax.axis_index("mp")
    targets, width = decoder_in.shape[1:]
    capacity = key_mask.shape[1]
    block = width // size
    outer = size // 4
    half = width // 2
    heads = bias_table.shape[1]
    which_core = core.reshape(1)

    spots = jnp.arange(width, dtype=jnp.int32)
    spot = spots // block
    masks = spot // (2 * outer) + 2 * (spot // outer % 2) + 4 * (spot % outer)
    source = jnp.broadcast_to(((rank ^ masks) * block + spots % block)[None], (8, width))

    weights = gather_outer(
        low(
            self_query, self_key, self_value, self_output.T,
            cross_query, cross_output.T, cross_key, cross_value,
        ),
        size,
    )
    gains = jnp.concatenate(
        [norm_one[None], norm_two[None], norm_three[None], jnp.zeros((5, width), F32)]
    )
    tokens, cot, cot_t, gains, order, turned, normed_one = kernel_call(
        rows_kernel,
        [decoder_in[0], cotangent[0], gains, source],
        [
            struct((targets, width), F32),
            struct((targets, width), BF16),
            struct((width, targets), BF16),
            struct((8, width), F32),
            struct((width, width), BF16),
            struct((width, width), BF16),
            struct((targets, width), BF16),
        ],
        [],
    )
    ffn = low(ffn_gate, ffn_up, ffn_down.T)

    sent = lax.dynamic_slice_in_dim(encoder_out, core * half, half, 2)[assign]
    weights, ffn, normed_one, sent = after((weights, ffn, normed_one, sent))
    weights = gather_first(weights, size)
    weights, ffn, sent = after((weights, ffn, sent))
    weights = send_first(weights, size)
    own = lax.all_to_all(sent, "dp", split_axis=0, concat_axis=0, tiled=True)
    own = own.reshape(capacity, half)
    labels, bias_table, lengths = after((buckets[:, :TILE], bias_table, lengths), weights[0])
    mine = assign[rank]
    positions = jnp.arange(capacity, dtype=jnp.int32)
    live = (positions < lengths[mine]) & ((key_mask[mine] == 1) | (positions == 0))
    dead = jnp.broadcast_to(jnp.where(live, 0.0, NEGATIVE)[:, None], (capacity, TILE))
    which = labels[None, :, 0] == jnp.arange(bias_table.shape[0], dtype=jnp.int32)[:, None]
    bias = jnp.sum(jnp.where(which[None], bias_table.T[:, :, None], 0.0), axis=1)
    bias = jnp.pad(bias.reshape(heads // 2, 2, targets), ((0, 0), (0, 6), (0, 0)))

    weights, ffn, bias, dead = after((weights, ffn, bias, dead))
    weights = gather_second(weights, size, time=40)
    weights, ffn = after((weights, ffn))
    weights = send_second(weights, size)
    ffn = gather_outer(ffn, size, own)

    weights, own, ffn = after((weights, own, ffn))
    ffn = gather_first(ffn, size)
    ffn, weights, own = after((ffn, weights, own))
    ffn = send_first(ffn, size)
    own_peer = swap_cores(own)
    left, right = weights
    mixed, attended, lse_self, partial_one = self_forward(normed_one, bias, left)
    ffn, mixed, attended, lse_self, partial_one, own, own_peer = after(
        (ffn, mixed, attended, lse_self, partial_one, own, own_peer)
    )
    ffn = gather_second(ffn, size)
    ffn, partial_one, own = after((ffn, partial_one, own))
    ffn = send_second(ffn, size)
    peer_one = swap_cores(partial_one)
    encoded, key_value = encoder_call(which_core, own, own_peer, order, right)
    h_one, normed_two, cross_q, cross_att, lse_cross, *partial_two = cross_forward(
        tokens, partial_one, peer_one, gains, key_value, dead, right
    )
    peer_two = [swap_cores(value) for value in partial_two]
    h_two, partial_down, partial_three, *grads = ffn_call(
        h_one, partial_two, peer_two, gains, cot, cot_t, ffn[0] + ffn[1]
    )

    ffn = scatter_first(grads, size)
    peer_three = swap_cores(partial_three)
    peer_down = swap_cores(partial_down)
    g_two, low_two, dq, dkv, partial_four, gain_three = cross_backward(
        cot, partial_three, peer_three, h_two, gains, cross_q, key_value, dead, lse_cross, right
    )
    ffn, dq, dkv, low_two, partial_four, peer_down = after(
        (ffn, dq, dkv, low_two, partial_four, peer_down)
    )
    ffn = scatter_second_parts(ffn)
    ffn, dq, dkv, low_two, partial_four = after((ffn, dq, dkv, low_two, partial_four))
    ffn = scatter_second_send(ffn, size)
    peer_four = swap_cores(partial_four)
    kept, given, *grads = cross_grads(
        which_core, normed_two, dq, low_two, cross_att, turned, encoded, dkv, right
    )
    ffn, kept, given, grads, peer_four = after((ffn, kept, given, grads, peer_four))
    ffn = scatter_outer_parts(ffn, 0, 1)
    ffn, kept, given, grads, peer_four = after((ffn, kept, given, grads, peer_four))
    cross = scatter_first(grads, size)
    ffn = scatter_outer_send(ffn, size)
    g_one, partial_five, small, *grads = self_backward(
        g_two, partial_four, peer_four, h_one, gains, mixed, bias, lse_self, attended,
        normed_one, tokens, gain_three, turned, labels, left,
    )
    ffn, cross, given, partial_five, small, grads = after(
        (ffn, cross, given, partial_five, small, grads)
    )
    last = scatter_first(grads, size)
    peer_five = swap_cores(partial_five)
    taken = swap_cores(given)
    cross = scatter_second_send(scatter_second_parts(cross), size)

    terms = (kept.astype(F32) + taken.astype(F32)).astype(BF16).reshape(size, -1, half)
    count = terms.shape[1]
    terms = jnp.concatenate(
        [terms, jnp.broadcast_to(small[None], (size, *small.shape))], axis=1
    )
    back = lax.all_to_all(terms, "dp", split_axis=0, concat_axis=0, tiled=True)
    decoder_grad, layer_out = last_call(
        g_one, partial_five, peer_five, tokens, h_two, partial_down, peer_down, gains, turned
    )
    cross, layer_out = after((cross, layer_out))
    if size == 16:
        cross_keep, cross_out = scatter_pair_parts(cross)
        cross_out, last = after((cross_out, last))
        last = scatter_second_send(scatter_second_parts(last, time=40), size)
        cross_in = swap(cross_out, 4, size)
        last, ffn = after((last, ffn))
        last = scatter_outer_parts(last, 0, 1)
        last, cross_in, back, ffn = after((last, cross_in, back, ffn))
        last = scatter_outer_send(last, size)
        cross = scatter_pair_send(cross_keep, cross_in, size)
    else:
        cross = scatter_outer_send(scatter_outer_parts(cross, 0, 1), size)
        last = scatter_second_send(scatter_second_parts(last), size)
        last = scatter_outer_send(scatter_outer_parts(last, 0, 1), size)
    inverse = jnp.zeros_like(assign).at[assign].set(jnp.arange(size, dtype=jnp.int32))
    encoder_grad = back[:, :count][inverse]
    small = jnp.sum(back[:, count:].astype(F32), axis=0)
    small = small[:8] + small[8:]
    both = small + swap_cores(small)
    sum_ffn, sum_cross, sum_self = scatter_last(ffn), scatter_last(cross), scatter_last(last)
    table = small[6:8].reshape(2, heads // 2, TILE)[:, :, : bias_table.shape[0]]
    grad_table = table.transpose(1, 0, 2).reshape(heads, -1).T

    def parts(value, count):
        step = value.shape[1] // count
        return [value[:, i * step : (i + 1) * step] for i in range(count)]

    grad_self_query, grad_self_key, grad_self_value, grad_output_one = parts(sum_self, 4)
    grad_cross_query, grad_output_two, grad_cross_key, grad_cross_value = parts(sum_cross, 4)
    grad_ffn_gate, grad_ffn_up, grad_ffn_down = parts(sum_ffn, 3)
    return (
        layer_out[None],
        decoder_grad[None],
        encoder_grad,
        both[0:4:3].reshape(-1),
        small[1:5:3].reshape(-1),
        small[2:6:3].reshape(-1),
        grad_self_query,
        grad_self_key,
        grad_self_value,
        grad_output_one.T,
        grad_cross_query,
        grad_cross_key,
        grad_cross_value,
        grad_output_two.T,
        grad_ffn_gate,
        grad_ffn_up,
        grad_ffn_down.T,
        grad_table,
    )


def solution(mesh):
    in_specs = (
        P("dp", None, None),
        P(None, "dp", None),
        P(),
        P(),
        P(),
        P(),
        P(),
        P(),
        P(),
        P("dp", "mp"),
        P("dp", "mp"),
        P("dp", "mp"),
        P("mp", "dp"),
        P("dp", "mp"),
        P("dp", "mp"),
        P("dp", "mp"),
        P("mp", "dp"),
        P("dp", "mp"),
        P("dp", "mp"),
        P("mp", "dp"),
        P(None, "mp"),
        P("dp", None, None),
    )
    out_specs = (
        P("dp", None, None),
        P("dp", None, None),
        P(None, "dp", "mp"),
        P(),
        P(),
        P(),
        P("dp", "mp"),
        P("dp", "mp"),
        P("dp", "mp"),
        P("mp", "dp"),
        P("dp", "mp"),
        P("dp", "mp"),
        P("dp", "mp"),
        P("mp", "dp"),
        P("dp", "mp"),
        P("dp", "mp"),
        P("mp", "dp"),
        P(None, "mp"),
    )
    body = functools.partial(shards, size=mesh.shape["dp"])
    return jax.shard_map(body, mesh=mesh, in_specs=in_specs, out_specs=out_specs, check_vma=False)
```

```python
import functools

import jax
import jax.numpy as jnp
from jax import lax
from jax.experimental import pallas as pl
from jax.experimental.pallas import tpu as pltpu
from jax.sharding import PartitionSpec as P

HEAD_DIM = 64
PAIR = 2 * HEAD_DIM
QUERIES = 256
KEYS = 1024
TILE = 128
WIDE = 256
HIDDEN = 512
CHUNKS = 4
ROWS = 64

EPS = 1e-06
NEGATIVE = -1000000000.0
GELU_ROOT = 0.7978845608028654
GELU_CUBE = 0.044715
BF16 = jnp.bfloat16
F32 = jnp.float32


def dot(left, right, dims):
    return lax.dot_general(left, right, (dims, ((), ())), preferred_element_type=F32)


def nn(left, right):
    return dot(left, right, ((1,), (0,)))


def nt(left, right):
    return dot(left, right, ((1,), (1,)))


def tn(left, right):
    return dot(left, right, ((0,), (0,)))


def struct(shape, dtype):
    return jax.ShapeDtypeStruct(shape, dtype)


def halves(value):
    high = value.astype(BF16)
    return high, (value - high.astype(F32)).astype(BF16)


def swap(value, mask, size):
    return lax.ppermute(value, "dp", [(i, i ^ mask) for i in range(size)])


def swap_cores(value):
    return lax.ppermute(value, "mp", [(0, 1), (1, 0)])


def after(values, *others):
    return lax.optimization_barrier((values, others))[0]


def gather_outer(shard, size, late=()):
    if size == 16:
        far, near = swap(shard, 8, size), swap(shard, 4, size)
        return [shard, near, far, swap(after(far, late), 4, size)]
    shard = after(shard, late)
    mask = 4
    while mask < size:
        shard = jnp.concatenate([shard, swap(shard, mask, size)])
        mask *= 2
    return [shard]


def gather_first(pieces, size):
    rows, half = sum(piece.shape[0] for piece in pieces), pieces[0].shape[1] // 2
    return kernel_call(stack_kernel, list(pieces), [struct((rows, half), BF16)] * 2, [])


def gather_second(state, size, time=2):
    rows = sum(value.shape[0] for value in state) // 2
    outs = [struct((rows, state[0].shape[1]), BF16)] * 2
    return kernel_call(join_kernel, list(state), outs, [], time=time)


def send_first(halves, size):
    left, right = halves
    return left, swap(left, 2, size), right, swap(right, 1, size)


def send_second(halves, size):
    left, right = halves
    return [left, swap(left, 1, size)], [right, swap(right, 2, size)]


def send_apart(state, size):
    left, left_in, right, right_in = state
    return (
        [left, left_in, swap(left, 1, size), swap(left_in, 1, size)],
        [right, right_in, swap(right, 2, size), swap(right_in, 2, size)],
    )


def scatter_first(grads, size):
    left, left_out, right, right_out = grads
    return left, right, swap(left_out, 1, size), swap(right_out, 2, size)


def scatter_second_parts(state, time=2):
    left = state[0]
    rows, half = left.shape[0] // 2, left.shape[1]
    outs = kernel_call(
        scatter_second_kernel,
        list(state),
        [struct((rows, half), BF16)] * 2,
        [],
        time=time,
        grid=(1,),
        in_specs=[pl.BlockSpec((rows, half), lambda i: (1, 0))] * 4,
        out_specs=[pl.BlockSpec((rows, half), lambda i: (0, 0))] * 2,
    )
    return (*state, *outs)


def scatter_second_send(parts, size):
    *state, left_out, right_out = parts
    return (*state, swap(left_out, 2, size), swap(right_out, 1, size))


def scatter_outer_parts(state, *sides):
    rows, half = state[-1].shape
    ins = [value for side in sides for value in state[side::2]]
    width = len(sides) * half
    return kernel_call(
        scatter_outer_kernel,
        ins,
        [struct((rows // 4, width), dtype) for dtype in (F32, BF16, BF16, BF16)],
        [],
        grid=(1,),
        in_specs=[pl.BlockSpec((rows, half), lambda i: (0, 0))] * len(ins),
        out_specs=[pl.BlockSpec((rows // 4, width), lambda i: (0, 0))] * 4,
    )


def scatter_pair_parts(state):
    rows, half = state[-1].shape
    outs = [struct((rows // 2, 2 * half), dtype) for dtype in (F32, BF16)]
    return kernel_call(
        scatter_pair_kernel,
        state[0::2] + state[1::2],
        outs,
        [],
        grid=(1,),
        in_specs=[pl.BlockSpec((rows, half), lambda i: (0, 0))] * 6,
        out_specs=[pl.BlockSpec((rows // 2, 2 * half), lambda i: (0, 0))] * 2,
    )


def scatter_pair_send(keep, taken, size):
    count = keep.shape[0] // 2
    rows = keep + taken.astype(F32)
    return [rows[:count], swap(rows[count:].astype(BF16), 8, size)]


def scatter_outer_send(parts, size):
    keep, *outs = parts
    if size == 16:
        return [keep] + [swap(out, 4 * (k + 1), size) for k, out in enumerate(outs)]
    rows = jnp.concatenate([keep] + [out.astype(F32) for out in outs])
    mask = size // 2
    while mask >= 4:
        count = rows.shape[0] // 2
        rows = rows[:count] + swap(rows[count:].astype(BF16), mask, size).astype(F32)
        mask //= 2
    return [rows]


def scatter_last(state):
    total = state[0]
    for value in state[1:]:
        total = total + value.astype(F32)
    return total


def kernel_call(kernel, ins, outs, scratch, time=2, grid=None, in_specs=None, out_specs=None):
    everywhere = pl.BlockSpec(memory_space=pltpu.VMEM)
    return pl.pallas_call(
        kernel,
        out_shape=outs,
        in_specs=in_specs or [everywhere] * len(ins),
        out_specs=out_specs or [everywhere] * len(outs),
        scratch_shapes=scratch,
        compiler_params=pltpu.CompilerParams(vmem_limit_bytes=58 * 1024 * 1024),
        cost_estimate=pl.CostEstimate(
            flops=time * 1000000000, bytes_accessed=1, transcendentals=0
        ),
        **({"grid": grid} if grid else {}),
    )(*ins)


IN_VMEM = pl.BlockSpec(memory_space=pltpu.VMEM)
IN_PLACE = pl.BlockSpec(memory_space=pl.ANY)
IN_SMEM = pl.BlockSpec(memory_space=pltpu.SMEM)


def stack_kernel(*refs):
    *in_refs, left_ref, right_ref = refs
    half = left_ref.shape[1]
    start = 0
    for ref in in_refs:
        rows = slice(start, start + ref.shape[0])
        left_ref[rows, :] = ref[:, :half]
        right_ref[rows, :] = ref[:, half:]
        start += ref.shape[0]


def join_kernel(*refs):
    *in_refs, left_out, right_out = refs
    for out_ref, pieces in (
        (left_out, in_refs[: len(in_refs) // 2]),
        (right_out, in_refs[len(in_refs) // 2 :]),
    ):
        start = 0
        for ref in pieces:
            out_ref[start : start + ref.shape[0], :] = ref[...]
            start += ref.shape[0]


def scatter_second_kernel(left_ref, right_ref, left_in_ref, right_in_ref, left_out, right_out):
    left_out[...] = (left_ref[...].astype(F32) + left_in_ref[...].astype(F32)).astype(BF16)
    right_out[...] = (right_ref[...].astype(F32) + right_in_ref[...].astype(F32)).astype(BF16)


def scatter_outer_kernel(*refs):
    *in_refs, keep_ref, first_ref, second_ref, third_ref = refs
    count = keep_ref.shape[0]
    for side in range(len(in_refs) // 3):
        own_ref, in_ref, more_ref = in_refs[3 * side : 3 * side + 3]
        half = own_ref.shape[1]
        cols = slice(side * half, (side + 1) * half)
        for k, out_ref in enumerate((keep_ref, first_ref, second_ref, third_ref)):
            rows = slice(k * count, (k + 1) * count)
            total = own_ref[rows, :].astype(F32) + in_ref[rows, :].astype(F32)
            out_ref[:, cols] = (total + more_ref[rows, :].astype(F32)).astype(out_ref.dtype)


def scatter_pair_kernel(*refs):
    *in_refs, keep_ref, out_ref = refs
    count = keep_ref.shape[0] // 2
    for side in range(2):
        own_ref, in_ref, more_ref = in_refs[3 * side : 3 * side + 3]
        half = own_ref.shape[1]
        cols = slice(side * half, (side + 1) * half)
        for k in range(4):
            rows = slice(k * count, (k + 1) * count)
            total = own_ref[rows, :].astype(F32) + in_ref[rows, :].astype(F32)
            target = out_ref if k % 2 else keep_ref
            spot = slice(k // 2 * count, (k // 2 + 1) * count)
            target[spot, cols] = (total + more_ref[rows, :].astype(F32)).astype(target.dtype)


def cast_kernel(*refs):
    *in_refs, out_ref = refs
    start = 0
    for ref in in_refs:
        out_ref[:, start : start + ref.shape[1]] = ref[...].astype(BF16)
        start += ref.shape[1]


def low(*values):
    width = sum(value.shape[1] for value in values)
    return kernel_call(
        cast_kernel, list(values), [struct((values[0].shape[0], width), BF16)], []
    )[0]


def each_rows(count, body, rows=ROWS):
    @pl.loop(0, count // rows)
    def step(i):
        body(pl.ds(pl.multiple_of(i * rows, rows), rows))


def each_tile(start, width, body):
    @pl.loop(0, width // WIDE)
    def step(i):
        body(pl.ds(pl.multiple_of(start + i * WIDE, WIDE), WIDE))


def fetch(left, right, weights_ref, sems, first=0):
    start = left[0].shape[1] if left else 0
    columns = weights_ref.shape[1] - start
    quarter = weights_ref.shape[0] // 4
    moves = []
    for i, ref in enumerate(left):
        count = ref.shape[0]
        moves.append((ref, weights_ref.at[i * count : (i + 1) * count, :start]))
    places = [0, 2, 1, 3]
    for ref in right:
        for x in range(ref.shape[0] // quarter):
            place = places.pop(0) * quarter
            moves.append(
                (
                    ref.at[x * quarter : (x + 1) * quarter, first : first + columns],
                    weights_ref.at[place : place + quarter, start:],
                )
            )
    copies = [pltpu.make_async_copy(*move, sems.at[i]) for i, move in enumerate(moves)]
    for copy in copies:
        copy.start()
    return copies


def deliver(grads_ref, out_refs, sems, columns, first=0):
    left, left_out, right, right_out = out_refs
    rows, half = left.shape[0] // 2, left.shape[1]
    side = columns.start // half
    if side == 0:
        moves = [(left, 0, 0, 2), (left_out, 0, 2, 2)]
    else:
        moves = [(right, 0, 0, 1), (right, 1, 2, 1), (right_out, 0, 1, 1), (right_out, 1, 3, 1)]
    copies = []
    for target, spot, place, count in moves:
        copies.append(
            pltpu.make_async_copy(
                grads_ref.at[place * rows : (place + count) * rows, columns],
                target.at[
                    spot * rows : (spot + count) * rows,
                    columns.start - side * half : columns.stop - side * half,
                ],
                sems.at[first + len(copies)],
            )
        )
    return copies


def deliver_all(grads_ref, out_refs, sems):
    half = out_refs[0].shape[1]
    copies = deliver(grads_ref, out_refs, sems, slice(0, half))
    copies += deliver(grads_ref, out_refs, sems, slice(half, 2 * half), 2)
    for copy in copies:
        copy.start()
    for copy in copies:
        copy.wait()


def grad_structs(width, columns):
    return [struct((width // 2, columns // 2), BF16)] * 4


def root_of(value):
    return lax.rsqrt(jnp.mean(value * value, axis=-1, keepdims=True) + EPS)


def norm_back(value, gain, grad):
    root = root_of(value)
    scaled = grad * gain
    inner = jnp.mean(value * scaled, axis=-1, keepdims=True)
    back = root * scaled - value * (root * root * root * inner)
    return back, jnp.sum(grad * value * root, axis=0, keepdims=True)


def rows_kernel(
    tokens_ref, cot_ref, gains_ref, source_ref,
    tokens_out, cot_out, cot_t_out, gains_out, order_ref, turned_ref, normed_ref,
):
    width = tokens_ref.shape[1]
    spot = lax.broadcasted_iota(jnp.int32, (width, width), 0)
    order_ref[...] = jnp.where(spot == source_ref[0:1, :], 1.0, 0.0).astype(BF16)
    order = order_ref[...]
    turned_ref[...] = order.T
    high = gains_ref[...].astype(BF16)
    middle, rest = halves(gains_ref[...] - high.astype(F32))
    gains_out[...] = nn(high, order) + (nn(middle, order) + nn(rest, order))
    tokens_out[...] = nn(tokens_ref[...], order)
    cot_out[...] = nn(cot_ref[...], order).astype(BF16)
    cot_t_out[...] = cot_out[...].T
    gain = gains_out[0:1, :]

    def norm(rows):
        value = tokens_out[rows, :]
        normed_ref[rows, :] = (value * root_of(value) * gain).astype(BF16)

    each_rows(tokens_ref.shape[0], norm)


def queries_of(capacity):
    return QUERIES if capacity <= 2 * KEYS else TILE


def each_chunk(count, size, body):
    if count == 1:
        body(0)
    else:
        pl.loop(0, count)(lambda step: body(pl.multiple_of(step * size, size)))


def each_pair(pairs, body):
    @pl.loop(0, pairs)
    def step(pair):
        body(pair, lambda which: pl.ds(pl.multiple_of((which * pairs + pair) * PAIR, PAIR), PAIR))


def row_of(value, head):
    line = lax.broadcasted_iota(jnp.int32, value.shape, 0)
    return jnp.sum(jnp.where(line == head, value, 0.0), axis=0, keepdims=True)


def of_head(value, head):
    lane = lax.broadcasted_iota(jnp.int32, value.shape, 1)
    return jnp.where(lane // HEAD_DIM == head, value, jnp.zeros_like(value))


def cross_forward_pair(q_ref, k_ref, v_ref, dead_ref, out_ref, lse_ref, s_ref, acc_ref):
    targets, capacity = q_ref.shape[0], k_ref.shape[0]
    size = min(capacity, KEYS)
    count = capacity // size
    queries = s_ref.shape[1]
    for head in range(2):
        rows = slice(head * HEAD_DIM, (head + 1) * HEAD_DIM)
        line = slice(head, head + 1)
        for start in range(0, targets, queries):
            cols = slice(start, start + queries)
            query = of_head(q_ref[cols, :], head)
            lse_ref[line, cols] = jnp.full((1, queries), NEGATIVE * 2, F32)

            def scores(base):
                keys = pl.ds(base, size)
                score = nt(k_ref[keys, :], query) + dead_ref[keys, 0:1]
                s_ref[keys, :] = score
                lse_ref[line, cols] = jnp.maximum(
                    lse_ref[line, cols], jnp.max(score, axis=0, keepdims=True)
                )

            each_chunk(count, size, scores)
            top = lse_ref[line, cols]
            lse_ref[line, cols] = jnp.zeros((1, queries), F32)

            def weights(base):
                keys = pl.ds(base, size)
                weight = jnp.exp(s_ref[keys, :] - top)
                s_ref[keys, :] = weight
                lse_ref[line, cols] += jnp.sum(weight, axis=0, keepdims=True)

            each_chunk(count, size, weights)
            total = lse_ref[line, cols]
            lse_ref[line, cols] = top + jnp.log(total)
            scale = 1.0 / total
            acc_ref[rows, cols] = jnp.zeros((HEAD_DIM, queries), F32)

            def mix(base):
                keys = pl.ds(base, size)
                probs = (s_ref[keys, :] * scale).astype(BF16)
                acc_ref[rows, cols] += tn(v_ref[keys, :], probs)[rows]

            each_chunk(count, size, mix)
    out_ref[...] = acc_ref[...].T.astype(BF16)


def cross_backward_pair(
    q_ref, k_ref, v_ref, dead_ref, lse_ref, go_ref, dq_ref, dk_ref, dv_ref,
    p_ref, dp_ref, dqt_ref, dk_acc, dv_acc, delta_ref,
):
    targets, capacity = q_ref.shape[0], k_ref.shape[0]
    size = min(capacity, KEYS)
    count = capacity // size
    queries = p_ref.shape[1]
    dk_acc[...] = jnp.zeros_like(dk_acc)
    dv_acc[...] = jnp.zeros_like(dv_acc)
    dqt_ref[...] = jnp.zeros_like(dqt_ref)

    @pl.loop(0, 2)
    def each_head(head):
        for start in range(0, targets, queries):
            cols = slice(start, start + queries)
            query = of_head(q_ref[cols, :], head)
            grad = of_head(go_ref[cols, :], head)
            lse = row_of(lse_ref[:, cols], head)
            delta_ref[...] = jnp.zeros_like(delta_ref)

            def first(base):
                keys = pl.ds(base, size)
                probs = jnp.exp(nt(k_ref[keys, :], query) + dead_ref[keys, 0:1] - lse)
                grad_probs = nt(v_ref[keys, :], grad)
                p_ref[keys, :] = probs
                dp_ref[keys, :] = grad_probs
                delta_ref[...] += jnp.sum(probs * grad_probs, axis=0, keepdims=True)

            each_chunk(count, size, first)
            delta = delta_ref[...]

            def second(base):
                keys = pl.ds(base, size)
                probs = p_ref[keys, :]
                dv_acc[keys, :] += nn(probs.astype(BF16), grad)
                low = (probs * (dp_ref[keys, :] - delta)).astype(BF16)
                dk_acc[keys, :] += nn(low, query)
                dqt_ref[:, cols] += tn(of_head(k_ref[keys, :], head), low)

            each_chunk(count, size, second)
    dq_ref[...] = dqt_ref[...].T.astype(BF16)
    dk_ref[...] = dk_acc[...].astype(BF16)
    dv_ref[...] = dv_acc[...].astype(BF16)


def skewed(row, block):
    before = row[:, (block - 1) * TILE : block * TILE] if block else jnp.zeros((1, TILE), F32)
    both = jnp.concatenate([before, row[:, block * TILE : (block + 1) * TILE]], axis=1)
    both = jnp.broadcast_to(both, (TILE, 2 * TILE))
    return pltpu.roll(both, 0, 1, stride=1, stride_axis=0)[:, TILE:]


def unskewed(tile):
    both = jnp.concatenate([jnp.zeros_like(tile), tile], axis=1)
    total = both[:8]
    for base in range(8, TILE, 8):
        total = total + pltpu.roll(both[base : base + 8], 2 * TILE - base, 1)
    row = lax.broadcasted_iota(jnp.int32, total.shape, 0)
    for bit in (1, 2, 4):
        total = jnp.where(row & bit != 0, pltpu.roll(total, 2 * TILE - bit, 1), total)
    return jnp.sum(total, axis=0, keepdims=True)


def self_scores(k_ref, query, tiles, start):
    keys = start + QUERIES
    columns = []
    for i in range(start // TILE, keys // TILE):
        columns.append(
            jnp.concatenate([tiles[max(i - j, 0)] for j in range(keys // TILE)], axis=0)
        )
    score = nt(k_ref[:keys, :], query) + jnp.concatenate(columns, axis=1)
    key = lax.broadcasted_iota(jnp.int32, score.shape, 0)
    spot = lax.broadcasted_iota(jnp.int32, score.shape, 1) + start
    return jnp.where(key <= spot, score, NEGATIVE)


def self_forward_pair(q_ref, k_ref, v_ref, bias_ref, out_ref, lse_ref, acc_ref):
    targets = q_ref.shape[0]
    for head in range(2):
        rows = slice(head * HEAD_DIM, (head + 1) * HEAD_DIM)
        row = bias_ref[head : head + 1, :]
        tiles = [skewed(row, block) for block in range(targets // TILE)]
        for start in range(0, targets, QUERIES):
            cols = slice(start, start + QUERIES)
            query = of_head(q_ref[cols, :], head)
            score = self_scores(k_ref, query, tiles, start)
            top = jnp.max(score, axis=0, keepdims=True)
            weight = jnp.exp(score - top)
            total = jnp.sum(weight, axis=0, keepdims=True)
            lse_ref[head : head + 1, cols] = top + jnp.log(total)
            probs = (weight * (1.0 / total)).astype(BF16)
            acc_ref[rows, cols] = tn(v_ref[: start + QUERIES, :], probs)[rows]
    out_ref[...] = acc_ref[...].T.astype(BF16)


def self_backward_pair(
    q_ref, k_ref, v_ref, bias_ref, lse_ref, go_ref, dq_ref, dk_ref, dv_ref, dbias_ref,
    dqt_ref, dk_acc, dv_acc,
):
    targets = q_ref.shape[0]
    dk_acc[...] = jnp.zeros_like(dk_acc)
    dv_acc[...] = jnp.zeros_like(dv_acc)
    blocks = targets // TILE
    dqt_ref[...] = jnp.zeros_like(dqt_ref)

    @pl.loop(0, 2)
    def each_head(head):
        row = row_of(bias_ref[...], head)
        tiles = [skewed(row, block) for block in range(blocks)]
        sums = [jnp.zeros((TILE, TILE), F32) for block in range(blocks)]
        for start in range(0, targets, QUERIES):
            cols = slice(start, start + QUERIES)
            keys = start + QUERIES
            query = of_head(q_ref[cols, :], head)
            grad = of_head(go_ref[cols, :], head)
            score = self_scores(k_ref, query, tiles, start)
            probs = jnp.exp(score - row_of(lse_ref[:, cols], head))
            grad_probs = nt(v_ref[:keys, :], grad)
            delta = jnp.sum(probs * grad_probs, axis=0, keepdims=True)
            dv_acc[:keys, :] += nn(probs.astype(BF16), grad)
            grad_scores = probs * (grad_probs - delta)
            for i in range(start // TILE, keys // TILE):
                for j in range(i + 1):
                    sums[i - j] = sums[i - j] + grad_scores[
                        j * TILE : (j + 1) * TILE, i * TILE - start : (i + 1) * TILE - start
                    ]
            low_scores = grad_scores.astype(BF16)
            dk_acc[:keys, :] += nn(low_scores, query)
            dqt_ref[:, cols] += tn(of_head(k_ref[:keys, :], head), low_scores)
        lines = [unskewed(tile) for tile in sums]
        parts = []
        for block in range(blocks):
            part = lines[block][:, TILE:]
            if block + 1 < blocks:
                part = part + lines[block + 1][:, :TILE]
            parts.append(part)
        row = jnp.concatenate(parts, axis=1)
        line = lax.broadcasted_iota(jnp.int32, dbias_ref.shape, 0)
        dbias_ref[...] = jnp.where(line == head, row, dbias_ref[...])
    dq_ref[...] = dqt_ref[...].T.astype(BF16)
    dk_ref[...] = dk_acc[...].astype(BF16)
    dv_ref[...] = dv_acc[...].astype(BF16)


def self_forward_kernel(
    normed_ref, bias_ref, *refs
):
    mixed_ref, attended_ref, lse_ref, partial_ref, weights_ref, acc_ref, sems = refs[2:]
    copies = fetch(refs[:2], [], weights_ref, sems)
    for copy in copies:
        copy.wait()
    part = attended_ref.shape[1]
    pairs = part // PAIR
    normed = normed_ref[...]

    @pl.loop(0, 3 * part // TILE)
    def project(i):
        cols = pl.ds(pl.multiple_of(i * TILE, TILE), TILE)
        mixed_ref[:, cols] = nn(normed, weights_ref[:, cols]).astype(BF16)

    def attend(pair, cols):
        self_forward_pair(
            *(mixed_ref.at[:, cols(i)] for i in range(3)),
            bias_ref.at[pair], attended_ref.at[:, cols(0)], lse_ref.at[pair], acc_ref,
        )

    each_pair(pairs, attend)
    partial_ref[...] = nt(attended_ref[...], weights_ref[:, 3 * part :])


def self_forward(normed, bias, quarters):
    targets, width = normed.shape
    columns = quarters[0].shape[1]
    part = columns // 4
    pairs = part // PAIR
    return kernel_call(
        self_forward_kernel,
        [normed, bias, *quarters],
        [
            struct((targets, 3 * part), BF16),
            struct((targets, part), BF16),
            struct((pairs, 8, targets), F32),
            struct((targets, width), F32),
        ],
        [
            pltpu.VMEM((width, columns), BF16),
            pltpu.VMEM((PAIR, targets), F32),
            pltpu.SemaphoreType.DMA((6,)),
        ],
        in_specs=[IN_VMEM] * 2 + [IN_PLACE] * 2,
        time=12,
    )


def encoder_kernel(core_ref, own_ref, peer_ref, order_ref, *refs):
    encoded_ref, out_ref, weights_ref, sems = refs[2:]

    @pl.when(pl.program_id(0) == 0)
    def load():
        for copy in fetch([], refs[:2], weights_ref, sems, weights_ref.shape[1]):
            copy.wait()

    core, half = core_ref[0], own_ref.shape[1]
    own_rows = pl.ds(pl.multiple_of(core * half, half), half)
    peer_rows = pl.ds(pl.multiple_of(half - core * half, half), half)
    encoded = nn(own_ref[...], order_ref[own_rows, :]) + nn(peer_ref[...], order_ref[peer_rows, :])
    encoded_ref[...] = encoded.astype(BF16)
    encoded = encoded_ref[...]

    def project(cols):
        out_ref[:, cols] = nn(encoded, weights_ref[:, cols]).astype(BF16)

    each_tile(0, out_ref.shape[1], project)


def encoder_call(core, own, peer, order, quarters):
    capacity, half = own.shape
    width = 2 * half
    columns = quarters[0].shape[1] // 2
    size = min(capacity, KEYS)
    block = lambda cols: pl.BlockSpec((size, cols), lambda i: (i, 0))
    return kernel_call(
        encoder_kernel,
        [core, own, peer, order, *quarters],
        [struct((capacity, width), BF16), struct((capacity, columns), BF16)],
        [pltpu.VMEM((width, columns), BF16), pltpu.SemaphoreType.DMA((4,))],
        grid=(capacity // size,),
        in_specs=[IN_SMEM, block(half), block(half), IN_VMEM] + [IN_PLACE] * 2,
        out_specs=[block(width), block(columns)],
        time=8,
    )


def cross_forward_kernel(tokens_ref, partial_ref, peer_ref, gains_ref, kv_ref, dead_ref, *refs):
    (
        h_ref, normed_ref, query_ref, att_ref, lse_ref, *out_refs,
        weights_ref, s_ref, acc_ref, sems,
    ) = refs[2:]
    copies = fetch([], refs[:2], weights_ref, sems)
    gain = gains_ref[1:2, :]

    def norm(rows):
        value = tokens_ref[rows, :] + (partial_ref[rows, :] + peer_ref[rows, :])
        h_ref[rows, :] = value
        normed_ref[rows, :] = (value * root_of(value) * gain).astype(BF16)

    each_rows(h_ref.shape[0], norm)
    for copy in copies:
        copy.wait()
    part = query_ref.shape[1]
    pairs = part // PAIR
    query_ref[...] = nn(normed_ref[...], weights_ref[:, :part]).astype(BF16)

    def attend(pair, cols):
        cross_forward_pair(
            query_ref.at[:, cols(0)], kv_ref.at[:, cols(0)], kv_ref.at[:, cols(1)], dead_ref,
            att_ref.at[:, cols(0)], lse_ref.at[pair], s_ref, acc_ref,
        )

    each_pair(pairs, attend)
    count = out_refs[0].shape[0]
    for i, out_ref in enumerate(out_refs):
        out_ref[...] = nt(att_ref[i * count : (i + 1) * count, :], weights_ref[:, part:])


def cross_forward(tokens, partial, peer, gains, key_value, dead, quarters):
    targets, width = tokens.shape
    capacity, columns = key_value.shape
    part = columns // 2
    pairs = part // PAIR
    return kernel_call(
        cross_forward_kernel,
        [tokens, partial, peer, gains, key_value, dead, *quarters],
        [
            struct((targets, width), F32),
            struct((targets, width), BF16),
            struct((targets, part), BF16),
            struct((targets, part), BF16),
            struct((pairs, 8, targets), F32),
            *[struct((targets // CHUNKS, width), F32)] * CHUNKS,
        ],
        [
            pltpu.VMEM((width, columns), BF16),
            pltpu.VMEM((capacity, queries_of(capacity)), F32),
            pltpu.VMEM((PAIR, targets), F32),
            pltpu.SemaphoreType.DMA((4,)),
        ],
        in_specs=[IN_VMEM] * 6 + [IN_PLACE] * 2,
        time=16,
    )


def ffn_kernel(before_ref, gains_ref, cot_ref, cot_t_ref, *refs):
    chunks, refs = refs[: 2 * CHUNKS], refs[2 * CHUNKS :]
    h_out, down_ref, back_ref, *outs = refs[8:15]
    weights_ref, grads_ref, h_ref, normed_ref, normed_t, in_sems, out_sems = refs[15:]
    copies = fetch(refs[:4], refs[4:8], weights_ref, in_sems)
    gain = gains_ref[2:3, :]
    count = chunks[0].shape[0]
    for i, (partial_ref, peer_ref) in enumerate(zip(chunks[:CHUNKS], chunks[CHUNKS:])):

        def norm(rows):
            own = pl.ds(pl.multiple_of(rows.start + i * count, rows.size), rows.size)
            value = before_ref[own, :] + (partial_ref[rows, :] + peer_ref[rows, :])
            h_ref[own, :] = value
            normed_ref[own, :] = (value * root_of(value) * gain).astype(BF16)

        each_rows(count, norm, 32)
    h_copy = pltpu.make_async_copy(h_ref, h_out, out_sems.at[36])
    h_copy.start()
    normed_t[...] = normed_ref[...].T
    down_ref[...] = jnp.zeros_like(down_ref)
    back_ref[...] = jnp.zeros_like(back_ref)
    for copy in copies:
        copy.wait()
    hidden = weights_ref.shape[1] // 3
    tiles = hidden // HIDDEN

    def sends(i):
        copies = []
        for k in range(3):
            columns = slice(k * hidden + i * HIDDEN, k * hidden + (i + 1) * HIDDEN)
            first = 6 * (i * 3 + k)
            copies += deliver(grads_ref, outs, out_sems, columns, first)
        return copies

    @pl.loop(0, tiles)
    def tile(i):
        gates, ups, downs = (
            pl.ds(pl.multiple_of(k * hidden + i * HIDDEN, HIDDEN), HIDDEN) for k in range(3)
        )
        normed = normed_ref[...]
        gate = nn(normed, weights_ref[:, gates])
        up = nn(normed, weights_ref[:, ups])
        grad_act = nn(cot_ref[...], weights_ref[:, downs]).astype(BF16).astype(F32)
        square = gate * gate
        curve = jnp.tanh(GELU_ROOT * (gate + GELU_CUBE * (square * gate)))
        share = 0.5 * (1.0 + curve)
        gelu = gate * share
        slope = share + (0.5 * gate) * (1.0 - curve * curve) * (
            GELU_ROOT * (1.0 + (3.0 * GELU_CUBE) * square)
        )
        act = (gelu * up).astype(BF16)
        grad_gate = (grad_act * up * slope).astype(BF16)
        grad_up = (grad_act * gelu).astype(BF16)
        grads_ref[:, gates] = nn(normed_t[...], grad_gate).astype(BF16)
        grads_ref[:, ups] = nn(normed_t[...], grad_up).astype(BF16)
        grads_ref[:, downs] = nn(cot_t_ref[...], act).astype(BF16)
        for each in range(tiles):

            @pl.when(i == each)
            def send():
                for copy in sends(each):
                    copy.start()

        back_ref[...] += nt(grad_gate, weights_ref[:, gates]) + nt(grad_up, weights_ref[:, ups])
        down_ref[...] += nt(act, weights_ref[:, downs])

    for i in range(tiles):
        for copy in sends(i):
            copy.wait()
    h_copy.wait()


def ffn_call(before, partials, peers, gains, cot, cot_t, quarters):
    targets, width = before.shape
    columns = 2 * quarters[0].shape[1]
    return kernel_call(
        ffn_kernel,
        [before, gains, cot, cot_t, *partials, *peers, *quarters],
        [struct((targets, width), F32)] * 3 + grad_structs(width, columns),
        [
            pltpu.VMEM((width, columns), BF16),
            pltpu.VMEM((width, columns), BF16),
            pltpu.VMEM((targets, width), F32),
            pltpu.VMEM((targets, width), BF16),
            pltpu.VMEM((width, targets), BF16),
            pltpu.SemaphoreType.DMA((8,)),
            pltpu.SemaphoreType.DMA((37,)),
        ],
        time=20,
        in_specs=[IN_VMEM] * (4 + 2 * CHUNKS) + [IN_PLACE] * 8,
        out_specs=[IN_PLACE] + [IN_VMEM] * 2 + [IN_PLACE] * 4,
    )


def cross_backward_kernel(
    cot_ref, partial_ref, peer_ref, h_ref, gains_ref, query_ref, kv_ref, dead_ref, lse_ref, *refs
):
    (
        g_ref, low_ref, dq_ref, dkv_ref, back_ref, gain_grad_ref,
        weights_ref, go_ref, p_ref, dp_ref, dqt_ref, dk_acc, dv_acc, delta_ref, sems,
    ) = refs[2:]
    copies = fetch([], refs[:2], weights_ref, sems)
    gain = gains_ref[2:3, :]
    gain_grad_ref[...] = jnp.zeros_like(gain_grad_ref)

    def norm(rows):
        back, gain_grad = norm_back(h_ref[rows, :], gain, partial_ref[rows, :] + peer_ref[rows, :])
        gain_grad_ref[0:1, :] += gain_grad
        value = cot_ref[rows, :].astype(F32) + back
        g_ref[rows, :] = value
        low_ref[rows, :] = value.astype(BF16)

    each_rows(h_ref.shape[0], norm)
    for copy in copies:
        copy.wait()
    part = query_ref.shape[1]
    pairs = part // PAIR
    go_ref[...] = nn(low_ref[...], weights_ref[:, part:]).astype(BF16)

    def attend(pair, cols):
        cross_backward_pair(
            query_ref.at[:, cols(0)], kv_ref.at[:, cols(0)], kv_ref.at[:, cols(1)], dead_ref,
            lse_ref.at[pair], go_ref.at[:, cols(0)],
            dq_ref.at[:, cols(0)], dkv_ref.at[:, cols(0)], dkv_ref.at[:, cols(1)],
            p_ref, dp_ref, dqt_ref, dk_acc, dv_acc, delta_ref,
        )

    each_pair(pairs, attend)
    back_ref[...] = nt(dq_ref[...], weights_ref[:, :part])


def cross_backward(cot, partial, peer, before, gains, query, key_value, dead, lse, quarters):
    targets, width = cot.shape
    capacity, columns = key_value.shape
    return kernel_call(
        cross_backward_kernel,
        [cot, partial, peer, before, gains, query, key_value, dead, lse, *quarters],
        [
            struct((targets, width), F32),
            struct((targets, width), BF16),
            struct(query.shape, BF16),
            struct(key_value.shape, BF16),
            struct((targets, width), F32),
            struct((8, width), F32),
        ],
        [
            pltpu.VMEM((width, columns), BF16),
            pltpu.VMEM(query.shape, BF16),
            pltpu.VMEM((capacity, queries_of(capacity)), F32),
            pltpu.VMEM((capacity, queries_of(capacity)), F32),
            pltpu.VMEM((PAIR, targets), F32),
            pltpu.VMEM((capacity, PAIR), F32),
            pltpu.VMEM((capacity, PAIR), F32),
            pltpu.VMEM((1, queries_of(capacity)), F32),
            pltpu.SemaphoreType.DMA((4,)),
        ],
        in_specs=[IN_VMEM] * 9 + [IN_PLACE] * 2,
        time=18,
    )


def cross_grads_kernel(
    core_ref, normed_ref, dq_ref, low_ref, att_ref, order_ref, encoded_ref, dkv_ref, *refs
):
    kept_ref, given_ref, *outs = refs[2:8]
    weights_ref, acc_ref, grads_ref, in_sems, out_sems = refs[8:]
    step = pl.program_id(0)
    part = dq_ref.shape[1]

    @pl.when(step == 0)
    def load():
        copies = fetch([], refs[:2], weights_ref, in_sems, weights_ref.shape[1])
        grads_ref[:, :part] = tn(normed_ref[...], dq_ref[...]).astype(BF16)
        grads_ref[:, part : 2 * part] = tn(low_ref[...], att_ref[...]).astype(BF16)
        acc_ref[...] = jnp.zeros_like(acc_ref)
        for copy in copies:
            copy.wait()

    encoded_t = encoded_ref[...].T

    def project(cols):
        acc_ref[:, cols] += nn(encoded_t, dkv_ref[:, cols])

    each_tile(0, acc_ref.shape[1], project)
    core, half = core_ref[0], kept_ref.shape[1]
    terms = nt(dkv_ref[...], weights_ref[...]).astype(BF16)
    own_cols = pl.ds(pl.multiple_of(core * half, half), half)
    peer_cols = pl.ds(pl.multiple_of(half - core * half, half), half)
    kept_ref[...] = nn(terms, order_ref[:, own_cols]).astype(BF16)
    given_ref[...] = nn(terms, order_ref[:, peer_cols]).astype(BF16)

    @pl.when(step == pl.num_programs(0) - 1)
    def store():
        grads_ref[:, 2 * part :] = acc_ref[...].astype(BF16)
        deliver_all(grads_ref, outs, out_sems)


def cross_grads(core, normed, dq, low_two, attended, order, encoded, dkv, quarters):
    capacity, width = encoded.shape
    columns = dkv.shape[1]
    size = min(capacity, KEYS)
    block = lambda cols: pl.BlockSpec((size, cols), lambda i: (i, 0))
    return kernel_call(
        cross_grads_kernel,
        [core, normed, dq, low_two, attended, order, encoded, dkv, *quarters],
        [struct((capacity, width // 2), BF16)] * 2 + grad_structs(width, 2 * columns),
        [
            pltpu.VMEM((width, columns), BF16),
            pltpu.VMEM((width, columns), F32),
            pltpu.VMEM((width, 2 * columns), BF16),
            pltpu.SemaphoreType.DMA((4,)),
            pltpu.SemaphoreType.DMA((6,)),
        ],
        grid=(capacity // size,),
        in_specs=[IN_SMEM] + [IN_VMEM] * 5 + [block(width), block(columns)] + [IN_PLACE] * 2,
        out_specs=[block(width // 2)] * 2 + [IN_PLACE] * 4,
        time=12,
    )


def self_backward_kernel(
    g_in_ref, partial_ref, peer_ref, h_ref, gains_ref, mixed_ref, bias_ref, lse_ref,
    attended_ref, normed_ref, tokens_ref, gain_three_ref, order_ref, labels_ref, *refs
):
    g_ref, back_ref, small_ref, *outs = refs[2:9]
    (
        weights_ref, grads_ref, low_ref, go_ref, dmixed_ref, dbias_ref,
        dqt_ref, dk_acc, dv_acc, gain_ref, pack_ref, in_sems, out_sems,
    ) = refs[9:]
    copies = fetch(refs[:2], [], weights_ref, in_sems)
    gain = gains_ref[1:2, :]
    gain_ref[...] = jnp.zeros_like(gain_ref)

    def norm(rows):
        back, gain_grad = norm_back(h_ref[rows, :], gain, partial_ref[rows, :] + peer_ref[rows, :])
        gain_ref[1:2, :] += gain_grad
        value = g_in_ref[rows, :] + back
        g_ref[rows, :] = value
        low_ref[rows, :] = value.astype(BF16)

    each_rows(h_ref.shape[0], norm)
    for copy in copies:
        copy.wait()
    part = attended_ref.shape[1]
    pairs = part // PAIR
    go_ref[...] = nn(low_ref[...], weights_ref[:, 3 * part :]).astype(BF16)
    dbias_ref[...] = jnp.zeros_like(dbias_ref)

    def attend(pair, cols):
        self_backward_pair(
            *(mixed_ref.at[:, cols(i)] for i in range(3)),
            bias_ref.at[pair], lse_ref.at[pair], go_ref.at[:, cols(0)],
            *(dmixed_ref.at[:, cols(i)] for i in range(3)),
            dbias_ref.at[pair], dqt_ref, dk_acc, dv_acc,
        )

    each_pair(pairs, attend)
    back_ref[...] = nt(dmixed_ref[...], weights_ref[:, : 3 * part])
    normed_t = normed_ref[...].T

    @pl.loop(0, 3 * part // TILE)
    def project(i):
        cols = pl.ds(pl.multiple_of(i * TILE, TILE), TILE)
        grads_ref[:, cols] = nn(normed_t, dmixed_ref[:, cols]).astype(BF16)

    grads_ref[:, 3 * part :] = tn(low_ref[...], attended_ref[...]).astype(BF16)

    def sums(rows):
        value = tokens_ref[rows, :]
        gain_ref[0:1, :] += jnp.sum(back_ref[rows, :] * value * root_of(value), axis=0, keepdims=True)

    each_rows(h_ref.shape[0], sums)
    gain_ref[2:3, :] = gain_three_ref[0:1, :]
    high, rest = halves(gain_ref[...])
    gain_ref[...] = nn(high, order_ref[...]) + nn(rest, order_ref[...])
    half = pack_ref.shape[1]
    pack_ref[0:3, :] = gain_ref[0:3, :half]
    pack_ref[3:6, :] = gain_ref[0:3, half:]
    bucket = lax.broadcasted_iota(jnp.int32, (labels_ref.shape[0], TILE), 1)
    which = jnp.where(labels_ref[:, 0:1] == bucket, 1.0, 0.0).astype(BF16)
    for pair in range(pairs):
        high, rest = halves(dbias_ref[pair])
        table = nn(high, which) + nn(rest, which)
        pack_ref[6:8, pair * TILE : (pair + 1) * TILE] = table[0:2]
    small_ref[...] = jnp.concatenate(halves(pack_ref[...]), axis=0)
    deliver_all(grads_ref, outs, out_sems)


def self_backward(
    g_in, partial, peer, before, gains, mixed, bias, lse, attended, normed, tokens,
    gain_three, order, labels, quarters,
):
    targets, width = g_in.shape
    part = attended.shape[1]
    pairs = part // PAIR
    return kernel_call(
        self_backward_kernel,
        [
            g_in, partial, peer, before, gains, mixed, bias, lse, attended, normed, tokens,
            gain_three, order, labels, *quarters,
        ],
        [
            struct((targets, width), F32),
            struct((targets, width), F32),
            struct((16, width // 2), BF16),
        ]
        + grad_structs(width, 4 * part),
        [
            pltpu.VMEM((width, 4 * part), BF16),
            pltpu.VMEM((width, 4 * part), BF16),
            pltpu.VMEM((targets, width), BF16),
            pltpu.VMEM((targets, part), BF16),
            pltpu.VMEM((targets, 3 * part), BF16),
            pltpu.VMEM((pairs, 8, targets), F32),
            pltpu.VMEM((PAIR, targets), F32),
            pltpu.VMEM((targets, PAIR), F32),
            pltpu.VMEM((targets, PAIR), F32),
            pltpu.VMEM((8, width), F32),
            pltpu.VMEM((8, width // 2), F32),
            pltpu.SemaphoreType.DMA((6,)),
            pltpu.SemaphoreType.DMA((6,)),
        ],
        in_specs=[IN_VMEM] * 14 + [IN_PLACE] * 2,
        out_specs=[IN_VMEM] * 3 + [IN_PLACE] * 4,
        time=22,
    )


def last_kernel(
    g_ref, partial_ref, peer_ref, tokens_ref, h_ref, down_ref, down_in_ref, gains_ref, order_ref,
    grad_ref, out_ref,
):
    order = order_ref[...]
    value = h_ref[...] + (down_ref[...] + down_in_ref[...])
    out_ref[...] = nn(value.astype(BF16), order).astype(BF16)
    back, unused = norm_back(tokens_ref[...], gains_ref[0:1, :], partial_ref[...] + peer_ref[...])
    high, rest = halves(g_ref[...] + back)
    grad_ref[...] = nn(high, order) + nn(rest, order)


def last_call(*ins):
    targets, width = ins[0].shape
    block = pl.BlockSpec((WIDE, width), lambda i: (i, 0))
    return kernel_call(
        last_kernel,
        list(ins),
        [struct((targets, width), F32), struct((targets, width), BF16)],
        [],
        time=1,
        grid=(targets // WIDE,),
        in_specs=[block] * 7 + [IN_VMEM] * 2,
        out_specs=[block] * 2,
    )


def shards(
    decoder_in,
    encoder_out,
    lengths,
    key_mask,
    assign,
    buckets,
    norm_one,
    norm_two,
    norm_three,
    self_query,
    self_key,
    self_value,
    self_output,
    cross_query,
    cross_key,
    cross_value,
    cross_output,
    ffn_gate,
    ffn_up,
    ffn_down,
    bias_table,
    cotangent,
    *,
    size,
):
    rank = lax.axis_index("dp")
    core = lax.axis_index("mp")
    targets, width = decoder_in.shape[1:]
    capacity = key_mask.shape[1]
    block = width // size
    outer = size // 4
    half = width // 2
    heads = bias_table.shape[1]
    which_core = core.reshape(1)

    spots = jnp.arange(width, dtype=jnp.int32)
    spot = spots // block
    masks = spot // (2 * outer) + 2 * (spot // outer % 2) + 4 * (spot % outer)
    source = jnp.broadcast_to(((rank ^ masks) * block + spots % block)[None], (8, width))

    weights = low(
        self_query, self_key, self_value, self_output.T,
        cross_query, cross_output.T, cross_key, cross_value,
    )
    if size == 16:
        pieces = [weights, swap(weights, 4, size), swap(weights, 8, size)]
    else:
        pieces = gather_outer(weights, size)
    gains = jnp.concatenate(
        [norm_one[None], norm_two[None], norm_three[None], jnp.zeros((5, width), F32)]
    )
    tokens, cot, cot_t, gains, order, turned, normed_one = kernel_call(
        rows_kernel,
        [decoder_in[0], cotangent[0], gains, source],
        [
            struct((targets, width), F32),
            struct((targets, width), BF16),
            struct((width, targets), BF16),
            struct((8, width), F32),
            struct((width, width), BF16),
            struct((width, width), BF16),
            struct((targets, width), BF16),
        ],
        [],
    )
    ffn = low(*after((ffn_gate, ffn_up, ffn_down.T), normed_one))

    sent = lax.dynamic_slice_in_dim(encoder_out, core * half, half, 2)[assign]
    pieces, normed_one = after((pieces, normed_one))
    if size == 16:
        more = swap(pieces[2], 4, size)
    weights = send_first(gather_first(pieces, size), size)
    if size == 16:
        more, ffn, sent = after((more, ffn, sent))
        more = gather_first([more], size)
        more, ffn, sent = after((more, ffn, sent))
        more = send_first(more, size)
    own = lax.all_to_all(sent, "dp", split_axis=0, concat_axis=0, tiled=True)
    own = own.reshape(capacity, half)
    labels, bias_table, lengths = after((buckets[:, :TILE], bias_table, lengths), weights[0])
    mine = assign[rank]
    positions = jnp.arange(capacity, dtype=jnp.int32)
    live = (positions < lengths[mine]) & ((key_mask[mine] == 1) | (positions == 0))
    dead = jnp.broadcast_to(jnp.where(live, 0.0, NEGATIVE)[:, None], (capacity, TILE))
    which = labels[None, :, 0] == jnp.arange(bias_table.shape[0], dtype=jnp.int32)[:, None]
    bias = jnp.sum(jnp.where(which[None], bias_table.T[:, :, None], 0.0), axis=1)
    bias = jnp.pad(bias.reshape(heads // 2, 2, targets), ((0, 0), (0, 6), (0, 0)))

    if size == 16:
        weights, more = after((weights, more))
        weights = [value for both in zip(weights, more) for value in both]
    weights, ffn, bias, dead = after((weights, ffn, bias, dead))
    weights = gather_second(weights, size, time=40)
    weights, ffn = after((weights, ffn))
    weights = send_second(weights, size)
    ffn = gather_outer(ffn, size, own)

    weights, own, ffn = after((weights, own, ffn))
    ffn = gather_first(ffn, size)
    ffn, weights, own = after((ffn, weights, own))
    ffn = send_first(ffn, size)
    own_peer = swap_cores(own)
    left, right = weights
    mixed, attended, lse_self, partial_one = self_forward(normed_one, bias, left)
    ffn, mixed, attended, lse_self, partial_one, own, own_peer = after(
        (ffn, mixed, attended, lse_self, partial_one, own, own_peer)
    )
    ffn = send_apart(ffn, size)
    peer_one = swap_cores(partial_one)
    encoded, key_value = encoder_call(which_core, own, own_peer, order, right)
    h_one, normed_two, cross_q, cross_att, lse_cross, *partial_two = cross_forward(
        tokens, partial_one, peer_one, gains, key_value, dead, right
    )
    peer_two = [swap_cores(value) for value in partial_two]
    h_two, partial_down, partial_three, *grads = ffn_call(
        h_one, partial_two, peer_two, gains, cot, cot_t, ffn[0] + ffn[1]
    )

    ffn = scatter_first(grads, size)
    peer_three = swap_cores(partial_three)
    peer_down = swap_cores(partial_down)
    g_two, low_two, dq, dkv, partial_four, gain_three = cross_backward(
        cot, partial_three, peer_three, h_two, gains, cross_q, key_value, dead, lse_cross, right
    )
    ffn, dq, dkv, low_two, partial_four, peer_down = after(
        (ffn, dq, dkv, low_two, partial_four, peer_down)
    )
    ffn = scatter_second_parts(ffn)
    ffn, dq, dkv, low_two, partial_four = after((ffn, dq, dkv, low_two, partial_four))
    ffn = scatter_second_send(ffn, size)
    peer_four = swap_cores(partial_four)
    kept, given, *grads = cross_grads(
        which_core, normed_two, dq, low_two, cross_att, turned, encoded, dkv, right
    )
    ffn, kept, given, grads, peer_four = after((ffn, kept, given, grads, peer_four))
    ffn = scatter_outer_parts(ffn, 0, 1)
    ffn, kept, given, grads, peer_four = after((ffn, kept, given, grads, peer_four))
    cross = scatter_first(grads, size)
    ffn = scatter_outer_send(ffn, size)
    g_one, partial_five, small, *grads = self_backward(
        g_two, partial_four, peer_four, h_one, gains, mixed, bias, lse_self, attended,
        normed_one, tokens, gain_three, turned, labels, left,
    )
    ffn, cross, given, partial_five, small, grads = after(
        (ffn, cross, given, partial_five, small, grads)
    )
    last = scatter_first(grads, size)
    peer_five = swap_cores(partial_five)
    taken = swap_cores(given)
    cross = scatter_second_send(scatter_second_parts(cross), size)

    terms = (kept.astype(F32) + taken.astype(F32)).astype(BF16).reshape(size, -1, half)
    count = terms.shape[1]
    terms = jnp.concatenate(
        [terms, jnp.broadcast_to(small[None], (size, *small.shape))], axis=1
    )
    back = lax.all_to_all(terms, "dp", split_axis=0, concat_axis=0, tiled=True)
    decoder_grad, layer_out = last_call(
        g_one, partial_five, peer_five, tokens, h_two, partial_down, peer_down, gains, turned
    )
    last, layer_out = after((last, layer_out))
    if size == 16:
        last = scatter_second_parts(last, time=40)
        cross = after(cross, last[-1])
        last = scatter_second_send(last, size)
        cross_keep, cross_out = scatter_pair_parts(cross)
        cross_in = swap(cross_out, 4, size)
        last, ffn = after((last, ffn), cross_out)
        last = scatter_outer_parts(last, 0, 1)
        last, back, ffn = after((last, back, ffn))
        last = scatter_outer_send(last, size)
        back, cross_in = after((back, cross_in), last[1])
        cross = scatter_pair_send(cross_keep, cross_in, size)
    else:
        cross = scatter_outer_send(scatter_outer_parts(cross, 0, 1), size)
        last = scatter_second_send(scatter_second_parts(last), size)
        last = scatter_outer_send(scatter_outer_parts(last, 0, 1), size)
    inverse = jnp.zeros_like(assign).at[assign].set(jnp.arange(size, dtype=jnp.int32))
    encoder_grad = back[:, :count][inverse]
    small = jnp.sum(back[:, count:].astype(F32), axis=0)
    small = small[:8] + small[8:]
    both = small + swap_cores(small)
    last, encoder_grad, small, both = after((last, encoder_grad, small, both))
    sum_ffn, sum_cross, sum_self = scatter_last(ffn), scatter_last(cross), scatter_last(last)
    table = small[6:8].reshape(2, heads // 2, TILE)[:, :, : bias_table.shape[0]]
    grad_table = table.transpose(1, 0, 2).reshape(heads, -1).T

    def parts(value, count):
        step = value.shape[1] // count
        return [value[:, i * step : (i + 1) * step] for i in range(count)]

    grad_self_query, grad_self_key, grad_self_value, grad_output_one = parts(sum_self, 4)
    grad_cross_query, grad_output_two, grad_cross_key, grad_cross_value = parts(sum_cross, 4)
    grad_ffn_gate, grad_ffn_up, grad_ffn_down = parts(sum_ffn, 3)
    return (
        layer_out[None],
        decoder_grad[None],
        encoder_grad,
        both[0:4:3].reshape(-1),
        small[1:5:3].reshape(-1),
        small[2:6:3].reshape(-1),
        grad_self_query,
        grad_self_key,
        grad_self_value,
        grad_output_one.T,
        grad_cross_query,
        grad_cross_key,
        grad_cross_value,
        grad_output_two.T,
        grad_ffn_gate,
        grad_ffn_up,
        grad_ffn_down.T,
        grad_table,
    )


def solution(mesh):
    in_specs = (
        P("dp", None, None),
        P(None, "dp", None),
        P(),
        P(),
        P(),
        P(),
        P(),
        P(),
        P(),
        P("dp", "mp"),
        P("dp", "mp"),
        P("dp", "mp"),
        P("mp", "dp"),
        P("dp", "mp"),
        P("dp", "mp"),
        P("dp", "mp"),
        P("mp", "dp"),
        P("dp", "mp"),
        P("dp", "mp"),
        P("mp", "dp"),
        P(None, "mp"),
        P("dp", None, None),
    )
    out_specs = (
        P("dp", None, None),
        P("dp", None, None),
        P(None, "dp", "mp"),
        P(),
        P(),
        P(),
        P("dp", "mp"),
        P("dp", "mp"),
        P("dp", "mp"),
        P("mp", "dp"),
        P("dp", "mp"),
        P("dp", "mp"),
        P("dp", "mp"),
        P("mp", "dp"),
        P("dp", "mp"),
        P("dp", "mp"),
        P("mp", "dp"),
        P(None, "mp"),
    )
    body = functools.partial(shards, size=mesh.shape["dp"])
    return jax.shard_map(body, mesh=mesh, in_specs=in_specs, out_specs=out_specs, check_vma=False)
```

```python
import functools

import jax
import jax.numpy as jnp
from jax import lax
from jax.experimental import pallas as pl
from jax.experimental.pallas import tpu as pltpu
from jax.sharding import PartitionSpec as P

HEAD_DIM = 64
PAIR = 2 * HEAD_DIM
QUERIES = 256
KEYS = 1024
TILE = 128
WIDE = 256
HIDDEN = 512
CHUNKS = 2
ROWS = 64

EPS = 1e-06
NEGATIVE = -1000000000.0
GELU_ROOT = 0.7978845608028654
GELU_CUBE = 0.044715
BF16 = jnp.bfloat16
F32 = jnp.float32


def dot(left, right, dims):
    return lax.dot_general(left, right, (dims, ((), ())), preferred_element_type=F32)


def nn(left, right):
    return dot(left, right, ((1,), (0,)))


def nt(left, right):
    return dot(left, right, ((1,), (1,)))


def tn(left, right):
    return dot(left, right, ((0,), (0,)))


def struct(shape, dtype):
    return jax.ShapeDtypeStruct(shape, dtype)


def halves(value):
    high = value.astype(BF16)
    return high, (value - high.astype(F32)).astype(BF16)


def swap(value, mask, size):
    return lax.ppermute(value, "dp", [(i, i ^ mask) for i in range(size)])


def swap_cores(value):
    return lax.ppermute(value, "mp", [(0, 1), (1, 0)])


def after(values, *others):
    return lax.optimization_barrier((values, others))[0]


def gather_outer(shard, size, late=()):
    if size == 16:
        far, near = swap(shard, 8, size), swap(shard, 4, size)
        return [shard, near, far, swap(after(far, late), 4, size)]
    shard = after(shard, late)
    mask = 4
    while mask < size:
        shard = jnp.concatenate([shard, swap(shard, mask, size)])
        mask *= 2
    return [shard]


def gather_first(pieces, size):
    rows, half = sum(piece.shape[0] for piece in pieces), pieces[0].shape[1] // 2
    return kernel_call(stack_kernel, list(pieces), [struct((rows, half), BF16)] * 2, [])


def gather_second(state, size, time=2):
    rows = sum(value.shape[0] for value in state) // 2
    outs = [struct((rows, state[0].shape[1]), BF16)] * 2
    return kernel_call(join_kernel, list(state), outs, [], time=time)


def send_first(halves, size):
    left, right = halves
    return left, swap(left, 2, size), right, swap(right, 1, size)


def send_second(halves, size):
    left, right = halves
    return [left, swap(left, 1, size)], [right, swap(right, 2, size)]


def send_apart(state, size):
    left, left_in, right, right_in = state
    return (
        [left, left_in, swap(left, 1, size), swap(left_in, 1, size)],
        [right, right_in, swap(right, 2, size), swap(right_in, 2, size)],
    )


def scatter_first(grads, size):
    left, left_out, right, right_out = grads
    return left, right, swap(left_out, 1, size), swap(right_out, 2, size)


def scatter_second_parts(state, time=2):
    left = state[0]
    rows, half = left.shape[0] // 2, left.shape[1]
    outs = kernel_call(
        scatter_second_kernel,
        list(state),
        [struct((rows, half), BF16)] * 2,
        [],
        time=time,
        grid=(1,),
        in_specs=[pl.BlockSpec((rows, half), lambda i: (1, 0))] * 4,
        out_specs=[pl.BlockSpec((rows, half), lambda i: (0, 0))] * 2,
    )
    return (*state, *outs)


def scatter_second_send(parts, size):
    *state, left_out, right_out = parts
    return (*state, swap(left_out, 2, size), swap(right_out, 1, size))


def scatter_outer_parts(state, *sides):
    rows, half = state[-1].shape
    ins = [value for side in sides for value in state[side::2]]
    width = len(sides) * half
    return kernel_call(
        scatter_outer_kernel,
        ins,
        [struct((rows // 4, width), dtype) for dtype in (F32, BF16, BF16, BF16)],
        [],
        grid=(1,),
        in_specs=[pl.BlockSpec((rows, half), lambda i: (0, 0))] * len(ins),
        out_specs=[pl.BlockSpec((rows // 4, width), lambda i: (0, 0))] * 4,
    )


def scatter_pair_parts(state):
    rows, half = state[-1].shape
    outs = [struct((rows // 2, 2 * half), dtype) for dtype in (F32, BF16)]
    return kernel_call(
        scatter_pair_kernel,
        state[0::2] + state[1::2],
        outs,
        [],
        grid=(1,),
        in_specs=[pl.BlockSpec((rows, half), lambda i: (0, 0))] * 6,
        out_specs=[pl.BlockSpec((rows // 2, 2 * half), lambda i: (0, 0))] * 2,
    )


def scatter_pair_send(keep, taken, size):
    count = keep.shape[0] // 2
    rows = keep + taken.astype(F32)
    return [rows[:count], swap(rows[count:].astype(BF16), 8, size)]


def scatter_outer_send(parts, size):
    keep, *outs = parts
    if size == 16:
        return [keep] + [swap(out, 4 * (k + 1), size) for k, out in enumerate(outs)]
    rows = jnp.concatenate([keep] + [out.astype(F32) for out in outs])
    mask = size // 2
    while mask >= 4:
        count = rows.shape[0] // 2
        rows = rows[:count] + swap(rows[count:].astype(BF16), mask, size).astype(F32)
        mask //= 2
    return [rows]


def scatter_last(state):
    total = state[0]
    for value in state[1:]:
        total = total + value.astype(F32)
    return total


def kernel_call(kernel, ins, outs, scratch, time=2, grid=None, in_specs=None, out_specs=None):
    everywhere = pl.BlockSpec(memory_space=pltpu.VMEM)
    return pl.pallas_call(
        kernel,
        out_shape=outs,
        in_specs=in_specs or [everywhere] * len(ins),
        out_specs=out_specs or [everywhere] * len(outs),
        scratch_shapes=scratch,
        compiler_params=pltpu.CompilerParams(vmem_limit_bytes=58 * 1024 * 1024),
        cost_estimate=pl.CostEstimate(
            flops=time * 1000000000, bytes_accessed=1, transcendentals=0
        ),
        **({"grid": grid} if grid else {}),
    )(*ins)


IN_VMEM = pl.BlockSpec(memory_space=pltpu.VMEM)
IN_PLACE = pl.BlockSpec(memory_space=pl.ANY)
IN_SMEM = pl.BlockSpec(memory_space=pltpu.SMEM)


def stack_kernel(*refs):
    *in_refs, left_ref, right_ref = refs
    half = left_ref.shape[1]
    start = 0
    for ref in in_refs:
        rows = slice(start, start + ref.shape[0])
        left_ref[rows, :] = ref[:, :half]
        right_ref[rows, :] = ref[:, half:]
        start += ref.shape[0]


def join_kernel(*refs):
    *in_refs, left_out, right_out = refs
    for out_ref, pieces in (
        (left_out, in_refs[: len(in_refs) // 2]),
        (right_out, in_refs[len(in_refs) // 2 :]),
    ):
        start = 0
        for ref in pieces:
            out_ref[start : start + ref.shape[0], :] = ref[...]
            start += ref.shape[0]


def scatter_second_kernel(left_ref, right_ref, left_in_ref, right_in_ref, left_out, right_out):
    left_out[...] = (left_ref[...].astype(F32) + left_in_ref[...].astype(F32)).astype(BF16)
    right_out[...] = (right_ref[...].astype(F32) + right_in_ref[...].astype(F32)).astype(BF16)


def scatter_outer_kernel(*refs):
    *in_refs, keep_ref, first_ref, second_ref, third_ref = refs
    count = keep_ref.shape[0]
    for side in range(len(in_refs) // 3):
        own_ref, in_ref, more_ref = in_refs[3 * side : 3 * side + 3]
        half = own_ref.shape[1]
        cols = slice(side * half, (side + 1) * half)
        for k, out_ref in enumerate((keep_ref, first_ref, second_ref, third_ref)):
            rows = slice(k * count, (k + 1) * count)
            total = own_ref[rows, :].astype(F32) + in_ref[rows, :].astype(F32)
            out_ref[:, cols] = (total + more_ref[rows, :].astype(F32)).astype(out_ref.dtype)


def scatter_pair_kernel(*refs):
    *in_refs, keep_ref, out_ref = refs
    count = keep_ref.shape[0] // 2
    for side in range(2):
        own_ref, in_ref, more_ref = in_refs[3 * side : 3 * side + 3]
        half = own_ref.shape[1]
        cols = slice(side * half, (side + 1) * half)
        for k in range(4):
            rows = slice(k * count, (k + 1) * count)
            total = own_ref[rows, :].astype(F32) + in_ref[rows, :].astype(F32)
            target = out_ref if k % 2 else keep_ref
            spot = slice(k // 2 * count, (k // 2 + 1) * count)
            target[spot, cols] = (total + more_ref[rows, :].astype(F32)).astype(target.dtype)


def cast_kernel(*refs):
    *in_refs, out_ref = refs
    start = 0
    for ref in in_refs:
        out_ref[:, start : start + ref.shape[1]] = ref[...].astype(BF16)
        start += ref.shape[1]


def low(*values):
    width = sum(value.shape[1] for value in values)
    return kernel_call(
        cast_kernel, list(values), [struct((values[0].shape[0], width), BF16)], []
    )[0]


def each_rows(count, body, rows=ROWS):
    @pl.loop(0, count // rows)
    def step(i):
        body(pl.ds(pl.multiple_of(i * rows, rows), rows))


def each_tile(start, width, body):
    @pl.loop(0, width // WIDE)
    def step(i):
        body(pl.ds(pl.multiple_of(start + i * WIDE, WIDE), WIDE))


def fetch(left, right, weights_ref, sems, first=0):
    start = left[0].shape[1] if left else 0
    columns = weights_ref.shape[1] - start
    quarter = weights_ref.shape[0] // 4
    moves = []
    for i, ref in enumerate(left):
        count = ref.shape[0]
        moves.append((ref, weights_ref.at[i * count : (i + 1) * count, :start]))
    places = [0, 2, 1, 3]
    for ref in right:
        for x in range(ref.shape[0] // quarter):
            place = places.pop(0) * quarter
            moves.append(
                (
                    ref.at[x * quarter : (x + 1) * quarter, first : first + columns],
                    weights_ref.at[place : place + quarter, start:],
                )
            )
    copies = [pltpu.make_async_copy(*move, sems.at[i]) for i, move in enumerate(moves)]
    for copy in copies:
        copy.start()
    return copies


def deliver(grads_ref, out_refs, sems, columns, first=0):
    left, left_out, right, right_out = out_refs
    rows, half = left.shape[0] // 2, left.shape[1]
    side = columns.start // half
    if side == 0:
        moves = [(left, 0, 0, 2), (left_out, 0, 2, 2)]
    else:
        moves = [(right, 0, 0, 1), (right, 1, 2, 1), (right_out, 0, 1, 1), (right_out, 1, 3, 1)]
    copies = []
    for target, spot, place, count in moves:
        copies.append(
            pltpu.make_async_copy(
                grads_ref.at[place * rows : (place + count) * rows, columns],
                target.at[
                    spot * rows : (spot + count) * rows,
                    columns.start - side * half : columns.stop - side * half,
                ],
                sems.at[first + len(copies)],
            )
        )
    return copies


def deliver_all(grads_ref, out_refs, sems):
    half = out_refs[0].shape[1]
    copies = deliver(grads_ref, out_refs, sems, slice(0, half))
    copies += deliver(grads_ref, out_refs, sems, slice(half, 2 * half), 2)
    for copy in copies:
        copy.start()
    for copy in copies:
        copy.wait()


def grad_structs(width, columns):
    return [struct((width // 2, columns // 2), BF16)] * 4


def both_of(own_ref, peer_ref, rows):
    return own_ref[rows, :].astype(F32) + peer_ref[rows, :].astype(F32)


def root_of(value):
    return lax.rsqrt(jnp.mean(value * value, axis=-1, keepdims=True) + EPS)


def norm_back(value, gain, grad):
    root = root_of(value)
    scaled = grad * gain
    inner = jnp.mean(value * scaled, axis=-1, keepdims=True)
    back = root * scaled - value * (root * root * root * inner)
    return back, jnp.sum(grad * value * root, axis=0, keepdims=True)


def rows_kernel(
    tokens_ref, cot_ref, gains_ref, source_ref,
    tokens_out, cot_out, cot_t_out, gains_out, order_ref, turned_ref, normed_ref,
):
    width = tokens_ref.shape[1]
    spot = lax.broadcasted_iota(jnp.int32, (width, width), 0)
    order_ref[...] = jnp.where(spot == source_ref[0:1, :], 1.0, 0.0).astype(BF16)
    order = order_ref[...]
    turned_ref[...] = order.T
    high = gains_ref[...].astype(BF16)
    middle, rest = halves(gains_ref[...] - high.astype(F32))
    gains_out[...] = nn(high, order) + (nn(middle, order) + nn(rest, order))
    tokens_out[...] = nn(tokens_ref[...], order)
    cot_out[...] = nn(cot_ref[...], order).astype(BF16)
    cot_t_out[...] = cot_out[...].T
    gain = gains_out[0:1, :]

    def norm(rows):
        value = tokens_out[rows, :]
        normed_ref[rows, :] = (value * root_of(value) * gain).astype(BF16)

    each_rows(tokens_ref.shape[0], norm)


def queries_of(capacity):
    return QUERIES if capacity <= 2 * KEYS else TILE


def each_chunk(count, size, body):
    if count == 1:
        body(0)
    else:
        pl.loop(0, count)(lambda step: body(pl.multiple_of(step * size, size)))


def each_pair(pairs, body):
    @pl.loop(0, pairs)
    def step(pair):
        body(pair, lambda which: pl.ds(pl.multiple_of((which * pairs + pair) * PAIR, PAIR), PAIR))


def row_of(value, head):
    line = lax.broadcasted_iota(jnp.int32, value.shape, 0)
    return jnp.sum(jnp.where(line == head, value, 0.0), axis=0, keepdims=True)


def of_head(value, head):
    lane = lax.broadcasted_iota(jnp.int32, value.shape, 1)
    return jnp.where(lane // HEAD_DIM == head, value, jnp.zeros_like(value))


def cross_forward_pair(q_ref, k_ref, v_ref, dead_ref, out_ref, lse_ref, s_ref, acc_ref):
    targets, capacity = q_ref.shape[0], k_ref.shape[0]
    size = min(capacity, KEYS)
    count = capacity // size
    queries = s_ref.shape[1]
    for head in range(2):
        rows = slice(head * HEAD_DIM, (head + 1) * HEAD_DIM)
        line = slice(head, head + 1)
        for start in range(0, targets, queries):
            cols = slice(start, start + queries)
            query = of_head(q_ref[cols, :], head)
            lse_ref[line, cols] = jnp.full((1, queries), NEGATIVE * 2, F32)

            def scores(base):
                keys = pl.ds(base, size)
                score = nt(k_ref[keys, :], query) + dead_ref[keys, 0:1]
                s_ref[keys, :] = score
                lse_ref[line, cols] = jnp.maximum(
                    lse_ref[line, cols], jnp.max(score, axis=0, keepdims=True)
                )

            each_chunk(count, size, scores)
            top = lse_ref[line, cols]
            lse_ref[line, cols] = jnp.zeros((1, queries), F32)

            def weights(base):
                keys = pl.ds(base, size)
                weight = jnp.exp(s_ref[keys, :] - top)
                s_ref[keys, :] = weight
                lse_ref[line, cols] += jnp.sum(weight, axis=0, keepdims=True)

            each_chunk(count, size, weights)
            total = lse_ref[line, cols]
            lse_ref[line, cols] = top + jnp.log(total)
            scale = 1.0 / total
            acc_ref[rows, cols] = jnp.zeros((HEAD_DIM, queries), F32)

            def mix(base):
                keys = pl.ds(base, size)
                probs = (s_ref[keys, :] * scale).astype(BF16)
                acc_ref[rows, cols] += tn(v_ref[keys, :], probs)[rows]

            each_chunk(count, size, mix)
    out_ref[...] = acc_ref[...].T.astype(BF16)


def cross_backward_pair(
    q_ref, k_ref, v_ref, dead_ref, lse_ref, go_ref, dq_ref, dk_ref, dv_ref,
    p_ref, dp_ref, dqt_ref, dk_acc, dv_acc, delta_ref,
):
    targets, capacity = q_ref.shape[0], k_ref.shape[0]
    size = min(capacity, KEYS)
    count = capacity // size
    queries = p_ref.shape[1]
    dk_acc[...] = jnp.zeros_like(dk_acc)
    dv_acc[...] = jnp.zeros_like(dv_acc)
    dqt_ref[...] = jnp.zeros_like(dqt_ref)

    @pl.loop(0, 2)
    def each_head(head):
        for start in range(0, targets, queries):
            cols = slice(start, start + queries)
            query = of_head(q_ref[cols, :], head)
            grad = of_head(go_ref[cols, :], head)
            lse = row_of(lse_ref[:, cols], head)
            delta_ref[...] = jnp.zeros_like(delta_ref)

            def first(base):
                keys = pl.ds(base, size)
                probs = jnp.exp(nt(k_ref[keys, :], query) + dead_ref[keys, 0:1] - lse)
                grad_probs = nt(v_ref[keys, :], grad)
                p_ref[keys, :] = probs
                dp_ref[keys, :] = grad_probs
                delta_ref[...] += jnp.sum(probs * grad_probs, axis=0, keepdims=True)

            each_chunk(count, size, first)
            delta = delta_ref[...]

            def second(base):
                keys = pl.ds(base, size)
                probs = p_ref[keys, :]
                dv_acc[keys, :] += nn(probs.astype(BF16), grad)
                low = (probs * (dp_ref[keys, :] - delta)).astype(BF16)
                dk_acc[keys, :] += nn(low, query)
                dqt_ref[:, cols] += tn(of_head(k_ref[keys, :], head), low)

            each_chunk(count, size, second)
    dq_ref[...] = dqt_ref[...].T.astype(BF16)
    dk_ref[...] = dk_acc[...].astype(BF16)
    dv_ref[...] = dv_acc[...].astype(BF16)


def skewed(row, block):
    before = row[:, (block - 1) * TILE : block * TILE] if block else jnp.zeros((1, TILE), F32)
    both = jnp.concatenate([before, row[:, block * TILE : (block + 1) * TILE]], axis=1)
    both = jnp.broadcast_to(both, (TILE, 2 * TILE))
    return pltpu.roll(both, 0, 1, stride=1, stride_axis=0)[:, TILE:]


def unskewed(tile):
    both = jnp.concatenate([jnp.zeros_like(tile), tile], axis=1)
    total = both[:8]
    for base in range(8, TILE, 8):
        total = total + pltpu.roll(both[base : base + 8], 2 * TILE - base, 1)
    row = lax.broadcasted_iota(jnp.int32, total.shape, 0)
    for bit in (1, 2, 4):
        total = jnp.where(row & bit != 0, pltpu.roll(total, 2 * TILE - bit, 1), total)
    return jnp.sum(total, axis=0, keepdims=True)


def self_scores(k_ref, query, tiles, start):
    keys = start + QUERIES
    columns = []
    for i in range(start // TILE, keys // TILE):
        columns.append(
            jnp.concatenate([tiles[max(i - j, 0)] for j in range(keys // TILE)], axis=0)
        )
    score = nt(k_ref[:keys, :], query) + jnp.concatenate(columns, axis=1)
    key = lax.broadcasted_iota(jnp.int32, score.shape, 0)
    spot = lax.broadcasted_iota(jnp.int32, score.shape, 1) + start
    return jnp.where(key <= spot, score, NEGATIVE)


def self_forward_pair(q_ref, k_ref, v_ref, bias_ref, out_ref, lse_ref, acc_ref):
    targets = q_ref.shape[0]
    for head in range(2):
        rows = slice(head * HEAD_DIM, (head + 1) * HEAD_DIM)
        row = bias_ref[head : head + 1, :]
        tiles = [skewed(row, block) for block in range(targets // TILE)]
        for start in range(0, targets, QUERIES):
            cols = slice(start, start + QUERIES)
            query = of_head(q_ref[cols, :], head)
            score = self_scores(k_ref, query, tiles, start)
            top = jnp.max(score, axis=0, keepdims=True)
            weight = jnp.exp(score - top)
            total = jnp.sum(weight, axis=0, keepdims=True)
            lse_ref[head : head + 1, cols] = top + jnp.log(total)
            probs = (weight * (1.0 / total)).astype(BF16)
            acc_ref[rows, cols] = tn(v_ref[: start + QUERIES, :], probs)[rows]
    out_ref[...] = acc_ref[...].T.astype(BF16)


def self_backward_pair(
    q_ref, k_ref, v_ref, bias_ref, lse_ref, go_ref, dq_ref, dk_ref, dv_ref, dbias_ref,
    dqt_ref, dk_acc, dv_acc,
):
    targets = q_ref.shape[0]
    dk_acc[...] = jnp.zeros_like(dk_acc)
    dv_acc[...] = jnp.zeros_like(dv_acc)
    blocks = targets // TILE
    dqt_ref[...] = jnp.zeros_like(dqt_ref)

    @pl.loop(0, 2)
    def each_head(head):
        row = row_of(bias_ref[...], head)
        tiles = [skewed(row, block) for block in range(blocks)]
        sums = [jnp.zeros((TILE, TILE), F32) for block in range(blocks)]
        for start in range(0, targets, QUERIES):
            cols = slice(start, start + QUERIES)
            keys = start + QUERIES
            query = of_head(q_ref[cols, :], head)
            grad = of_head(go_ref[cols, :], head)
            score = self_scores(k_ref, query, tiles, start)
            probs = jnp.exp(score - row_of(lse_ref[:, cols], head))
            grad_probs = nt(v_ref[:keys, :], grad)
            delta = jnp.sum(probs * grad_probs, axis=0, keepdims=True)
            dv_acc[:keys, :] += nn(probs.astype(BF16), grad)
            grad_scores = probs * (grad_probs - delta)
            for i in range(start // TILE, keys // TILE):
                for j in range(i + 1):
                    sums[i - j] = sums[i - j] + grad_scores[
                        j * TILE : (j + 1) * TILE, i * TILE - start : (i + 1) * TILE - start
                    ]
            low_scores = grad_scores.astype(BF16)
            dk_acc[:keys, :] += nn(low_scores, query)
            dqt_ref[:, cols] += tn(of_head(k_ref[:keys, :], head), low_scores)
        lines = [unskewed(tile) for tile in sums]
        parts = []
        for block in range(blocks):
            part = lines[block][:, TILE:]
            if block + 1 < blocks:
                part = part + lines[block + 1][:, :TILE]
            parts.append(part)
        row = jnp.concatenate(parts, axis=1)
        line = lax.broadcasted_iota(jnp.int32, dbias_ref.shape, 0)
        dbias_ref[...] = jnp.where(line == head, row, dbias_ref[...])
    dq_ref[...] = dqt_ref[...].T.astype(BF16)
    dk_ref[...] = dk_acc[...].astype(BF16)
    dv_ref[...] = dv_acc[...].astype(BF16)


def self_forward_kernel(
    normed_ref, bias_ref, *refs
):
    mixed_ref, attended_ref, lse_ref, partial_ref, weights_ref, acc_ref, sems = refs[2:]
    copies = fetch(refs[:2], [], weights_ref, sems)
    for copy in copies:
        copy.wait()
    part = attended_ref.shape[1]
    pairs = part // PAIR
    normed = normed_ref[...]

    @pl.loop(0, 3 * part // TILE)
    def project(i):
        cols = pl.ds(pl.multiple_of(i * TILE, TILE), TILE)
        mixed_ref[:, cols] = nn(normed, weights_ref[:, cols]).astype(BF16)

    def attend(pair, cols):
        self_forward_pair(
            *(mixed_ref.at[:, cols(i)] for i in range(3)),
            bias_ref.at[pair], attended_ref.at[:, cols(0)], lse_ref.at[pair], acc_ref,
        )

    each_pair(pairs, attend)
    partial_ref[...] = nt(attended_ref[...], weights_ref[:, 3 * part :]).astype(BF16)


def self_forward(normed, bias, quarters):
    targets, width = normed.shape
    columns = quarters[0].shape[1]
    part = columns // 4
    pairs = part // PAIR
    return kernel_call(
        self_forward_kernel,
        [normed, bias, *quarters],
        [
            struct((targets, 3 * part), BF16),
            struct((targets, part), BF16),
            struct((pairs, 8, targets), F32),
            struct((targets, width), BF16),
        ],
        [
            pltpu.VMEM((width, columns), BF16),
            pltpu.VMEM((PAIR, targets), F32),
            pltpu.SemaphoreType.DMA((6,)),
        ],
        in_specs=[IN_VMEM] * 2 + [IN_PLACE] * 2,
        time=12,
    )


def encoder_kernel(core_ref, own_ref, peer_ref, order_ref, *refs):
    encoded_ref, out_ref, weights_ref, sems = refs[2:]

    @pl.when(pl.program_id(0) == 0)
    def load():
        for copy in fetch([], refs[:2], weights_ref, sems, weights_ref.shape[1]):
            copy.wait()

    core, half = core_ref[0], own_ref.shape[1]
    own_rows = pl.ds(pl.multiple_of(core * half, half), half)
    peer_rows = pl.ds(pl.multiple_of(half - core * half, half), half)
    encoded = nn(own_ref[...], order_ref[own_rows, :]) + nn(peer_ref[...], order_ref[peer_rows, :])
    encoded_ref[...] = encoded.astype(BF16)
    encoded = encoded_ref[...]

    def project(cols):
        out_ref[:, cols] = nn(encoded, weights_ref[:, cols]).astype(BF16)

    each_tile(0, out_ref.shape[1], project)


def encoder_call(core, own, peer, order, quarters):
    capacity, half = own.shape
    width = 2 * half
    columns = quarters[0].shape[1] // 2
    size = min(capacity, KEYS)
    block = lambda cols: pl.BlockSpec((size, cols), lambda i: (i, 0))
    return kernel_call(
        encoder_kernel,
        [core, own, peer, order, *quarters],
        [struct((capacity, width), BF16), struct((capacity, columns), BF16)],
        [pltpu.VMEM((width, columns), BF16), pltpu.SemaphoreType.DMA((4,))],
        grid=(capacity // size,),
        in_specs=[IN_SMEM, block(half), block(half), IN_VMEM] + [IN_PLACE] * 2,
        out_specs=[block(width), block(columns)],
        time=8,
    )


def cross_forward_kernel(tokens_ref, partial_ref, peer_ref, gains_ref, kv_ref, dead_ref, *refs):
    (
        h_ref, normed_ref, query_ref, att_ref, lse_ref, *out_refs,
        weights_ref, s_ref, acc_ref, sems,
    ) = refs[2:]
    copies = fetch([], refs[:2], weights_ref, sems)
    gain = gains_ref[1:2, :]

    def norm(rows):
        value = tokens_ref[rows, :] + both_of(partial_ref, peer_ref, rows)
        h_ref[rows, :] = value
        normed_ref[rows, :] = (value * root_of(value) * gain).astype(BF16)

    each_rows(h_ref.shape[0], norm)
    for copy in copies:
        copy.wait()
    part = query_ref.shape[1]
    pairs = part // PAIR
    query_ref[...] = nn(normed_ref[...], weights_ref[:, :part]).astype(BF16)

    def attend(pair, cols):
        cross_forward_pair(
            query_ref.at[:, cols(0)], kv_ref.at[:, cols(0)], kv_ref.at[:, cols(1)], dead_ref,
            att_ref.at[:, cols(0)], lse_ref.at[pair], s_ref, acc_ref,
        )

    each_pair(pairs, attend)
    count = out_refs[0].shape[0]
    for i, out_ref in enumerate(out_refs):
        att = att_ref[i * count : (i + 1) * count, :]
        out_ref[...] = nt(att, weights_ref[:, part:]).astype(BF16)


def cross_forward(tokens, partial, peer, gains, key_value, dead, quarters):
    targets, width = tokens.shape
    capacity, columns = key_value.shape
    part = columns // 2
    pairs = part // PAIR
    return kernel_call(
        cross_forward_kernel,
        [tokens, partial, peer, gains, key_value, dead, *quarters],
        [
            struct((targets, width), F32),
            struct((targets, width), BF16),
            struct((targets, part), BF16),
            struct((targets, part), BF16),
            struct((pairs, 8, targets), F32),
            *[struct((targets // CHUNKS, width), BF16)] * CHUNKS,
        ],
        [
            pltpu.VMEM((width, columns), BF16),
            pltpu.VMEM((capacity, queries_of(capacity)), F32),
            pltpu.VMEM((PAIR, targets), F32),
            pltpu.SemaphoreType.DMA((4,)),
        ],
        in_specs=[IN_VMEM] * 6 + [IN_PLACE] * 2,
        time=16,
    )


def ffn_kernel(before_ref, gains_ref, cot_ref, cot_t_ref, *refs):
    chunks, refs = refs[: 2 * CHUNKS], refs[2 * CHUNKS :]
    h_out, down_ref, back_ref, *outs = refs[8:15]
    weights_ref, grads_ref, h_ref, normed_ref, normed_t, in_sems, out_sems = refs[15:]
    copies = fetch(refs[:4], refs[4:8], weights_ref, in_sems)
    gain = gains_ref[2:3, :]
    count = chunks[0].shape[0]
    for i, (partial_ref, peer_ref) in enumerate(zip(chunks[:CHUNKS], chunks[CHUNKS:])):

        def norm(rows):
            own = pl.ds(pl.multiple_of(rows.start + i * count, rows.size), rows.size)
            value = before_ref[own, :] + both_of(partial_ref, peer_ref, rows)
            h_ref[own, :] = value
            normed_ref[own, :] = (value * root_of(value) * gain).astype(BF16)

        each_rows(count, norm, 32)
    h_copy = pltpu.make_async_copy(h_ref, h_out, out_sems.at[36])
    h_copy.start()
    normed_t[...] = normed_ref[...].T
    down_ref[...] = jnp.zeros_like(down_ref)
    back_ref[...] = jnp.zeros_like(back_ref)
    for copy in copies:
        copy.wait()
    hidden = weights_ref.shape[1] // 3
    tiles = hidden // HIDDEN

    def sends(i):
        copies = []
        for k in range(3):
            columns = slice(k * hidden + i * HIDDEN, k * hidden + (i + 1) * HIDDEN)
            first = 6 * (i * 3 + k)
            copies += deliver(grads_ref, outs, out_sems, columns, first)
        return copies

    @pl.loop(0, tiles)
    def tile(i):
        gates, ups, downs = (
            pl.ds(pl.multiple_of(k * hidden + i * HIDDEN, HIDDEN), HIDDEN) for k in range(3)
        )
        normed = normed_ref[...]
        gate = nn(normed, weights_ref[:, gates])
        up = nn(normed, weights_ref[:, ups])
        grad_act = nn(cot_ref[...], weights_ref[:, downs]).astype(BF16).astype(F32)
        square = gate * gate
        curve = jnp.tanh(GELU_ROOT * (gate + GELU_CUBE * (square * gate)))
        share = 0.5 * (1.0 + curve)
        gelu = gate * share
        slope = share + (0.5 * gate) * (1.0 - curve * curve) * (
            GELU_ROOT * (1.0 + (3.0 * GELU_CUBE) * square)
        )
        act = (gelu * up).astype(BF16)
        grad_gate = (grad_act * up * slope).astype(BF16)
        grad_up = (grad_act * gelu).astype(BF16)
        grads_ref[:, gates] = nn(normed_t[...], grad_gate).astype(BF16)
        grads_ref[:, ups] = nn(normed_t[...], grad_up).astype(BF16)
        grads_ref[:, downs] = nn(cot_t_ref[...], act).astype(BF16)
        for each in range(tiles):

            @pl.when(i == each)
            def send():
                for copy in sends(each):
                    copy.start()

        back_ref[...] += nt(grad_gate, weights_ref[:, gates]) + nt(grad_up, weights_ref[:, ups])
        down_ref[...] += nt(act, weights_ref[:, downs])

    for i in range(tiles):
        for copy in sends(i):
            copy.wait()
    h_copy.wait()


def ffn_call(before, partials, peers, gains, cot, cot_t, quarters):
    targets, width = before.shape
    columns = 2 * quarters[0].shape[1]
    return kernel_call(
        ffn_kernel,
        [before, gains, cot, cot_t, *partials, *peers, *quarters],
        [struct((targets, width), F32)] * 3 + grad_structs(width, columns),
        [
            pltpu.VMEM((width, columns), BF16),
            pltpu.VMEM((width, columns), BF16),
            pltpu.VMEM((targets, width), F32),
            pltpu.VMEM((targets, width), BF16),
            pltpu.VMEM((width, targets), BF16),
            pltpu.SemaphoreType.DMA((8,)),
            pltpu.SemaphoreType.DMA((37,)),
        ],
        time=20,
        in_specs=[IN_VMEM] * (4 + 2 * CHUNKS) + [IN_PLACE] * 8,
        out_specs=[IN_PLACE] + [IN_VMEM] * 2 + [IN_PLACE] * 4,
    )


def cross_backward_kernel(
    cot_ref, partial_ref, peer_ref, h_ref, gains_ref, query_ref, kv_ref, dead_ref, lse_ref, *refs
):
    (
        g_ref, low_ref, dq_ref, dkv_ref, back_ref, gain_grad_ref,
        weights_ref, go_ref, p_ref, dp_ref, dqt_ref, dk_acc, dv_acc, delta_ref, sems,
    ) = refs[2:]
    copies = fetch([], refs[:2], weights_ref, sems)
    gain = gains_ref[2:3, :]
    gain_grad_ref[...] = jnp.zeros_like(gain_grad_ref)

    def norm(rows):
        back, gain_grad = norm_back(h_ref[rows, :], gain, partial_ref[rows, :] + peer_ref[rows, :])
        gain_grad_ref[0:1, :] += gain_grad
        value = cot_ref[rows, :].astype(F32) + back
        g_ref[rows, :] = value
        low_ref[rows, :] = value.astype(BF16)

    each_rows(h_ref.shape[0], norm)
    for copy in copies:
        copy.wait()
    part = query_ref.shape[1]
    pairs = part // PAIR
    go_ref[...] = nn(low_ref[...], weights_ref[:, part:]).astype(BF16)

    def attend(pair, cols):
        cross_backward_pair(
            query_ref.at[:, cols(0)], kv_ref.at[:, cols(0)], kv_ref.at[:, cols(1)], dead_ref,
            lse_ref.at[pair], go_ref.at[:, cols(0)],
            dq_ref.at[:, cols(0)], dkv_ref.at[:, cols(0)], dkv_ref.at[:, cols(1)],
            p_ref, dp_ref, dqt_ref, dk_acc, dv_acc, delta_ref,
        )

    each_pair(pairs, attend)
    back_ref[...] = nt(dq_ref[...], weights_ref[:, :part])


def cross_backward(cot, partial, peer, before, gains, query, key_value, dead, lse, quarters):
    targets, width = cot.shape
    capacity, columns = key_value.shape
    return kernel_call(
        cross_backward_kernel,
        [cot, partial, peer, before, gains, query, key_value, dead, lse, *quarters],
        [
            struct((targets, width), F32),
            struct((targets, width), BF16),
            struct(query.shape, BF16),
            struct(key_value.shape, BF16),
            struct((targets, width), F32),
            struct((8, width), F32),
        ],
        [
            pltpu.VMEM((width, columns), BF16),
            pltpu.VMEM(query.shape, BF16),
            pltpu.VMEM((capacity, queries_of(capacity)), F32),
            pltpu.VMEM((capacity, queries_of(capacity)), F32),
            pltpu.VMEM((PAIR, targets), F32),
            pltpu.VMEM((capacity, PAIR), F32),
            pltpu.VMEM((capacity, PAIR), F32),
            pltpu.VMEM((1, queries_of(capacity)), F32),
            pltpu.SemaphoreType.DMA((4,)),
        ],
        in_specs=[IN_VMEM] * 9 + [IN_PLACE] * 2,
        time=18,
    )


def cross_grads_kernel(
    core_ref, normed_ref, dq_ref, low_ref, att_ref, order_ref, encoded_ref, dkv_ref, *refs
):
    kept_ref, given_ref, *outs = refs[2:8]
    weights_ref, acc_ref, grads_ref, in_sems, out_sems = refs[8:]
    step = pl.program_id(0)
    part = dq_ref.shape[1]

    @pl.when(step == 0)
    def load():
        copies = fetch([], refs[:2], weights_ref, in_sems, weights_ref.shape[1])
        grads_ref[:, :part] = tn(normed_ref[...], dq_ref[...]).astype(BF16)
        grads_ref[:, part : 2 * part] = tn(low_ref[...], att_ref[...]).astype(BF16)
        acc_ref[...] = jnp.zeros_like(acc_ref)
        for copy in copies:
            copy.wait()

    encoded_t = encoded_ref[...].T

    def project(cols):
        acc_ref[:, cols] += nn(encoded_t, dkv_ref[:, cols])

    each_tile(0, acc_ref.shape[1], project)
    core, half = core_ref[0], kept_ref.shape[1]
    terms = nt(dkv_ref[...], weights_ref[...]).astype(BF16)
    own_cols = pl.ds(pl.multiple_of(core * half, half), half)
    peer_cols = pl.ds(pl.multiple_of(half - core * half, half), half)
    kept_ref[...] = nn(terms, order_ref[:, own_cols]).astype(BF16)
    given_ref[...] = nn(terms, order_ref[:, peer_cols]).astype(BF16)

    @pl.when(step == pl.num_programs(0) - 1)
    def store():
        grads_ref[:, 2 * part :] = acc_ref[...].astype(BF16)
        deliver_all(grads_ref, outs, out_sems)


def cross_grads(core, normed, dq, low_two, attended, order, encoded, dkv, quarters):
    capacity, width = encoded.shape
    columns = dkv.shape[1]
    size = min(capacity, KEYS)
    block = lambda cols: pl.BlockSpec((size, cols), lambda i: (i, 0))
    return kernel_call(
        cross_grads_kernel,
        [core, normed, dq, low_two, attended, order, encoded, dkv, *quarters],
        [struct((capacity, width // 2), BF16)] * 2 + grad_structs(width, 2 * columns),
        [
            pltpu.VMEM((width, columns), BF16),
            pltpu.VMEM((width, columns), F32),
            pltpu.VMEM((width, 2 * columns), BF16),
            pltpu.SemaphoreType.DMA((4,)),
            pltpu.SemaphoreType.DMA((6,)),
        ],
        grid=(capacity // size,),
        in_specs=[IN_SMEM] + [IN_VMEM] * 5 + [block(width), block(columns)] + [IN_PLACE] * 2,
        out_specs=[block(width // 2)] * 2 + [IN_PLACE] * 4,
        time=12,
    )


def self_backward_kernel(
    g_in_ref, partial_ref, peer_ref, h_ref, gains_ref, mixed_ref, bias_ref, lse_ref,
    attended_ref, normed_ref, tokens_ref, gain_three_ref, order_ref, labels_ref, *refs
):
    g_ref, back_ref, small_ref, *outs = refs[2:9]
    (
        weights_ref, grads_ref, low_ref, go_ref, dmixed_ref, dbias_ref,
        dqt_ref, dk_acc, dv_acc, gain_ref, pack_ref, in_sems, out_sems,
    ) = refs[9:]
    copies = fetch(refs[:2], [], weights_ref, in_sems)
    gain = gains_ref[1:2, :]
    gain_ref[...] = jnp.zeros_like(gain_ref)

    def norm(rows):
        back, gain_grad = norm_back(h_ref[rows, :], gain, partial_ref[rows, :] + peer_ref[rows, :])
        gain_ref[1:2, :] += gain_grad
        value = g_in_ref[rows, :] + back
        g_ref[rows, :] = value
        low_ref[rows, :] = value.astype(BF16)

    each_rows(h_ref.shape[0], norm)
    for copy in copies:
        copy.wait()
    part = attended_ref.shape[1]
    pairs = part // PAIR
    go_ref[...] = nn(low_ref[...], weights_ref[:, 3 * part :]).astype(BF16)
    dbias_ref[...] = jnp.zeros_like(dbias_ref)

    def attend(pair, cols):
        self_backward_pair(
            *(mixed_ref.at[:, cols(i)] for i in range(3)),
            bias_ref.at[pair], lse_ref.at[pair], go_ref.at[:, cols(0)],
            *(dmixed_ref.at[:, cols(i)] for i in range(3)),
            dbias_ref.at[pair], dqt_ref, dk_acc, dv_acc,
        )

    each_pair(pairs, attend)
    back_ref[...] = nt(dmixed_ref[...], weights_ref[:, : 3 * part])
    normed_t = normed_ref[...].T

    @pl.loop(0, 3 * part // TILE)
    def project(i):
        cols = pl.ds(pl.multiple_of(i * TILE, TILE), TILE)
        grads_ref[:, cols] = nn(normed_t, dmixed_ref[:, cols]).astype(BF16)

    grads_ref[:, 3 * part :] = tn(low_ref[...], attended_ref[...]).astype(BF16)

    def sums(rows):
        value = tokens_ref[rows, :]
        gain_ref[0:1, :] += jnp.sum(back_ref[rows, :] * value * root_of(value), axis=0, keepdims=True)

    each_rows(h_ref.shape[0], sums)
    gain_ref[2:3, :] = gain_three_ref[0:1, :]
    high, rest = halves(gain_ref[...])
    gain_ref[...] = nn(high, order_ref[...]) + nn(rest, order_ref[...])
    half = pack_ref.shape[1]
    pack_ref[0:3, :] = gain_ref[0:3, :half]
    pack_ref[3:6, :] = gain_ref[0:3, half:]
    bucket = lax.broadcasted_iota(jnp.int32, (labels_ref.shape[0], TILE), 1)
    which = jnp.where(labels_ref[:, 0:1] == bucket, 1.0, 0.0).astype(BF16)
    for pair in range(pairs):
        high, rest = halves(dbias_ref[pair])
        table = nn(high, which) + nn(rest, which)
        pack_ref[6:8, pair * TILE : (pair + 1) * TILE] = table[0:2]
    small_ref[...] = jnp.concatenate(halves(pack_ref[...]), axis=0)
    deliver_all(grads_ref, outs, out_sems)


def self_backward(
    g_in, partial, peer, before, gains, mixed, bias, lse, attended, normed, tokens,
    gain_three, order, labels, quarters,
):
    targets, width = g_in.shape
    part = attended.shape[1]
    pairs = part // PAIR
    return kernel_call(
        self_backward_kernel,
        [
            g_in, partial, peer, before, gains, mixed, bias, lse, attended, normed, tokens,
            gain_three, order, labels, *quarters,
        ],
        [
            struct((targets, width), F32),
            struct((targets, width), F32),
            struct((16, width // 2), BF16),
        ]
        + grad_structs(width, 4 * part),
        [
            pltpu.VMEM((width, 4 * part), BF16),
            pltpu.VMEM((width, 4 * part), BF16),
            pltpu.VMEM((targets, width), BF16),
            pltpu.VMEM((targets, part), BF16),
            pltpu.VMEM((targets, 3 * part), BF16),
            pltpu.VMEM((pairs, 8, targets), F32),
            pltpu.VMEM((PAIR, targets), F32),
            pltpu.VMEM((targets, PAIR), F32),
            pltpu.VMEM((targets, PAIR), F32),
            pltpu.VMEM((8, width), F32),
            pltpu.VMEM((8, width // 2), F32),
            pltpu.SemaphoreType.DMA((6,)),
            pltpu.SemaphoreType.DMA((6,)),
        ],
        in_specs=[IN_VMEM] * 14 + [IN_PLACE] * 2,
        out_specs=[IN_VMEM] * 3 + [IN_PLACE] * 4,
        time=22,
    )


def last_kernel(
    g_ref, partial_ref, peer_ref, tokens_ref, h_ref, down_ref, down_in_ref, gains_ref, order_ref,
    grad_ref, out_ref,
):
    order = order_ref[...]
    value = h_ref[...] + (down_ref[...] + down_in_ref[...])
    out_ref[...] = nn(value.astype(BF16), order).astype(BF16)
    back, unused = norm_back(tokens_ref[...], gains_ref[0:1, :], partial_ref[...] + peer_ref[...])
    high, rest = halves(g_ref[...] + back)
    grad_ref[...] = nn(high, order) + nn(rest, order)


def last_call(*ins):
    targets, width = ins[0].shape
    block = pl.BlockSpec((WIDE, width), lambda i: (i, 0))
    return kernel_call(
        last_kernel,
        list(ins),
        [struct((targets, width), F32), struct((targets, width), BF16)],
        [],
        time=1,
        grid=(targets // WIDE,),
        in_specs=[block] * 7 + [IN_VMEM] * 2,
        out_specs=[block] * 2,
    )


def shards(
    decoder_in,
    encoder_out,
    lengths,
    key_mask,
    assign,
    buckets,
    norm_one,
    norm_two,
    norm_three,
    self_query,
    self_key,
    self_value,
    self_output,
    cross_query,
    cross_key,
    cross_value,
    cross_output,
    ffn_gate,
    ffn_up,
    ffn_down,
    bias_table,
    cotangent,
    *,
    size,
):
    rank = lax.axis_index("dp")
    core = lax.axis_index("mp")
    targets, width = decoder_in.shape[1:]
    capacity = key_mask.shape[1]
    block = width // size
    outer = size // 4
    half = width // 2
    heads = bias_table.shape[1]
    which_core = core.reshape(1)

    spots = jnp.arange(width, dtype=jnp.int32)
    spot = spots // block
    masks = spot // (2 * outer) + 2 * (spot // outer % 2) + 4 * (spot % outer)
    source = jnp.broadcast_to(((rank ^ masks) * block + spots % block)[None], (8, width))

    weights = low(
        self_query, self_key, self_value, self_output.T,
        cross_query, cross_output.T, cross_key, cross_value,
    )
    if size == 16:
        pieces = [weights, swap(weights, 4, size), swap(weights, 8, size)]
    else:
        pieces = gather_outer(weights, size)
    gains = jnp.concatenate(
        [norm_one[None], norm_two[None], norm_three[None], jnp.zeros((5, width), F32)]
    )
    tokens, cot, cot_t, gains, order, turned, normed_one = kernel_call(
        rows_kernel,
        [decoder_in[0], cotangent[0], gains, source],
        [
            struct((targets, width), F32),
            struct((targets, width), BF16),
            struct((width, targets), BF16),
            struct((8, width), F32),
            struct((width, width), BF16),
            struct((width, width), BF16),
            struct((targets, width), BF16),
        ],
        [],
    )
    ffn = low(*after((ffn_gate, ffn_up, ffn_down.T), normed_one))

    sent = lax.dynamic_slice_in_dim(encoder_out, core * half, half, 2)[assign]
    pieces, normed_one = after((pieces, normed_one))
    if size == 16:
        more = swap(pieces[2], 4, size)
    weights = send_first(gather_first(pieces, size), size)
    if size == 16:
        more, ffn, sent = after((more, ffn, sent))
        more = gather_first([more], size)
        more, ffn, sent = after((more, ffn, sent))
        more = send_first(more, size)
    own = lax.all_to_all(sent, "dp", split_axis=0, concat_axis=0, tiled=True)
    own = own.reshape(capacity, half)
    labels, bias_table, lengths = after((buckets[:, :TILE], bias_table, lengths), weights[0])
    mine = assign[rank]
    positions = jnp.arange(capacity, dtype=jnp.int32)
    live = (positions < lengths[mine]) & ((key_mask[mine] == 1) | (positions == 0))
    dead = jnp.broadcast_to(jnp.where(live, 0.0, NEGATIVE)[:, None], (capacity, TILE))
    which = labels[None, :, 0] == jnp.arange(bias_table.shape[0], dtype=jnp.int32)[:, None]
    bias = jnp.sum(jnp.where(which[None], bias_table.T[:, :, None], 0.0), axis=1)
    bias = jnp.pad(bias.reshape(heads // 2, 2, targets), ((0, 0), (0, 6), (0, 0)))

    if size == 16:
        weights, more = after((weights, more))
        weights = [value for both in zip(weights, more) for value in both]
    weights, ffn, bias, dead = after((weights, ffn, bias, dead))
    weights = gather_second(weights, size, time=40)
    weights, ffn = after((weights, ffn))
    weights = send_second(weights, size)
    ffn = gather_outer(ffn, size, own)

    weights, own, ffn = after((weights, own, ffn))
    ffn = gather_first(ffn, size)
    ffn, weights, own = after((ffn, weights, own))
    ffn = send_first(ffn, size)
    own_peer = swap_cores(own)
    left, right = weights
    mixed, attended, lse_self, partial_one = self_forward(normed_one, bias, left)
    ffn, mixed, attended, lse_self, partial_one, own, own_peer = after(
        (ffn, mixed, attended, lse_self, partial_one, own, own_peer)
    )
    ffn = send_apart(ffn, size)
    peer_one = swap_cores(partial_one)
    encoded, key_value = encoder_call(which_core, own, own_peer, order, right)
    h_one, normed_two, cross_q, cross_att, lse_cross, *partial_two = cross_forward(
        tokens, partial_one, peer_one, gains, key_value, dead, right
    )
    peer_two = [swap_cores(value) for value in partial_two]
    h_two, partial_down, partial_three, *grads = ffn_call(
        h_one, partial_two, peer_two, gains, cot, cot_t, ffn[0] + ffn[1]
    )

    ffn = scatter_first(grads, size)
    peer_three = swap_cores(partial_three)
    peer_down = swap_cores(partial_down)
    g_two, low_two, dq, dkv, partial_four, gain_three = cross_backward(
        cot, partial_three, peer_three, h_two, gains, cross_q, key_value, dead, lse_cross, right
    )
    ffn, dq, dkv, low_two, partial_four, peer_down = after(
        (ffn, dq, dkv, low_two, partial_four, peer_down)
    )
    ffn = scatter_second_parts(ffn)
    ffn, dq, dkv, low_two, partial_four = after((ffn, dq, dkv, low_two, partial_four))
    ffn = scatter_second_send(ffn, size)
    peer_four = swap_cores(partial_four)
    kept, given, *grads = cross_grads(
        which_core, normed_two, dq, low_two, cross_att, turned, encoded, dkv, right
    )
    ffn, kept, given, grads, peer_four = after((ffn, kept, given, grads, peer_four))
    ffn = scatter_outer_parts(ffn, 0, 1)
    ffn, kept, given, grads, peer_four = after((ffn, kept, given, grads, peer_four))
    cross = scatter_first(grads, size)
    ffn = scatter_outer_send(ffn, size)
    g_one, partial_five, small, *grads = self_backward(
        g_two, partial_four, peer_four, h_one, gains, mixed, bias, lse_self, attended,
        normed_one, tokens, gain_three, turned, labels, left,
    )
    ffn, cross, given, partial_five, small, grads = after(
        (ffn, cross, given, partial_five, small, grads)
    )
    last = scatter_first(grads, size)
    peer_five = swap_cores(partial_five)
    taken = swap_cores(given)
    cross = scatter_second_send(scatter_second_parts(cross), size)

    terms = (kept.astype(F32) + taken.astype(F32)).astype(BF16).reshape(size, -1, half)
    count = terms.shape[1]
    terms = jnp.concatenate(
        [terms, jnp.broadcast_to(small[None], (size, *small.shape))], axis=1
    )
    back = lax.all_to_all(terms, "dp", split_axis=0, concat_axis=0, tiled=True)
    decoder_grad, layer_out = last_call(
        g_one, partial_five, peer_five, tokens, h_two, partial_down, peer_down, gains, turned
    )
    last, layer_out = after((last, layer_out))
    if size == 16:
        last = scatter_second_parts(last, time=40)
        cross = after(cross, last[-1])
        last = scatter_second_send(last, size)
        cross_keep, cross_out = scatter_pair_parts(cross)
        cross_in = swap(cross_out, 4, size)
        last, ffn = after((last, ffn), cross_out)
        last = scatter_outer_parts(last, 0, 1)
        last, back, ffn = after((last, back, ffn))
        last = scatter_outer_send(last, size)
        back, cross_in = after((back, cross_in), last[1])
        cross = scatter_pair_send(cross_keep, cross_in, size)
    else:
        cross = scatter_outer_send(scatter_outer_parts(cross, 0, 1), size)
        last = scatter_second_send(scatter_second_parts(last), size)
        last = scatter_outer_send(scatter_outer_parts(last, 0, 1), size)
    inverse = jnp.zeros_like(assign).at[assign].set(jnp.arange(size, dtype=jnp.int32))
    encoder_grad = back[:, :count][inverse]
    small = jnp.sum(back[:, count:].astype(F32), axis=0)
    small = small[:8] + small[8:]
    both = small + swap_cores(small)
    table = small[6:8].reshape(2, heads // 2, TILE)[:, :, : bias_table.shape[0]]
    grad_table = table.transpose(1, 0, 2).reshape(heads, -1).T
    grad_gains = [both[0:4:3].reshape(-1), small[1:5:3].reshape(-1), small[2:6:3].reshape(-1)]
    last, encoder_grad, grad_gains, grad_table = after(
        (last, encoder_grad, grad_gains, grad_table)
    )
    sum_ffn, sum_cross, sum_self = scatter_last(ffn), scatter_last(cross), scatter_last(last)

    def parts(value, count):
        step = value.shape[1] // count
        return [value[:, i * step : (i + 1) * step] for i in range(count)]

    grad_self_query, grad_self_key, grad_self_value, grad_output_one = parts(sum_self, 4)
    grad_cross_query, grad_output_two, grad_cross_key, grad_cross_value = parts(sum_cross, 4)
    grad_ffn_gate, grad_ffn_up, grad_ffn_down = parts(sum_ffn, 3)
    return (
        layer_out[None],
        decoder_grad[None],
        encoder_grad,
        *grad_gains,
        grad_self_query,
        grad_self_key,
        grad_self_value,
        grad_output_one.T,
        grad_cross_query,
        grad_cross_key,
        grad_cross_value,
        grad_output_two.T,
        grad_ffn_gate,
        grad_ffn_up,
        grad_ffn_down.T,
        grad_table,
    )


def solution(mesh):
    in_specs = (
        P("dp", None, None),
        P(None, "dp", None),
        P(),
        P(),
        P(),
        P(),
        P(),
        P(),
        P(),
        P("dp", "mp"),
        P("dp", "mp"),
        P("dp", "mp"),
        P("mp", "dp"),
        P("dp", "mp"),
        P("dp", "mp"),
        P("dp", "mp"),
        P("mp", "dp"),
        P("dp", "mp"),
        P("dp", "mp"),
        P("mp", "dp"),
        P(None, "mp"),
        P("dp", None, None),
    )
    out_specs = (
        P("dp", None, None),
        P("dp", None, None),
        P(None, "dp", "mp"),
        P(),
        P(),
        P(),
        P("dp", "mp"),
        P("dp", "mp"),
        P("dp", "mp"),
        P("mp", "dp"),
        P("dp", "mp"),
        P("dp", "mp"),
        P("dp", "mp"),
        P("mp", "dp"),
        P("dp", "mp"),
        P("dp", "mp"),
        P("mp", "dp"),
        P(None, "mp"),
    )
    body = functools.partial(shards, size=mesh.shape["dp"])
    return jax.shard_map(body, mesh=mesh, in_specs=in_specs, out_specs=out_specs, check_vma=False)
```

```python
import functools

import jax
import jax.numpy as jnp
from jax import lax
from jax.experimental import pallas as pl
from jax.experimental.pallas import tpu as pltpu
from jax.sharding import PartitionSpec as P

HEAD_DIM = 64
PAIR = 2 * HEAD_DIM
QUERIES = 256
KEYS = 1024
TILE = 128
WIDE = 256
HIDDEN = 512
CHUNKS = 2
ROWS = 64

EPS = 1e-06
NEGATIVE = -1000000000.0
GELU_ROOT = 0.7978845608028654
GELU_CUBE = 0.044715
BF16 = jnp.bfloat16
F32 = jnp.float32


def dot(left, right, dims):
    return lax.dot_general(left, right, (dims, ((), ())), preferred_element_type=F32)


def nn(left, right):
    return dot(left, right, ((1,), (0,)))


def nt(left, right):
    return dot(left, right, ((1,), (1,)))


def tn(left, right):
    return dot(left, right, ((0,), (0,)))


def struct(shape, dtype):
    return jax.ShapeDtypeStruct(shape, dtype)


def halves(value):
    high = value.astype(BF16)
    return high, (value - high.astype(F32)).astype(BF16)


def swap(value, mask, size):
    return lax.ppermute(value, "dp", [(i, i ^ mask) for i in range(size)])


def swap_cores(value):
    return lax.ppermute(value, "mp", [(0, 1), (1, 0)])


def after(values, *others):
    return lax.optimization_barrier((values, others))[0]


def gather_outer(shard, size, late=()):
    if size == 16:
        far, near = swap(shard, 8, size), swap(shard, 4, size)
        return [shard, near, far, swap(after(far, late), 4, size)]
    shard = after(shard, late)
    mask = 4
    while mask < size:
        shard = jnp.concatenate([shard, swap(shard, mask, size)])
        mask *= 2
    return [shard]


def gather_first(pieces, size):
    rows, half = sum(piece.shape[0] for piece in pieces), pieces[0].shape[1] // 2
    return kernel_call(stack_kernel, list(pieces), [struct((rows, half), BF16)] * 2, [])


def gather_second(state, size, time=2):
    rows = sum(value.shape[0] for value in state) // 2
    outs = [struct((rows, state[0].shape[1]), BF16)] * 2
    return kernel_call(join_kernel, list(state), outs, [], time=time)


def send_first(halves, size):
    left, right = halves
    return left, swap(left, 2, size), right, swap(right, 1, size)


def send_second(halves, size):
    left, right = halves
    return [left, swap(left, 1, size)], [right, swap(right, 2, size)]


def send_apart(state, size):
    left, left_in, right, right_in = state
    return (
        [left, left_in, swap(left, 1, size), swap(left_in, 1, size)],
        [right, right_in, swap(right, 2, size), swap(right_in, 2, size)],
    )


def scatter_first(grads, size):
    left, left_out, right, right_out = grads
    return left, right, swap(left_out, 1, size), swap(right_out, 2, size)


def scatter_second_parts(state, time=2):
    left = state[0]
    rows, half = left.shape[0] // 2, left.shape[1]
    outs = kernel_call(
        scatter_second_kernel,
        list(state),
        [struct((rows, half), BF16)] * 2,
        [],
        time=time,
        grid=(1,),
        in_specs=[pl.BlockSpec((rows, half), lambda i: (1, 0))] * 4,
        out_specs=[pl.BlockSpec((rows, half), lambda i: (0, 0))] * 2,
    )
    return (*state, *outs)


def scatter_second_send(parts, size):
    *state, left_out, right_out = parts
    return (*state, swap(left_out, 2, size), swap(right_out, 1, size))


def scatter_outer_parts(state, *sides):
    rows, half = state[-1].shape
    ins = [value for side in sides for value in state[side::2]]
    width = len(sides) * half
    return kernel_call(
        scatter_outer_kernel,
        ins,
        [struct((rows // 4, width), dtype) for dtype in (F32, BF16, BF16, BF16)],
        [],
        grid=(1,),
        in_specs=[pl.BlockSpec((rows, half), lambda i: (0, 0))] * len(ins),
        out_specs=[pl.BlockSpec((rows // 4, width), lambda i: (0, 0))] * 4,
    )


def scatter_pair_parts(state):
    rows, half = state[-1].shape
    outs = [struct((rows // 2, 2 * half), dtype) for dtype in (F32, BF16)]
    return kernel_call(
        scatter_pair_kernel,
        state[0::2] + state[1::2],
        outs,
        [],
        grid=(1,),
        in_specs=[pl.BlockSpec((rows, half), lambda i: (0, 0))] * 6,
        out_specs=[pl.BlockSpec((rows // 2, 2 * half), lambda i: (0, 0))] * 2,
    )


def scatter_pair_send(keep, taken, size):
    count = keep.shape[0] // 2
    rows = keep + taken.astype(F32)
    return [rows[:count], swap(rows[count:].astype(BF16), 8, size)]


def scatter_outer_send(parts, size):
    keep, *outs = parts
    if size == 16:
        return [keep] + [swap(out, 4 * (k + 1), size) for k, out in enumerate(outs)]
    rows = jnp.concatenate([keep] + [out.astype(F32) for out in outs])
    mask = size // 2
    while mask >= 4:
        count = rows.shape[0] // 2
        rows = rows[:count] + swap(rows[count:].astype(BF16), mask, size).astype(F32)
        mask //= 2
    return [rows]


def scatter_last(state):
    total = state[0]
    for value in state[1:]:
        total = total + value.astype(F32)
    return total


def kernel_call(kernel, ins, outs, scratch, time=2, grid=None, in_specs=None, out_specs=None):
    everywhere = pl.BlockSpec(memory_space=pltpu.VMEM)
    return pl.pallas_call(
        kernel,
        out_shape=outs,
        in_specs=in_specs or [everywhere] * len(ins),
        out_specs=out_specs or [everywhere] * len(outs),
        scratch_shapes=scratch,
        compiler_params=pltpu.CompilerParams(vmem_limit_bytes=58 * 1024 * 1024),
        cost_estimate=pl.CostEstimate(
            flops=time * 1000000000, bytes_accessed=1, transcendentals=0
        ),
        **({"grid": grid} if grid else {}),
    )(*ins)


IN_VMEM = pl.BlockSpec(memory_space=pltpu.VMEM)
IN_PLACE = pl.BlockSpec(memory_space=pl.ANY)
IN_SMEM = pl.BlockSpec(memory_space=pltpu.SMEM)


def stack_kernel(*refs):
    *in_refs, left_ref, right_ref = refs
    half = left_ref.shape[1]
    start = 0
    for ref in in_refs:
        rows = slice(start, start + ref.shape[0])
        left_ref[rows, :] = ref[:, :half]
        right_ref[rows, :] = ref[:, half:]
        start += ref.shape[0]


def join_kernel(*refs):
    *in_refs, left_out, right_out = refs
    for out_ref, pieces in (
        (left_out, in_refs[: len(in_refs) // 2]),
        (right_out, in_refs[len(in_refs) // 2 :]),
    ):
        start = 0
        for ref in pieces:
            out_ref[start : start + ref.shape[0], :] = ref[...]
            start += ref.shape[0]


def scatter_second_kernel(left_ref, right_ref, left_in_ref, right_in_ref, left_out, right_out):
    left_out[...] = (left_ref[...].astype(F32) + left_in_ref[...].astype(F32)).astype(BF16)
    right_out[...] = (right_ref[...].astype(F32) + right_in_ref[...].astype(F32)).astype(BF16)


def scatter_outer_kernel(*refs):
    *in_refs, keep_ref, first_ref, second_ref, third_ref = refs
    count = keep_ref.shape[0]
    for side in range(len(in_refs) // 3):
        own_ref, in_ref, more_ref = in_refs[3 * side : 3 * side + 3]
        half = own_ref.shape[1]
        cols = slice(side * half, (side + 1) * half)
        for k, out_ref in enumerate((keep_ref, first_ref, second_ref, third_ref)):
            rows = slice(k * count, (k + 1) * count)
            total = own_ref[rows, :].astype(F32) + in_ref[rows, :].astype(F32)
            out_ref[:, cols] = (total + more_ref[rows, :].astype(F32)).astype(out_ref.dtype)


def scatter_pair_kernel(*refs):
    *in_refs, keep_ref, out_ref = refs
    count = keep_ref.shape[0] // 2
    for side in range(2):
        own_ref, in_ref, more_ref = in_refs[3 * side : 3 * side + 3]
        half = own_ref.shape[1]
        cols = slice(side * half, (side + 1) * half)
        for k in range(4):
            rows = slice(k * count, (k + 1) * count)
            total = own_ref[rows, :].astype(F32) + in_ref[rows, :].astype(F32)
            target = out_ref if k % 2 else keep_ref
            spot = slice(k // 2 * count, (k // 2 + 1) * count)
            target[spot, cols] = (total + more_ref[rows, :].astype(F32)).astype(target.dtype)


def cast_kernel(*refs):
    *in_refs, out_ref = refs
    start = 0
    for ref in in_refs:
        out_ref[:, start : start + ref.shape[1]] = ref[...].astype(BF16)
        start += ref.shape[1]


def low(*values):
    width = sum(value.shape[1] for value in values)
    return kernel_call(
        cast_kernel, list(values), [struct((values[0].shape[0], width), BF16)], []
    )[0]


def each_rows(count, body, rows=ROWS):
    @pl.loop(0, count // rows)
    def step(i):
        body(pl.ds(pl.multiple_of(i * rows, rows), rows))


def each_tile(start, width, body):
    @pl.loop(0, width // WIDE)
    def step(i):
        body(pl.ds(pl.multiple_of(start + i * WIDE, WIDE), WIDE))


def fetch(left, right, weights_ref, sems, first=0):
    start = left[0].shape[1] if left else 0
    columns = weights_ref.shape[1] - start
    quarter = weights_ref.shape[0] // 4
    moves = []
    for i, ref in enumerate(left):
        count = ref.shape[0]
        moves.append((ref, weights_ref.at[i * count : (i + 1) * count, :start]))
    places = [0, 2, 1, 3]
    for ref in right:
        for x in range(ref.shape[0] // quarter):
            place = places.pop(0) * quarter
            moves.append(
                (
                    ref.at[x * quarter : (x + 1) * quarter, first : first + columns],
                    weights_ref.at[place : place + quarter, start:],
                )
            )
    copies = [pltpu.make_async_copy(*move, sems.at[i]) for i, move in enumerate(moves)]
    for copy in copies:
        copy.start()
    return copies


def deliver(grads_ref, out_refs, sems, columns, first=0):
    left, left_out, right, right_out = out_refs
    rows, half = left.shape[0] // 2, left.shape[1]
    side = columns.start // half
    if side == 0:
        moves = [(left, 0, 0, 2), (left_out, 0, 2, 2)]
    else:
        moves = [(right, 0, 0, 1), (right, 1, 2, 1), (right_out, 0, 1, 1), (right_out, 1, 3, 1)]
    copies = []
    for target, spot, place, count in moves:
        copies.append(
            pltpu.make_async_copy(
                grads_ref.at[place * rows : (place + count) * rows, columns],
                target.at[
                    spot * rows : (spot + count) * rows,
                    columns.start - side * half : columns.stop - side * half,
                ],
                sems.at[first + len(copies)],
            )
        )
    return copies


def deliver_all(grads_ref, out_refs, sems):
    half = out_refs[0].shape[1]
    copies = deliver(grads_ref, out_refs, sems, slice(0, half))
    copies += deliver(grads_ref, out_refs, sems, slice(half, 2 * half), 2)
    for copy in copies:
        copy.start()
    for copy in copies:
        copy.wait()


def grad_structs(width, columns):
    return [struct((width // 2, columns // 2), BF16)] * 4


def both_of(own_ref, peer_ref, rows):
    return own_ref[rows, :].astype(F32) + peer_ref[rows, :].astype(F32)


def root_of(value):
    return lax.rsqrt(jnp.mean(value * value, axis=-1, keepdims=True) + EPS)


def norm_back(value, gain, grad):
    root = root_of(value)
    scaled = grad * gain
    inner = jnp.mean(value * scaled, axis=-1, keepdims=True)
    back = root * scaled - value * (root * root * root * inner)
    return back, jnp.sum(grad * value * root, axis=0, keepdims=True)


def rows_kernel(
    tokens_ref, cot_ref, gains_ref, source_ref,
    tokens_out, cot_out, cot_t_out, gains_out, order_ref, turned_ref, normed_ref,
):
    width = tokens_ref.shape[1]
    spot = lax.broadcasted_iota(jnp.int32, (width, width), 0)
    order_ref[...] = jnp.where(spot == source_ref[0:1, :], 1.0, 0.0).astype(BF16)
    order = order_ref[...]
    turned_ref[...] = order.T
    high = gains_ref[...].astype(BF16)
    middle, rest = halves(gains_ref[...] - high.astype(F32))
    gains_out[...] = nn(high, order) + (nn(middle, order) + nn(rest, order))
    tokens_out[...] = nn(tokens_ref[...], order)
    cot_out[...] = nn(cot_ref[...], order).astype(BF16)
    cot_t_out[...] = cot_out[...].T
    gain = gains_out[0:1, :]

    def norm(rows):
        value = tokens_out[rows, :]
        normed_ref[rows, :] = (value * root_of(value) * gain).astype(BF16)

    each_rows(tokens_ref.shape[0], norm)


def queries_of(capacity):
    return QUERIES if capacity <= 2 * KEYS else TILE


def each_chunk(count, size, body):
    if count == 1:
        body(0)
    else:
        pl.loop(0, count)(lambda step: body(pl.multiple_of(step * size, size)))


def each_pair(pairs, body):
    @pl.loop(0, pairs)
    def step(pair):
        body(pair, lambda which: pl.ds(pl.multiple_of((which * pairs + pair) * PAIR, PAIR), PAIR))


def row_of(value, head):
    line = lax.broadcasted_iota(jnp.int32, value.shape, 0)
    return jnp.sum(jnp.where(line == head, value, 0.0), axis=0, keepdims=True)


def of_head(value, head):
    lane = lax.broadcasted_iota(jnp.int32, value.shape, 1)
    return jnp.where(lane // HEAD_DIM == head, value, jnp.zeros_like(value))


def cross_forward_pair(q_ref, k_ref, v_ref, dead_ref, out_ref, lse_ref, s_ref, acc_ref):
    targets, capacity = q_ref.shape[0], k_ref.shape[0]
    size = min(capacity, KEYS)
    count = capacity // size
    queries = s_ref.shape[1]
    for head in range(2):
        rows = slice(head * HEAD_DIM, (head + 1) * HEAD_DIM)
        line = slice(head, head + 1)
        for start in range(0, targets, queries):
            cols = slice(start, start + queries)
            query = of_head(q_ref[cols, :], head)
            lse_ref[line, cols] = jnp.full((1, queries), NEGATIVE * 2, F32)

            def scores(base):
                keys = pl.ds(base, size)
                score = nt(k_ref[keys, :], query) + dead_ref[keys, 0:1]
                s_ref[keys, :] = score
                lse_ref[line, cols] = jnp.maximum(
                    lse_ref[line, cols], jnp.max(score, axis=0, keepdims=True)
                )

            each_chunk(count, size, scores)
            top = lse_ref[line, cols]
            lse_ref[line, cols] = jnp.zeros((1, queries), F32)

            def weights(base):
                keys = pl.ds(base, size)
                weight = jnp.exp(s_ref[keys, :] - top)
                s_ref[keys, :] = weight
                lse_ref[line, cols] += jnp.sum(weight, axis=0, keepdims=True)

            each_chunk(count, size, weights)
            total = lse_ref[line, cols]
            lse_ref[line, cols] = top + jnp.log(total)
            scale = 1.0 / total
            acc_ref[rows, cols] = jnp.zeros((HEAD_DIM, queries), F32)

            def mix(base):
                keys = pl.ds(base, size)
                probs = (s_ref[keys, :] * scale).astype(BF16)
                acc_ref[rows, cols] += tn(v_ref[keys, :], probs)[rows]

            each_chunk(count, size, mix)
    out_ref[...] = acc_ref[...].T.astype(BF16)


def cross_backward_pair(
    q_ref, k_ref, v_ref, dead_ref, lse_ref, go_ref, dq_ref, dk_ref, dv_ref,
    p_ref, dp_ref, dqt_ref, dk_acc, dv_acc, delta_ref,
):
    targets, capacity = q_ref.shape[0], k_ref.shape[0]
    size = min(capacity, KEYS)
    count = capacity // size
    queries = p_ref.shape[1]
    dk_acc[...] = jnp.zeros_like(dk_acc)
    dv_acc[...] = jnp.zeros_like(dv_acc)
    dqt_ref[...] = jnp.zeros_like(dqt_ref)

    @pl.loop(0, 2)
    def each_head(head):
        for start in range(0, targets, queries):
            cols = slice(start, start + queries)
            query = of_head(q_ref[cols, :], head)
            grad = of_head(go_ref[cols, :], head)
            lse = row_of(lse_ref[:, cols], head)
            delta_ref[...] = jnp.zeros_like(delta_ref)

            def first(base):
                keys = pl.ds(base, size)
                probs = jnp.exp(nt(k_ref[keys, :], query) + dead_ref[keys, 0:1] - lse)
                grad_probs = nt(v_ref[keys, :], grad)
                p_ref[keys, :] = probs
                dp_ref[keys, :] = grad_probs
                delta_ref[...] += jnp.sum(probs * grad_probs, axis=0, keepdims=True)

            each_chunk(count, size, first)
            delta = delta_ref[...]

            def second(base):
                keys = pl.ds(base, size)
                probs = p_ref[keys, :]
                dv_acc[keys, :] += nn(probs.astype(BF16), grad)
                low = (probs * (dp_ref[keys, :] - delta)).astype(BF16)
                dk_acc[keys, :] += nn(low, query)
                dqt_ref[:, cols] += tn(of_head(k_ref[keys, :], head), low)

            each_chunk(count, size, second)
    dq_ref[...] = dqt_ref[...].T.astype(BF16)
    dk_ref[...] = dk_acc[...].astype(BF16)
    dv_ref[...] = dv_acc[...].astype(BF16)


def skewed(row, block):
    before = row[:, (block - 1) * TILE : block * TILE] if block else jnp.zeros((1, TILE), F32)
    both = jnp.concatenate([before, row[:, block * TILE : (block + 1) * TILE]], axis=1)
    both = jnp.broadcast_to(both, (TILE, 2 * TILE))
    return pltpu.roll(both, 0, 1, stride=1, stride_axis=0)[:, TILE:]


def unskewed(tile):
    both = jnp.concatenate([jnp.zeros_like(tile), tile], axis=1)
    total = both[:8]
    for base in range(8, TILE, 8):
        total = total + pltpu.roll(both[base : base + 8], 2 * TILE - base, 1)
    row = lax.broadcasted_iota(jnp.int32, total.shape, 0)
    for bit in (1, 2, 4):
        total = jnp.where(row & bit != 0, pltpu.roll(total, 2 * TILE - bit, 1), total)
    return jnp.sum(total, axis=0, keepdims=True)


def self_scores(k_ref, query, tiles, start):
    keys = start + QUERIES
    columns = []
    for i in range(start // TILE, keys // TILE):
        columns.append(
            jnp.concatenate([tiles[max(i - j, 0)] for j in range(keys // TILE)], axis=0)
        )
    score = nt(k_ref[:keys, :], query) + jnp.concatenate(columns, axis=1)
    key = lax.broadcasted_iota(jnp.int32, score.shape, 0)
    spot = lax.broadcasted_iota(jnp.int32, score.shape, 1) + start
    return jnp.where(key <= spot, score, NEGATIVE)


def self_forward_pair(q_ref, k_ref, v_ref, bias_ref, out_ref, lse_ref, acc_ref):
    targets = q_ref.shape[0]
    for head in range(2):
        rows = slice(head * HEAD_DIM, (head + 1) * HEAD_DIM)
        row = bias_ref[head : head + 1, :]
        tiles = [skewed(row, block) for block in range(targets // TILE)]
        for start in range(0, targets, QUERIES):
            cols = slice(start, start + QUERIES)
            query = of_head(q_ref[cols, :], head)
            score = self_scores(k_ref, query, tiles, start)
            top = jnp.max(score, axis=0, keepdims=True)
            weight = jnp.exp(score - top)
            total = jnp.sum(weight, axis=0, keepdims=True)
            lse_ref[head : head + 1, cols] = top + jnp.log(total)
            probs = (weight * (1.0 / total)).astype(BF16)
            acc_ref[rows, cols] = tn(v_ref[: start + QUERIES, :], probs)[rows]
    out_ref[...] = acc_ref[...].T.astype(BF16)


def self_backward_pair(
    q_ref, k_ref, v_ref, bias_ref, lse_ref, go_ref, dq_ref, dk_ref, dv_ref, dbias_ref,
    dqt_ref, dk_acc, dv_acc,
):
    targets = q_ref.shape[0]
    dk_acc[...] = jnp.zeros_like(dk_acc)
    dv_acc[...] = jnp.zeros_like(dv_acc)
    blocks = targets // TILE
    dqt_ref[...] = jnp.zeros_like(dqt_ref)

    @pl.loop(0, 2)
    def each_head(head):
        row = row_of(bias_ref[...], head)
        tiles = [skewed(row, block) for block in range(blocks)]
        sums = [jnp.zeros((TILE, TILE), F32) for block in range(blocks)]
        for start in range(0, targets, QUERIES):
            cols = slice(start, start + QUERIES)
            keys = start + QUERIES
            query = of_head(q_ref[cols, :], head)
            grad = of_head(go_ref[cols, :], head)
            score = self_scores(k_ref, query, tiles, start)
            probs = jnp.exp(score - row_of(lse_ref[:, cols], head))
            grad_probs = nt(v_ref[:keys, :], grad)
            delta = jnp.sum(probs * grad_probs, axis=0, keepdims=True)
            dv_acc[:keys, :] += nn(probs.astype(BF16), grad)
            grad_scores = probs * (grad_probs - delta)
            for i in range(start // TILE, keys // TILE):
                for j in range(i + 1):
                    sums[i - j] = sums[i - j] + grad_scores[
                        j * TILE : (j + 1) * TILE, i * TILE - start : (i + 1) * TILE - start
                    ]
            low_scores = grad_scores.astype(BF16)
            dk_acc[:keys, :] += nn(low_scores, query)
            dqt_ref[:, cols] += tn(of_head(k_ref[:keys, :], head), low_scores)
        lines = [unskewed(tile) for tile in sums]
        parts = []
        for block in range(blocks):
            part = lines[block][:, TILE:]
            if block + 1 < blocks:
                part = part + lines[block + 1][:, :TILE]
            parts.append(part)
        row = jnp.concatenate(parts, axis=1)
        line = lax.broadcasted_iota(jnp.int32, dbias_ref.shape, 0)
        dbias_ref[...] = jnp.where(line == head, row, dbias_ref[...])
    dq_ref[...] = dqt_ref[...].T.astype(BF16)
    dk_ref[...] = dk_acc[...].astype(BF16)
    dv_ref[...] = dv_acc[...].astype(BF16)


def self_forward_kernel(
    normed_ref, bias_ref, *refs
):
    mixed_ref, attended_ref, lse_ref, partial_ref, weights_ref, acc_ref, sems = refs[2:]
    copies = fetch(refs[:2], [], weights_ref, sems)
    for copy in copies:
        copy.wait()
    part = attended_ref.shape[1]
    pairs = part // PAIR
    normed = normed_ref[...]

    @pl.loop(0, 3 * part // TILE)
    def project(i):
        cols = pl.ds(pl.multiple_of(i * TILE, TILE), TILE)
        mixed_ref[:, cols] = nn(normed, weights_ref[:, cols]).astype(BF16)

    def attend(pair, cols):
        self_forward_pair(
            *(mixed_ref.at[:, cols(i)] for i in range(3)),
            bias_ref.at[pair], attended_ref.at[:, cols(0)], lse_ref.at[pair], acc_ref,
        )

    each_pair(pairs, attend)
    partial_ref[...] = nt(attended_ref[...], weights_ref[:, 3 * part :]).astype(BF16)


def self_forward(normed, bias, quarters):
    targets, width = normed.shape
    columns = quarters[0].shape[1]
    part = columns // 4
    pairs = part // PAIR
    return kernel_call(
        self_forward_kernel,
        [normed, bias, *quarters],
        [
            struct((targets, 3 * part), BF16),
            struct((targets, part), BF16),
            struct((pairs, 8, targets), F32),
            struct((targets, width), BF16),
        ],
        [
            pltpu.VMEM((width, columns), BF16),
            pltpu.VMEM((PAIR, targets), F32),
            pltpu.SemaphoreType.DMA((6,)),
        ],
        in_specs=[IN_VMEM] * 2 + [IN_PLACE] * 2,
        time=12,
    )


def encoder_kernel(core_ref, own_ref, peer_ref, order_ref, *refs):
    encoded_ref, out_ref, weights_ref, sems = refs[2:]

    @pl.when(pl.program_id(0) == 0)
    def load():
        for copy in fetch([], refs[:2], weights_ref, sems, weights_ref.shape[1]):
            copy.wait()

    core, half = core_ref[0], own_ref.shape[1]
    own_rows = pl.ds(pl.multiple_of(core * half, half), half)
    peer_rows = pl.ds(pl.multiple_of(half - core * half, half), half)
    encoded = nn(own_ref[...], order_ref[own_rows, :]) + nn(peer_ref[...], order_ref[peer_rows, :])
    encoded_ref[...] = encoded.astype(BF16)
    encoded = encoded_ref[...]

    def project(cols):
        out_ref[:, cols] = nn(encoded, weights_ref[:, cols]).astype(BF16)

    each_tile(0, out_ref.shape[1], project)


def encoder_call(core, own, peer, order, quarters):
    capacity, half = own.shape
    width = 2 * half
    columns = quarters[0].shape[1] // 2
    size = min(capacity, KEYS)
    block = lambda cols: pl.BlockSpec((size, cols), lambda i: (i, 0))
    return kernel_call(
        encoder_kernel,
        [core, own, peer, order, *quarters],
        [struct((capacity, width), BF16), struct((capacity, columns), BF16)],
        [pltpu.VMEM((width, columns), BF16), pltpu.SemaphoreType.DMA((4,))],
        grid=(capacity // size,),
        in_specs=[IN_SMEM, block(half), block(half), IN_VMEM] + [IN_PLACE] * 2,
        out_specs=[block(width), block(columns)],
        time=8,
    )


def cross_forward_kernel(tokens_ref, partial_ref, peer_ref, gains_ref, kv_ref, dead_ref, *refs):
    (
        h_ref, normed_ref, query_ref, att_ref, lse_ref, *out_refs,
        weights_ref, s_ref, acc_ref, sems,
    ) = refs[2:]
    copies = fetch([], refs[:2], weights_ref, sems)
    gain = gains_ref[1:2, :]

    def norm(rows):
        value = tokens_ref[rows, :] + both_of(partial_ref, peer_ref, rows)
        h_ref[rows, :] = value
        normed_ref[rows, :] = (value * root_of(value) * gain).astype(BF16)

    each_rows(h_ref.shape[0], norm)
    for copy in copies:
        copy.wait()
    part = query_ref.shape[1]
    pairs = part // PAIR
    query_ref[...] = nn(normed_ref[...], weights_ref[:, :part]).astype(BF16)

    def attend(pair, cols):
        cross_forward_pair(
            query_ref.at[:, cols(0)], kv_ref.at[:, cols(0)], kv_ref.at[:, cols(1)], dead_ref,
            att_ref.at[:, cols(0)], lse_ref.at[pair], s_ref, acc_ref,
        )

    each_pair(pairs, attend)
    count = out_refs[0].shape[0]
    for i, out_ref in enumerate(out_refs):
        att = att_ref[i * count : (i + 1) * count, :]
        out_ref[...] = nt(att, weights_ref[:, part:]).astype(BF16)


def cross_forward(tokens, partial, peer, gains, key_value, dead, quarters):
    targets, width = tokens.shape
    capacity, columns = key_value.shape
    part = columns // 2
    pairs = part // PAIR
    return kernel_call(
        cross_forward_kernel,
        [tokens, partial, peer, gains, key_value, dead, *quarters],
        [
            struct((targets, width), F32),
            struct((targets, width), BF16),
            struct((targets, part), BF16),
            struct((targets, part), BF16),
            struct((pairs, 8, targets), F32),
            *[struct((targets // CHUNKS, width), BF16)] * CHUNKS,
        ],
        [
            pltpu.VMEM((width, columns), BF16),
            pltpu.VMEM((capacity, queries_of(capacity)), F32),
            pltpu.VMEM((PAIR, targets), F32),
            pltpu.SemaphoreType.DMA((4,)),
        ],
        in_specs=[IN_VMEM] * 6 + [IN_PLACE] * 2,
        time=16,
    )


def cross_whole_kernel(
    core_ref, own_ref, peer_ref, order_ref, tokens_ref, partial_ref, partial_in_ref, gains_ref,
    dead_ref, *refs
):
    (
        encoded_ref, kv_ref, h_ref, normed_ref, query_ref, att_ref, lse_ref, *out_refs,
        weights_ref, s_ref, acc_ref, sems,
    ) = refs[2:]
    copies = fetch([], refs[:2], weights_ref, sems)
    core, half = core_ref[0], own_ref.shape[1]
    own_rows = pl.ds(pl.multiple_of(core * half, half), half)
    peer_rows = pl.ds(pl.multiple_of(half - core * half, half), half)
    encoded = nn(own_ref[...], order_ref[own_rows, :]) + nn(peer_ref[...], order_ref[peer_rows, :])
    encoded_ref[...] = encoded.astype(BF16)
    gain = gains_ref[1:2, :]

    def norm(rows):
        value = tokens_ref[rows, :] + both_of(partial_ref, partial_in_ref, rows)
        h_ref[rows, :] = value
        normed_ref[rows, :] = (value * root_of(value) * gain).astype(BF16)

    each_rows(h_ref.shape[0], norm)
    for copy in copies:
        copy.wait()
    part = query_ref.shape[1]
    pairs = part // PAIR

    @pl.loop(0, 2 * part // WIDE)
    def project(i):
        cols = pl.ds(pl.multiple_of(i * WIDE, WIDE), WIDE)
        source = pl.ds(pl.multiple_of(2 * part + i * WIDE, WIDE), WIDE)
        kv_ref[:, cols] = nn(encoded_ref[...], weights_ref[:, source]).astype(BF16)

    query_ref[...] = nn(normed_ref[...], weights_ref[:, :part]).astype(BF16)

    def attend(pair, cols):
        cross_forward_pair(
            query_ref.at[:, cols(0)], kv_ref.at[:, cols(0)], kv_ref.at[:, cols(1)], dead_ref,
            att_ref.at[:, cols(0)], lse_ref.at[pair], s_ref, acc_ref,
        )

    each_pair(pairs, attend)
    count = out_refs[0].shape[0]
    for i, out_ref in enumerate(out_refs):
        att = att_ref[i * count : (i + 1) * count, :]
        out_ref[...] = nt(att, weights_ref[:, part : 2 * part]).astype(BF16)


def cross_whole(core, own, peer, order, tokens, partial, partial_in, gains, dead, quarters):
    targets, width = tokens.shape
    capacity = own.shape[0]
    columns = quarters[0].shape[1]
    part = columns // 4
    pairs = part // PAIR
    return kernel_call(
        cross_whole_kernel,
        [core, own, peer, order, tokens, partial, partial_in, gains, dead, *quarters],
        [
            struct((capacity, width), BF16),
            struct((capacity, 2 * part), BF16),
            struct((targets, width), F32),
            struct((targets, width), BF16),
            struct((targets, part), BF16),
            struct((targets, part), BF16),
            struct((pairs, 8, targets), F32),
            *[struct((targets // CHUNKS, width), BF16)] * CHUNKS,
        ],
        [
            pltpu.VMEM((width, columns), BF16),
            pltpu.VMEM((capacity, queries_of(capacity)), F32),
            pltpu.VMEM((PAIR, targets), F32),
            pltpu.SemaphoreType.DMA((4,)),
        ],
        in_specs=[IN_SMEM] + [IN_VMEM] * 8 + [IN_PLACE] * 2,
        time=24,
    )


def ffn_kernel(before_ref, gains_ref, cot_ref, cot_t_ref, *refs):
    chunks, refs = refs[: 2 * CHUNKS], refs[2 * CHUNKS :]
    h_out, down_ref, back_ref, *outs = refs[8:15]
    weights_ref, grads_ref, h_ref, normed_ref, normed_t, in_sems, out_sems = refs[15:]
    copies = fetch(refs[:4], refs[4:8], weights_ref, in_sems)
    gain = gains_ref[2:3, :]
    count = chunks[0].shape[0]
    for i, (partial_ref, peer_ref) in enumerate(zip(chunks[:CHUNKS], chunks[CHUNKS:])):

        def norm(rows):
            own = pl.ds(pl.multiple_of(rows.start + i * count, rows.size), rows.size)
            value = before_ref[own, :] + both_of(partial_ref, peer_ref, rows)
            h_ref[own, :] = value
            normed_ref[own, :] = (value * root_of(value) * gain).astype(BF16)

        each_rows(count, norm, 32)
    h_copy = pltpu.make_async_copy(h_ref, h_out, out_sems.at[36])
    h_copy.start()
    normed_t[...] = normed_ref[...].T
    down_ref[...] = jnp.zeros_like(down_ref)
    back_ref[...] = jnp.zeros_like(back_ref)
    for copy in copies:
        copy.wait()
    hidden = weights_ref.shape[1] // 3
    tiles = hidden // HIDDEN

    def sends(i):
        copies = []
        for k in range(3):
            columns = slice(k * hidden + i * HIDDEN, k * hidden + (i + 1) * HIDDEN)
            first = 6 * (i * 3 + k)
            copies += deliver(grads_ref, outs, out_sems, columns, first)
        return copies

    @pl.loop(0, tiles)
    def tile(i):
        gates, ups, downs = (
            pl.ds(pl.multiple_of(k * hidden + i * HIDDEN, HIDDEN), HIDDEN) for k in range(3)
        )
        normed = normed_ref[...]
        gate = nn(normed, weights_ref[:, gates])
        up = nn(normed, weights_ref[:, ups])
        grad_act = nn(cot_ref[...], weights_ref[:, downs]).astype(BF16).astype(F32)
        square = gate * gate
        curve = jnp.tanh(GELU_ROOT * (gate + GELU_CUBE * (square * gate)))
        share = 0.5 * (1.0 + curve)
        gelu = gate * share
        slope = share + (0.5 * gate) * (1.0 - curve * curve) * (
            GELU_ROOT * (1.0 + (3.0 * GELU_CUBE) * square)
        )
        act = (gelu * up).astype(BF16)
        grad_gate = (grad_act * up * slope).astype(BF16)
        grad_up = (grad_act * gelu).astype(BF16)
        grads_ref[:, gates] = nn(normed_t[...], grad_gate).astype(BF16)
        grads_ref[:, ups] = nn(normed_t[...], grad_up).astype(BF16)
        grads_ref[:, downs] = nn(cot_t_ref[...], act).astype(BF16)
        for each in range(tiles):

            @pl.when(i == each)
            def send():
                for copy in sends(each):
                    copy.start()

        back_ref[...] += nt(grad_gate, weights_ref[:, gates]) + nt(grad_up, weights_ref[:, ups])
        down_ref[...] += nt(act, weights_ref[:, downs])

    for i in range(tiles):
        for copy in sends(i):
            copy.wait()
    h_copy.wait()


def ffn_call(before, partials, peers, gains, cot, cot_t, quarters):
    targets, width = before.shape
    columns = 2 * quarters[0].shape[1]
    return kernel_call(
        ffn_kernel,
        [before, gains, cot, cot_t, *partials, *peers, *quarters],
        [struct((targets, width), F32)] * 3 + grad_structs(width, columns),
        [
            pltpu.VMEM((width, columns), BF16),
            pltpu.VMEM((width, columns), BF16),
            pltpu.VMEM((targets, width), F32),
            pltpu.VMEM((targets, width), BF16),
            pltpu.VMEM((width, targets), BF16),
            pltpu.SemaphoreType.DMA((8,)),
            pltpu.SemaphoreType.DMA((37,)),
        ],
        time=20,
        in_specs=[IN_VMEM] * (4 + 2 * CHUNKS) + [IN_PLACE] * 8,
        out_specs=[IN_PLACE] + [IN_VMEM] * 2 + [IN_PLACE] * 4,
    )


def cross_backward_kernel(
    cot_ref, partial_ref, peer_ref, h_ref, gains_ref, query_ref, kv_ref, dead_ref, lse_ref, *refs
):
    (
        g_ref, low_ref, dq_ref, dkv_ref, back_ref, gain_grad_ref,
        weights_ref, go_ref, p_ref, dp_ref, dqt_ref, dk_acc, dv_acc, delta_ref, sems,
    ) = refs[2:]
    copies = fetch([], refs[:2], weights_ref, sems)
    gain = gains_ref[2:3, :]
    gain_grad_ref[...] = jnp.zeros_like(gain_grad_ref)

    def norm(rows):
        back, gain_grad = norm_back(h_ref[rows, :], gain, partial_ref[rows, :] + peer_ref[rows, :])
        gain_grad_ref[0:1, :] += gain_grad
        value = cot_ref[rows, :].astype(F32) + back
        g_ref[rows, :] = value
        low_ref[rows, :] = value.astype(BF16)

    each_rows(h_ref.shape[0], norm)
    for copy in copies:
        copy.wait()
    part = query_ref.shape[1]
    pairs = part // PAIR
    go_ref[...] = nn(low_ref[...], weights_ref[:, part:]).astype(BF16)

    def attend(pair, cols):
        cross_backward_pair(
            query_ref.at[:, cols(0)], kv_ref.at[:, cols(0)], kv_ref.at[:, cols(1)], dead_ref,
            lse_ref.at[pair], go_ref.at[:, cols(0)],
            dq_ref.at[:, cols(0)], dkv_ref.at[:, cols(0)], dkv_ref.at[:, cols(1)],
            p_ref, dp_ref, dqt_ref, dk_acc, dv_acc, delta_ref,
        )

    each_pair(pairs, attend)
    back_ref[...] = nt(dq_ref[...], weights_ref[:, :part])


def cross_backward(cot, partial, peer, before, gains, query, key_value, dead, lse, quarters):
    targets, width = cot.shape
    capacity, columns = key_value.shape
    return kernel_call(
        cross_backward_kernel,
        [cot, partial, peer, before, gains, query, key_value, dead, lse, *quarters],
        [
            struct((targets, width), F32),
            struct((targets, width), BF16),
            struct(query.shape, BF16),
            struct(key_value.shape, BF16),
            struct((targets, width), F32),
            struct((8, width), F32),
        ],
        [
            pltpu.VMEM((width, columns), BF16),
            pltpu.VMEM(query.shape, BF16),
            pltpu.VMEM((capacity, queries_of(capacity)), F32),
            pltpu.VMEM((capacity, queries_of(capacity)), F32),
            pltpu.VMEM((PAIR, targets), F32),
            pltpu.VMEM((capacity, PAIR), F32),
            pltpu.VMEM((capacity, PAIR), F32),
            pltpu.VMEM((1, queries_of(capacity)), F32),
            pltpu.SemaphoreType.DMA((4,)),
        ],
        in_specs=[IN_VMEM] * 9 + [IN_PLACE] * 2,
        time=18,
    )


def cross_grads_kernel(
    core_ref, normed_ref, dq_ref, low_ref, att_ref, order_ref, encoded_ref, dkv_ref, *refs
):
    kept_ref, given_ref, *outs = refs[2:8]
    weights_ref, acc_ref, grads_ref, in_sems, out_sems = refs[8:]
    step = pl.program_id(0)
    part = dq_ref.shape[1]

    @pl.when(step == 0)
    def load():
        copies = fetch([], refs[:2], weights_ref, in_sems, weights_ref.shape[1])
        grads_ref[:, :part] = tn(normed_ref[...], dq_ref[...]).astype(BF16)
        grads_ref[:, part : 2 * part] = tn(low_ref[...], att_ref[...]).astype(BF16)
        acc_ref[...] = jnp.zeros_like(acc_ref)
        for copy in copies:
            copy.wait()

    encoded_t = encoded_ref[...].T

    def project(cols):
        acc_ref[:, cols] += nn(encoded_t, dkv_ref[:, cols])

    each_tile(0, acc_ref.shape[1], project)
    core, half = core_ref[0], kept_ref.shape[1]
    terms = nt(dkv_ref[...], weights_ref[...]).astype(BF16)
    own_cols = pl.ds(pl.multiple_of(core * half, half), half)
    peer_cols = pl.ds(pl.multiple_of(half - core * half, half), half)
    kept_ref[...] = nn(terms, order_ref[:, own_cols]).astype(BF16)
    given_ref[...] = nn(terms, order_ref[:, peer_cols]).astype(BF16)

    @pl.when(step == pl.num_programs(0) - 1)
    def store():
        grads_ref[:, 2 * part :] = acc_ref[...].astype(BF16)
        deliver_all(grads_ref, outs, out_sems)


def cross_grads(core, normed, dq, low_two, attended, order, encoded, dkv, quarters):
    capacity, width = encoded.shape
    columns = dkv.shape[1]
    size = min(capacity, KEYS)
    block = lambda cols: pl.BlockSpec((size, cols), lambda i: (i, 0))
    return kernel_call(
        cross_grads_kernel,
        [core, normed, dq, low_two, attended, order, encoded, dkv, *quarters],
        [struct((capacity, width // 2), BF16)] * 2 + grad_structs(width, 2 * columns),
        [
            pltpu.VMEM((width, columns), BF16),
            pltpu.VMEM((width, columns), F32),
            pltpu.VMEM((width, 2 * columns), BF16),
            pltpu.SemaphoreType.DMA((4,)),
            pltpu.SemaphoreType.DMA((6,)),
        ],
        grid=(capacity // size,),
        in_specs=[IN_SMEM] + [IN_VMEM] * 5 + [block(width), block(columns)] + [IN_PLACE] * 2,
        out_specs=[block(width // 2)] * 2 + [IN_PLACE] * 4,
        time=12,
    )


def self_backward_kernel(
    g_in_ref, partial_ref, peer_ref, h_ref, gains_ref, mixed_ref, bias_ref, lse_ref,
    attended_ref, normed_ref, tokens_ref, gain_three_ref, order_ref, labels_ref, *refs
):
    g_ref, back_ref, small_ref, *outs = refs[2:9]
    (
        weights_ref, grads_ref, low_ref, go_ref, dmixed_ref, dbias_ref,
        dqt_ref, dk_acc, dv_acc, gain_ref, pack_ref, in_sems, out_sems,
    ) = refs[9:]
    copies = fetch(refs[:2], [], weights_ref, in_sems)
    gain = gains_ref[1:2, :]
    gain_ref[...] = jnp.zeros_like(gain_ref)

    def norm(rows):
        back, gain_grad = norm_back(h_ref[rows, :], gain, partial_ref[rows, :] + peer_ref[rows, :])
        gain_ref[1:2, :] += gain_grad
        value = g_in_ref[rows, :] + back
        g_ref[rows, :] = value
        low_ref[rows, :] = value.astype(BF16)

    each_rows(h_ref.shape[0], norm)
    for copy in copies:
        copy.wait()
    part = attended_ref.shape[1]
    pairs = part // PAIR
    go_ref[...] = nn(low_ref[...], weights_ref[:, 3 * part :]).astype(BF16)
    dbias_ref[...] = jnp.zeros_like(dbias_ref)

    def attend(pair, cols):
        self_backward_pair(
            *(mixed_ref.at[:, cols(i)] for i in range(3)),
            bias_ref.at[pair], lse_ref.at[pair], go_ref.at[:, cols(0)],
            *(dmixed_ref.at[:, cols(i)] for i in range(3)),
            dbias_ref.at[pair], dqt_ref, dk_acc, dv_acc,
        )

    each_pair(pairs, attend)
    back_ref[...] = nt(dmixed_ref[...], weights_ref[:, : 3 * part])
    normed_t = normed_ref[...].T

    @pl.loop(0, 3 * part // TILE)
    def project(i):
        cols = pl.ds(pl.multiple_of(i * TILE, TILE), TILE)
        grads_ref[:, cols] = nn(normed_t, dmixed_ref[:, cols]).astype(BF16)

    grads_ref[:, 3 * part :] = tn(low_ref[...], attended_ref[...]).astype(BF16)

    def sums(rows):
        value = tokens_ref[rows, :]
        gain_ref[0:1, :] += jnp.sum(back_ref[rows, :] * value * root_of(value), axis=0, keepdims=True)

    each_rows(h_ref.shape[0], sums)
    gain_ref[2:3, :] = gain_three_ref[0:1, :]
    high, rest = halves(gain_ref[...])
    gain_ref[...] = nn(high, order_ref[...]) + nn(rest, order_ref[...])
    half = pack_ref.shape[1]
    pack_ref[0:3, :] = gain_ref[0:3, :half]
    pack_ref[3:6, :] = gain_ref[0:3, half:]
    bucket = lax.broadcasted_iota(jnp.int32, (labels_ref.shape[0], TILE), 1)
    which = jnp.where(labels_ref[:, 0:1] == bucket, 1.0, 0.0).astype(BF16)
    for pair in range(pairs):
        high, rest = halves(dbias_ref[pair])
        table = nn(high, which) + nn(rest, which)
        pack_ref[6:8, pair * TILE : (pair + 1) * TILE] = table[0:2]
    small_ref[...] = jnp.concatenate(halves(pack_ref[...]), axis=0)
    deliver_all(grads_ref, outs, out_sems)


def self_backward(
    g_in, partial, peer, before, gains, mixed, bias, lse, attended, normed, tokens,
    gain_three, order, labels, quarters,
):
    targets, width = g_in.shape
    part = attended.shape[1]
    pairs = part // PAIR
    return kernel_call(
        self_backward_kernel,
        [
            g_in, partial, peer, before, gains, mixed, bias, lse, attended, normed, tokens,
            gain_three, order, labels, *quarters,
        ],
        [
            struct((targets, width), F32),
            struct((targets, width), F32),
            struct((16, width // 2), BF16),
        ]
        + grad_structs(width, 4 * part),
        [
            pltpu.VMEM((width, 4 * part), BF16),
            pltpu.VMEM((width, 4 * part), BF16),
            pltpu.VMEM((targets, width), BF16),
            pltpu.VMEM((targets, part), BF16),
            pltpu.VMEM((targets, 3 * part), BF16),
            pltpu.VMEM((pairs, 8, targets), F32),
            pltpu.VMEM((PAIR, targets), F32),
            pltpu.VMEM((targets, PAIR), F32),
            pltpu.VMEM((targets, PAIR), F32),
            pltpu.VMEM((8, width), F32),
            pltpu.VMEM((8, width // 2), F32),
            pltpu.SemaphoreType.DMA((6,)),
            pltpu.SemaphoreType.DMA((6,)),
        ],
        in_specs=[IN_VMEM] * 14 + [IN_PLACE] * 2,
        out_specs=[IN_VMEM] * 3 + [IN_PLACE] * 4,
        time=22,
    )


def last_kernel(
    g_ref, partial_ref, peer_ref, tokens_ref, h_ref, down_ref, down_in_ref, gains_ref, order_ref,
    grad_ref, out_ref,
):
    order = order_ref[...]
    value = h_ref[...] + (down_ref[...] + down_in_ref[...])
    out_ref[...] = nn(value.astype(BF16), order).astype(BF16)
    back, unused = norm_back(tokens_ref[...], gains_ref[0:1, :], partial_ref[...] + peer_ref[...])
    high, rest = halves(g_ref[...] + back)
    grad_ref[...] = nn(high, order) + nn(rest, order)


def last_call(*ins):
    targets, width = ins[0].shape
    block = pl.BlockSpec((WIDE, width), lambda i: (i, 0))
    return kernel_call(
        last_kernel,
        list(ins),
        [struct((targets, width), F32), struct((targets, width), BF16)],
        [],
        time=1,
        grid=(targets // WIDE,),
        in_specs=[block] * 7 + [IN_VMEM] * 2,
        out_specs=[block] * 2,
    )


def shards(
    decoder_in,
    encoder_out,
    lengths,
    key_mask,
    assign,
    buckets,
    norm_one,
    norm_two,
    norm_three,
    self_query,
    self_key,
    self_value,
    self_output,
    cross_query,
    cross_key,
    cross_value,
    cross_output,
    ffn_gate,
    ffn_up,
    ffn_down,
    bias_table,
    cotangent,
    *,
    size,
):
    rank = lax.axis_index("dp")
    core = lax.axis_index("mp")
    targets, width = decoder_in.shape[1:]
    capacity = key_mask.shape[1]
    block = width // size
    outer = size // 4
    half = width // 2
    heads = bias_table.shape[1]
    which_core = core.reshape(1)

    spots = jnp.arange(width, dtype=jnp.int32)
    spot = spots // block
    masks = spot // (2 * outer) + 2 * (spot // outer % 2) + 4 * (spot % outer)
    source = jnp.broadcast_to(((rank ^ masks) * block + spots % block)[None], (8, width))

    weights = low(
        self_query, self_key, self_value, self_output.T,
        cross_query, cross_output.T, cross_key, cross_value,
    )
    if size == 16:
        pieces = [weights, swap(weights, 4, size), swap(weights, 8, size)]
    else:
        pieces = gather_outer(weights, size)
    gains = jnp.concatenate(
        [norm_one[None], norm_two[None], norm_three[None], jnp.zeros((5, width), F32)]
    )
    tokens, cot, cot_t, gains, order, turned, normed_one = kernel_call(
        rows_kernel,
        [decoder_in[0], cotangent[0], gains, source],
        [
            struct((targets, width), F32),
            struct((targets, width), BF16),
            struct((width, targets), BF16),
            struct((8, width), F32),
            struct((width, width), BF16),
            struct((width, width), BF16),
            struct((targets, width), BF16),
        ],
        [],
    )
    ffn = low(*after((ffn_gate, ffn_up, ffn_down.T), normed_one))

    sent = lax.dynamic_slice_in_dim(encoder_out, core * half, half, 2)[assign]
    pieces, normed_one = after((pieces, normed_one))
    if size == 16:
        more = swap(pieces[2], 4, size)
    weights = send_first(gather_first(pieces, size), size)
    if size == 16:
        more, ffn, sent = after((more, ffn, sent))
        more = gather_first([more], size)
        more, ffn, sent = after((more, ffn, sent))
        more = send_first(more, size)
    own = lax.all_to_all(sent, "dp", split_axis=0, concat_axis=0, tiled=True)
    own = own.reshape(capacity, half)
    labels, bias_table, lengths = after((buckets[:, :TILE], bias_table, lengths), weights[0])
    mine = assign[rank]
    positions = jnp.arange(capacity, dtype=jnp.int32)
    live = (positions < lengths[mine]) & ((key_mask[mine] == 1) | (positions == 0))
    dead = jnp.broadcast_to(jnp.where(live, 0.0, NEGATIVE)[:, None], (capacity, TILE))
    which = labels[None, :, 0] == jnp.arange(bias_table.shape[0], dtype=jnp.int32)[:, None]
    bias = jnp.sum(jnp.where(which[None], bias_table.T[:, :, None], 0.0), axis=1)
    bias = jnp.pad(bias.reshape(heads // 2, 2, targets), ((0, 0), (0, 6), (0, 0)))

    if size == 16:
        weights, more = after((weights, more))
        weights = [value for both in zip(weights, more) for value in both]
    weights, ffn, bias, dead = after((weights, ffn, bias, dead))
    weights = gather_second(weights, size, time=40)
    weights, ffn = after((weights, ffn))
    weights = send_second(weights, size)
    ffn = gather_outer(ffn, size, own)

    weights, own, ffn = after((weights, own, ffn))
    ffn = gather_first(ffn, size)
    ffn, weights, own = after((ffn, weights, own))
    ffn = send_first(ffn, size)
    own_peer = swap_cores(own)
    left, right = weights
    mixed, attended, lse_self, partial_one = self_forward(normed_one, bias, left)
    ffn, mixed, attended, lse_self, partial_one, own, own_peer = after(
        (ffn, mixed, attended, lse_self, partial_one, own, own_peer)
    )
    ffn = send_apart(ffn, size)
    peer_one = swap_cores(partial_one)
    if capacity <= KEYS:
        (
            encoded, key_value, h_one, normed_two, cross_q, cross_att, lse_cross, *partial_two
        ) = cross_whole(
            which_core, own, own_peer, order, tokens, partial_one, peer_one, gains, dead, right
        )
    else:
        encoded, key_value = encoder_call(which_core, own, own_peer, order, right)
        h_one, normed_two, cross_q, cross_att, lse_cross, *partial_two = cross_forward(
            tokens, partial_one, peer_one, gains, key_value, dead, right
        )
    peer_two = [swap_cores(value) for value in partial_two]
    h_two, partial_down, partial_three, *grads = ffn_call(
        h_one, partial_two, peer_two, gains, cot, cot_t, ffn[0] + ffn[1]
    )

    ffn = scatter_first(grads, size)
    peer_three = swap_cores(partial_three)
    peer_down = swap_cores(partial_down)
    g_two, low_two, dq, dkv, partial_four, gain_three = cross_backward(
        cot, partial_three, peer_three, h_two, gains, cross_q, key_value, dead, lse_cross, right
    )
    ffn, dq, dkv, low_two, partial_four, peer_down = after(
        (ffn, dq, dkv, low_two, partial_four, peer_down)
    )
    ffn = scatter_second_parts(ffn)
    ffn, dq, dkv, low_two, partial_four = after((ffn, dq, dkv, low_two, partial_four))
    ffn = scatter_second_send(ffn, size)
    peer_four = swap_cores(partial_four)
    kept, given, *grads = cross_grads(
        which_core, normed_two, dq, low_two, cross_att, turned, encoded, dkv, right
    )
    ffn, kept, given, grads, peer_four = after((ffn, kept, given, grads, peer_four))
    ffn = scatter_outer_parts(ffn, 0, 1)
    ffn, kept, given, grads, peer_four = after((ffn, kept, given, grads, peer_four))
    cross = scatter_first(grads, size)
    ffn = scatter_outer_send(ffn, size)
    g_one, partial_five, small, *grads = self_backward(
        g_two, partial_four, peer_four, h_one, gains, mixed, bias, lse_self, attended,
        normed_one, tokens, gain_three, turned, labels, left,
    )
    ffn, cross, given, partial_five, small, grads = after(
        (ffn, cross, given, partial_five, small, grads)
    )
    last = scatter_first(grads, size)
    peer_five = swap_cores(partial_five)
    taken = swap_cores(given)
    cross = scatter_second_send(scatter_second_parts(cross), size)

    terms = (kept.astype(F32) + taken.astype(F32)).astype(BF16).reshape(size, -1, half)
    count = terms.shape[1]
    terms = jnp.concatenate(
        [terms, jnp.broadcast_to(small[None], (size, *small.shape))], axis=1
    )
    back = lax.all_to_all(terms, "dp", split_axis=0, concat_axis=0, tiled=True)
    decoder_grad, layer_out = last_call(
        g_one, partial_five, peer_five, tokens, h_two, partial_down, peer_down, gains, turned
    )
    last, layer_out = after((last, layer_out))
    if size == 16:
        last = scatter_second_parts(last, time=40)
        cross = after(cross, last[-1])
        last = scatter_second_send(last, size)
        cross_keep, cross_out = scatter_pair_parts(cross)
        cross_in = swap(cross_out, 4, size)
        last, ffn = after((last, ffn), cross_out)
        last = scatter_outer_parts(last, 0, 1)
        last, back, ffn = after((last, back, ffn))
        last = scatter_outer_send(last, size)
        back, cross_in = after((back, cross_in), last[1])
        cross = scatter_pair_send(cross_keep, cross_in, size)
    else:
        cross = scatter_outer_send(scatter_outer_parts(cross, 0, 1), size)
        last = scatter_second_send(scatter_second_parts(last), size)
        last = scatter_outer_send(scatter_outer_parts(last, 0, 1), size)
    inverse = jnp.zeros_like(assign).at[assign].set(jnp.arange(size, dtype=jnp.int32))
    encoder_grad = back[:, :count][inverse]
    small = jnp.sum(back[:, count:].astype(F32), axis=0)
    small = small[:8] + small[8:]
    both = small + swap_cores(small)
    table = small[6:8].reshape(2, heads // 2, TILE)[:, :, : bias_table.shape[0]]
    grad_table = table.transpose(1, 0, 2).reshape(heads, -1).T
    grad_gains = [both[0:4:3].reshape(-1), small[1:5:3].reshape(-1), small[2:6:3].reshape(-1)]
    last, encoder_grad, grad_gains, grad_table = after(
        (last, encoder_grad, grad_gains, grad_table)
    )
    sum_ffn, sum_cross, sum_self = scatter_last(ffn), scatter_last(cross), scatter_last(last)

    def parts(value, count):
        step = value.shape[1] // count
        return [value[:, i * step : (i + 1) * step] for i in range(count)]

    grad_self_query, grad_self_key, grad_self_value, grad_output_one = parts(sum_self, 4)
    grad_cross_query, grad_output_two, grad_cross_key, grad_cross_value = parts(sum_cross, 4)
    grad_ffn_gate, grad_ffn_up, grad_ffn_down = parts(sum_ffn, 3)
    return (
        layer_out[None],
        decoder_grad[None],
        encoder_grad,
        *grad_gains,
        grad_self_query,
        grad_self_key,
        grad_self_value,
        grad_output_one.T,
        grad_cross_query,
        grad_cross_key,
        grad_cross_value,
        grad_output_two.T,
        grad_ffn_gate,
        grad_ffn_up,
        grad_ffn_down.T,
        grad_table,
    )


def solution(mesh):
    in_specs = (
        P("dp", None, None),
        P(None, "dp", None),
        P(),
        P(),
        P(),
        P(),
        P(),
        P(),
        P(),
        P("dp", "mp"),
        P("dp", "mp"),
        P("dp", "mp"),
        P("mp", "dp"),
        P("dp", "mp"),
        P("dp", "mp"),
        P("dp", "mp"),
        P("mp", "dp"),
        P("dp", "mp"),
        P("dp", "mp"),
        P("mp", "dp"),
        P(None, "mp"),
        P("dp", None, None),
    )
    out_specs = (
        P("dp", None, None),
        P("dp", None, None),
        P(None, "dp", "mp"),
        P(),
        P(),
        P(),
        P("dp", "mp"),
        P("dp", "mp"),
        P("dp", "mp"),
        P("mp", "dp"),
        P("dp", "mp"),
        P("dp", "mp"),
        P("dp", "mp"),
        P("mp", "dp"),
        P("dp", "mp"),
        P("dp", "mp"),
        P("mp", "dp"),
        P(None, "mp"),
    )
    body = functools.partial(shards, size=mesh.shape["dp"])
    return jax.shard_map(body, mesh=mesh, in_specs=in_specs, out_specs=out_specs, check_vma=False)
```

```python
import functools

import jax
import jax.numpy as jnp
from jax import lax
from jax.experimental import pallas as pl
from jax.experimental.pallas import tpu as pltpu
from jax.sharding import PartitionSpec as P

HEAD_DIM = 64
PAIR = 2 * HEAD_DIM
QUERIES = 256
KEYS = 1024
TILE = 128
WIDE = 256
HIDDEN = 512
CHUNKS = 2
ROWS = 64

EPS = 1e-06
NEGATIVE = -1000000000.0
GELU_ROOT = 0.7978845608028654
GELU_CUBE = 0.044715
BF16 = jnp.bfloat16
F32 = jnp.float32


def dot(left, right, dims):
    return lax.dot_general(left, right, (dims, ((), ())), preferred_element_type=F32)


def nn(left, right):
    return dot(left, right, ((1,), (0,)))


def nt(left, right):
    return dot(left, right, ((1,), (1,)))


def tn(left, right):
    return dot(left, right, ((0,), (0,)))


def struct(shape, dtype):
    return jax.ShapeDtypeStruct(shape, dtype)


def halves(value):
    high = value.astype(BF16)
    return high, (value - high.astype(F32)).astype(BF16)


def swap(value, mask, size):
    return lax.ppermute(value, "dp", [(i, i ^ mask) for i in range(size)])


def swap_cores(value):
    return lax.ppermute(value, "mp", [(0, 1), (1, 0)])


def after(values, *others):
    return lax.optimization_barrier((values, others))[0]


def gather_outer(shard, size, late=()):
    if size == 16:
        far, near = swap(shard, 8, size), swap(shard, 4, size)
        return [shard, near, far, swap(after(far, late), 4, size)]
    shard = after(shard, late)
    mask = 4
    while mask < size:
        shard = jnp.concatenate([shard, swap(shard, mask, size)])
        mask *= 2
    return [shard]


def gather_first(pieces, size):
    rows, half = sum(piece.shape[0] for piece in pieces), pieces[0].shape[1] // 2
    return kernel_call(stack_kernel, list(pieces), [struct((rows, half), BF16)] * 2, [])


def gather_second(state, size, time=2):
    rows = sum(value.shape[0] for value in state) // 2
    outs = [struct((rows, state[0].shape[1]), BF16)] * 2
    return kernel_call(join_kernel, list(state), outs, [], time=time)


def send_first(halves, size):
    left, right = halves
    return left, swap(left, 2, size), right, swap(right, 1, size)


def send_second(halves, size):
    left, right = halves
    return [left, swap(left, 1, size)], [right, swap(right, 2, size)]


def send_apart(state, size):
    left, left_in, right, right_in = state
    return (
        [left, left_in, swap(left, 1, size), swap(left_in, 1, size)],
        [right, right_in, swap(right, 2, size), swap(right_in, 2, size)],
    )


def scatter_first(grads, size):
    left, left_out, right, right_out = grads
    return left, right, swap(left_out, 1, size), swap(right_out, 2, size)


def scatter_second_parts(state, time=2):
    left = state[0]
    rows, half = left.shape[0] // 2, left.shape[1]
    outs = kernel_call(
        scatter_second_kernel,
        list(state),
        [struct((rows, half), BF16)] * 2,
        [],
        time=time,
        grid=(1,),
        in_specs=[pl.BlockSpec((rows, half), lambda i: (1, 0))] * 4,
        out_specs=[pl.BlockSpec((rows, half), lambda i: (0, 0))] * 2,
    )
    return (*state, *outs)


def scatter_second_send(parts, size):
    *state, left_out, right_out = parts
    return (*state, swap(left_out, 2, size), swap(right_out, 1, size))


def scatter_outer_parts(state, *sides):
    rows, half = state[-1].shape
    ins = [value for side in sides for value in state[side::2]]
    width = len(sides) * half
    return kernel_call(
        scatter_outer_kernel,
        ins,
        [struct((rows // 4, width), dtype) for dtype in (F32, BF16, BF16, BF16)],
        [],
        grid=(1,),
        in_specs=[pl.BlockSpec((rows, half), lambda i: (0, 0))] * len(ins),
        out_specs=[pl.BlockSpec((rows // 4, width), lambda i: (0, 0))] * 4,
    )


def scatter_pair_parts(state):
    rows, half = state[-1].shape
    outs = [struct((rows // 2, 2 * half), dtype) for dtype in (F32, BF16)]
    return kernel_call(
        scatter_pair_kernel,
        state[0::2] + state[1::2],
        outs,
        [],
        grid=(1,),
        in_specs=[pl.BlockSpec((rows, half), lambda i: (0, 0))] * 6,
        out_specs=[pl.BlockSpec((rows // 2, 2 * half), lambda i: (0, 0))] * 2,
    )


def scatter_pair_send(keep, taken, size):
    count = keep.shape[0] // 2
    rows = keep + taken.astype(F32)
    return [rows[:count], swap(rows[count:].astype(BF16), 8, size)]


def scatter_outer_send(parts, size):
    keep, *outs = parts
    if size == 16:
        return [keep] + [swap(out, 4 * (k + 1), size) for k, out in enumerate(outs)]
    rows = jnp.concatenate([keep] + [out.astype(F32) for out in outs])
    mask = size // 2
    while mask >= 4:
        count = rows.shape[0] // 2
        rows = rows[:count] + swap(rows[count:].astype(BF16), mask, size).astype(F32)
        mask //= 2
    return [rows]


def scatter_last(state):
    total = state[0]
    for value in state[1:]:
        total = total + value.astype(F32)
    return total


def kernel_call(kernel, ins, outs, scratch, time=2, grid=None, in_specs=None, out_specs=None):
    everywhere = pl.BlockSpec(memory_space=pltpu.VMEM)
    return pl.pallas_call(
        kernel,
        out_shape=outs,
        in_specs=in_specs or [everywhere] * len(ins),
        out_specs=out_specs or [everywhere] * len(outs),
        scratch_shapes=scratch,
        compiler_params=pltpu.CompilerParams(vmem_limit_bytes=58 * 1024 * 1024),
        cost_estimate=pl.CostEstimate(
            flops=time * 1000000000, bytes_accessed=1, transcendentals=0
        ),
        **({"grid": grid} if grid else {}),
    )(*ins)


IN_VMEM = pl.BlockSpec(memory_space=pltpu.VMEM)
IN_PLACE = pl.BlockSpec(memory_space=pl.ANY)
IN_SMEM = pl.BlockSpec(memory_space=pltpu.SMEM)


def stack_kernel(*refs):
    *in_refs, left_ref, right_ref = refs
    half = left_ref.shape[1]
    start = 0
    for ref in in_refs:
        rows = slice(start, start + ref.shape[0])
        left_ref[rows, :] = ref[:, :half]
        right_ref[rows, :] = ref[:, half:]
        start += ref.shape[0]


def join_kernel(*refs):
    *in_refs, left_out, right_out = refs
    for out_ref, pieces in (
        (left_out, in_refs[: len(in_refs) // 2]),
        (right_out, in_refs[len(in_refs) // 2 :]),
    ):
        start = 0
        for ref in pieces:
            out_ref[start : start + ref.shape[0], :] = ref[...]
            start += ref.shape[0]


def scatter_second_kernel(left_ref, right_ref, left_in_ref, right_in_ref, left_out, right_out):
    left_out[...] = (left_ref[...].astype(F32) + left_in_ref[...].astype(F32)).astype(BF16)
    right_out[...] = (right_ref[...].astype(F32) + right_in_ref[...].astype(F32)).astype(BF16)


def scatter_outer_kernel(*refs):
    *in_refs, keep_ref, first_ref, second_ref, third_ref = refs
    count = keep_ref.shape[0]
    for side in range(len(in_refs) // 3):
        own_ref, in_ref, more_ref = in_refs[3 * side : 3 * side + 3]
        half = own_ref.shape[1]
        cols = slice(side * half, (side + 1) * half)
        for k, out_ref in enumerate((keep_ref, first_ref, second_ref, third_ref)):
            rows = slice(k * count, (k + 1) * count)
            total = own_ref[rows, :].astype(F32) + in_ref[rows, :].astype(F32)
            out_ref[:, cols] = (total + more_ref[rows, :].astype(F32)).astype(out_ref.dtype)


def scatter_pair_kernel(*refs):
    *in_refs, keep_ref, out_ref = refs
    count = keep_ref.shape[0] // 2
    for side in range(2):
        own_ref, in_ref, more_ref = in_refs[3 * side : 3 * side + 3]
        half = own_ref.shape[1]
        cols = slice(side * half, (side + 1) * half)
        for k in range(4):
            rows = slice(k * count, (k + 1) * count)
            total = own_ref[rows, :].astype(F32) + in_ref[rows, :].astype(F32)
            target = out_ref if k % 2 else keep_ref
            spot = slice(k // 2 * count, (k // 2 + 1) * count)
            target[spot, cols] = (total + more_ref[rows, :].astype(F32)).astype(target.dtype)


def cast_kernel(*refs):
    *in_refs, out_ref = refs
    start = 0
    for ref in in_refs:
        out_ref[:, start : start + ref.shape[1]] = ref[...].astype(BF16)
        start += ref.shape[1]


def low(*values):
    width = sum(value.shape[1] for value in values)
    return kernel_call(
        cast_kernel, list(values), [struct((values[0].shape[0], width), BF16)], []
    )[0]


def each_rows(count, body, rows=ROWS):
    @pl.loop(0, count // rows)
    def step(i):
        body(pl.ds(pl.multiple_of(i * rows, rows), rows))


def each_tile(start, width, body):
    @pl.loop(0, width // WIDE)
    def step(i):
        body(pl.ds(pl.multiple_of(start + i * WIDE, WIDE), WIDE))


def fetch(left, right, weights_ref, sems, first=0):
    start = left[0].shape[1] if left else 0
    columns = weights_ref.shape[1] - start
    quarter = weights_ref.shape[0] // 4
    moves = []
    for i, ref in enumerate(left):
        count = ref.shape[0]
        moves.append((ref, weights_ref.at[i * count : (i + 1) * count, :start]))
    places = [0, 2, 1, 3]
    for ref in right:
        for x in range(ref.shape[0] // quarter):
            place = places.pop(0) * quarter
            moves.append(
                (
                    ref.at[x * quarter : (x + 1) * quarter, first : first + columns],
                    weights_ref.at[place : place + quarter, start:],
                )
            )
    copies = [pltpu.make_async_copy(*move, sems.at[i]) for i, move in enumerate(moves)]
    for copy in copies:
        copy.start()
    return copies


def deliver(grads_ref, out_refs, sems, columns, first=0):
    left, left_out, right, right_out = out_refs
    rows, half = left.shape[0] // 2, left.shape[1]
    side = columns.start // half
    if side == 0:
        moves = [(left, 0, 0, 2), (left_out, 0, 2, 2)]
    else:
        moves = [(right, 0, 0, 1), (right, 1, 2, 1), (right_out, 0, 1, 1), (right_out, 1, 3, 1)]
    copies = []
    for target, spot, place, count in moves:
        copies.append(
            pltpu.make_async_copy(
                grads_ref.at[place * rows : (place + count) * rows, columns],
                target.at[
                    spot * rows : (spot + count) * rows,
                    columns.start - side * half : columns.stop - side * half,
                ],
                sems.at[first + len(copies)],
            )
        )
    return copies


def deliver_all(grads_ref, out_refs, sems):
    half = out_refs[0].shape[1]
    copies = deliver(grads_ref, out_refs, sems, slice(0, half))
    copies += deliver(grads_ref, out_refs, sems, slice(half, 2 * half), 2)
    for copy in copies:
        copy.start()
    for copy in copies:
        copy.wait()


def grad_structs(width, columns):
    return [struct((width // 2, columns // 2), BF16)] * 4


def both_of(own_ref, peer_ref, rows):
    return own_ref[rows, :].astype(F32) + peer_ref[rows, :].astype(F32)


def root_of(value):
    return lax.rsqrt(jnp.mean(value * value, axis=-1, keepdims=True) + EPS)


def norm_back(value, gain, grad):
    root = root_of(value)
    scaled = grad * gain
    inner = jnp.mean(value * scaled, axis=-1, keepdims=True)
    back = root * scaled - value * (root * root * root * inner)
    return back, jnp.sum(grad * value * root, axis=0, keepdims=True)


def rows_kernel(
    tokens_ref, cot_ref, gains_ref, source_ref,
    tokens_out, cot_out, cot_t_out, gains_out, order_ref, turned_ref, normed_ref,
):
    width = tokens_ref.shape[1]
    spot = lax.broadcasted_iota(jnp.int32, (width, width), 0)
    order_ref[...] = jnp.where(spot == source_ref[0:1, :], 1.0, 0.0).astype(BF16)
    order = order_ref[...]
    turned_ref[...] = order.T
    high = gains_ref[...].astype(BF16)
    middle, rest = halves(gains_ref[...] - high.astype(F32))
    gains_out[...] = nn(high, order) + (nn(middle, order) + nn(rest, order))
    tokens_out[...] = nn(tokens_ref[...], order)
    cot_out[...] = nn(cot_ref[...], order).astype(BF16)
    cot_t_out[...] = cot_out[...].T
    gain = gains_out[0:1, :]

    def norm(rows):
        value = tokens_out[rows, :]
        normed_ref[rows, :] = (value * root_of(value) * gain).astype(BF16)

    each_rows(tokens_ref.shape[0], norm)


def queries_of(capacity):
    return QUERIES if capacity <= 2 * KEYS else TILE


def each_chunk(count, size, body):
    if count == 1:
        body(0)
    else:
        pl.loop(0, count)(lambda step: body(pl.multiple_of(step * size, size)))


def each_pair(pairs, body):
    @pl.loop(0, pairs)
    def step(pair):
        body(pair, lambda which: pl.ds(pl.multiple_of((which * pairs + pair) * PAIR, PAIR), PAIR))


def row_of(value, head):
    line = lax.broadcasted_iota(jnp.int32, value.shape, 0)
    return jnp.sum(jnp.where(line == head, value, 0.0), axis=0, keepdims=True)


def of_head(value, head):
    lane = lax.broadcasted_iota(jnp.int32, value.shape, 1)
    return jnp.where(lane // HEAD_DIM == head, value, jnp.zeros_like(value))


def cross_forward_pair(q_ref, k_ref, v_ref, dead_ref, out_ref, lse_ref, s_ref, acc_ref):
    targets, capacity = q_ref.shape[0], k_ref.shape[0]
    size = min(capacity, KEYS)
    count = capacity // size
    queries = s_ref.shape[1]
    for head in range(2):
        rows = slice(head * HEAD_DIM, (head + 1) * HEAD_DIM)
        line = slice(head, head + 1)
        for start in range(0, targets, queries):
            cols = slice(start, start + queries)
            query = of_head(q_ref[cols, :], head)
            lse_ref[line, cols] = jnp.full((1, queries), NEGATIVE * 2, F32)

            def scores(base):
                keys = pl.ds(base, size)
                score = nt(k_ref[keys, :], query) + dead_ref[keys, 0:1]
                s_ref[keys, :] = score
                lse_ref[line, cols] = jnp.maximum(
                    lse_ref[line, cols], jnp.max(score, axis=0, keepdims=True)
                )

            each_chunk(count, size, scores)
            top = lse_ref[line, cols]
            lse_ref[line, cols] = jnp.zeros((1, queries), F32)

            def weights(base):
                keys = pl.ds(base, size)
                weight = jnp.exp(s_ref[keys, :] - top)
                s_ref[keys, :] = weight
                lse_ref[line, cols] += jnp.sum(weight, axis=0, keepdims=True)

            each_chunk(count, size, weights)
            total = lse_ref[line, cols]
            lse_ref[line, cols] = top + jnp.log(total)
            scale = 1.0 / total
            acc_ref[rows, cols] = jnp.zeros((HEAD_DIM, queries), F32)

            def mix(base):
                keys = pl.ds(base, size)
                probs = (s_ref[keys, :] * scale).astype(BF16)
                acc_ref[rows, cols] += tn(v_ref[keys, :], probs)[rows]

            each_chunk(count, size, mix)
    out_ref[...] = acc_ref[...].T.astype(BF16)


def cross_backward_pair(
    q_ref, k_ref, v_ref, dead_ref, lse_ref, go_ref, dq_ref, dk_ref, dv_ref,
    p_ref, dp_ref, dqt_ref, dk_acc, dv_acc, delta_ref,
):
    targets, capacity = q_ref.shape[0], k_ref.shape[0]
    size = min(capacity, KEYS)
    count = capacity // size
    queries = p_ref.shape[1]
    dk_acc[...] = jnp.zeros_like(dk_acc)
    dv_acc[...] = jnp.zeros_like(dv_acc)
    dqt_ref[...] = jnp.zeros_like(dqt_ref)

    @pl.loop(0, 2)
    def each_head(head):
        for start in range(0, targets, queries):
            cols = slice(start, start + queries)
            query = of_head(q_ref[cols, :], head)
            grad = of_head(go_ref[cols, :], head)
            lse = row_of(lse_ref[:, cols], head)
            delta_ref[...] = jnp.zeros_like(delta_ref)

            def first(base):
                keys = pl.ds(base, size)
                probs = jnp.exp(nt(k_ref[keys, :], query) + dead_ref[keys, 0:1] - lse)
                grad_probs = nt(v_ref[keys, :], grad)
                p_ref[keys, :] = probs
                dp_ref[keys, :] = grad_probs
                delta_ref[...] += jnp.sum(probs * grad_probs, axis=0, keepdims=True)

            each_chunk(count, size, first)
            delta = delta_ref[...]

            def second(base):
                keys = pl.ds(base, size)
                probs = p_ref[keys, :]
                dv_acc[keys, :] += nn(probs.astype(BF16), grad)
                low = (probs * (dp_ref[keys, :] - delta)).astype(BF16)
                dk_acc[keys, :] += nn(low, query)
                dqt_ref[:, cols] += tn(of_head(k_ref[keys, :], head), low)

            each_chunk(count, size, second)
    dq_ref[...] = dqt_ref[...].T.astype(BF16)
    dk_ref[...] = dk_acc[...].astype(BF16)
    dv_ref[...] = dv_acc[...].astype(BF16)


def skewed(row, block):
    before = row[:, (block - 1) * TILE : block * TILE] if block else jnp.zeros((1, TILE), F32)
    both = jnp.concatenate([before, row[:, block * TILE : (block + 1) * TILE]], axis=1)
    both = jnp.broadcast_to(both, (TILE, 2 * TILE))
    return pltpu.roll(both, 0, 1, stride=1, stride_axis=0)[:, TILE:]


def unskewed(tile):
    both = jnp.concatenate([jnp.zeros_like(tile), tile], axis=1)
    total = both[:8]
    for base in range(8, TILE, 8):
        total = total + pltpu.roll(both[base : base + 8], 2 * TILE - base, 1)
    row = lax.broadcasted_iota(jnp.int32, total.shape, 0)
    for bit in (1, 2, 4):
        total = jnp.where(row & bit != 0, pltpu.roll(total, 2 * TILE - bit, 1), total)
    return jnp.sum(total, axis=0, keepdims=True)


def self_scores(k_ref, query, tiles, start):
    keys = start + QUERIES
    columns = []
    for i in range(start // TILE, keys // TILE):
        columns.append(
            jnp.concatenate([tiles[max(i - j, 0)] for j in range(keys // TILE)], axis=0)
        )
    score = nt(k_ref[:keys, :], query) + jnp.concatenate(columns, axis=1)
    key = lax.broadcasted_iota(jnp.int32, score.shape, 0)
    spot = lax.broadcasted_iota(jnp.int32, score.shape, 1) + start
    return jnp.where(key <= spot, score, NEGATIVE)


def self_forward_pair(q_ref, k_ref, v_ref, bias_ref, out_ref, lse_ref, acc_ref):
    targets = q_ref.shape[0]
    for head in range(2):
        rows = slice(head * HEAD_DIM, (head + 1) * HEAD_DIM)
        row = bias_ref[head : head + 1, :]
        tiles = [skewed(row, block) for block in range(targets // TILE)]
        for start in range(0, targets, QUERIES):
            cols = slice(start, start + QUERIES)
            query = of_head(q_ref[cols, :], head)
            score = self_scores(k_ref, query, tiles, start)
            top = jnp.max(score, axis=0, keepdims=True)
            weight = jnp.exp(score - top)
            total = jnp.sum(weight, axis=0, keepdims=True)
            lse_ref[head : head + 1, cols] = top + jnp.log(total)
            probs = (weight * (1.0 / total)).astype(BF16)
            acc_ref[rows, cols] = tn(v_ref[: start + QUERIES, :], probs)[rows]
    out_ref[...] = acc_ref[...].T.astype(BF16)


def self_backward_pair(
    q_ref, k_ref, v_ref, bias_ref, lse_ref, go_ref, dq_ref, dk_ref, dv_ref, dbias_ref,
    dqt_ref, dk_acc, dv_acc,
):
    targets = q_ref.shape[0]
    dk_acc[...] = jnp.zeros_like(dk_acc)
    dv_acc[...] = jnp.zeros_like(dv_acc)
    blocks = targets // TILE
    dqt_ref[...] = jnp.zeros_like(dqt_ref)

    @pl.loop(0, 2)
    def each_head(head):
        row = row_of(bias_ref[...], head)
        tiles = [skewed(row, block) for block in range(blocks)]
        sums = [jnp.zeros((TILE, TILE), F32) for block in range(blocks)]
        for start in range(0, targets, QUERIES):
            cols = slice(start, start + QUERIES)
            keys = start + QUERIES
            query = of_head(q_ref[cols, :], head)
            grad = of_head(go_ref[cols, :], head)
            score = self_scores(k_ref, query, tiles, start)
            probs = jnp.exp(score - row_of(lse_ref[:, cols], head))
            grad_probs = nt(v_ref[:keys, :], grad)
            delta = jnp.sum(probs * grad_probs, axis=0, keepdims=True)
            dv_acc[:keys, :] += nn(probs.astype(BF16), grad)
            grad_scores = probs * (grad_probs - delta)
            for i in range(start // TILE, keys // TILE):
                for j in range(i + 1):
                    sums[i - j] = sums[i - j] + grad_scores[
                        j * TILE : (j + 1) * TILE, i * TILE - start : (i + 1) * TILE - start
                    ]
            low_scores = grad_scores.astype(BF16)
            dk_acc[:keys, :] += nn(low_scores, query)
            dqt_ref[:, cols] += tn(of_head(k_ref[:keys, :], head), low_scores)
        lines = [unskewed(tile) for tile in sums]
        parts = []
        for block in range(blocks):
            part = lines[block][:, TILE:]
            if block + 1 < blocks:
                part = part + lines[block + 1][:, :TILE]
            parts.append(part)
        row = jnp.concatenate(parts, axis=1)
        line = lax.broadcasted_iota(jnp.int32, dbias_ref.shape, 0)
        dbias_ref[...] = jnp.where(line == head, row, dbias_ref[...])
    dq_ref[...] = dqt_ref[...].T.astype(BF16)
    dk_ref[...] = dk_acc[...].astype(BF16)
    dv_ref[...] = dv_acc[...].astype(BF16)


def self_forward_kernel(
    normed_ref, bias_ref, *refs
):
    mixed_ref, attended_ref, lse_ref, partial_ref, weights_ref, acc_ref, sems = refs[2:]
    copies = fetch(refs[:2], [], weights_ref, sems)
    for copy in copies:
        copy.wait()
    part = attended_ref.shape[1]
    pairs = part // PAIR
    normed = normed_ref[...]

    @pl.loop(0, 3 * part // TILE)
    def project(i):
        cols = pl.ds(pl.multiple_of(i * TILE, TILE), TILE)
        mixed_ref[:, cols] = nn(normed, weights_ref[:, cols]).astype(BF16)

    def attend(pair, cols):
        self_forward_pair(
            *(mixed_ref.at[:, cols(i)] for i in range(3)),
            bias_ref.at[pair], attended_ref.at[:, cols(0)], lse_ref.at[pair], acc_ref,
        )

    each_pair(pairs, attend)
    partial_ref[...] = nt(attended_ref[...], weights_ref[:, 3 * part :]).astype(BF16)


def self_forward(normed, bias, quarters):
    targets, width = normed.shape
    columns = quarters[0].shape[1]
    part = columns // 4
    pairs = part // PAIR
    return kernel_call(
        self_forward_kernel,
        [normed, bias, *quarters],
        [
            struct((targets, 3 * part), BF16),
            struct((targets, part), BF16),
            struct((pairs, 8, targets), F32),
            struct((targets, width), BF16),
        ],
        [
            pltpu.VMEM((width, columns), BF16),
            pltpu.VMEM((PAIR, targets), F32),
            pltpu.SemaphoreType.DMA((6,)),
        ],
        in_specs=[IN_VMEM] * 2 + [IN_PLACE] * 2,
        time=12,
    )


def encoder_kernel(core_ref, own_ref, peer_ref, order_ref, *refs):
    encoded_ref, out_ref, weights_ref, sems = refs[2:]

    @pl.when(pl.program_id(0) == 0)
    def load():
        for copy in fetch([], refs[:2], weights_ref, sems, weights_ref.shape[1]):
            copy.wait()

    core, half = core_ref[0], own_ref.shape[1]
    own_rows = pl.ds(pl.multiple_of(core * half, half), half)
    peer_rows = pl.ds(pl.multiple_of(half - core * half, half), half)
    encoded = nn(own_ref[...], order_ref[own_rows, :]) + nn(peer_ref[...], order_ref[peer_rows, :])
    encoded_ref[...] = encoded.astype(BF16)
    encoded = encoded_ref[...]

    def project(cols):
        out_ref[:, cols] = nn(encoded, weights_ref[:, cols]).astype(BF16)

    each_tile(0, out_ref.shape[1], project)


def encoder_call(core, own, peer, order, quarters):
    capacity, half = own.shape
    width = 2 * half
    columns = quarters[0].shape[1] // 2
    size = min(capacity, KEYS)
    block = lambda cols: pl.BlockSpec((size, cols), lambda i: (i, 0))
    return kernel_call(
        encoder_kernel,
        [core, own, peer, order, *quarters],
        [struct((capacity, width), BF16), struct((capacity, columns), BF16)],
        [pltpu.VMEM((width, columns), BF16), pltpu.SemaphoreType.DMA((4,))],
        grid=(capacity // size,),
        in_specs=[IN_SMEM, block(half), block(half), IN_VMEM] + [IN_PLACE] * 2,
        out_specs=[block(width), block(columns)],
        time=8,
    )


def cross_forward_kernel(tokens_ref, partial_ref, peer_ref, gains_ref, kv_ref, dead_ref, *refs):
    (
        h_ref, normed_ref, query_ref, att_ref, lse_ref, *out_refs,
        weights_ref, s_ref, acc_ref, sems,
    ) = refs[2:]
    copies = fetch([], refs[:2], weights_ref, sems)
    gain = gains_ref[1:2, :]

    def norm(rows):
        value = tokens_ref[rows, :] + both_of(partial_ref, peer_ref, rows)
        h_ref[rows, :] = value
        normed_ref[rows, :] = (value * root_of(value) * gain).astype(BF16)

    each_rows(h_ref.shape[0], norm)
    for copy in copies:
        copy.wait()
    part = query_ref.shape[1]
    pairs = part // PAIR
    query_ref[...] = nn(normed_ref[...], weights_ref[:, :part]).astype(BF16)

    def attend(pair, cols):
        cross_forward_pair(
            query_ref.at[:, cols(0)], kv_ref.at[:, cols(0)], kv_ref.at[:, cols(1)], dead_ref,
            att_ref.at[:, cols(0)], lse_ref.at[pair], s_ref, acc_ref,
        )

    each_pair(pairs, attend)
    count = out_refs[0].shape[0]
    for i, out_ref in enumerate(out_refs):
        att = att_ref[i * count : (i + 1) * count, :]
        out_ref[...] = nt(att, weights_ref[:, part:]).astype(BF16)


def cross_forward(tokens, partial, peer, gains, key_value, dead, quarters):
    targets, width = tokens.shape
    capacity, columns = key_value.shape
    part = columns // 2
    pairs = part // PAIR
    return kernel_call(
        cross_forward_kernel,
        [tokens, partial, peer, gains, key_value, dead, *quarters],
        [
            struct((targets, width), F32),
            struct((targets, width), BF16),
            struct((targets, part), BF16),
            struct((targets, part), BF16),
            struct((pairs, 8, targets), F32),
            *[struct((targets // CHUNKS, width), BF16)] * CHUNKS,
        ],
        [
            pltpu.VMEM((width, columns), BF16),
            pltpu.VMEM((capacity, queries_of(capacity)), F32),
            pltpu.VMEM((PAIR, targets), F32),
            pltpu.SemaphoreType.DMA((4,)),
        ],
        in_specs=[IN_VMEM] * 6 + [IN_PLACE] * 2,
        time=16,
    )


def cross_whole_kernel(
    core_ref, own_ref, peer_ref, order_ref, tokens_ref, partial_ref, partial_in_ref, gains_ref,
    dead_ref, *refs
):
    (
        encoded_ref, kv_ref, h_ref, normed_ref, query_ref, att_ref, lse_ref, *out_refs,
        weights_ref, s_ref, acc_ref, sems,
    ) = refs[2:]
    copies = fetch([], refs[:2], weights_ref, sems)
    core, half = core_ref[0], own_ref.shape[1]
    own_rows = pl.ds(pl.multiple_of(core * half, half), half)
    peer_rows = pl.ds(pl.multiple_of(half - core * half, half), half)
    encoded = nn(own_ref[...], order_ref[own_rows, :]) + nn(peer_ref[...], order_ref[peer_rows, :])
    encoded_ref[...] = encoded.astype(BF16)
    gain = gains_ref[1:2, :]

    def norm(rows):
        value = tokens_ref[rows, :] + both_of(partial_ref, partial_in_ref, rows)
        h_ref[rows, :] = value
        normed_ref[rows, :] = (value * root_of(value) * gain).astype(BF16)

    each_rows(h_ref.shape[0], norm)
    for copy in copies:
        copy.wait()
    part = query_ref.shape[1]
    pairs = part // PAIR

    @pl.loop(0, 2 * part // WIDE)
    def project(i):
        cols = pl.ds(pl.multiple_of(i * WIDE, WIDE), WIDE)
        source = pl.ds(pl.multiple_of(2 * part + i * WIDE, WIDE), WIDE)
        kv_ref[:, cols] = nn(encoded_ref[...], weights_ref[:, source]).astype(BF16)

    query_ref[...] = nn(normed_ref[...], weights_ref[:, :part]).astype(BF16)

    def attend(pair, cols):
        cross_forward_pair(
            query_ref.at[:, cols(0)], kv_ref.at[:, cols(0)], kv_ref.at[:, cols(1)], dead_ref,
            att_ref.at[:, cols(0)], lse_ref.at[pair], s_ref, acc_ref,
        )

    each_pair(pairs, attend)
    count = out_refs[0].shape[0]
    for i, out_ref in enumerate(out_refs):
        att = att_ref[i * count : (i + 1) * count, :]
        out_ref[...] = nt(att, weights_ref[:, part : 2 * part]).astype(BF16)


def cross_whole(core, own, peer, order, tokens, partial, partial_in, gains, dead, quarters):
    targets, width = tokens.shape
    capacity = own.shape[0]
    columns = quarters[0].shape[1]
    part = columns // 4
    pairs = part // PAIR
    return kernel_call(
        cross_whole_kernel,
        [core, own, peer, order, tokens, partial, partial_in, gains, dead, *quarters],
        [
            struct((capacity, width), BF16),
            struct((capacity, 2 * part), BF16),
            struct((targets, width), F32),
            struct((targets, width), BF16),
            struct((targets, part), BF16),
            struct((targets, part), BF16),
            struct((pairs, 8, targets), F32),
            *[struct((targets // CHUNKS, width), BF16)] * CHUNKS,
        ],
        [
            pltpu.VMEM((width, columns), BF16),
            pltpu.VMEM((capacity, queries_of(capacity)), F32),
            pltpu.VMEM((PAIR, targets), F32),
            pltpu.SemaphoreType.DMA((4,)),
        ],
        in_specs=[IN_SMEM] + [IN_VMEM] * 8 + [IN_PLACE] * 2,
        time=24,
    )


def ffn_kernel(before_ref, gains_ref, cot_ref, cot_t_ref, *refs):
    chunks, refs = refs[: 2 * CHUNKS], refs[2 * CHUNKS :]
    h_out, down_out, back_out, *outs = refs[8:15]
    (
        weights_ref, grads_ref, h_ref, down_ref, back_ref, normed_ref, normed_t, in_sems, out_sems,
    ) = refs[15:]
    copies = fetch(refs[:4], refs[4:8], weights_ref, in_sems)
    gain = gains_ref[2:3, :]
    count = chunks[0].shape[0]
    for i, (partial_ref, peer_ref) in enumerate(zip(chunks[:CHUNKS], chunks[CHUNKS:])):

        def norm(rows):
            own = pl.ds(pl.multiple_of(rows.start + i * count, rows.size), rows.size)
            value = before_ref[own, :] + both_of(partial_ref, peer_ref, rows)
            h_ref[own, :] = value
            normed_ref[own, :] = (value * root_of(value) * gain).astype(BF16)

        each_rows(count, norm, 32)
    h_copy = pltpu.make_async_copy(h_ref, h_out, out_sems.at[36])
    h_copy.start()
    normed_t[...] = normed_ref[...].T
    down_ref[...] = jnp.zeros_like(down_ref)
    back_ref[...] = jnp.zeros_like(back_ref)
    for copy in copies:
        copy.wait()
    hidden = weights_ref.shape[1] // 3
    tiles = hidden // HIDDEN
    back_copy = pltpu.make_async_copy(back_ref, back_out, out_sems.at[37])

    def sends(i):
        copies = []
        for k in range(3):
            columns = slice(k * hidden + i * HIDDEN, k * hidden + (i + 1) * HIDDEN)
            first = 6 * (i * 3 + k)
            copies += deliver(grads_ref, outs, out_sems, columns, first)
        return copies

    @pl.loop(0, tiles)
    def tile(i):
        gates, ups, downs = (
            pl.ds(pl.multiple_of(k * hidden + i * HIDDEN, HIDDEN), HIDDEN) for k in range(3)
        )
        normed = normed_ref[...]
        gate = nn(normed, weights_ref[:, gates])
        up = nn(normed, weights_ref[:, ups])
        grad_act = nn(cot_ref[...], weights_ref[:, downs]).astype(BF16).astype(F32)
        square = gate * gate
        curve = jnp.tanh(GELU_ROOT * (gate + GELU_CUBE * (square * gate)))
        share = 0.5 * (1.0 + curve)
        gelu = gate * share
        slope = share + (0.5 * gate) * (1.0 - curve * curve) * (
            GELU_ROOT * (1.0 + (3.0 * GELU_CUBE) * square)
        )
        act = (gelu * up).astype(BF16)
        grad_gate = (grad_act * up * slope).astype(BF16)
        grad_up = (grad_act * gelu).astype(BF16)
        grads_ref[:, gates] = nn(normed_t[...], grad_gate).astype(BF16)
        grads_ref[:, ups] = nn(normed_t[...], grad_up).astype(BF16)
        grads_ref[:, downs] = nn(cot_t_ref[...], act).astype(BF16)
        for each in range(tiles):

            @pl.when(i == each)
            def send():
                for copy in sends(each):
                    copy.start()

        back_ref[...] += nt(grad_gate, weights_ref[:, gates]) + nt(grad_up, weights_ref[:, ups])

        @pl.when(i == tiles - 1)
        def send_back():
            back_copy.start()

        down_ref[...] += nt(act, weights_ref[:, downs])

    down_copy = pltpu.make_async_copy(down_ref, down_out, out_sems.at[38])
    down_copy.start()
    back_copy.wait()
    down_copy.wait()
    for i in range(tiles):
        for copy in sends(i):
            copy.wait()
    h_copy.wait()


def ffn_call(before, partials, peers, gains, cot, cot_t, quarters):
    targets, width = before.shape
    columns = 2 * quarters[0].shape[1]
    return kernel_call(
        ffn_kernel,
        [before, gains, cot, cot_t, *partials, *peers, *quarters],
        [struct((targets, width), F32)] * 3 + grad_structs(width, columns),
        [
            pltpu.VMEM((width, columns), BF16),
            pltpu.VMEM((width, columns), BF16),
            pltpu.VMEM((targets, width), F32),
            pltpu.VMEM((targets, width), F32),
            pltpu.VMEM((targets, width), F32),
            pltpu.VMEM((targets, width), BF16),
            pltpu.VMEM((width, targets), BF16),
            pltpu.SemaphoreType.DMA((8,)),
            pltpu.SemaphoreType.DMA((39,)),
        ],
        time=20,
        in_specs=[IN_VMEM] * (4 + 2 * CHUNKS) + [IN_PLACE] * 8,
        out_specs=[IN_PLACE] * 7,
    )


def cross_backward_kernel(
    cot_ref, partial_ref, peer_ref, h_ref, gains_ref, query_ref, kv_ref, dead_ref, lse_ref, *refs
):
    (
        g_ref, low_ref, dq_ref, dkv_ref, back_ref, gain_grad_ref,
        weights_ref, go_ref, p_ref, dp_ref, dqt_ref, dk_acc, dv_acc, delta_ref, sems,
    ) = refs[2:]
    copies = fetch([], refs[:2], weights_ref, sems)
    gain = gains_ref[2:3, :]
    gain_grad_ref[...] = jnp.zeros_like(gain_grad_ref)

    def norm(rows):
        back, gain_grad = norm_back(h_ref[rows, :], gain, partial_ref[rows, :] + peer_ref[rows, :])
        gain_grad_ref[0:1, :] += gain_grad
        value = cot_ref[rows, :].astype(F32) + back
        g_ref[rows, :] = value
        low_ref[rows, :] = value.astype(BF16)

    each_rows(h_ref.shape[0], norm)
    for copy in copies:
        copy.wait()
    part = query_ref.shape[1]
    pairs = part // PAIR
    go_ref[...] = nn(low_ref[...], weights_ref[:, part:]).astype(BF16)

    def attend(pair, cols):
        cross_backward_pair(
            query_ref.at[:, cols(0)], kv_ref.at[:, cols(0)], kv_ref.at[:, cols(1)], dead_ref,
            lse_ref.at[pair], go_ref.at[:, cols(0)],
            dq_ref.at[:, cols(0)], dkv_ref.at[:, cols(0)], dkv_ref.at[:, cols(1)],
            p_ref, dp_ref, dqt_ref, dk_acc, dv_acc, delta_ref,
        )

    each_pair(pairs, attend)
    back_ref[...] = nt(dq_ref[...], weights_ref[:, :part])


def cross_backward(cot, partial, peer, before, gains, query, key_value, dead, lse, quarters):
    targets, width = cot.shape
    capacity, columns = key_value.shape
    return kernel_call(
        cross_backward_kernel,
        [cot, partial, peer, before, gains, query, key_value, dead, lse, *quarters],
        [
            struct((targets, width), F32),
            struct((targets, width), BF16),
            struct(query.shape, BF16),
            struct(key_value.shape, BF16),
            struct((targets, width), F32),
            struct((8, width), F32),
        ],
        [
            pltpu.VMEM((width, columns), BF16),
            pltpu.VMEM(query.shape, BF16),
            pltpu.VMEM((capacity, queries_of(capacity)), F32),
            pltpu.VMEM((capacity, queries_of(capacity)), F32),
            pltpu.VMEM((PAIR, targets), F32),
            pltpu.VMEM((capacity, PAIR), F32),
            pltpu.VMEM((capacity, PAIR), F32),
            pltpu.VMEM((1, queries_of(capacity)), F32),
            pltpu.SemaphoreType.DMA((4,)),
        ],
        in_specs=[IN_VMEM] * 9 + [IN_PLACE] * 2,
        time=18,
    )


def cross_grads_kernel(
    core_ref, normed_ref, dq_ref, low_ref, att_ref, order_ref, encoded_ref, dkv_ref, *refs
):
    kept_ref, given_ref, *outs = refs[2:8]
    weights_ref, acc_ref, grads_ref, in_sems, out_sems = refs[8:]
    step = pl.program_id(0)
    part = dq_ref.shape[1]

    @pl.when(step == 0)
    def load():
        copies = fetch([], refs[:2], weights_ref, in_sems, weights_ref.shape[1])
        grads_ref[:, :part] = tn(normed_ref[...], dq_ref[...]).astype(BF16)
        grads_ref[:, part : 2 * part] = tn(low_ref[...], att_ref[...]).astype(BF16)
        acc_ref[...] = jnp.zeros_like(acc_ref)
        for copy in copies:
            copy.wait()

    encoded_t = encoded_ref[...].T

    def project(cols):
        acc_ref[:, cols] += nn(encoded_t, dkv_ref[:, cols])

    each_tile(0, acc_ref.shape[1], project)
    core, half = core_ref[0], kept_ref.shape[1]
    terms = nt(dkv_ref[...], weights_ref[...]).astype(BF16)
    own_cols = pl.ds(pl.multiple_of(core * half, half), half)
    peer_cols = pl.ds(pl.multiple_of(half - core * half, half), half)
    kept_ref[...] = nn(terms, order_ref[:, own_cols]).astype(BF16)
    given_ref[...] = nn(terms, order_ref[:, peer_cols]).astype(BF16)

    @pl.when(step == pl.num_programs(0) - 1)
    def store():
        grads_ref[:, 2 * part :] = acc_ref[...].astype(BF16)
        deliver_all(grads_ref, outs, out_sems)


def cross_grads(core, normed, dq, low_two, attended, order, encoded, dkv, quarters):
    capacity, width = encoded.shape
    columns = dkv.shape[1]
    size = min(capacity, KEYS)
    block = lambda cols: pl.BlockSpec((size, cols), lambda i: (i, 0))
    return kernel_call(
        cross_grads_kernel,
        [core, normed, dq, low_two, attended, order, encoded, dkv, *quarters],
        [struct((capacity, width // 2), BF16)] * 2 + grad_structs(width, 2 * columns),
        [
            pltpu.VMEM((width, columns), BF16),
            pltpu.VMEM((width, columns), F32),
            pltpu.VMEM((width, 2 * columns), BF16),
            pltpu.SemaphoreType.DMA((4,)),
            pltpu.SemaphoreType.DMA((6,)),
        ],
        grid=(capacity // size,),
        in_specs=[IN_SMEM] + [IN_VMEM] * 5 + [block(width), block(columns)] + [IN_PLACE] * 2,
        out_specs=[block(width // 2)] * 2 + [IN_PLACE] * 4,
        time=12,
    )


def self_backward_kernel(
    g_in_ref, partial_ref, peer_ref, h_ref, gains_ref, mixed_ref, bias_ref, lse_ref,
    attended_ref, normed_ref, tokens_ref, gain_three_ref, order_ref, labels_ref, *refs
):
    g_ref, back_ref, small_ref, *outs = refs[2:9]
    (
        weights_ref, grads_ref, low_ref, go_ref, dmixed_ref, dbias_ref,
        dqt_ref, dk_acc, dv_acc, gain_ref, pack_ref, in_sems, out_sems,
    ) = refs[9:]
    copies = fetch(refs[:2], [], weights_ref, in_sems)
    gain = gains_ref[1:2, :]
    gain_ref[...] = jnp.zeros_like(gain_ref)

    def norm(rows):
        back, gain_grad = norm_back(h_ref[rows, :], gain, partial_ref[rows, :] + peer_ref[rows, :])
        gain_ref[1:2, :] += gain_grad
        value = g_in_ref[rows, :] + back
        g_ref[rows, :] = value
        low_ref[rows, :] = value.astype(BF16)

    each_rows(h_ref.shape[0], norm)
    for copy in copies:
        copy.wait()
    part = attended_ref.shape[1]
    pairs = part // PAIR
    go_ref[...] = nn(low_ref[...], weights_ref[:, 3 * part :]).astype(BF16)
    dbias_ref[...] = jnp.zeros_like(dbias_ref)

    def attend(pair, cols):
        self_backward_pair(
            *(mixed_ref.at[:, cols(i)] for i in range(3)),
            bias_ref.at[pair], lse_ref.at[pair], go_ref.at[:, cols(0)],
            *(dmixed_ref.at[:, cols(i)] for i in range(3)),
            dbias_ref.at[pair], dqt_ref, dk_acc, dv_acc,
        )

    each_pair(pairs, attend)
    back_ref[...] = nt(dmixed_ref[...], weights_ref[:, : 3 * part])
    normed_t = normed_ref[...].T

    @pl.loop(0, 3 * part // TILE)
    def project(i):
        cols = pl.ds(pl.multiple_of(i * TILE, TILE), TILE)
        grads_ref[:, cols] = nn(normed_t, dmixed_ref[:, cols]).astype(BF16)

    grads_ref[:, 3 * part :] = tn(low_ref[...], attended_ref[...]).astype(BF16)

    def sums(rows):
        value = tokens_ref[rows, :]
        gain_ref[0:1, :] += jnp.sum(back_ref[rows, :] * value * root_of(value), axis=0, keepdims=True)

    each_rows(h_ref.shape[0], sums)
    gain_ref[2:3, :] = gain_three_ref[0:1, :]
    high, rest = halves(gain_ref[...])
    gain_ref[...] = nn(high, order_ref[...]) + nn(rest, order_ref[...])
    half = pack_ref.shape[1]
    pack_ref[0:3, :] = gain_ref[0:3, :half]
    pack_ref[3:6, :] = gain_ref[0:3, half:]
    bucket = lax.broadcasted_iota(jnp.int32, (labels_ref.shape[0], TILE), 1)
    which = jnp.where(labels_ref[:, 0:1] == bucket, 1.0, 0.0).astype(BF16)
    for pair in range(pairs):
        high, rest = halves(dbias_ref[pair])
        table = nn(high, which) + nn(rest, which)
        pack_ref[6:8, pair * TILE : (pair + 1) * TILE] = table[0:2]
    small_ref[...] = jnp.concatenate(halves(pack_ref[...]), axis=0)
    deliver_all(grads_ref, outs, out_sems)


def self_backward(
    g_in, partial, peer, before, gains, mixed, bias, lse, attended, normed, tokens,
    gain_three, order, labels, quarters,
):
    targets, width = g_in.shape
    part = attended.shape[1]
    pairs = part // PAIR
    return kernel_call(
        self_backward_kernel,
        [
            g_in, partial, peer, before, gains, mixed, bias, lse, attended, normed, tokens,
            gain_three, order, labels, *quarters,
        ],
        [
            struct((targets, width), F32),
            struct((targets, width), F32),
            struct((16, width // 2), BF16),
        ]
        + grad_structs(width, 4 * part),
        [
            pltpu.VMEM((width, 4 * part), BF16),
            pltpu.VMEM((width, 4 * part), BF16),
            pltpu.VMEM((targets, width), BF16),
            pltpu.VMEM((targets, part), BF16),
            pltpu.VMEM((targets, 3 * part), BF16),
            pltpu.VMEM((pairs, 8, targets), F32),
            pltpu.VMEM((PAIR, targets), F32),
            pltpu.VMEM((targets, PAIR), F32),
            pltpu.VMEM((targets, PAIR), F32),
            pltpu.VMEM((8, width), F32),
            pltpu.VMEM((8, width // 2), F32),
            pltpu.SemaphoreType.DMA((6,)),
            pltpu.SemaphoreType.DMA((6,)),
        ],
        in_specs=[IN_VMEM] * 14 + [IN_PLACE] * 2,
        out_specs=[IN_VMEM] * 3 + [IN_PLACE] * 4,
        time=22,
    )


def last_kernel(
    g_ref, partial_ref, peer_ref, tokens_ref, h_ref, down_ref, down_in_ref, gains_ref, order_ref,
    grad_ref, out_ref,
):
    order = order_ref[...]
    value = h_ref[...] + (down_ref[...] + down_in_ref[...])
    out_ref[...] = nn(value.astype(BF16), order).astype(BF16)
    back, unused = norm_back(tokens_ref[...], gains_ref[0:1, :], partial_ref[...] + peer_ref[...])
    high, rest = halves(g_ref[...] + back)
    grad_ref[...] = nn(high, order) + nn(rest, order)


def last_call(*ins):
    targets, width = ins[0].shape
    block = pl.BlockSpec((WIDE, width), lambda i: (i, 0))
    return kernel_call(
        last_kernel,
        list(ins),
        [struct((targets, width), F32), struct((targets, width), BF16)],
        [],
        time=1,
        grid=(targets // WIDE,),
        in_specs=[block] * 7 + [IN_VMEM] * 2,
        out_specs=[block] * 2,
    )


def shards(
    decoder_in,
    encoder_out,
    lengths,
    key_mask,
    assign,
    buckets,
    norm_one,
    norm_two,
    norm_three,
    self_query,
    self_key,
    self_value,
    self_output,
    cross_query,
    cross_key,
    cross_value,
    cross_output,
    ffn_gate,
    ffn_up,
    ffn_down,
    bias_table,
    cotangent,
    *,
    size,
):
    rank = lax.axis_index("dp")
    core = lax.axis_index("mp")
    targets, width = decoder_in.shape[1:]
    capacity = key_mask.shape[1]
    block = width // size
    outer = size // 4
    half = width // 2
    heads = bias_table.shape[1]
    which_core = core.reshape(1)

    spots = jnp.arange(width, dtype=jnp.int32)
    spot = spots // block
    masks = spot // (2 * outer) + 2 * (spot // outer % 2) + 4 * (spot % outer)
    source = jnp.broadcast_to(((rank ^ masks) * block + spots % block)[None], (8, width))

    weights = low(
        self_query, self_key, self_value, self_output.T,
        cross_query, cross_output.T, cross_key, cross_value,
    )
    if size == 16:
        pieces = [weights, swap(weights, 4, size), swap(weights, 8, size)]
    else:
        pieces = gather_outer(weights, size)
    gains = jnp.concatenate(
        [norm_one[None], norm_two[None], norm_three[None], jnp.zeros((5, width), F32)]
    )
    tokens, cot, cot_t, gains, order, turned, normed_one = kernel_call(
        rows_kernel,
        [decoder_in[0], cotangent[0], gains, source],
        [
            struct((targets, width), F32),
            struct((targets, width), BF16),
            struct((width, targets), BF16),
            struct((8, width), F32),
            struct((width, width), BF16),
            struct((width, width), BF16),
            struct((targets, width), BF16),
        ],
        [],
    )
    ffn = low(*after((ffn_gate, ffn_up, ffn_down.T), normed_one))

    sent = lax.dynamic_slice_in_dim(encoder_out, core * half, half, 2)[assign]
    pieces, normed_one = after((pieces, normed_one))
    if size == 16:
        more = swap(pieces[2], 4, size)
    weights = send_first(gather_first(pieces, size), size)
    if size == 16:
        more, ffn, sent = after((more, ffn, sent))
        more = gather_first([more], size)
        more, ffn, sent = after((more, ffn, sent))
        more = send_first(more, size)
    own = lax.all_to_all(sent, "dp", split_axis=0, concat_axis=0, tiled=True)
    own = own.reshape(capacity, half)
    labels, bias_table, lengths = after((buckets[:, :TILE], bias_table, lengths), weights[0])
    mine = assign[rank]
    positions = jnp.arange(capacity, dtype=jnp.int32)
    live = (positions < lengths[mine]) & ((key_mask[mine] == 1) | (positions == 0))
    dead = jnp.broadcast_to(jnp.where(live, 0.0, NEGATIVE)[:, None], (capacity, TILE))
    which = labels[None, :, 0] == jnp.arange(bias_table.shape[0], dtype=jnp.int32)[:, None]
    bias = jnp.sum(jnp.where(which[None], bias_table.T[:, :, None], 0.0), axis=1)
    bias = jnp.pad(bias.reshape(heads // 2, 2, targets), ((0, 0), (0, 6), (0, 0)))

    if size == 16:
        weights, more = after((weights, more))
        weights = [value for both in zip(weights, more) for value in both]
    weights, ffn, bias, dead = after((weights, ffn, bias, dead))
    weights = gather_second(weights, size, time=40)
    weights, ffn = after((weights, ffn))
    weights = send_second(weights, size)
    ffn = gather_outer(ffn, size, own)

    weights, own, ffn = after((weights, own, ffn))
    ffn = gather_first(ffn, size)
    ffn, weights, own = after((ffn, weights, own))
    ffn = send_first(ffn, size)
    own_peer = swap_cores(own)
    left, right = weights
    mixed, attended, lse_self, partial_one = self_forward(normed_one, bias, left)
    ffn, mixed, attended, lse_self, partial_one, own, own_peer = after(
        (ffn, mixed, attended, lse_self, partial_one, own, own_peer)
    )
    ffn = send_apart(ffn, size)
    peer_one = swap_cores(partial_one)
    if capacity <= KEYS:
        (
            encoded, key_value, h_one, normed_two, cross_q, cross_att, lse_cross, *partial_two
        ) = cross_whole(
            which_core, own, own_peer, order, tokens, partial_one, peer_one, gains, dead, right
        )
    else:
        encoded, key_value = encoder_call(which_core, own, own_peer, order, right)
        h_one, normed_two, cross_q, cross_att, lse_cross, *partial_two = cross_forward(
            tokens, partial_one, peer_one, gains, key_value, dead, right
        )
    peer_two = [swap_cores(value) for value in partial_two]
    h_two, partial_down, partial_three, *grads = ffn_call(
        h_one, partial_two, peer_two, gains, cot, cot_t, ffn[0] + ffn[1]
    )

    ffn = scatter_first(grads, size)
    peer_three = swap_cores(partial_three)
    peer_down = swap_cores(partial_down)
    g_two, low_two, dq, dkv, partial_four, gain_three = cross_backward(
        cot, partial_three, peer_three, h_two, gains, cross_q, key_value, dead, lse_cross, right
    )
    ffn, dq, dkv, low_two, partial_four, peer_down = after(
        (ffn, dq, dkv, low_two, partial_four, peer_down)
    )
    ffn = scatter_second_parts(ffn)
    ffn, dq, dkv, low_two, partial_four = after((ffn, dq, dkv, low_two, partial_four))
    ffn = scatter_second_send(ffn, size)
    peer_four = swap_cores(partial_four)
    kept, given, *grads = cross_grads(
        which_core, normed_two, dq, low_two, cross_att, turned, encoded, dkv, right
    )
    ffn, kept, given, grads, peer_four = after((ffn, kept, given, grads, peer_four))
    ffn = scatter_outer_parts(ffn, 0, 1)
    ffn, kept, given, grads, peer_four = after((ffn, kept, given, grads, peer_four))
    cross = scatter_first(grads, size)
    ffn = scatter_outer_send(ffn, size)
    g_one, partial_five, small, *grads = self_backward(
        g_two, partial_four, peer_four, h_one, gains, mixed, bias, lse_self, attended,
        normed_one, tokens, gain_three, turned, labels, left,
    )
    ffn, cross, given, partial_five, small, grads = after(
        (ffn, cross, given, partial_five, small, grads)
    )
    last = scatter_first(grads, size)
    peer_five = swap_cores(partial_five)
    taken = swap_cores(given)
    cross = scatter_second_send(scatter_second_parts(cross), size)

    terms = (kept.astype(F32) + taken.astype(F32)).astype(BF16).reshape(size, -1, half)
    count = terms.shape[1]
    terms = jnp.concatenate(
        [terms, jnp.broadcast_to(small[None], (size, *small.shape))], axis=1
    )
    back = lax.all_to_all(terms, "dp", split_axis=0, concat_axis=0, tiled=True)
    decoder_grad, layer_out = last_call(
        g_one, partial_five, peer_five, tokens, h_two, partial_down, peer_down, gains, turned
    )
    last, layer_out = after((last, layer_out))
    if size == 16:
        last = scatter_second_parts(last, time=40)
        cross = after(cross, last[-1])
        last = scatter_second_send(last, size)
        cross_keep, cross_out = scatter_pair_parts(cross)
        cross_in = swap(cross_out, 4, size)
        last, ffn = after((last, ffn), cross_out)
        last = scatter_outer_parts(last, 0, 1)
        last, back, ffn = after((last, back, ffn))
        last = scatter_outer_send(last, size)
        back, cross_in = after((back, cross_in), last[1])
        cross = scatter_pair_send(cross_keep, cross_in, size)
    else:
        cross = scatter_outer_send(scatter_outer_parts(cross, 0, 1), size)
        last = scatter_second_send(scatter_second_parts(last), size)
        last = scatter_outer_send(scatter_outer_parts(last, 0, 1), size)
    inverse = jnp.zeros_like(assign).at[assign].set(jnp.arange(size, dtype=jnp.int32))
    encoder_grad = back[:, :count][inverse]
    small = jnp.sum(back[:, count:].astype(F32), axis=0)
    small = small[:8] + small[8:]
    both = small + swap_cores(small)
    table = small[6:8].reshape(2, heads // 2, TILE)[:, :, : bias_table.shape[0]]
    grad_table = table.transpose(1, 0, 2).reshape(heads, -1).T
    grad_gains = [both[0:4:3].reshape(-1), small[1:5:3].reshape(-1), small[2:6:3].reshape(-1)]
    last, encoder_grad, grad_gains, grad_table = after(
        (last, encoder_grad, grad_gains, grad_table)
    )
    sum_ffn, sum_cross, sum_self = scatter_last(ffn), scatter_last(cross), scatter_last(last)

    def parts(value, count):
        step = value.shape[1] // count
        return [value[:, i * step : (i + 1) * step] for i in range(count)]

    grad_self_query, grad_self_key, grad_self_value, grad_output_one = parts(sum_self, 4)
    grad_cross_query, grad_output_two, grad_cross_key, grad_cross_value = parts(sum_cross, 4)
    grad_ffn_gate, grad_ffn_up, grad_ffn_down = parts(sum_ffn, 3)
    return (
        layer_out[None],
        decoder_grad[None],
        encoder_grad,
        *grad_gains,
        grad_self_query,
        grad_self_key,
        grad_self_value,
        grad_output_one.T,
        grad_cross_query,
        grad_cross_key,
        grad_cross_value,
        grad_output_two.T,
        grad_ffn_gate,
        grad_ffn_up,
        grad_ffn_down.T,
        grad_table,
    )


def solution(mesh):
    in_specs = (
        P("dp", None, None),
        P(None, "dp", None),
        P(),
        P(),
        P(),
        P(),
        P(),
        P(),
        P(),
        P("dp", "mp"),
        P("dp", "mp"),
        P("dp", "mp"),
        P("mp", "dp"),
        P("dp", "mp"),
        P("dp", "mp"),
        P("dp", "mp"),
        P("mp", "dp"),
        P("dp", "mp"),
        P("dp", "mp"),
        P("mp", "dp"),
        P(None, "mp"),
        P("dp", None, None),
    )
    out_specs = (
        P("dp", None, None),
        P("dp", None, None),
        P(None, "dp", "mp"),
        P(),
        P(),
        P(),
        P("dp", "mp"),
        P("dp", "mp"),
        P("dp", "mp"),
        P("mp", "dp"),
        P("dp", "mp"),
        P("dp", "mp"),
        P("dp", "mp"),
        P("mp", "dp"),
        P("dp", "mp"),
        P("dp", "mp"),
        P("mp", "dp"),
        P(None, "mp"),
    )
    body = functools.partial(shards, size=mesh.shape["dp"])
    return jax.shard_map(body, mesh=mesh, in_specs=in_specs, out_specs=out_specs, check_vma=False)
```
